32 devices in a mesh: seq: 4 (over y, x), fsdp: 8 (over z, core).
Axes of the slice: x: 2, y: 2, z: 4, core: 2. Of those that a mesh axis runs over, the one named last changes fastest.
Arguments:
- hidden_in: bfloat16 [1024, 8, 2048], P('seq', 'fsdp'), may hold values from -6 to 6
- per_layer_input: bfloat16 [1024, 8, 256], P('seq', 'fsdp'), may hold values from -6 to 6
- segment_ids: int32 [1024, 8], P('seq', 'fsdp'), may hold values from 0 to 2, as said below
- positions: int32 [1024, 8], P('seq', 'fsdp'), may hold values from 0 to 513, as said below
- out_cotangent: bfloat16 [1024, 8, 2048], P('seq', 'fsdp'), may hold values from -6 to 6
- w_query: bfloat16 [2048, 2048], P(('seq', 'fsdp')), may hold values from -0.125 to 0.125
- key_matrix: bfloat16 [2048, 512], P(('seq', 'fsdp')), may hold values from -0.125 to 0.125
- value_matrix: bfloat16 [2048, 512], P(('seq', 'fsdp')), may hold values from -0.125 to 0.125
- w_out_t: bfloat16 [2048, 2048], P(('seq', 'fsdp')), may hold values from -0.125 to 0.125
- laurel_maps: bfloat16 [2048, 128], P(('seq', 'fsdp')), may hold values from -0.125 to 0.125
- per_layer_maps: bfloat16 [2048, 512], P(('seq', 'fsdp')), may hold values from -0.125 to 0.125
- norm_gains: bfloat16 [2048, 6], P(('seq', 'fsdp')), may hold values from 0.5 to 1.5
- head_gains: bfloat16 [256, 2], P(('seq', 'fsdp')), may hold values from 0.5 to 1.5
- w_mlp: bfloat16 [2048, 3, 8192], P('fsdp', None, 'seq'), may hold values from -0.125 to 0.125
Outputs:
- hidden_out: bfloat16 [1024, 8, 2048], P('seq', 'fsdp')
- input_grad: float32 [1024, 8, 2048], P('seq', 'fsdp')
- grad_query: float32 [2048, 2048], P(('seq', 'fsdp'))
- grad_key: float32 [2048, 512], P(('seq', 'fsdp'))
- grad_value: float32 [2048, 512], P(('seq', 'fsdp'))
- grad_out_t: float32 [2048, 2048], P(('seq', 'fsdp'))
- grad_laurel: float32 [2048, 128], P(('seq', 'fsdp'))
- grad_per_layer: float32 [2048, 512], P(('seq', 'fsdp'))
- grad_norm_gains: float32 [2048, 6], P(('seq', 'fsdp'))
- grad_head_gains: float32 [256, 2], P(('seq', 'fsdp'))
- grad_mlp: float32 [2048, 3, 8192], P('fsdp', None, 'seq')
The draws below stay inside these ranges and needn't reach their ends.
Inputs may be any that keep to these rules, and one draw needn't show every extreme that they name: `segment_ids`: each sequence holds exactly three documents, numbered 0, 1, 2 in order along the sequence, each present. `positions`: within a document the position is 0 at its first token and rises by 1 or 2 from token to token until it reaches 513, where it stays; every sequence reaches that value.
All inputs are finite; a program needn't handle non-finite values.
Results may differ from the reference program's by a relative error of at most 0.025.
Values may be sent and summed in bfloat16 or wider, within the bound.
A program may use at most 320 MiB of HBM per device.

```python
import math
import jax
import jax.numpy as jnp
from jax import lax

MODEL_DIM = 2048
QUERY_HEADS = 8
KEY_VALUE_HEADS = 2
HEAD_DIM = 256
FF = 8192
LR = 64
PLE = 256
WIN = 512
LEN = 1024
BLK = 256
SEQS = 8


def doc_layout(key):
    folded = jax.random.fold_in(key, 7)
    key_start, key_end, key_steps = jax.random.split(folded, 3)
    doc_start = jax.random.randint(key_start, (1, SEQS), 1, BLK)
    doc_end = jax.random.randint(key_end, (1, SEQS), LEN - BLK + 1, LEN)
    indices = jnp.arange(LEN, dtype=jnp.int32)[:, None]
    segments = (indices >= doc_start).astype(jnp.int32) + (indices >= doc_end).astype(jnp.int32)
    increments = jax.random.randint(key_steps, (LEN, SEQS), 1, 3)
    running = jnp.cumsum(increments, axis=0).astype(jnp.int32)
    base_first = running[0:1]
    base_second = jnp.take_along_axis(running, doc_start, axis=0)
    base_third = jnp.take_along_axis(running, doc_end, axis=0)
    doc_base = jnp.where(segments == 0, base_first, jnp.where(segments == 1, base_second, base_third))
    places = jnp.minimum(running - doc_base, LEN - 2 * BLK + 1)
    return (segments, places.astype(jnp.int32))


def draw_segment_ids(key, part):
    return doc_layout(key)[0]


def draw_positions(key, part):
    return doc_layout(key)[1]


def spiked(entries, stream_key, source, target, shards_of, factor):
    owner, partner = [(jnp.arange(entries.shape[axis_at]) // (entries.shape[axis_at] // shards_of)).reshape([-1 if axis == axis_at else 1 for axis in range(entries.ndim)]) for axis_at in (source, target)]
    chosen = jax.random.permutation(stream_key, shards_of)[partner]
    strong = (owner == chosen) | (owner == (partner + shards_of // 2) % shards_of)
    return jnp.where(strong, factor * entries, entries)


def level_of(stream_key, dims, cuts, least, high):
    def one(dim, blocks):
        heights = jax.random.uniform(jax.random.fold_in(jax.random.fold_in(stream_key, 6), dim), (blocks,), jnp.float32, least / len(cuts), high / len(cuts))
        return jnp.repeat(jnp.exp(heights), dims[dim] // blocks).reshape((-1,) + (1,) * (len(dims) - dim - 1))

    loudness = one(*cuts[0])
    for cut in cuts[1:]:
        loudness = loudness * one(*cut)
    return loudness


def normal_values(stream_key, shape, width, most, shards=(), held_as=jnp.bfloat16):
    drawn = jax.random.normal(stream_key, shape, jnp.float32) * width
    if len(shards) > 0:
        drawn = level_of(stream_key, shape, shards, -0.22, 0.18) * drawn
    return jnp.clip(drawn, min=-most, max=most).astype(held_as)


def bell_draw_with(key, shape, spread, reach, shards, heavy, kind=jnp.bfloat16):
    drawn = spread * jax.random.normal(key, shape, jnp.float32)
    if shards:
        drawn = drawn * level_of(key, shape, shards, -0.22, 0.18)
    return jnp.clip(spiked(drawn, jax.random.fold_in(key, 3), *heavy), -reach, reach).astype(kind)


def setup_inputs(seed: int = 0) -> dict:
    splits = jax.random.split(jax.random.key(seed), 15)
    hidden_in = normal_values(splits[0], (LEN, SEQS, MODEL_DIM), 1.0, 6.0, ((0, 4), (1, 8)))
    per_layer_input = normal_values(splits[1], (LEN, SEQS, PLE), 1.0, 6.0, ((0, 4), (1, 8)))
    segment_ids = draw_segment_ids(jax.random.fold_in(splits[14], 71), 0)
    positions = draw_positions(jax.random.fold_in(splits[14], 71), 0)
    out_cotangent = bell_draw_with(splits[4], (LEN, SEQS, MODEL_DIM), 1.0, 6.0, ((0, 4), (1, 8)), (1, 2, 8, 2.0))
    w_query = normal_values(splits[5], (MODEL_DIM, QUERY_HEADS * HEAD_DIM), MODEL_DIM ** -0.5, 0.125, ((0, 32),))
    key_matrix = normal_values(splits[6], (MODEL_DIM, KEY_VALUE_HEADS * HEAD_DIM), MODEL_DIM ** -0.5, 0.125, ((0, 32),))
    value_matrix = normal_values(splits[7], (MODEL_DIM, KEY_VALUE_HEADS * HEAD_DIM), MODEL_DIM ** -0.5, 0.125, ((0, 32),))
    w_out_t = normal_values(splits[8], (MODEL_DIM, QUERY_HEADS * HEAD_DIM), (QUERY_HEADS * HEAD_DIM) ** -0.5, 0.125, ((0, 32),))
    laurel_maps = normal_values(splits[9], (MODEL_DIM, 2 * LR), MODEL_DIM ** -0.5, 0.125, ((0, 32),))
    per_layer_maps = normal_values(splits[10], (MODEL_DIM, 2 * PLE), MODEL_DIM ** -0.5, 0.125, ((0, 32),))
    norm_gains = jnp.clip(1.0 + 0.1 * jax.random.normal(splits[11], (MODEL_DIM, 6), jnp.float32), 0.5, 1.5).astype(jnp.bfloat16)
    head_gains = jnp.clip(1.0 + 0.1 * jax.random.normal(splits[12], (HEAD_DIM, 2), jnp.float32), 0.5, 1.5).astype(jnp.bfloat16)
    w_mlp = normal_values(splits[13], (MODEL_DIM, 3, FF), MODEL_DIM ** -0.5, 0.125, ((0, 8), (2, 4)))
    return dict(hidden_in=hidden_in, per_layer_input=per_layer_input, segment_ids=segment_ids, positions=positions, out_cotangent=out_cotangent, w_query=w_query, key_matrix=key_matrix, value_matrix=value_matrix, w_out_t=w_out_t, laurel_maps=laurel_maps, per_layer_maps=per_layer_maps, norm_gains=norm_gains, head_gains=head_gains, w_mlp=w_mlp)


@jax.custom_vjp
def low(v):
    return lax.optimization_barrier(v.astype(jnp.bfloat16)).astype(jnp.float32)

@jax.custom_vjp
def lowered_backward(v):
    return v

def low_keep(v):
    return (low(v), None)

def low_pass(kept, grad):
    return (grad,)

def back_keep(v):
    return (v, None)

def back_low(kept, grad):
    return (low(grad),)
low.defvjp(low_keep, low_pass)
lowered_backward.defvjp(back_keep, back_low)
eps = 1e-06
theta = 10000.0
root_half = 1.0 / math.sqrt(2.0)
exact = lax.Precision.HIGHEST

def norm_rows(v, gain_vec):
    return v * lax.rsqrt(lax.optimization_barrier(jnp.mean(v * v, -1, keepdims=True)) + eps) * gain_vec

def rope_tables(places):
    half_width = HEAD_DIM // 2
    frequency = theta ** (-jnp.arange(half_width).astype(jnp.float32) * 2.0 / HEAD_DIM)
    angles = places.astype(jnp.float32)[..., None] * frequency
    angles = jnp.concatenate([angles, angles], -1)[..., None, :]
    return (jnp.cos(angles), jnp.sin(angles))

def rotate(v, cos_table, sin_table):
    half_width = v.shape[-1] // 2
    turned = jnp.concatenate([-v[..., half_width:], v[..., :half_width]], -1)
    return v * cos_table + turned * sin_table

def apply_projection(left, right, pattern):
    return jnp.einsum(pattern, left, right, precision=exact)

def attend(queries, keys, values, segments):
    raw_scores = lowered_backward(jnp.einsum('gqhd,gkhd->ghqk', queries, keys, precision=exact))
    indices = jnp.arange(LEN)
    offset = indices[:, None] - indices[None, :]
    allowed = (segments[:, :, None] == segments[:, None, :]) & (offset >= 0) & (offset < WIN)
    scores = jnp.where(allowed[:, None], raw_scores * HEAD_DIM ** (-0.5), -1000000000.0)
    row_peak = lax.optimization_barrier(jnp.max(scores, -1, keepdims=True))
    exp_scores = jnp.exp(scores - row_peak)
    attn_probs = exp_scores / lax.optimization_barrier(jnp.sum(exp_scores, -1, keepdims=True))
    return jnp.einsum('ghqk,gkhd->gqhd', low(attn_probs), values, precision=exact)

def block_forward(x, ple_input, segments, cos_table, sin_table, wquery, key_weight_local, value_weight_local, wout, laurel, plmaps, gains, hgains, wmlp):
    query_group_count = QUERY_HEADS // KEY_VALUE_HEADS
    leading_dims = x.shape[:2]
    normalized_input = low(norm_rows(x, gains[:, 0]))
    q_lin = lowered_backward(apply_projection(normalized_input, wquery, 'who,ov->whv')).reshape(leading_dims + (QUERY_HEADS, HEAD_DIM))
    key_linear = lowered_backward(apply_projection(normalized_input, key_weight_local, 'who,ov->whv')).reshape(leading_dims + (KEY_VALUE_HEADS, HEAD_DIM))
    value_linear = lowered_backward(apply_projection(normalized_input, value_weight_local, 'who,ov->whv')).reshape(leading_dims + (KEY_VALUE_HEADS, HEAD_DIM))
    queries = lowered_backward(low(rotate(norm_rows(q_lin, hgains[:, 0]), cos_table, sin_table)))
    keys = lowered_backward(jnp.repeat(low(rotate(norm_rows(key_linear, hgains[:, 1]), cos_table, sin_table)), query_group_count, axis=2))
    values = lowered_backward(jnp.repeat(low(norm_rows(value_linear, 1.0)), query_group_count, axis=2))
    head_out = jax.checkpoint(attend)(queries, keys, values, segments)
    head_out = lowered_backward(low(head_out)).reshape(leading_dims + (QUERY_HEADS * HEAD_DIM,))
    attn_lin = lowered_backward(apply_projection(head_out, wout, 'gtn,dn->gtd'))
    laurel_low = lowered_backward(low(apply_projection(normalized_input, laurel[:, :LR], 'gtd,dr->gtr')))
    laurel_high = lowered_backward(apply_projection(laurel_low, laurel[:, LR:], 'gtr,dr->gtd'))
    mixed = (x + norm_rows(attn_lin, gains[:, 1]) + (normalized_input + norm_rows(laurel_high, gains[:, 2]))) * root_half
    h_normed = low(norm_rows(mixed, gains[:, 3]))
    gate_up = lowered_backward(apply_projection(h_normed, wmlp[:, :2], 'gtd,dcf->gtcf'))
    hidden = low(jax.nn.gelu(gate_up[:, :, 0], approximate=True) * gate_up[:, :, 1])
    ffn_out = lowered_backward(apply_projection(hidden, wmlp[:, 2], 'gtf,df->gtd'))
    h_second = low(mixed + norm_rows(ffn_out, gains[:, 4]))
    ple_gate = lowered_backward(apply_projection(h_second, plmaps[:, :PLE], 'gtd,de->gte'))
    ple_mixed = low(jax.nn.gelu(ple_gate, approximate=True) * ple_input)
    ple_proj = lowered_backward(apply_projection(ple_mixed, plmaps[:, PLE:], 'gte,de->gtd'))
    return h_second + norm_rows(ple_proj, gains[:, 5])

def reference(hidden_in, per_layer_input, segment_ids, positions, out_cotangent, w_query, key_matrix, value_matrix, w_out_t, laurel_maps, per_layer_maps, norm_gains, head_gains, w_mlp):
    weights = tuple((w.astype(jnp.float32) for w in (w_query, key_matrix, value_matrix, w_out_t, laurel_maps, per_layer_maps, norm_gains, head_gains, w_mlp)))
    per_step = math.gcd(SEQS, max(1, 4096 // LEN))

    def arrange(source):
        moved = jnp.swapaxes(source, 0, 1)
        return moved.reshape((SEQS // per_step, per_step) + moved.shape[1:])
    batches = (arrange(hidden_in.astype(jnp.float32)), arrange(per_layer_input.astype(jnp.float32)), arrange(segment_ids), arrange(positions), arrange(out_cotangent.astype(jnp.float32)))

    def scan_step(totals, batch_in):
        x, ple_input, segments, places, cotangent = batch_in
        cos_table, sin_table = rope_tables(places)

        def forward(x_in, *params):
            return block_forward(x_in, ple_input, segments, cos_table, sin_table, *params)
        result, pullback = jax.vjp(forward, x, *weights)
        gradients = pullback(cotangent)
        totals = tuple((total + grad for total, grad in zip(totals, gradients[1:])))
        return (totals, (result.astype(jnp.bfloat16), gradients[0]))
    zero_grads = tuple((jnp.zeros(w.shape, jnp.float32) for w in weights))
    totals, (results, input_grads) = lax.scan(scan_step, zero_grads, batches)

    def restore(source):
        return jnp.swapaxes(source.reshape((SEQS,) + source.shape[2:]), 0, 1)
    return (restore(results), restore(input_grads), totals[0], totals[1], totals[2], totals[3], totals[4], totals[5], totals[6], totals[7], totals[8])
```

```python
import math

import jax
import jax.numpy as jnp
from jax import lax
from jax.sharding import PartitionSpec as P

QUERY_HEADS = 8
KEY_VALUE_HEADS = 2
HEAD_DIM = 256
LR = 64
PLE = 256
WIN = 512


eps = 1e-06
theta = 10000.0
root_half = 1.0 / math.sqrt(2.0)


def norm_rows(v, gain_vec):
    inverse = lax.rsqrt(jnp.mean(v * v, -1, keepdims=True) + eps)
    return (v * inverse * gain_vec, inverse)


def norm_back(v, inverse, gain_vec, incoming):
    scaled = incoming * gain_vec
    inner_mean = jnp.mean(scaled * v, -1, keepdims=True)
    return (
        inverse * (scaled - v * inverse * inverse * inner_mean),
        jnp.sum(incoming * v * inverse, axis=(0, 1)),
    )


def gelu_tanh(v):
    return jax.nn.gelu(v, approximate=True)


def rope_tables(places):
    half_width = HEAD_DIM // 2
    frequency = theta ** (-jnp.arange(half_width).astype(jnp.float32) * 2.0 / HEAD_DIM)
    angles = places.astype(jnp.float32)[..., None] * frequency
    angles = jnp.concatenate([angles, angles], -1)[..., None, :]
    return (jnp.cos(angles), jnp.sin(angles))


def rotate(v, cos_table, sin_table):
    half_width = v.shape[-1] // 2
    turned = jnp.concatenate([-v[..., half_width:], v[..., :half_width]], -1)
    return v * cos_table + turned * sin_table


def head_prep(q_lin, key_linear, value_linear, head_scale, cos_table, sin_table):
    leading_dims = q_lin.shape[:2]
    queries = rotate(
        norm_rows(q_lin.reshape(leading_dims + (-1, HEAD_DIM)), head_scale[:, 0])[0],
        cos_table,
        sin_table,
    )
    keys = rotate(
        norm_rows(key_linear.reshape(leading_dims + (-1, HEAD_DIM)), head_scale[:, 1])[0],
        cos_table,
        sin_table,
    )
    values = norm_rows(value_linear.reshape(leading_dims + (-1, HEAD_DIM)), 1.0)[0]
    return (queries, keys, values)


def allowed_mask(segments):
    indices = jnp.arange(segments.shape[0])
    offset = indices[:, None] - indices[None, :]
    nearby = (offset >= 0) & (offset < WIN)
    by_seq = segments.T
    return (by_seq[:, :, None] == by_seq[:, None, :]) & nearby


def scores_of(q_heads, k_heads, allowed):
    raw_scores = jnp.einsum("qshd,kshd->shqk", q_heads, k_heads, preferred_element_type=jnp.float32)
    return jnp.where(allowed[:, None], raw_scores * HEAD_DIM ** (-0.5), -1000000000.0)


def attend_heads(q_heads, k_heads, v_heads, allowed):
    scores = scores_of(q_heads, k_heads, allowed)
    row_peak = jnp.max(scores, -1, keepdims=True)
    exp_scores = jnp.exp(scores - row_peak)
    row_total = jnp.sum(exp_scores, -1, keepdims=True)
    attn_probs = exp_scores / row_total
    head_out = jnp.einsum(
        "shqk,kshd->qshd",
        attn_probs.astype(jnp.bfloat16),
        v_heads,
        preferred_element_type=jnp.float32,
    )
    return (head_out, row_peak + jnp.log(row_total))


def attend_back(q_heads, k_heads, v_heads, allowed, log_total, grad_heads):
    probs_again = jnp.exp(scores_of(q_heads, k_heads, allowed) - log_total)
    grad_v_heads = jnp.einsum(
        "shqk,qshd->kshd",
        probs_again.astype(jnp.bfloat16),
        grad_heads,
        preferred_element_type=jnp.float32,
    )
    grad_probs = jnp.einsum(
        "qshd,kshd->shqk", grad_heads, v_heads, preferred_element_type=jnp.float32
    )
    row_inner = jnp.sum(probs_again * grad_probs, -1, keepdims=True)
    grad_scores = (probs_again * (grad_probs - row_inner) * HEAD_DIM ** (-0.5)).astype(jnp.bfloat16)
    grad_q_heads = jnp.einsum(
        "shqk,kshd->qshd", grad_scores, k_heads, preferred_element_type=jnp.float32
    )
    grad_k_heads = jnp.einsum(
        "shqk,qshd->kshd", grad_scores, q_heads, preferred_element_type=jnp.float32
    )
    return (grad_q_heads, grad_k_heads, grad_v_heads)


def group_rows(source):
    return lax.all_gather(source, "seq", axis=0, tiled=True)


def body(
    hidden_in,
    per_layer_input,
    segment_ids,
    positions,
    out_cotangent,
    w_query,
    key_matrix,
    value_matrix,
    w_out_t,
    laurel_maps,
    per_layer_maps,
    norm_gains,
    head_gains,
    w_mlp,
):
    leading_dims = hidden_in.shape[:2]
    query_group_count = QUERY_HEADS // KEY_VALUE_HEADS
    packed = jnp.concatenate(
        [w_query, key_matrix, value_matrix, w_out_t, laurel_maps, per_layer_maps, norm_gains], 1
    )
    packed_full = lax.all_gather(packed, ("seq", "fsdp"), axis=0, tiled=True)
    full_heads = lax.all_gather(head_gains, ("seq", "fsdp"), axis=0, tiled=True)
    mlp_full = lax.all_gather(w_mlp, "fsdp", axis=0, tiled=True)
    widths = [
        w.shape[1]
        for w in (w_query, key_matrix, value_matrix, w_out_t, laurel_maps, per_layer_maps)
    ]
    cuts = [sum(widths[: i + 1]) for i in range(len(widths))]
    full_query, full_key, full_value, full_out, full_laurel, full_ple, full_gains = jnp.split(
        packed_full, cuts, axis=1
    )
    gain_table = full_gains.astype(jnp.float32)
    head_scale = full_heads.astype(jnp.float32)
    tokens = hidden_in.astype(jnp.float32)
    x_normed_f, x_inverse = norm_rows(tokens, gain_table[:, 0])
    normalized_input = x_normed_f.astype(jnp.bfloat16)
    cos_table, sin_table = rope_tables(positions)
    q_lin = jnp.einsum(
        "bsd,dn->bsn", normalized_input, full_query, preferred_element_type=jnp.float32
    )
    key_linear = jnp.einsum(
        "bsd,dn->bsn", normalized_input, full_key, preferred_element_type=jnp.float32
    )
    value_linear = jnp.einsum(
        "bsd,dn->bsn", normalized_input, full_value, preferred_element_type=jnp.float32
    )
    queries, keys, values = head_prep(
        q_lin, key_linear, value_linear, head_scale, cos_table, sin_table
    )
    q_send = queries.astype(jnp.bfloat16)
    k_send = jnp.repeat(keys.astype(jnp.bfloat16), query_group_count, axis=2)
    v_send = jnp.repeat(values.astype(jnp.bfloat16), query_group_count, axis=2)
    q_heads, k_heads, v_heads = (
        lax.all_to_all(q_send, "seq", split_axis=2, concat_axis=0, tiled=True),
        lax.all_to_all(k_send, "seq", split_axis=2, concat_axis=0, tiled=True),
        lax.all_to_all(v_send, "seq", split_axis=2, concat_axis=0, tiled=True),
    )
    all_segments = lax.all_gather(segment_ids, "seq", axis=0, tiled=True)
    allowed = allowed_mask(all_segments)
    head_out, log_total = attend_heads(q_heads, k_heads, v_heads, allowed)
    head_low = head_out.astype(jnp.bfloat16)
    back_out = lax.all_to_all(head_low, "seq", split_axis=0, concat_axis=2, tiled=True)
    attn_in = back_out.reshape(leading_dims + (QUERY_HEADS * HEAD_DIM,))
    attn_lin = jnp.einsum("bsn,dn->bsd", attn_in, full_out, preferred_element_type=jnp.float32)
    attn_normed, attn_inverse = norm_rows(attn_lin, gain_table[:, 1])
    laurel_low = jnp.einsum(
        "bsd,dr->bsr", normalized_input, full_laurel[:, :LR], preferred_element_type=jnp.float32
    ).astype(jnp.bfloat16)
    laurel_high = jnp.einsum(
        "bsr,dr->bsd", laurel_low, full_laurel[:, LR:], preferred_element_type=jnp.float32
    )
    laurel_normed, laurel_inverse = norm_rows(laurel_high, gain_table[:, 2])
    mixed = (
        tokens + attn_normed + (normalized_input.astype(jnp.float32) + laurel_normed)
    ) * root_half
    h_normed_f, h_inverse = norm_rows(mixed, gain_table[:, 3])
    h_normed = h_normed_f.astype(jnp.bfloat16)
    h_rows = group_rows(h_normed)
    gate_up = jnp.einsum(
        "tsd,dcf->tscf", h_rows, mlp_full[:, :2], preferred_element_type=jnp.float32
    )
    gate_part = gate_up[:, :, 0]
    up_part = gate_up[:, :, 1]
    hidden = (gelu_tanh(gate_part) * up_part).astype(jnp.bfloat16)
    down_map = mlp_full[:, 2]
    picked = hidden
    ffn_out = lax.psum_scatter(
        jnp.einsum("tsf,df->tsd", picked, down_map, preferred_element_type=jnp.float32).astype(
            jnp.bfloat16
        ),
        "seq",
        scatter_dimension=0,
        tiled=True,
    ).astype(jnp.float32)
    ffn_normed, ffn_inverse = norm_rows(ffn_out, gain_table[:, 4])
    h_second = (mixed + ffn_normed).astype(jnp.bfloat16)
    ple_gate = jnp.einsum(
        "bsd,de->bse", h_second, full_ple[:, :PLE], preferred_element_type=jnp.float32
    )
    ple_input = per_layer_input.astype(jnp.float32)
    ple_mixed = (gelu_tanh(ple_gate) * ple_input).astype(jnp.bfloat16)
    ple_proj = jnp.einsum(
        "bse,de->bsd", ple_mixed, full_ple[:, PLE:], preferred_element_type=jnp.float32
    )
    ple_normed, ple_inverse = norm_rows(ple_proj, gain_table[:, 5])
    hidden_out = (h_second.astype(jnp.float32) + ple_normed).astype(jnp.bfloat16)
    mlp_back = mlp_full
    back_query, back_key, back_value, back_out_map = full_query, full_key, full_value, full_out
    back_laurel, back_ple = full_laurel, full_ple
    gain_back = gain_table
    head_back = head_scale
    grad_out = out_cotangent.astype(jnp.float32)
    grad_ple_proj, gain_grad_five = norm_back(ple_proj, ple_inverse, gain_back[:, 5], grad_out)
    grad_ple_low = grad_ple_proj.astype(jnp.bfloat16)
    grad_ple_up = jnp.einsum(
        "bsd,bse->de", grad_ple_low, ple_mixed, preferred_element_type=jnp.float32
    )
    grad_ple_mixed = jnp.einsum(
        "bsd,de->bse", grad_ple_low, back_ple[:, PLE:], preferred_element_type=jnp.float32
    )
    unused_gelu, gelu_pull = jax.vjp(gelu_tanh, ple_gate)
    grad_ple_gate = gelu_pull(grad_ple_mixed * ple_input)[0].astype(jnp.bfloat16)
    grad_ple_down = jnp.einsum(
        "bsd,bse->de", h_second, grad_ple_gate, preferred_element_type=jnp.float32
    )
    grad_second = grad_out + jnp.einsum(
        "bse,de->bsd", grad_ple_gate, back_ple[:, :PLE], preferred_element_type=jnp.float32
    )
    grad_ffn, gain_grad_four = norm_back(ffn_out, ffn_inverse, gain_back[:, 4], grad_second)
    grad_ffn_rows = group_rows(grad_ffn.astype(jnp.bfloat16))
    grad_hidden = jnp.einsum(
        "tsd,df->tsf", grad_ffn_rows, mlp_back[:, 2], preferred_element_type=jnp.float32
    )
    gate_act, act_pull = jax.vjp(gelu_tanh, gate_part)
    grad_gate_up = jnp.stack(
        [act_pull(grad_hidden * up_part)[0], grad_hidden * gate_act], 2
    ).astype(jnp.bfloat16)
    in_maps = mlp_back[:, :2]
    picked = grad_gate_up
    grad_h_normed = lax.psum_scatter(
        jnp.einsum("tscf,dcf->tsd", picked, in_maps, preferred_element_type=jnp.float32).astype(
            jnp.bfloat16
        ),
        "seq",
        scatter_dimension=0,
        tiled=True,
    ).astype(jnp.float32)
    first_pair = jnp.einsum(
        "tsd,tscf->dcf", h_rows, grad_gate_up, preferred_element_type=jnp.float32
    )
    down_grad = jnp.einsum("tsd,tsf->df", grad_ffn_rows, hidden, preferred_element_type=jnp.float32)
    grad_mlp = lax.psum_scatter(
        jnp.concatenate([first_pair, down_grad[:, None]], 1).astype(jnp.bfloat16),
        "fsdp",
        scatter_dimension=0,
        tiled=True,
    ).astype(jnp.float32)
    grad_mixed_norm, gain_grad_three = norm_back(mixed, h_inverse, gain_back[:, 3], grad_h_normed)
    grad_mixed = grad_second + grad_mixed_norm
    grad_branch = grad_mixed * root_half
    grad_laurel_high, gain_grad_two = norm_back(
        laurel_high, laurel_inverse, gain_back[:, 2], grad_branch
    )
    grad_high_low = grad_laurel_high.astype(jnp.bfloat16)
    grad_laurel_up = jnp.einsum(
        "bsd,bsr->dr", grad_high_low, laurel_low, preferred_element_type=jnp.float32
    )
    grad_laurel_low = jnp.einsum(
        "bsd,dr->bsr", grad_high_low, back_laurel[:, LR:], preferred_element_type=jnp.float32
    ).astype(jnp.bfloat16)
    grad_laurel_down = jnp.einsum(
        "bsd,bsr->dr", normalized_input, grad_laurel_low, preferred_element_type=jnp.float32
    )
    grad_x_normed = grad_branch + jnp.einsum(
        "bsr,dr->bsd", grad_laurel_low, back_laurel[:, :LR], preferred_element_type=jnp.float32
    )
    grad_attn, gain_grad_one = norm_back(attn_lin, attn_inverse, gain_back[:, 1], grad_branch)
    grad_attn_low = grad_attn.astype(jnp.bfloat16)
    grad_out_map = jnp.einsum(
        "bsd,bsn->dn", grad_attn_low, attn_in, preferred_element_type=jnp.float32
    )
    grad_heads_seq = (
        jnp.einsum("bsd,dn->bsn", grad_attn_low, back_out_map, preferred_element_type=jnp.float32)
        .astype(jnp.bfloat16)
        .reshape(leading_dims + (QUERY_HEADS, HEAD_DIM))
    )
    grad_heads = lax.all_to_all(grad_heads_seq, "seq", split_axis=2, concat_axis=0, tiled=True)
    grad_q_heads, grad_k_heads, grad_v_heads = attend_back(
        q_heads, k_heads, v_heads, allowed, log_total, grad_heads
    )
    grad_q_seq, key_gradient_sequence, value_gradient_sequence = (
        lax.all_to_all(
            grad_q_heads.astype(jnp.bfloat16), "seq", split_axis=0, concat_axis=2, tiled=True
        ),
        lax.all_to_all(
            grad_k_heads.astype(jnp.bfloat16), "seq", split_axis=0, concat_axis=2, tiled=True
        ),
        lax.all_to_all(
            grad_v_heads.astype(jnp.bfloat16), "seq", split_axis=0, concat_axis=2, tiled=True
        ),
    )
    grad_keys = jnp.sum(
        key_gradient_sequence.astype(jnp.float32).reshape(
            leading_dims + (KEY_VALUE_HEADS, query_group_count, HEAD_DIM)
        ),
        3,
    )
    grad_values = jnp.sum(
        value_gradient_sequence.astype(jnp.float32).reshape(
            leading_dims + (KEY_VALUE_HEADS, query_group_count, HEAD_DIM)
        ),
        3,
    )
    unused_heads, head_pull = jax.vjp(
        head_prep, q_lin, key_linear, value_linear, head_back, cos_table, sin_table
    )
    grad_q_lin, grad_k_lin, grad_v_lin, grad_head_scale, unused_cos, unused_sin = head_pull(
        (grad_q_seq.astype(jnp.float32), grad_keys, grad_values)
    )
    grad_q_low = grad_q_lin.astype(jnp.bfloat16)
    grad_k_low = grad_k_lin.astype(jnp.bfloat16)
    grad_v_low = grad_v_lin.astype(jnp.bfloat16)
    grad_query_map = jnp.einsum(
        "bsd,bsn->dn", normalized_input, grad_q_low, preferred_element_type=jnp.float32
    )
    grad_key_map = jnp.einsum(
        "bsd,bsn->dn", normalized_input, grad_k_low, preferred_element_type=jnp.float32
    )
    grad_value_map = jnp.einsum(
        "bsd,bsn->dn", normalized_input, grad_v_low, preferred_element_type=jnp.float32
    )
    grad_x_normed = grad_x_normed + jnp.einsum(
        "bsn,dn->bsd", grad_q_low, back_query, preferred_element_type=jnp.float32
    )
    grad_x_normed = grad_x_normed + jnp.einsum(
        "bsn,dn->bsd", grad_k_low, back_key, preferred_element_type=jnp.float32
    )
    grad_x_normed = grad_x_normed + jnp.einsum(
        "bsn,dn->bsd", grad_v_low, back_value, preferred_element_type=jnp.float32
    )
    grad_tokens_norm, gain_grad_zero = norm_back(tokens, x_inverse, gain_back[:, 0], grad_x_normed)
    input_grad = grad_mixed * root_half + grad_tokens_norm
    gain_grads = jnp.stack(
        [
            gain_grad_zero,
            gain_grad_one,
            gain_grad_two,
            gain_grad_three,
            gain_grad_four,
            gain_grad_five,
        ],
        1,
    )
    laurel_grad = jnp.concatenate([grad_laurel_down, grad_laurel_up], 1)
    ple_grad = jnp.concatenate([grad_ple_down, grad_ple_up], 1)
    packed_grads = jnp.concatenate(
        [
            grad_query_map,
            grad_key_map,
            grad_value_map,
            grad_out_map,
            laurel_grad,
            ple_grad,
            gain_grads,
        ],
        1,
    ).astype(jnp.bfloat16)
    packed_sum = lax.psum_scatter(
        packed_grads, ("seq", "fsdp"), scatter_dimension=0, tiled=True
    ).astype(jnp.float32)
    summed = jnp.split(packed_sum, cuts, axis=1) + [
        lax.psum_scatter(grad_head_scale, ("seq", "fsdp"), scatter_dimension=0, tiled=True)
    ]
    return (
        hidden_out,
        input_grad,
        summed[0],
        summed[1],
        summed[2],
        summed[3],
        summed[4],
        summed[5],
        summed[6],
        summed[7],
        grad_mlp,
    )


def solution(mesh):
    placed = (
        P("seq", "fsdp", None),
        P("seq", "fsdp", None),
        P("seq", "fsdp"),
        P("seq", "fsdp"),
        P("seq", "fsdp", None),
        P(("seq", "fsdp"), None),
        P(("seq", "fsdp"), None),
        P(("seq", "fsdp"), None),
        P(("seq", "fsdp"), None),
        P(("seq", "fsdp"), None),
        P(("seq", "fsdp"), None),
        P(("seq", "fsdp"), None),
        P(("seq", "fsdp"), None),
        P("fsdp", None, "seq"),
    )
    return jax.shard_map(
        body,
        mesh=mesh,
        in_specs=placed,
        out_specs=(
            P("seq", "fsdp", None),
            P("seq", "fsdp", None),
            P(("seq", "fsdp"), None),
            P(("seq", "fsdp"), None),
            P(("seq", "fsdp"), None),
            P(("seq", "fsdp"), None),
            P(("seq", "fsdp"), None),
            P(("seq", "fsdp"), None),
            P(("seq", "fsdp"), None),
            P(("seq", "fsdp"), None),
            P("fsdp", None, "seq"),
        ),
        check_vma=False,
    )
```

```python
import functools
import math

import jax
import jax.numpy as jnp
from jax import lax
from jax.experimental import pallas as pl
from jax.experimental.pallas import tpu as pltpu
from jax.sharding import PartitionSpec as P

QUERY_HEADS = 8
KEY_VALUE_HEADS = 2
HEAD_DIM = 256
LR = 64
PLE = 256
WIN = 512

MESH = pl.DeviceIdType.MESH
eps = 1e-06
theta = 10000.0
root_half = 1.0 / math.sqrt(2.0)
low = jnp.bfloat16
full = jnp.float32


def gather_kernel(sizes, head_ref, rest_ref, mark_ref, head_out, rest_out, mark_out, *sems):
    (local, head_s1, head_r1, head_s2, head_r2, head_s3, head_r3) = sems[:7]
    (rest_s1, rest_r1, rest_s2, rest_r2, rest_s3, rest_r3, mark_s, mark_r) = sems[7:]
    ranks, pairs = sizes["seq"], sizes["pair"]
    rank = lax.axis_index("seq")
    fsdp_index = lax.axis_index("fsdp")
    pair, core = fsdp_index // 2, fsdp_index % 2
    sibling = (rank, pair * 2 + 1 - core)

    def on_seq(step):
        return ((rank + step) % ranks, fsdp_index)

    def on_pair(step):
        return (rank, ((pair + step) % pairs) * 2 + core)

    def remote(source, target, send, recv, device):
        return pltpu.make_async_remote_copy(
            src_ref=source,
            dst_ref=target,
            send_sem=send,
            recv_sem=recv,
            device_id=device,
            device_id_type=MESH,
        )

    barrier = pltpu.get_barrier_semaphore()
    devices = [on_seq(i) for i in range(1, ranks)] + [on_pair(i) for i in range(1, pairs)]
    for device in devices + [sibling]:
        pl.semaphore_signal(barrier, inc=1, device_id=device, device_id_type=MESH)
    pl.semaphore_wait(barrier, len(devices) + 1)

    sent = []

    def go(copy):
        copy.start()
        sent.append(copy)
        return copy

    head_seq = [
        go(
            remote(
                head_ref.at[on_seq(i)[0]],
                head_out.at[rank, pair, core],
                head_s1.at[i - 1],
                head_r1.at[i - 1],
                on_seq(i),
            )
        )
        for i in range(1, ranks)
    ]
    rest_pair = [
        go(
            remote(
                rest_ref,
                rest_out.at[rank, pair, core],
                rest_s1.at[i - 1],
                rest_r1.at[i - 1],
                on_pair(i),
            )
        )
        for i in range(1, pairs)
    ]
    own_head = pltpu.make_async_copy(head_ref.at[rank], head_out.at[rank, pair, core], local.at[0])
    own_head.start()
    own_rest = pltpu.make_async_copy(rest_ref, rest_out.at[rank, pair, core], local.at[1])
    own_rest.start()
    marks = [
        go(remote(mark_ref, mark_out.at[rank], mark_s.at[i - 1], mark_r.at[i - 1], on_seq(i)))
        for i in range(1, ranks)
    ]
    own_mark = pltpu.make_async_copy(mark_ref, mark_out.at[rank], local.at[2])
    own_mark.start()

    own_head.wait()
    for copy in head_seq:
        copy.wait_recv()
    mine = head_out.at[:, pair, core]
    head_pair = [
        go(remote(mine, mine, head_s2.at[i - 1], head_r2.at[i - 1], on_pair(i)))
        for i in range(1, pairs)
    ]
    head_core = [go(remote(mine, mine, head_s3.at[0], head_r3.at[0], sibling))]

    own_rest.wait()
    for copy in rest_pair:
        copy.wait_recv()
    row = rest_out.at[rank, :, core]
    rest_seq = [
        go(remote(row, row, rest_s2.at[i - 1], rest_r2.at[i - 1], on_seq(i)))
        for i in range(1, ranks)
    ]
    rest_core = [go(remote(row, row, rest_s3.at[0], rest_r3.at[0], sibling))]
    for i in range(1, ranks):
        rest_seq[i - 1].wait_recv()
        row = rest_out.at[(rank + ranks - i) % ranks, :, core]
        rest_core.append(go(remote(row, row, rest_s3.at[i], rest_r3.at[i], sibling)))
    for i in range(1, pairs):
        head_pair[i - 1].wait_recv()
        part = head_out.at[:, (pair + pairs - i) % pairs, core]
        head_core.append(go(remote(part, part, head_s3.at[i], head_r3.at[i], sibling)))
    own_mark.wait()
    for copy in marks + head_core + rest_core:
        copy.wait_recv()
    for copy in sent:
        copy.wait_send()


def gather_weights(sizes, head, rest, marks):
    ranks, pairs = sizes["seq"], sizes["pair"]
    dma = lambda n: pltpu.SemaphoreType.DMA((n,))
    anywhere = pl.BlockSpec(memory_space=pl.ANY)
    return pl.pallas_call(
        functools.partial(gather_kernel, sizes),
        out_shape=(
            jax.ShapeDtypeStruct((ranks, pairs, 2) + head.shape[1:], head.dtype),
            jax.ShapeDtypeStruct((ranks, pairs, 2) + rest.shape, rest.dtype),
            jax.ShapeDtypeStruct((ranks,) + marks.shape, marks.dtype),
        ),
        in_specs=[anywhere] * 3,
        out_specs=(anywhere,) * 3,
        scratch_shapes=[
            dma(3),
            *[dma(ranks - 1)] * 2,
            *[dma(pairs - 1)] * 2,
            *[dma(pairs)] * 2,
            *[dma(pairs - 1)] * 2,
            *[dma(ranks - 1)] * 2,
            *[dma(ranks)] * 2,
            *[dma(ranks - 1)] * 2,
        ],
        compiler_params=pltpu.CompilerParams(collective_id=0, has_side_effects=True),
    )(head, rest, marks)


def permute(v, axis, offset):
    size = lax.axis_size(axis)
    return lax.ppermute(v, axis, [(i, i ^ offset) for i in range(size)])


def gather_seq(v, ranks):
    if ranks != 4:
        return [v] + [permute(v, "seq", k) for k in range(1, ranks)]
    half = v.shape[1] // 2
    first, second = permute(v, "seq", 1), permute(v, "seq", 2)
    left = permute(first[:, :half], "seq", 2)
    right = permute(second[:, half:], "seq", 1)
    return [v, first, second, jnp.concatenate([left, right], 1)]


def sum_seq(blocks, ranks):
    up = lambda v: v.astype(full)
    if ranks != 4:
        return sum((up(permute(blocks[k], "seq", k)) for k in range(1, ranks)), up(blocks[0]))
    half = blocks[0].shape[1] // 2
    left = [b[:, :half] for b in blocks]
    right = [b[:, half:] for b in blocks]
    left_far, right_far = permute(left[3], "seq", 1), permute(right[3], "seq", 2)
    left_near, right_near = permute(left[1], "seq", 1), permute(right[2], "seq", 2)
    left_far = permute((up(left[2]) + up(left_far)).astype(low), "seq", 2)
    right_far = permute((up(right[1]) + up(right_far)).astype(low), "seq", 1)
    return jnp.concatenate(
        [
            up(left[0]) + up(left_near) + up(left_far),
            up(right[0]) + up(right_near) + up(right_far),
        ],
        1,
    )


def take(v, axis, index):
    return lax.dynamic_index_in_dim(v, index, axis, keepdims=False)


def scatter_fsdp(v, pair_axis, pairs):
    index = lax.axis_index("fsdp")
    pair, core = index // 2, index % 2
    other = permute(take(v, pair_axis + 1, 1 - core), "fsdp", 1)
    v = (take(v, pair_axis + 1, core).astype(full) + other.astype(full)).astype(low)
    parts = [take(v, pair_axis, pair).astype(full)]
    for k in range(1, pairs):
        parts.append(permute(take(v, pair_axis, pair ^ k), "fsdp", 2 * k).astype(full))
    return sum(parts[1:], parts[0])


def dot(left, right, over):
    return lax.dot_general(left, right, (over, ((), ())), preferred_element_type=full)


def mm(left, right):
    return dot(left, right, ((1,), (0,)))


def mm_nt(left, right):
    return dot(left, right, ((1,), (1,)))


def mm_tn(left, right):
    return dot(left, right, ((0,), (0,)))


def norm_rows(v, gain_vec):
    inverse = lax.rsqrt(jnp.mean(v * v, -1, keepdims=True) + eps)
    return (v * inverse * gain_vec, inverse)


def norm_back(v, inverse, gain_vec, incoming):
    scaled = incoming * gain_vec
    inner_mean = jnp.mean(scaled * v, -1, keepdims=True)
    return (
        inverse * (scaled - v * inverse * inverse * inner_mean),
        jnp.sum(incoming * v * inverse, axis=0),
    )


def gelu_tanh(v):
    return jax.nn.gelu(v, approximate=True)


def rope_tables(places):
    half_width = HEAD_DIM // 2
    frequency = theta ** (-jnp.arange(half_width).astype(full) * 2.0 / HEAD_DIM)
    angles = places.astype(full)[:, None] * frequency
    angles = jnp.concatenate([angles, angles], -1)[:, None, :]
    return (jnp.cos(angles), jnp.sin(angles))


def rotate(v, cos_table, sin_table):
    half_width = v.shape[-1] // 2
    turned = jnp.concatenate([-v[..., half_width:], v[..., :half_width]], -1)
    return v * cos_table + turned * sin_table


def head_prep(qkv, head_scale, cos_table, sin_table):
    per_head = qkv.reshape(qkv.shape[0], -1, HEAD_DIM)
    queries = rotate(norm_rows(per_head[:, :-2], head_scale[:, 0])[0], cos_table, sin_table)
    keys = rotate(norm_rows(per_head[:, -2:-1], head_scale[:, 1])[0], cos_table, sin_table)
    values = norm_rows(per_head[:, -1:], 1.0)[0]
    return (queries, keys, values)


def allowed_mask(segments, indices):
    offset = indices[:, None] - indices[None, :]
    nearby = (offset >= 0) & (offset < WIN)
    return (segments[:, None] == segments[None, :]) & nearby


def scores_of(q_heads, keys, allowed):
    raw_scores = jnp.einsum("qhd,kd->hqk", q_heads, keys, preferred_element_type=full)
    return jnp.where(allowed[None], raw_scores * HEAD_DIM ** (-0.5), -1000000000.0)


def attend_heads(q_heads, keys, values, allowed):
    scores = scores_of(q_heads, keys, allowed)
    row_peak = jnp.max(scores, -1, keepdims=True)
    exp_scores = jnp.exp(scores - row_peak)
    row_total = jnp.sum(exp_scores, -1, keepdims=True)
    attn_probs = exp_scores / row_total
    head_out = jnp.einsum(
        "hqk,kd->qhd", attn_probs.astype(low), values, preferred_element_type=full
    )
    return (head_out, row_peak + jnp.log(row_total))


def attend_back(q_heads, keys, values, allowed, log_total, grad_heads):
    probs_again = jnp.exp(scores_of(q_heads, keys, allowed) - log_total)
    grad_values = jnp.einsum(
        "hqk,qhd->kd", probs_again.astype(low), grad_heads, preferred_element_type=full
    )
    grad_probs = jnp.einsum("qhd,kd->hqk", grad_heads, values, preferred_element_type=full)
    row_inner = jnp.sum(probs_again * grad_probs, -1, keepdims=True)
    grad_scores = (probs_again * (grad_probs - row_inner) * HEAD_DIM ** (-0.5)).astype(low)
    grad_queries = jnp.einsum("hqk,kd->qhd", grad_scores, keys, preferred_element_type=full)
    grad_keys = jnp.einsum("hqk,qhd->kd", grad_scores, q_heads, preferred_element_type=full)
    return (grad_queries, grad_keys, grad_values)


def body(
    sizes,
    hidden_in,
    per_layer_input,
    segment_ids,
    positions,
    out_cotangent,
    w_query,
    key_matrix,
    value_matrix,
    w_out_t,
    laurel_maps,
    per_layer_maps,
    norm_gains,
    head_gains,
    w_mlp,
):
    ranks, pairs = sizes["seq"], sizes["pair"]
    block, _, width = hidden_in.shape
    rows = w_query.shape[0]
    q_width = QUERY_HEADS // ranks * HEAD_DIM
    share = QUERY_HEADS // KEY_VALUE_HEADS
    kv_of = [rank * (QUERY_HEADS // ranks) // share for rank in range(ranks)]
    length = block * ranks
    rank = lax.axis_index("seq")
    relative = [rank ^ k for k in range(ranks)]
    cut = lambda v: [v[k * block : (k + 1) * block] for k in range(ranks)]
    join = lambda blocks: jnp.concatenate(blocks, 0)

    in_maps = lax.all_gather(w_mlp[:, :2], "fsdp", axis=0, tiled=True)
    down_map = lax.all_gather(w_mlp[:, 2], "fsdp", axis=0, tiled=True)

    by_rank = lambda m: m.reshape(rows, ranks, q_width).transpose(1, 0, 2)
    by_kv = lambda m: jnp.stack([m[:, j * HEAD_DIM : (j + 1) * HEAD_DIM] for j in kv_of])
    head_pack = jnp.concatenate(
        [by_rank(w_query), by_kv(key_matrix), by_kv(value_matrix), by_rank(w_out_t)], 2
    )
    head_rows = head_gains.shape[0]
    small = jnp.concatenate(
        [norm_gains, jnp.pad(head_gains, ((0, rows - head_rows), (0, 0)))], 1
    )
    small = jnp.pad(small, ((0, 0), (0, 128 - small.shape[1])))
    rest_pack = jnp.concatenate([laurel_maps, per_layer_maps, small], 1)
    marks = jnp.pad(jnp.concatenate([segment_ids.T, positions.T], 0), ((0, 6), (0, 0)))
    x_local = hidden_in.reshape(block, width)

    head_all, rest_all, marks_all = gather_weights(sizes, head_pack, rest_pack, marks)
    x_all = join(gather_seq(x_local, ranks))
    marks_all = jnp.concatenate([take(marks_all, 0, r) for r in relative], 1)
    head_all = head_all.reshape(width, -1)
    rest_all = rest_all.reshape(width, -1)
    qkv_map, out_map = head_all[:, :-q_width], head_all[:, -q_width:]
    laurel = rest_all[:, : 2 * LR]
    ple = rest_all[:, 2 * LR : 2 * LR + 2 * PLE]
    gains = rest_all[:, 2 * LR + 2 * PLE :].astype(full)
    gain = [gains[:, i] for i in range(6)]
    head_scale = gains[:, 6:8].reshape(-1, rows, 2)[:, :head_rows].reshape(HEAD_DIM, 2)

    tokens_all = x_all.astype(full)
    normed_all_f, all_inverse = norm_rows(tokens_all, gain[0])
    normed_all = normed_all_f.astype(low)
    tokens = x_local.astype(full)
    x_normed_f, x_inverse = norm_rows(tokens, gain[0])
    normed = x_normed_f.astype(low)
    indices = jnp.concatenate([r * block + jnp.arange(block) for r in relative])
    cos_table, sin_table = rope_tables(marks_all[1])
    allowed = allowed_mask(marks_all[0], indices)

    qkv = mm(normed_all, qkv_map)
    queries, keys, values = head_prep(qkv, head_scale, cos_table, sin_table)
    q_heads = queries.astype(low)
    k_head = keys[:, 0].astype(low)
    v_head = values[:, 0].astype(low)
    head_out, log_total = attend_heads(q_heads, k_head, v_head, allowed)
    attn_in = head_out.astype(low).reshape(length, q_width)
    attn_lin = sum_seq(cut(mm_nt(attn_in, out_map).astype(low)), ranks)

    attn_normed, attn_inverse = norm_rows(attn_lin, gain[1])
    laurel_low = mm(normed, laurel[:, :LR]).astype(low)
    laurel_high = mm_nt(laurel_low, laurel[:, LR:])
    laurel_normed, laurel_inverse = norm_rows(laurel_high, gain[2])
    mixed = (tokens + attn_normed + (normed.astype(full) + laurel_normed)) * root_half
    h_normed_f, h_inverse = norm_rows(mixed, gain[3])
    h_rows = join(gather_seq(h_normed_f.astype(low), ranks))

    gate_up = dot(h_rows, in_maps, ((1,), (0,)))
    gate_part, up_part = gate_up[:, 0], gate_up[:, 1]
    hidden = (gelu_tanh(gate_part) * up_part).astype(low)
    ffn_out = sum_seq(cut(mm_nt(hidden, down_map).astype(low)), ranks)

    ffn_normed, ffn_inverse = norm_rows(ffn_out, gain[4])
    h_second = (mixed + ffn_normed).astype(low)
    ple_gate = mm(h_second, ple[:, :PLE])
    ple_input = per_layer_input.reshape(block, PLE).astype(full)
    ple_mixed = (gelu_tanh(ple_gate) * ple_input).astype(low)
    ple_proj = mm_nt(ple_mixed, ple[:, PLE:])
    ple_normed, ple_inverse = norm_rows(ple_proj, gain[5])
    hidden_out = (h_second.astype(full) + ple_normed).astype(low)

    grad_out = out_cotangent.reshape(block, width).astype(full)
    grad_ple_proj, gain_grad_five = norm_back(ple_proj, ple_inverse, gain[5], grad_out)
    grad_ple_low = grad_ple_proj.astype(low)
    grad_ple_mixed = mm(grad_ple_low, ple[:, PLE:])
    unused_gelu, gelu_pull = jax.vjp(gelu_tanh, ple_gate)
    grad_ple_gate = gelu_pull(grad_ple_mixed * ple_input)[0].astype(low)
    grad_second = grad_out + mm_nt(grad_ple_gate, ple[:, :PLE])
    grad_ffn, gain_grad_four = norm_back(ffn_out, ffn_inverse, gain[4], grad_second)
    grad_ffn_rows = join(gather_seq(grad_ffn.astype(low), ranks))

    down_grad = mm_tn(grad_ffn_rows, hidden).astype(low)
    down_sum = lax.psum_scatter(down_grad, "fsdp", scatter_dimension=0, tiled=True)
    grad_hidden = mm(grad_ffn_rows, down_map)
    gate_act, act_pull = jax.vjp(gelu_tanh, gate_part)
    grad_gate_up = jnp.stack(
        [act_pull(grad_hidden * up_part)[0], grad_hidden * gate_act], 1
    ).astype(low)
    in_grad = dot(h_rows, grad_gate_up, ((0,), (0,))).astype(low)
    in_sum = lax.psum_scatter(in_grad, "fsdp", scatter_dimension=0, tiled=True)
    h_part = dot(grad_gate_up, in_maps, ((1, 2), (1, 2))).astype(low)
    grad_h_normed = sum_seq(cut(h_part), ranks)

    grad_ple_up = mm_tn(grad_ple_low, ple_mixed)
    grad_ple_down = mm_tn(h_second, grad_ple_gate)
    grad_mixed_norm, gain_grad_three = norm_back(mixed, h_inverse, gain[3], grad_h_normed)
    grad_mixed = grad_second + grad_mixed_norm
    grad_branch = grad_mixed * root_half
    grad_attn, gain_grad_one = norm_back(attn_lin, attn_inverse, gain[1], grad_branch)
    grad_attn_rows = join(gather_seq(grad_attn.astype(low), ranks))
    grad_out_map = mm_tn(grad_attn_rows, attn_in)
    grad_heads = mm(grad_attn_rows, out_map).astype(low).reshape(length, -1, HEAD_DIM)
    grad_queries, grad_keys, grad_values = attend_back(
        q_heads, k_head, v_head, allowed, log_total, grad_heads
    )
    unused_heads, head_pull = jax.vjp(head_prep, qkv, head_scale, cos_table, sin_table)
    grad_qkv, grad_head_scale, unused_cos, unused_sin = head_pull(
        (grad_queries, grad_keys[:, None], grad_values[:, None])
    )
    grad_qkv = grad_qkv.astype(low)
    grad_qkv_map = mm_tn(normed_all, grad_qkv)
    x_part = mm_nt(grad_qkv, qkv_map)

    grad_laurel_high, gain_grad_two = norm_back(
        laurel_high, laurel_inverse, gain[2], grad_branch
    )
    grad_high_low = grad_laurel_high.astype(low)
    grad_laurel_up = mm_tn(grad_high_low, laurel_low)
    grad_laurel_low = mm(grad_high_low, laurel[:, LR:]).astype(low)
    grad_laurel_down = mm_tn(normed, grad_laurel_low)

    head_grad = jnp.concatenate([grad_qkv_map, grad_out_map], 1).astype(low)
    head_sum = scatter_fsdp(head_grad.reshape(ranks, pairs, 2, rows, -1), 1, pairs).astype(low)
    head_ranks = [take(head_sum, 0, rank)] + [
        permute(take(head_sum, 0, relative[k]), "seq", k) for k in range(1, ranks)
    ]
    stacked = jnp.stack(head_ranks)
    head_ranks = jnp.stack([take(stacked, 0, r ^ rank) for r in range(ranks)]).astype(full)

    x_here = grad_branch + mm_nt(grad_laurel_low, laurel[:, :LR])
    grad_x_normed = x_here + sum_seq(cut(x_part.astype(low)), ranks)
    grad_tokens_norm = norm_back(tokens, x_inverse, gain[0], grad_x_normed)[0]
    input_grad = grad_mixed * root_half + grad_tokens_norm
    gain_grad_zero = jnp.sum(x_here * tokens * x_inverse, 0) + jnp.sum(
        x_part * tokens_all * all_inverse, 0
    )

    gain_grads = jnp.stack(
        [
            gain_grad_zero,
            gain_grad_one,
            gain_grad_two,
            gain_grad_three,
            gain_grad_four,
            gain_grad_five,
        ],
        1,
    )
    head_scale_grad = jnp.pad(
        grad_head_scale.reshape(-1, head_rows, 2), ((0, 0), (0, rows - head_rows), (0, 0))
    ).reshape(width, 2)
    small_grad = jnp.concatenate([gain_grads, head_scale_grad], 1)
    small_grad = jnp.pad(small_grad, ((0, 0), (0, 128 - small_grad.shape[1])))
    rest_grad = jnp.concatenate(
        [grad_laurel_down, grad_laurel_up, grad_ple_down, grad_ple_up, small_grad], 1
    ).astype(low)
    rest_grad = rest_grad.reshape(ranks, -1, rest_grad.shape[1])
    rest_own = take(rest_grad, 0, rank).astype(full) + sum(
        permute(take(rest_grad, 0, relative[k]), "seq", k).astype(full) for k in range(1, ranks)
    )
    rest_sum = scatter_fsdp(rest_own.astype(low).reshape(pairs, 2, rows, -1), 0, pairs)

    whole = lambda part: part.transpose(1, 0, 2).reshape(rows, -1)

    def of_kv(part):
        return jnp.concatenate(
            [
                sum(part[rank] for rank in range(ranks) if kv_of[rank] == j)
                for j in range(KEY_VALUE_HEADS)
            ],
            1,
        )

    ple_end = 2 * LR + 2 * PLE
    scale_sum = rest_sum[:head_rows, ple_end + 6 : ple_end + 8]
    grad_mlp = jnp.concatenate([in_sum, down_sum[:, None]], 1).astype(full)
    lead = (block, 1, width)
    return (
        hidden_out.reshape(lead),
        input_grad.reshape(lead),
        whole(head_ranks[:, :, :q_width]),
        of_kv(head_ranks[:, :, q_width : q_width + HEAD_DIM]),
        of_kv(head_ranks[:, :, q_width + HEAD_DIM : q_width + 2 * HEAD_DIM]),
        whole(head_ranks[:, :, -q_width:]),
        rest_sum[:, : 2 * LR],
        rest_sum[:, 2 * LR : ple_end],
        rest_sum[:, ple_end : ple_end + 6],
        scale_sum,
        grad_mlp,
    )


def solution(mesh):
    sizes = {"seq": mesh.shape["seq"], "pair": mesh.shape["fsdp"] // 2, "core": 2}
    spread = P(("seq", "fsdp"), None)
    tokens = P("seq", "fsdp", None)
    return jax.shard_map(
        functools.partial(body, sizes),
        mesh=mesh,
        in_specs=(tokens, tokens, P("seq", "fsdp"), P("seq", "fsdp"), tokens)
        + (spread,) * 8
        + (P("fsdp", None, "seq"),),
        out_specs=(tokens, tokens) + (spread,) * 8 + (P("fsdp", None, "seq"),),
        check_vma=False,
    )
```

```python
import functools
import math

import jax
import jax.numpy as jnp
from jax import lax
from jax.experimental import pallas as pl
from jax.experimental.pallas import tpu as pltpu
from jax.sharding import PartitionSpec as P

QUERY_HEADS = 8
KEY_VALUE_HEADS = 2
HEAD_DIM = 256
LR = 64
PLE = 256
WIN = 512

MESH = pl.DeviceIdType.MESH
eps = 1e-06
theta = 10000.0
root_half = 1.0 / math.sqrt(2.0)
low = jnp.bfloat16
full = jnp.float32


def flip(index, offset, size):
    value, bit = 0, 1
    while bit < size:
        has = (index // bit) % 2
        value = value + bit * ((1 - has) if offset & bit else has)
        bit *= 2
    return value


def gather_kernel(
    sizes, head_ref, rest_ref, mark_ref, x_ref, head_out, rest_out, mark_out, x_out, *sems
):
    (local, head_s1, head_r1, right_s, right_r, left_s, left_r, head_s3, head_r3) = sems[:9]
    (rest_s1, rest_r1, rest_s2, rest_r2, rest_s3, rest_r3, mark_s, mark_r, x_s, x_r) = sems[9:]
    ranks, pairs = sizes["seq"], sizes["pair"]
    rank = lax.axis_index("seq")
    fsdp_index = lax.axis_index("fsdp")
    pair, core = fsdp_index // 2, fsdp_index % 2
    sibling = (rank, pair * 2 + 1 - core)

    def on_seq(step):
        return (flip(rank, step, ranks), fsdp_index)

    def on_pair(step):
        return (rank, ((pair + step) % pairs) * 2 + core)

    def remote(source, target, send, recv, device):
        return pltpu.make_async_remote_copy(
            src_ref=source,
            dst_ref=target,
            send_sem=send,
            recv_sem=recv,
            device_id=device,
            device_id_type=MESH,
        )

    barrier = pltpu.get_barrier_semaphore()
    devices = [on_seq(i) for i in range(1, ranks)] + [on_pair(i) for i in range(1, pairs)]
    for device in devices + [sibling]:
        pl.semaphore_signal(barrier, inc=1, device_id=device, device_id_type=MESH)
    pl.semaphore_wait(barrier, len(devices) + 1)

    sent = []

    def go(copy):
        copy.start()
        sent.append(copy)
        return copy

    head_seq = [
        go(
            remote(
                head_ref.at[on_seq(i)[0]],
                head_out.at[rank, pair, core],
                head_s1.at[i - 1],
                head_r1.at[i - 1],
                on_seq(i),
            )
        )
        for i in range(1, ranks)
    ]
    rest_pair = [
        go(
            remote(
                rest_ref,
                rest_out.at[rank, pair, core],
                rest_s1.at[i - 1],
                rest_r1.at[i - 1],
                on_pair(i),
            )
        )
        for i in range(1, pairs)
    ]
    owns = [
        pltpu.make_async_copy(head_ref.at[rank], head_out.at[rank, pair, core], local.at[0]),
        pltpu.make_async_copy(rest_ref, rest_out.at[rank, pair, core], local.at[1]),
        pltpu.make_async_copy(mark_ref, mark_out.at[0], local.at[2]),
        pltpu.make_async_copy(x_ref, x_out.at[0], local.at[3]),
    ]
    for copy in owns:
        copy.start()
    marks = [
        go(remote(mark_ref, mark_out.at[i], mark_s.at[i - 1], mark_r.at[i - 1], on_seq(i)))
        for i in range(1, ranks)
    ]

    owns[0].wait()
    for copy in head_seq:
        copy.wait_recv()

    def right(t):
        part = head_out.at[:, pair - (t - 1), core]
        return remote(part, part, right_s.at[t - 1], right_r.at[t - 1], (rank, fsdp_index + 2))

    def left(t):
        part = head_out.at[:, pair + (t - 1), core]
        return remote(part, part, left_s.at[t - 1], left_r.at[t - 1], (rank, fsdp_index - 2))

    def to_sibling(at, slot):
        part = head_out.at[:, at, core]
        return remote(part, part, head_s3.at[slot], head_r3.at[slot], sibling)

    sends_right = lambda t: (pair - (t - 1) >= 0) & (pair + 1 < pairs)
    sends_left = lambda t: (pair + (t - 1) < pairs) & (pair - 1 >= 0)
    pl.when(sends_right(1))(lambda: right(1).start())
    pl.when(sends_left(1))(lambda: left(1).start())
    to_sibling(pair, 0).start()

    x_seq = [
        go(remote(x_ref, x_out.at[i], x_s.at[i - 1], x_r.at[i - 1], on_seq(i)))
        for i in range(1, ranks)
    ]
    owns[1].wait()
    for copy in rest_pair:
        copy.wait_recv()
    row = rest_out.at[rank, :, core]
    rest_seq = [
        go(remote(row, row, rest_s2.at[i - 1], rest_r2.at[i - 1], on_seq(i)))
        for i in range(1, ranks)
    ]
    rest_core = [go(remote(row, row, rest_s3.at[0], rest_r3.at[0], sibling))]

    for t in range(1, pairs):

        def from_left(t=t):
            part = head_out.at[:, pair - t, core]
            remote(part, part, right_s.at[t - 1], right_r.at[t - 1], sibling).wait_recv()
            if t + 1 < pairs:
                pl.when(pair + 1 < pairs)(lambda: right(t + 1).start())
            to_sibling(pair - t, t).start()

        def from_right(t=t):
            part = head_out.at[:, pair + t, core]
            remote(part, part, left_s.at[t - 1], left_r.at[t - 1], sibling).wait_recv()
            if t + 1 < pairs:
                pl.when(pair - 1 >= 0)(lambda: left(t + 1).start())
            to_sibling(pair + t, pairs - 1 + t).start()

        pl.when(pair - t >= 0)(from_left)
        pl.when(pair + t < pairs)(from_right)

    for i in range(1, ranks):
        rest_seq[i - 1].wait_recv()
        row = rest_out.at[flip(rank, i, ranks), :, core]
        rest_core.append(go(remote(row, row, rest_s3.at[i], rest_r3.at[i], sibling)))
    for copy in owns[2:]:
        copy.wait()
    for copy in marks + x_seq + rest_core:
        copy.wait_recv()
    to_sibling(pair, 0).wait()
    for t in range(1, pairs):
        pl.when(pair - t >= 0)(lambda t=t: to_sibling(pair - t, t).wait())
        pl.when(pair + t < pairs)(lambda t=t: to_sibling(pair + t, pairs - 1 + t).wait())
        pl.when(sends_right(t))(lambda t=t: right(t).wait_send())
        pl.when(sends_left(t))(lambda t=t: left(t).wait_send())
    for copy in sent:
        copy.wait_send()


def gather_weights(sizes, head, rest, marks, x):
    ranks, pairs = sizes["seq"], sizes["pair"]
    dma = lambda n: pltpu.SemaphoreType.DMA((n,))
    anywhere = pl.BlockSpec(memory_space=pl.ANY)
    return pl.pallas_call(
        functools.partial(gather_kernel, sizes),
        out_shape=(
            jax.ShapeDtypeStruct((ranks, pairs, 2) + head.shape[1:], head.dtype),
            jax.ShapeDtypeStruct((ranks, pairs, 2) + rest.shape, rest.dtype),
            jax.ShapeDtypeStruct((ranks,) + marks.shape, marks.dtype),
            jax.ShapeDtypeStruct((ranks,) + x.shape, x.dtype),
        ),
        in_specs=[anywhere] * 4,
        out_specs=(anywhere,) * 4,
        scratch_shapes=[
            dma(4),
            *[dma(ranks - 1)] * 2,
            *[dma(pairs - 1)] * 4,
            *[dma(2 * pairs - 1)] * 2,
            *[dma(pairs - 1)] * 2,
            *[dma(ranks - 1)] * 2,
            *[dma(ranks)] * 2,
            *[dma(ranks - 1)] * 4,
        ],
        compiler_params=pltpu.CompilerParams(collective_id=0, has_side_effects=True),
    )(head, rest, marks, x)


def permute(v, axis, offset):
    size = lax.axis_size(axis)
    return lax.ppermute(v, axis, [(i, i ^ offset) for i in range(size)])


def gather_seq(v, ranks):
    if ranks != 4:
        return [v] + [permute(v, "seq", k) for k in range(1, ranks)]
    half = v.shape[1] // 2
    first, second = permute(v, "seq", 1), permute(v, "seq", 2)
    left = permute(first[:, :half], "seq", 2)
    right = permute(second[:, half:], "seq", 1)
    return [v, first, second, left, right]


def whole_rows(blocks):
    if blocks[-1].shape[1] < blocks[0].shape[1]:
        blocks = blocks[:-2] + [jnp.concatenate(blocks[-2:], 1)]
    return jnp.concatenate(blocks, 0)


def sum_seq(blocks, ranks):
    up = lambda v: v.astype(full)
    if ranks != 4:
        return sum((up(permute(blocks[k], "seq", k)) for k in range(1, ranks)), up(blocks[0]))
    half = blocks[0].shape[1] // 2
    left = [b[:, :half] for b in blocks]
    right = [b[:, half:] for b in blocks]
    left_far, right_far = permute(left[3], "seq", 1), permute(right[3], "seq", 2)
    left_near, right_near = permute(left[1], "seq", 1), permute(right[2], "seq", 2)
    left_far = permute((up(left[2]) + up(left_far)).astype(low), "seq", 2)
    right_far = permute((up(right[1]) + up(right_far)).astype(low), "seq", 1)
    return jnp.concatenate(
        [
            up(left[0]) + up(left_near) + up(left_far),
            up(right[0]) + up(right_near) + up(right_far),
        ],
        1,
    )


def take(v, axis, index):
    return lax.dynamic_index_in_dim(v, index, axis, keepdims=False)


def dot(left, right, over):
    return lax.dot_general(left, right, (over, ((), ())), preferred_element_type=full)


def mm(left, right):
    return dot(left, right, ((1,), (0,)))


def mm_nt(left, right):
    return dot(left, right, ((1,), (1,)))


def mm_tn(left, right):
    return dot(left, right, ((0,), (0,)))


def norm_rows(v, gain_vec):
    inverse = lax.rsqrt(jnp.mean(v * v, -1, keepdims=True) + eps)
    return (v * inverse * gain_vec, inverse)


def norm_back(v, inverse, gain_vec, incoming):
    scaled = incoming * gain_vec
    inner_mean = jnp.mean(scaled * v, -1, keepdims=True)
    return (
        inverse * (scaled - v * inverse * inverse * inner_mean),
        jnp.sum(incoming * v * inverse, axis=0),
    )


def gelu_tanh(v):
    return jax.nn.gelu(v, approximate=True)


def rope_tables(places):
    half_width = HEAD_DIM // 2
    frequency = theta ** (-jnp.arange(half_width).astype(full) * 2.0 / HEAD_DIM)
    angles = places.astype(full)[:, None] * frequency
    angles = jnp.concatenate([angles, angles], -1)[:, None, :]
    return (jnp.cos(angles), jnp.sin(angles))


def rotate(v, cos_table, sin_table):
    half_width = v.shape[-1] // 2
    turned = jnp.concatenate([-v[..., half_width:], v[..., :half_width]], -1)
    return v * cos_table + turned * sin_table


def head_prep(qkv, head_scale, cos_table, sin_table):
    per_head = qkv.reshape(qkv.shape[0], -1, HEAD_DIM)
    queries = rotate(norm_rows(per_head[:, :-2], head_scale[:, 0])[0], cos_table, sin_table)
    keys = rotate(norm_rows(per_head[:, -2:-1], head_scale[:, 1])[0], cos_table, sin_table)
    values = norm_rows(per_head[:, -1:], 1.0)[0]
    return (queries, keys, values)


def allowed_mask(segments, indices):
    offset = indices[:, None] - indices[None, :]
    nearby = (offset >= 0) & (offset < WIN)
    return (segments[:, None] == segments[None, :]) & nearby


def scores_of(q_heads, keys, allowed):
    raw_scores = jnp.einsum("qhd,kd->hqk", q_heads, keys, preferred_element_type=full)
    return jnp.where(allowed[None], raw_scores * HEAD_DIM ** (-0.5), -1000000000.0)


def attend_heads(q_heads, keys, values, allowed):
    scores = scores_of(q_heads, keys, allowed)
    row_peak = jnp.max(scores, -1, keepdims=True)
    exp_scores = jnp.exp(scores - row_peak)
    row_total = jnp.sum(exp_scores, -1, keepdims=True)
    attn_probs = exp_scores / row_total
    head_out = jnp.einsum(
        "hqk,kd->qhd", attn_probs.astype(low), values, preferred_element_type=full
    )
    return (head_out, row_peak + jnp.log(row_total))


def norm_rope_back(lin, gain, incoming):
    inverse = lax.rsqrt(jnp.mean(lin * lin, -1, keepdims=True) + eps)
    scaled = incoming * gain
    inner_mean = jnp.mean(scaled * lin, -1, keepdims=True)
    return (
        inverse * (scaled - lin * inverse * inverse * inner_mean),
        jnp.sum(incoming * lin * inverse, 0, keepdims=True),
    )


def attend_back_kernel(
    ranks,
    block,
    qkv_ref,
    q_ref,
    k_ref,
    v_ref,
    grad_ref,
    total_ref,
    code_col_ref,
    code_row_ref,
    cos_ref,
    sin_ref,
    gain_ref,
    out_ref,
    gain_out_ref,
    key_acc,
    value_acc,
    query_acc,
    row_acc,
    probs_ref,
    grad_probs_ref,
):
    head, mine = pl.program_id(0), pl.program_id(1)
    heads = pl.num_programs(0)
    rank = lax.axis_index("seq")
    scale = HEAD_DIM ** (-0.5)
    half = HEAD_DIM // 2

    @pl.when((head == 0) & (mine == 0))
    def _():
        key_acc[...] = jnp.zeros_like(key_acc)
        value_acc[...] = jnp.zeros_like(value_acc)
        gain_out_ref[...] = jnp.zeros_like(gain_out_ref)

    rows = pl.ds(pl.multiple_of(mine * block, block), block)
    columns = pl.ds(pl.multiple_of(head * HEAD_DIM, HEAD_DIM), HEAD_DIM)
    q, grad = q_ref[rows, columns], grad_ref[rows, columns]
    code = code_col_ref[rows, :]
    peaks = total_ref[head, rows, :]
    row_acc[...] = jnp.zeros_like(row_acc)
    query_acc[...] = jnp.zeros_like(query_acc)

    def reaches(other):
        apart = (rank ^ mine) - (rank ^ other)
        return (apart >= 0) & (apart * block - (block - 1) < WIN)

    for other in range(ranks):
        span = slice(other * block, (other + 1) * block)

        @pl.when(reaches(other))
        def _():
            scores = mm_nt(q, k_ref[span, :]) * scale
            offset = code - code_row_ref[:, span]
            probs = jnp.where((offset >= 0) & (offset < WIN), jnp.exp(scores - peaks), 0.0)
            grad_probs = mm_nt(grad, v_ref[span, :])
            probs_ref[other] = probs
            grad_probs_ref[other] = grad_probs
            row_acc[...] += jnp.sum(probs * grad_probs, -1, keepdims=True)

    inner = row_acc[...]
    for other in range(ranks):
        span = slice(other * block, (other + 1) * block)

        @pl.when(reaches(other))
        def _():
            probs = probs_ref[other]
            grad_scores = (probs * (grad_probs_ref[other] - inner) * scale).astype(low)
            query_acc[...] += mm(grad_scores, k_ref[span, :])
            key_acc[span, :] += mm_tn(grad_scores, q)
            value_acc[span, :] += mm_tn(probs.astype(low), grad)

    def turned_back(v, cos_table, sin_table):
        first, second = v[:, :half], v[:, half:]
        return jnp.concatenate(
            [
                first * cos_table + second * sin_table,
                second * cos_table - first * sin_table,
            ],
            1,
        )

    incoming = turned_back(query_acc[...].astype(low).astype(full), cos_ref[rows, :], sin_ref[rows, :])
    grad_lin, grad_gain = norm_rope_back(qkv_ref[rows, columns], gain_ref[0:1, :], incoming)
    out_ref[rows, columns] = grad_lin.astype(low)
    gain_out_ref[0:1, :] += grad_gain

    @pl.when((head == heads - 1) & (mine == ranks - 1))
    def _():
        base = out_ref.shape[1] - 2 * HEAD_DIM
        for other in range(ranks):
            span = slice(other * block, (other + 1) * block)
            incoming = turned_back(key_acc[span, :], cos_ref[span, :], sin_ref[span, :])
            grad_lin, grad_gain = norm_rope_back(
                qkv_ref[span, base : base + HEAD_DIM], gain_ref[1:2, :], incoming
            )
            out_ref[span, base : base + HEAD_DIM] = grad_lin.astype(low)
            gain_out_ref[1:2, :] += grad_gain
            grad_lin = norm_rope_back(qkv_ref[span, base + HEAD_DIM :], 1.0, value_acc[span, :])[0]
            out_ref[span, base + HEAD_DIM :] = grad_lin.astype(low)


def attend_back(ranks, qkv, q, k, v, grad, total, codes, cos_table, sin_table, gains):
    length = qkv.shape[0]
    block = length // ranks
    heads = q.shape[1] // HEAD_DIM
    whole = lambda v: pl.BlockSpec(
        v.shape, lambda i, j, n=len(v.shape): (0,) * n, pipeline_mode=pl.Buffered(1)
    )
    operands = (qkv, q, k, v, grad, total, codes[:, None], codes[None], cos_table, sin_table, gains)
    results = (
        jax.ShapeDtypeStruct(qkv.shape, low),
        jax.ShapeDtypeStruct((8, HEAD_DIM), full),
    )
    return pl.pallas_call(
        functools.partial(attend_back_kernel, ranks, block),
        grid=(heads, ranks),
        out_shape=results,
        in_specs=[whole(v) for v in operands],
        out_specs=tuple(whole(v) for v in results),
        scratch_shapes=[
            pltpu.VMEM((length, HEAD_DIM), full),
            pltpu.VMEM((length, HEAD_DIM), full),
            pltpu.VMEM((block, HEAD_DIM), full),
            pltpu.VMEM((block, 1), full),
            pltpu.VMEM((ranks, block, block), full),
            pltpu.VMEM((ranks, block, block), full),
        ],
        compiler_params=pltpu.CompilerParams(vmem_limit_bytes=40 << 20),
        cost_estimate=pl.CostEstimate(
            flops=10 * heads * length * length * HEAD_DIM * 9 // 16,
            bytes_accessed=16 * length * HEAD_DIM * (heads + 2),
            transcendentals=heads * length * length,
        ),
    )(*operands)


def weight_grad_kernel(count, half_tiles, *refs):
    lefts, right_ref, out_ref = refs[:count], refs[count], refs[-1]
    pieces = [ref[...] for ref in lefts]
    if half_tiles:
        pieces[-2:] = [jnp.where(pl.program_id(0) < half_tiles, pieces[-2], pieces[-1])]
    result, start = None, 0
    for piece in pieces:
        part = mm_tn(piece, right_ref[start : start + piece.shape[0], :])
        result = part if result is None else result + part
        start += piece.shape[0]
    if len(refs) > count + 2:
        map_ref, gain_ref, late_ref = refs[count + 1 : count + 4]
        maps = map_ref[:, : result.shape[1]].astype(full)
        of_gain = jnp.sum(maps * result, -1, keepdims=True) / gain_ref[...]
        late = late_ref[...]
        lane = lax.broadcasted_iota(jnp.int32, late.shape, 1)
        result = jnp.concatenate([result, jnp.where(lane == 0, of_gain, late)], 1)
    out_ref[...] = result.astype(low).reshape(out_ref.shape)


def weight_grad(ranks, parts, lefts, right, *extras):
    width = lefts[0].shape[1]
    length, columns = right.shape
    rows = width // (ranks * parts)
    tile = max(min(256, rows * parts), rows)
    each = tile // rows
    wide = columns + (128 if extras else 0)
    half_tiles = lefts[-1].shape[1] // tile if lefts[-1].shape[1] < width else 0

    def place(i):
        return (((i * each) % parts) // each, (i * each) // parts, 0, 0)

    left_specs = [pl.BlockSpec((v.shape[0], tile), lambda i: (0, i)) for v in lefts]
    if half_tiles:
        left_specs[-2:] = [
            pl.BlockSpec((lefts[-1].shape[0], tile), lambda i: (0, jnp.minimum(i, half_tiles - 1))),
            pl.BlockSpec((lefts[-1].shape[0], tile), lambda i: (0, jnp.maximum(i - half_tiles, 0))),
        ]
    return pl.pallas_call(
        functools.partial(weight_grad_kernel, len(lefts), half_tiles),
        grid=(width // tile,),
        out_shape=jax.ShapeDtypeStruct((parts, ranks, rows, wide), low),
        in_specs=left_specs
        + [pl.BlockSpec((length, columns), lambda i: (0, 0))]
        + [pl.BlockSpec((tile, v.shape[1]), lambda i: (i, 0)) for v in extras],
        out_specs=pl.BlockSpec((each, 1, rows, wide), place),
        compiler_params=pltpu.CompilerParams(vmem_limit_bytes=32 << 20),
        cost_estimate=pl.CostEstimate(
            flops=2 * length * width * columns,
            bytes_accessed=2 * (length * (width + columns) + width * columns),
            transcendentals=0,
        ),
    )(*lefts, right, *extras)


def body(
    sizes,
    hidden_in,
    per_layer_input,
    segment_ids,
    positions,
    out_cotangent,
    w_query,
    key_matrix,
    value_matrix,
    w_out_t,
    laurel_maps,
    per_layer_maps,
    norm_gains,
    head_gains,
    w_mlp,
):
    ranks, pairs = sizes["seq"], sizes["pair"]
    block, _, width = hidden_in.shape
    rows = w_query.shape[0]
    q_width = QUERY_HEADS // ranks * HEAD_DIM
    share = QUERY_HEADS // KEY_VALUE_HEADS
    kv_of = [rank * (QUERY_HEADS // ranks) // share for rank in range(ranks)]
    length = block * ranks
    rank = lax.axis_index("seq")
    relative = [rank ^ k for k in range(ranks)]
    cut = lambda v: [v[k * block : (k + 1) * block] for k in range(ranks)]

    by_rank = lambda m: m.reshape(rows, ranks, q_width).transpose(1, 0, 2)
    by_kv = lambda m: jnp.stack([m[:, j * HEAD_DIM : (j + 1) * HEAD_DIM] for j in kv_of])
    head_pack = jnp.concatenate(
        [by_rank(w_query), by_kv(key_matrix), by_kv(value_matrix), by_rank(w_out_t)], 2
    )
    head_rows = head_gains.shape[0]
    small = jnp.concatenate(
        [norm_gains, jnp.pad(head_gains, ((0, rows - head_rows), (0, 0)))], 1
    )
    small = jnp.pad(small, ((0, 0), (0, 128 - small.shape[1])))
    rest_pack = jnp.concatenate([laurel_maps, per_layer_maps, small], 1)
    marks = jnp.pad(jnp.concatenate([segment_ids.T, positions.T], 0), ((0, 6), (0, 0)))
    x_local = hidden_in.reshape(block, width)

    head_all, rest_all, marks_all, x_all = gather_weights(
        sizes, head_pack, rest_pack, marks, x_local
    )
    in_rows, down_rows, head_all = lax.optimization_barrier(
        (w_mlp[:, :2], w_mlp[:, 2], head_all)
    )
    in_maps = lax.all_gather(in_rows, "fsdp", axis=0, tiled=True)
    down_map = lax.all_gather(down_rows, "fsdp", axis=0, tiled=True)
    x_all = x_all.reshape(length, width)
    head_all = head_all.reshape(width, -1)
    rest_all = rest_all.reshape(width, -1)
    qkv_map, out_map = head_all[:, :-q_width], head_all[:, -q_width:]
    laurel = rest_all[:, : 2 * LR]
    ple = rest_all[:, 2 * LR : 2 * LR + 2 * PLE]
    gains = rest_all[:, 2 * LR + 2 * PLE :].astype(full)
    gain = [gains[:, i] for i in range(6)]
    head_scale = gains[:, 6:8].reshape(-1, rows, 2)[:, :head_rows].reshape(HEAD_DIM, 2)

    tokens_all = x_all.astype(full)
    normed_all = norm_rows(tokens_all, gain[0])[0].astype(low)
    tokens = x_local.astype(full)
    x_normed_f, x_inverse = norm_rows(tokens, gain[0])
    normed = x_normed_f.astype(low)
    indices = jnp.concatenate([r * block + jnp.arange(block) for r in relative])
    cos_table, sin_table = rope_tables(marks_all[:, 1].reshape(length))
    allowed = allowed_mask(marks_all[:, 0].reshape(length), indices)

    qkv = mm(normed_all, qkv_map)
    queries, keys, values = head_prep(qkv, head_scale, cos_table, sin_table)
    q_heads = queries.astype(low)
    k_head = keys[:, 0].astype(low)
    v_head = values[:, 0].astype(low)
    head_out, log_total = attend_heads(q_heads, k_head, v_head, allowed)
    attn_in = head_out.astype(low).reshape(length, q_width)
    attn_lin = sum_seq(cut(mm_nt(attn_in, out_map).astype(low)), ranks)

    attn_normed, attn_inverse = norm_rows(attn_lin, gain[1])
    laurel_low = mm(normed, laurel[:, :LR]).astype(low)
    laurel_high = mm_nt(laurel_low, laurel[:, LR:])
    laurel_normed, laurel_inverse = norm_rows(laurel_high, gain[2])
    mixed = (tokens + attn_normed + (normed.astype(full) + laurel_normed)) * root_half
    h_normed_f, h_inverse = norm_rows(mixed, gain[3])
    h_blocks = gather_seq(h_normed_f.astype(low), ranks)
    gate_up = dot(whole_rows(h_blocks), in_maps, ((1,), (0,)))
    gate_part, up_part = gate_up[:, 0], gate_up[:, 1]
    hidden = (gelu_tanh(gate_part) * up_part).astype(low)
    hidden, down_map = lax.optimization_barrier((hidden, down_map))
    ffn_out = sum_seq(cut(mm_nt(hidden, down_map).astype(low)), ranks)

    ffn_normed, ffn_inverse = norm_rows(ffn_out, gain[4])
    h_second = (mixed + ffn_normed).astype(low)
    ple_gate = mm(h_second, ple[:, :PLE])
    ple_input = per_layer_input.reshape(block, PLE).astype(full)
    ple_mixed = (gelu_tanh(ple_gate) * ple_input).astype(low)
    ple_proj = mm_nt(ple_mixed, ple[:, PLE:])
    ple_normed, ple_inverse = norm_rows(ple_proj, gain[5])
    hidden_out = (h_second.astype(full) + ple_normed).astype(low)

    grad_out = out_cotangent.reshape(block, width).astype(full)
    grad_ple_proj, gain_grad_five = norm_back(ple_proj, ple_inverse, gain[5], grad_out)
    grad_ple_low = grad_ple_proj.astype(low)
    grad_ple_mixed = mm(grad_ple_low, ple[:, PLE:])
    unused_gelu, gelu_pull = jax.vjp(gelu_tanh, ple_gate)
    grad_ple_gate = gelu_pull(grad_ple_mixed * ple_input)[0].astype(low)
    grad_second = grad_out + mm_nt(grad_ple_gate, ple[:, :PLE])
    grad_ffn, gain_grad_four = norm_back(ffn_out, ffn_inverse, gain[4], grad_second)
    grad_ffn_blocks = gather_seq(grad_ffn.astype(low), ranks)

    down_grad = mm_tn(whole_rows(grad_ffn_blocks), hidden).astype(low)
    down_sum = lax.psum_scatter(down_grad, "fsdp", scatter_dimension=0, tiled=True)
    grad_ffn_blocks, down_grad = lax.optimization_barrier((grad_ffn_blocks, down_grad))
    grad_hidden = mm(whole_rows(grad_ffn_blocks), down_map)
    gate_act, act_pull = jax.vjp(gelu_tanh, gate_part)
    grad_gate_up = jnp.stack(
        [act_pull(grad_hidden * up_part)[0], grad_hidden * gate_act], 1
    ).astype(low)
    h_part = dot(grad_gate_up, in_maps, ((1, 2), (1, 2))).astype(low)
    grad_h_normed = sum_seq(cut(h_part), ranks)
    h_blocks, h_part = lax.optimization_barrier((h_blocks, h_part))
    in_grad = dot(whole_rows(h_blocks), grad_gate_up, ((0,), (0,))).astype(low)
    in_sum = lax.psum_scatter(in_grad, "fsdp", scatter_dimension=0, tiled=True)

    grad_ple_up = mm_tn(grad_ple_low, ple_mixed)
    grad_ple_down = mm_tn(h_second, grad_ple_gate)
    grad_mixed_norm, gain_grad_three = norm_back(mixed, h_inverse, gain[3], grad_h_normed)
    grad_mixed = grad_second + grad_mixed_norm
    grad_branch = grad_mixed * root_half
    grad_attn, gain_grad_one = norm_back(attn_lin, attn_inverse, gain[1], grad_branch)
    grad_attn_blocks = gather_seq(grad_attn.astype(low), ranks)
    grad_laurel_high, gain_grad_two = norm_back(
        laurel_high, laurel_inverse, gain[2], grad_branch
    )
    grad_high_low = grad_laurel_high.astype(low)
    grad_laurel_up = mm_tn(grad_high_low, laurel_low)
    grad_laurel_low = mm(grad_high_low, laurel[:, LR:]).astype(low)
    grad_laurel_down = mm_tn(normed, grad_laurel_low)

    x_here = grad_branch + mm_nt(grad_laurel_low, laurel[:, :LR])
    gain_grad_zero = jnp.sum(x_here * tokens * x_inverse, 0)
    small_grad = jnp.stack(
        [gain_grad_zero, gain_grad_one, gain_grad_two, gain_grad_three, gain_grad_four, gain_grad_five], 1
    )
    small_grad = jnp.pad(small_grad, ((0, 0), (0, 128 - small_grad.shape[1])))
    rest_grad = jnp.concatenate(
        [grad_ple_down, grad_ple_up, grad_laurel_down, grad_laurel_up, small_grad], 1
    ).astype(low)
    rest_grad = rest_grad.reshape(ranks, -1, rest_grad.shape[1])
    rest_grad, grad_attn_blocks = lax.optimization_barrier((rest_grad, grad_attn_blocks))
    rest_own = take(rest_grad, 0, rank).astype(full) + sum(
        permute(take(rest_grad, 0, relative[k]), "seq", k).astype(full) for k in range(1, ranks)
    )
    rest_own = rest_own.astype(low).reshape(pairs * 2, rows, -1)
    out_grad = weight_grad(ranks, pairs * 2, grad_attn_blocks, attn_in)
    grad_heads = mm(whole_rows(grad_attn_blocks), out_map).astype(low)
    codes = marks_all[:, 0].reshape(length) * (4 * length) + indices
    grad_qkv, grad_gains = attend_back(
        ranks,
        qkv,
        q_heads.reshape(length, q_width),
        k_head,
        v_head,
        grad_heads,
        log_total,
        codes,
        cos_table[:, 0, : HEAD_DIM // 2],
        sin_table[:, 0, : HEAD_DIM // 2],
        head_scale.T,
    )
    grad_head_scale = grad_gains[:2].T
    head_scale_grad = jnp.pad(
        grad_head_scale.reshape(-1, head_rows, 2), ((0, 0), (0, rows - head_rows), (0, 0))
    ).reshape(width, 2)
    late_grad = jnp.pad(head_scale_grad, ((0, 0), (1, 125)))
    last = weight_grad(
        ranks, pairs * 2, [normed_all], grad_qkv, head_all, gain[0][:, None], late_grad
    )
    last, grad_qkv = lax.optimization_barrier((last, grad_qkv))
    x_part = mm_nt(grad_qkv, qkv_map).astype(low)

    half = rows // 2
    folded = jnp.concatenate(
        [rest_own[:, :half, 2 * PLE :], rest_own[:, half:, 2 * PLE :]], 2
    )
    out_grad = out_grad.reshape(pairs * 2, ranks * rows, q_width)
    first = [out_grad, rest_own[:, :, : 2 * PLE], folded]
    if q_width != 2 * PLE:
        first[0] = out_grad.reshape(pairs * 2, -1, 2 * PLE)
    first = jnp.concatenate(first, 1)
    first, last, x_part, in_sum, down_sum = lax.optimization_barrier(
        (first, last, x_part, in_sum, down_sum)
    )
    first_sum = lax.psum_scatter(first, "fsdp", scatter_dimension=0, tiled=False).astype(low)
    last = last.reshape(width, -1)
    last_sum = lax.psum_scatter(last, "fsdp", scatter_dimension=0, tiled=True)
    last_sum = last_sum.reshape(ranks, rows, -1)

    out_end = first.shape[1] - rows - half
    out_sum = first_sum[:out_end].reshape(ranks, rows, q_width)
    ple_sum = first_sum[out_end : out_end + rows].astype(full)
    folded = first_sum[out_end + rows :].astype(full)
    other_sum = jnp.concatenate([folded[:, : folded.shape[1] // 2], folded[:, folded.shape[1] // 2 :]], 0)

    def across(part):
        got = jnp.stack(
            [take(part, 0, rank)]
            + [permute(take(part, 0, relative[k]), "seq", k) for k in range(1, ranks)]
        )
        return [take(got, 0, r ^ rank).astype(full) for r in range(ranks)]

    out_ranks, last_ranks = across(out_sum), across(last_sum)

    grad_x_normed = x_here + sum_seq(cut(x_part), ranks)
    grad_tokens_norm = norm_back(tokens, x_inverse, gain[0], grad_x_normed)[0]
    input_grad = grad_mixed * root_half + grad_tokens_norm

    late_sum = sum(part[:, q_width + 2 * HEAD_DIM :] for part in last_ranks)
    gain_sum = other_sum[:, 2 * LR : 2 * LR + 6]
    gain_sum = jnp.concatenate([gain_sum[:, :1] + late_sum[:, :1], gain_sum[:, 1:]], 1)
    scale_sum = late_sum[:head_rows, 1:3]

    def of_kv(parts):
        return jnp.concatenate(
            [
                sum(parts[r] for r in range(ranks) if kv_of[r] == j)
                for j in range(KEY_VALUE_HEADS)
            ],
            1,
        )

    grad_mlp = jnp.concatenate([in_sum, down_sum[:, None]], 1).astype(full)
    lead = (block, 1, width)
    return (
        hidden_out.reshape(lead),
        input_grad.reshape(lead),
        jnp.concatenate([part[:, :q_width] for part in last_ranks], 1),
        of_kv([part[:, q_width : q_width + HEAD_DIM] for part in last_ranks]),
        of_kv([part[:, q_width + HEAD_DIM : q_width + 2 * HEAD_DIM] for part in last_ranks]),
        jnp.concatenate(out_ranks, 1),
        other_sum[:, : 2 * LR],
        ple_sum,
        gain_sum,
        scale_sum,
        grad_mlp,
    )


def solution(mesh):
    sizes = {"seq": mesh.shape["seq"], "pair": mesh.shape["fsdp"] // 2, "core": 2}
    spread = P(("seq", "fsdp"), None)
    tokens = P("seq", "fsdp", None)
    return jax.shard_map(
        functools.partial(body, sizes),
        mesh=mesh,
        in_specs=(tokens, tokens, P("seq", "fsdp"), P("seq", "fsdp"), tokens)
        + (spread,) * 8
        + (P("fsdp", None, "seq"),),
        out_specs=(tokens, tokens) + (spread,) * 8 + (P("fsdp", None, "seq"),),
        check_vma=False,
    )
```

```python
import functools
import math

import jax
import jax.numpy as jnp
from jax import lax
from jax.experimental import pallas as pl
from jax.experimental.pallas import tpu as pltpu
from jax.sharding import PartitionSpec as P

QUERY_HEADS = 8
KEY_VALUE_HEADS = 2
HEAD_DIM = 256
LR = 64
PLE = 256
WIN = 512

MESH = pl.DeviceIdType.MESH
eps = 1e-06
theta = 10000.0
root_half = 1.0 / math.sqrt(2.0)
low = jnp.bfloat16
full = jnp.float32


def flip(index, offset, size):
    value, bit = 0, 1
    while bit < size:
        has = (index // bit) % 2
        value = value + bit * ((1 - has) if offset & bit else has)
        bit *= 2
    return value


def gather_kernel(
    sizes, head_ref, rest_ref, mark_ref, x_ref, head_out, rest_out, mark_out, x_out, *sems
):
    (local, head_s1, head_r1, right_s, right_r, left_s, left_r, head_s3, head_r3) = sems[:9]
    (rest_s1, rest_r1, rest_s2, rest_r2, rest_s3, rest_r3, mark_s, mark_r, x_s, x_r) = sems[9:]
    ranks, pairs = sizes["seq"], sizes["pair"]
    rank = lax.axis_index("seq")
    fsdp_index = lax.axis_index("fsdp")
    pair, core = fsdp_index // 2, fsdp_index % 2
    sibling = (rank, pair * 2 + 1 - core)

    def on_seq(step):
        return (flip(rank, step, ranks), fsdp_index)

    def on_pair(step):
        return (rank, ((pair + step) % pairs) * 2 + core)

    def remote(source, target, send, recv, device):
        return pltpu.make_async_remote_copy(
            src_ref=source,
            dst_ref=target,
            send_sem=send,
            recv_sem=recv,
            device_id=device,
            device_id_type=MESH,
        )

    barrier = pltpu.get_barrier_semaphore()
    devices = [on_seq(i) for i in range(1, ranks)] + [on_pair(i) for i in range(1, pairs)]
    for device in devices + [sibling]:
        pl.semaphore_signal(barrier, inc=1, device_id=device, device_id_type=MESH)
    pl.semaphore_wait(barrier, len(devices) + 1)

    sent = []

    def go(copy):
        copy.start()
        sent.append(copy)
        return copy

    def part(at, k):
        return head_out.at[flip(rank, k, ranks), at, core]

    def right(t, k):
        source = head_ref.at[rank] if t == 1 and k == 0 else part(pair - (t - 1), k)
        slot = (t - 1) * ranks + k
        target = part(pair - (t - 1), k)
        return remote(source, target, right_s.at[slot], right_r.at[slot], (rank, fsdp_index + 2))

    def left(t, k):
        source = head_ref.at[rank] if t == 1 and k == 0 else part(pair + (t - 1), k)
        slot = (t - 1) * ranks + k
        target = part(pair + (t - 1), k)
        return remote(source, target, left_s.at[slot], left_r.at[slot], (rank, fsdp_index - 2))

    def to_sibling(t, k):
        source = head_ref.at[rank] if t == 0 and k == 0 else part(pair - t, k)
        slot = (t + pairs - 1) * ranks + k
        return remote(source, part(pair - t, k), head_s3.at[slot], head_r3.at[slot], sibling)

    sends_right = lambda t: (pair - (t - 1) >= 0) & (pair + 1 < pairs)
    sends_left = lambda t: (pair + (t - 1) < pairs) & (pair - 1 >= 0)

    def begin(k):
        pl.when(sends_right(1))(lambda: right(1, k).start())
        pl.when(sends_left(1))(lambda: left(1, k).start())
        to_sibling(0, k).start()

    begin(0)
    head_seq = [
        go(
            remote(
                head_ref.at[on_seq(i)[0]],
                head_out.at[rank, pair, core],
                head_s1.at[i - 1],
                head_r1.at[i - 1],
                on_seq(i),
            )
        )
        for i in range(1, ranks)
    ]
    rest_pair = [
        go(
            remote(
                rest_ref,
                rest_out.at[rank, pair, core],
                rest_s1.at[i - 1],
                rest_r1.at[i - 1],
                on_pair(i),
            )
        )
        for i in range(1, pairs)
    ]
    owns = [
        pltpu.make_async_copy(head_ref.at[rank], head_out.at[rank, pair, core], local.at[0]),
        pltpu.make_async_copy(rest_ref, rest_out.at[rank, pair, core], local.at[1]),
        pltpu.make_async_copy(mark_ref, mark_out.at[0], local.at[2]),
        pltpu.make_async_copy(x_ref, x_out.at[0], local.at[3]),
    ]
    for copy in owns:
        copy.start()
    marks = [
        go(remote(mark_ref, mark_out.at[i], mark_s.at[i - 1], mark_r.at[i - 1], on_seq(i)))
        for i in range(1, ranks)
    ]
    for k in range(1, ranks):
        head_seq[k - 1].wait_recv()
        begin(k)

    half = x_ref.shape[1] // 2
    first, second = slice(0, half), slice(half, 2 * half)
    x_seq, relays = [], []
    if ranks == 4:
        for order in range(2):
            for i, columns in ((1, (first, second)[order]), (2, (second, first)[order])):
                slot = (i - 1) * 2 + order
                x_seq.append(
                    go(
                        remote(
                            x_ref.at[:, columns],
                            x_out.at[i, :, columns],
                            x_s.at[slot],
                            x_r.at[slot],
                            on_seq(i),
                        )
                    )
                )
    else:
        for i in range(1, ranks):
            x_seq.append(
                go(remote(x_ref, x_out.at[i], x_s.at[i - 1], x_r.at[i - 1], on_seq(i)))
            )

    owns[1].wait()
    for copy in rest_pair:
        copy.wait_recv()
    row = rest_out.at[rank, :, core]
    rest_seq = [
        go(remote(row, row, rest_s2.at[i - 1], rest_r2.at[i - 1], on_seq(i)))
        for i in range(1, ranks)
    ]
    rest_core = [go(remote(row, row, rest_s3.at[0], rest_r3.at[0], sibling))]

    for t in range(1, pairs):
        for k in range(ranks):

            def from_left(t=t, k=k):
                slot = (t - 1) * ranks + k
                target = part(pair - t, k)
                remote(target, target, right_s.at[slot], right_r.at[slot], sibling).wait_recv()
                if t + 1 < pairs:
                    pl.when(pair + 1 < pairs)(lambda: right(t + 1, k).start())
                to_sibling(t, k).start()

            def from_right(t=t, k=k):
                slot = (t - 1) * ranks + k
                target = part(pair + t, k)
                remote(target, target, left_s.at[slot], left_r.at[slot], sibling).wait_recv()
                if t + 1 < pairs:
                    pl.when(pair - 1 >= 0)(lambda: left(t + 1, k).start())
                to_sibling(-t, k).start()

            pl.when(pair - t >= 0)(from_left)
            pl.when(pair + t < pairs)(from_right)
        if t == 1 and ranks == 4:
            x_seq[0].wait_recv()
            x_seq[1].wait_recv()
            for slot, i, columns, to in ((4, 1, first, 2), (5, 2, second, 1)):
                relays.append(
                    go(
                        remote(
                            x_out.at[i, :, columns],
                            x_out.at[3, :, columns],
                            x_s.at[slot],
                            x_r.at[slot],
                            on_seq(to),
                        )
                    )
                )

    for i in range(1, ranks):
        rest_seq[i - 1].wait_recv()
        row = rest_out.at[flip(rank, i, ranks), :, core]
        rest_core.append(go(remote(row, row, rest_s3.at[i], rest_r3.at[i], sibling)))
    owns[0].wait()
    for copy in owns[2:]:
        copy.wait()
    for copy in marks + x_seq[2 if ranks == 4 else 0 :] + relays + rest_core:
        copy.wait_recv()
    for k in range(ranks):
        to_sibling(0, k).wait()
        for t in range(1, pairs):
            pl.when(pair - t >= 0)(lambda t=t, k=k: to_sibling(t, k).wait())
            pl.when(pair + t < pairs)(lambda t=t, k=k: to_sibling(-t, k).wait())
            pl.when(sends_right(t))(lambda t=t, k=k: right(t, k).wait_send())
            pl.when(sends_left(t))(lambda t=t, k=k: left(t, k).wait_send())
    for copy in sent:
        copy.wait_send()


def gather_weights(sizes, head, rest, marks, x):
    ranks, pairs = sizes["seq"], sizes["pair"]
    dma = lambda n: pltpu.SemaphoreType.DMA((n,))
    anywhere = pl.BlockSpec(memory_space=pl.ANY)
    return pl.pallas_call(
        functools.partial(gather_kernel, sizes),
        out_shape=(
            jax.ShapeDtypeStruct((ranks, pairs, 2) + head.shape[1:], head.dtype),
            jax.ShapeDtypeStruct((ranks, pairs, 2) + rest.shape, rest.dtype),
            jax.ShapeDtypeStruct((ranks,) + marks.shape, marks.dtype),
            jax.ShapeDtypeStruct((ranks,) + x.shape, x.dtype),
        ),
        in_specs=[anywhere] * 4,
        out_specs=(anywhere,) * 4,
        scratch_shapes=[
            dma(4),
            *[dma(ranks - 1)] * 2,
            *[dma((pairs - 1) * ranks)] * 4,
            *[dma((2 * pairs - 1) * ranks)] * 2,
            *[dma(pairs - 1)] * 2,
            *[dma(ranks - 1)] * 2,
            *[dma(ranks)] * 2,
            *[dma(ranks - 1)] * 2,
            *[dma(2 * ranks - 2)] * 2,
        ],
        compiler_params=pltpu.CompilerParams(collective_id=0, has_side_effects=True),
    )(head, rest, marks, x)


def permute(v, axis, offset):
    size = lax.axis_size(axis)
    return lax.ppermute(v, axis, [(i, i ^ offset) for i in range(size)])


def gather_seq(v, ranks):
    if ranks != 4:
        return [v] + [permute(v, "seq", k) for k in range(1, ranks)]
    half = v.shape[1] // 2
    first, second = permute(v, "seq", 1), permute(v, "seq", 2)
    left = permute(first[:, :half], "seq", 2)
    right = permute(second[:, half:], "seq", 1)
    return [v, first, second, left, right]


def whole_rows(blocks):
    if blocks[-1].shape[1] < blocks[0].shape[1]:
        blocks = blocks[:-2] + [jnp.concatenate(blocks[-2:], 1)]
    return jnp.concatenate(blocks, 0)


def sum_seq(blocks, ranks):
    up = lambda v: v.astype(full)
    if ranks != 4:
        return sum((up(permute(blocks[k], "seq", k)) for k in range(1, ranks)), up(blocks[0]))
    half = blocks[0].shape[1] // 2
    left = [b[:, :half] for b in blocks]
    right = [b[:, half:] for b in blocks]
    left_far, right_far = permute(left[3], "seq", 1), permute(right[3], "seq", 2)
    left_near, right_near = permute(left[1], "seq", 1), permute(right[2], "seq", 2)
    left_far = permute((up(left[2]) + up(left_far)).astype(low), "seq", 2)
    right_far = permute((up(right[1]) + up(right_far)).astype(low), "seq", 1)
    return jnp.concatenate(
        [
            up(left[0]) + up(left_near) + up(left_far),
            up(right[0]) + up(right_near) + up(right_far),
        ],
        1,
    )


def take(v, axis, index):
    return lax.dynamic_index_in_dim(v, index, axis, keepdims=False)


def gather_everywhere(v, after, ranks, pairs):
    v, after = lax.optimization_barrier((v, after))
    index, rank = lax.axis_index("fsdp"), lax.axis_index("seq")
    pair, core = index // 2, index % 2

    def spread(part, axis, offsets, mine):
        got = jnp.stack([part] + [permute(part, axis, k) for k in offsets])
        return jnp.stack([take(got, 0, mine ^ i) for i in range(len(offsets) + 1)])

    v = spread(v, "fsdp", [2 * k for k in range(1, pairs)], pair)
    v = spread(v, "seq", range(1, ranks), rank)
    v = spread(v, "fsdp", [1], core)
    return jnp.moveaxis(v, 0, 2).reshape(-1, v.shape[-1])


def dot(left, right, over):
    return lax.dot_general(left, right, (over, ((), ())), preferred_element_type=full)


def mm(left, right):
    return dot(left, right, ((1,), (0,)))


def mm_nt(left, right):
    return dot(left, right, ((1,), (1,)))


def mm_tn(left, right):
    return dot(left, right, ((0,), (0,)))


def norm_rows(v, gain_vec):
    inverse = lax.rsqrt(jnp.mean(v * v, -1, keepdims=True) + eps)
    return (v * inverse * gain_vec, inverse)


def norm_back(v, inverse, gain_vec, incoming):
    scaled = incoming * gain_vec
    inner_mean = jnp.mean(scaled * v, -1, keepdims=True)
    return (
        inverse * (scaled - v * inverse * inverse * inner_mean),
        jnp.sum(incoming * v * inverse, axis=0),
    )


def gelu_tanh(v):
    return jax.nn.gelu(v, approximate=True)


def rope_tables(places):
    half_width = HEAD_DIM // 2
    frequency = theta ** (-jnp.arange(half_width).astype(full) * 2.0 / HEAD_DIM)
    angles = places.astype(full)[:, None] * frequency
    angles = jnp.concatenate([angles, angles], -1)[:, None, :]
    return (jnp.cos(angles), jnp.sin(angles))


def rotate(v, cos_table, sin_table):
    half_width = v.shape[-1] // 2
    turned = jnp.concatenate([-v[..., half_width:], v[..., :half_width]], -1)
    return v * cos_table + turned * sin_table


def head_prep(qkv, head_scale, cos_table, sin_table):
    per_head = qkv.reshape(qkv.shape[0], -1, HEAD_DIM)
    queries = rotate(norm_rows(per_head[:, :-2], head_scale[:, 0])[0], cos_table, sin_table)
    keys = rotate(norm_rows(per_head[:, -2:-1], head_scale[:, 1])[0], cos_table, sin_table)
    values = norm_rows(per_head[:, -1:], 1.0)[0]
    return (queries, keys, values)


def allowed_mask(segments, indices):
    offset = indices[:, None] - indices[None, :]
    nearby = (offset >= 0) & (offset < WIN)
    return (segments[:, None] == segments[None, :]) & nearby


def scores_of(q_heads, keys, allowed):
    raw_scores = jnp.einsum("qhd,kd->hqk", q_heads, keys, preferred_element_type=full)
    return jnp.where(allowed[None], raw_scores * HEAD_DIM ** (-0.5), -1000000000.0)


def attend_heads(q_heads, keys, values, allowed):
    scores = scores_of(q_heads, keys, allowed)
    row_peak = jnp.max(scores, -1, keepdims=True)
    exp_scores = jnp.exp(scores - row_peak)
    row_total = jnp.sum(exp_scores, -1, keepdims=True)
    attn_probs = exp_scores / row_total
    head_out = jnp.einsum(
        "hqk,kd->qhd", attn_probs.astype(low), values, preferred_element_type=full
    )
    return (head_out, row_peak + jnp.log(row_total))


def norm_rope_back(lin, gain, incoming):
    inverse = lax.rsqrt(jnp.mean(lin * lin, -1, keepdims=True) + eps)
    scaled = incoming * gain
    inner_mean = jnp.mean(scaled * lin, -1, keepdims=True)
    return (
        inverse * (scaled - lin * inverse * inverse * inner_mean),
        jnp.sum(incoming * lin * inverse, 0, keepdims=True),
    )


def attend_back_kernel(
    ranks,
    block,
    qkv_ref,
    q_ref,
    k_ref,
    v_ref,
    grad_ref,
    total_ref,
    code_col_ref,
    code_row_ref,
    cos_ref,
    sin_ref,
    gain_ref,
    out_ref,
    gain_out_ref,
    key_acc,
    value_acc,
    query_acc,
    row_acc,
    probs_ref,
    grad_probs_ref,
):
    head, mine = pl.program_id(0), pl.program_id(1)
    heads = pl.num_programs(0)
    rank = lax.axis_index("seq")
    scale = HEAD_DIM ** (-0.5)
    half = HEAD_DIM // 2

    @pl.when((head == 0) & (mine == 0))
    def _():
        key_acc[...] = jnp.zeros_like(key_acc)
        value_acc[...] = jnp.zeros_like(value_acc)
        gain_out_ref[...] = jnp.zeros_like(gain_out_ref)

    rows = pl.ds(pl.multiple_of(mine * block, block), block)
    columns = pl.ds(pl.multiple_of(head * HEAD_DIM, HEAD_DIM), HEAD_DIM)
    q, grad = q_ref[rows, columns], grad_ref[rows, columns]
    code = code_col_ref[rows, :]
    peaks = total_ref[head, rows, :]
    row_acc[...] = jnp.zeros_like(row_acc)
    query_acc[...] = jnp.zeros_like(query_acc)

    def reaches(other):
        apart = (rank ^ mine) - (rank ^ other)
        return (apart >= 0) & (apart * block - (block - 1) < WIN)

    for other in range(ranks):
        span = slice(other * block, (other + 1) * block)

        @pl.when(reaches(other))
        def _():
            scores = mm_nt(q, k_ref[span, :]) * scale
            offset = code - code_row_ref[:, span]
            probs = jnp.where((offset >= 0) & (offset < WIN), jnp.exp(scores - peaks), 0.0)
            grad_probs = mm_nt(grad, v_ref[span, :])
            probs_ref[other] = probs
            grad_probs_ref[other] = grad_probs
            row_acc[...] += jnp.sum(probs * grad_probs, -1, keepdims=True)

    inner = row_acc[...]
    for other in range(ranks):
        span = slice(other * block, (other + 1) * block)

        @pl.when(reaches(other))
        def _():
            probs = probs_ref[other]
            grad_scores = (probs * (grad_probs_ref[other] - inner) * scale).astype(low)
            query_acc[...] += mm(grad_scores, k_ref[span, :])
            key_acc[span, :] += mm_tn(grad_scores, q)
            value_acc[span, :] += mm_tn(probs.astype(low), grad)

    def turned_back(v, cos_table, sin_table):
        first, second = v[:, :half], v[:, half:]
        return jnp.concatenate(
            [
                first * cos_table + second * sin_table,
                second * cos_table - first * sin_table,
            ],
            1,
        )

    incoming = turned_back(query_acc[...].astype(low).astype(full), cos_ref[rows, :], sin_ref[rows, :])
    grad_lin, grad_gain = norm_rope_back(qkv_ref[rows, columns], gain_ref[0:1, :], incoming)
    out_ref[rows, columns] = grad_lin.astype(low)
    gain_out_ref[0:1, :] += grad_gain

    @pl.when((head == heads - 1) & (mine == ranks - 1))
    def _():
        base = out_ref.shape[1] - 2 * HEAD_DIM
        for other in range(ranks):
            span = slice(other * block, (other + 1) * block)
            incoming = turned_back(key_acc[span, :], cos_ref[span, :], sin_ref[span, :])
            grad_lin, grad_gain = norm_rope_back(
                qkv_ref[span, base : base + HEAD_DIM], gain_ref[1:2, :], incoming
            )
            out_ref[span, base : base + HEAD_DIM] = grad_lin.astype(low)
            gain_out_ref[1:2, :] += grad_gain
            grad_lin = norm_rope_back(qkv_ref[span, base + HEAD_DIM :], 1.0, value_acc[span, :])[0]
            out_ref[span, base + HEAD_DIM :] = grad_lin.astype(low)


def attend_back(ranks, qkv, q, k, v, grad, total, codes, cos_table, sin_table, gains):
    length = qkv.shape[0]
    block = length // ranks
    heads = q.shape[1] // HEAD_DIM
    whole = lambda v: pl.BlockSpec(
        v.shape, lambda i, j, n=len(v.shape): (0,) * n, pipeline_mode=pl.Buffered(1)
    )
    operands = (qkv, q, k, v, grad, total, codes[:, None], codes[None], cos_table, sin_table, gains)
    results = (
        jax.ShapeDtypeStruct(qkv.shape, low),
        jax.ShapeDtypeStruct((8, HEAD_DIM), full),
    )
    return pl.pallas_call(
        functools.partial(attend_back_kernel, ranks, block),
        grid=(heads, ranks),
        out_shape=results,
        in_specs=[whole(v) for v in operands],
        out_specs=tuple(whole(v) for v in results),
        scratch_shapes=[
            pltpu.VMEM((length, HEAD_DIM), full),
            pltpu.VMEM((length, HEAD_DIM), full),
            pltpu.VMEM((block, HEAD_DIM), full),
            pltpu.VMEM((block, 1), full),
            pltpu.VMEM((ranks, block, block), full),
            pltpu.VMEM((ranks, block, block), full),
        ],
        compiler_params=pltpu.CompilerParams(vmem_limit_bytes=40 << 20),
        cost_estimate=pl.CostEstimate(
            flops=10 * heads * length * length * HEAD_DIM * 9 // 16,
            bytes_accessed=16 * length * HEAD_DIM * (heads + 2),
            transcendentals=heads * length * length,
        ),
    )(*operands)


def weight_grad_kernel(count, half_tiles, *refs):
    lefts, right_ref, out_ref = refs[:count], refs[count], refs[-1]
    pieces = [ref[...] for ref in lefts]
    if half_tiles:
        pieces[-2:] = [jnp.where(pl.program_id(0) < half_tiles, pieces[-2], pieces[-1])]
    result, start = None, 0
    for piece in pieces:
        part = mm_tn(piece, right_ref[start : start + piece.shape[0], :])
        result = part if result is None else result + part
        start += piece.shape[0]
    if len(refs) > count + 2:
        map_ref, gain_ref, late_ref = refs[count + 1 : count + 4]
        maps = map_ref[:, : result.shape[1]].astype(full)
        of_gain = jnp.sum(maps * result, -1, keepdims=True) / gain_ref[...]
        late = late_ref[...]
        lane = lax.broadcasted_iota(jnp.int32, late.shape, 1)
        result = jnp.concatenate([result, jnp.where(lane == 0, of_gain, late)], 1)
    out_ref[...] = result.astype(low).reshape(out_ref.shape)


def weight_grad(ranks, parts, lefts, right, *extras):
    width = lefts[0].shape[1]
    length, columns = right.shape
    rows = width // (ranks * parts)
    tile = max(min(256, rows * parts), rows)
    each = tile // rows
    wide = columns + (128 if extras else 0)
    half_tiles = lefts[-1].shape[1] // tile if lefts[-1].shape[1] < width else 0

    def place(i):
        return (((i * each) % parts) // each, (i * each) // parts, 0, 0)

    left_specs = [pl.BlockSpec((v.shape[0], tile), lambda i: (0, i)) for v in lefts]
    if half_tiles:
        left_specs[-2:] = [
            pl.BlockSpec((lefts[-1].shape[0], tile), lambda i: (0, jnp.minimum(i, half_tiles - 1))),
            pl.BlockSpec((lefts[-1].shape[0], tile), lambda i: (0, jnp.maximum(i - half_tiles, 0))),
        ]
    return pl.pallas_call(
        functools.partial(weight_grad_kernel, len(lefts), half_tiles),
        grid=(width // tile,),
        out_shape=jax.ShapeDtypeStruct((parts, ranks, rows, wide), low),
        in_specs=left_specs
        + [pl.BlockSpec((length, columns), lambda i: (0, 0))]
        + [pl.BlockSpec((tile, v.shape[1]), lambda i: (i, 0)) for v in extras],
        out_specs=pl.BlockSpec((each, 1, rows, wide), place),
        compiler_params=pltpu.CompilerParams(vmem_limit_bytes=32 << 20),
        cost_estimate=pl.CostEstimate(
            flops=2 * length * width * columns,
            bytes_accessed=2 * (length * (width + columns) + width * columns),
            transcendentals=0,
        ),
    )(*lefts, right, *extras)


def middle_kernel(
    block,
    parts,
    hidden_ref,
    map_ref,
    mixed_ref,
    gain_ref,
    ple_gate_ref,
    ple_proj_ref,
    ple_input_ref,
    cotangent_ref,
    rows_ref,
    grad_map_ref,
    out_ref,
    second_ref,
    grad_second_ref,
    grad_ple_ref,
    ple_mixed_ref,
    grad_gate_ref,
    gain_out_ref,
    maps,
    own,
    keep_left,
    keep_right,
    send_x,
    send_y,
    got_x,
    got_y,
    relay_x,
    relay_y,
    far_x,
    far_y,
    stage,
    map_sem,
    stage_sem,
    *sems,
):
    (sx_s, sx_r, sy_s, sy_r, rx_s, rx_r, ry_s, ry_r) = sems[:8]
    (gx_s, gx_r, gy_s, gy_r, fx_s, fx_r, fy_s, fy_r) = sems[8:]
    rank = lax.axis_index("seq")
    fsdp_index = lax.axis_index("fsdp")
    by_x, by_y = (flip(rank, 1, 4), fsdp_index), (flip(rank, 2, 4), fsdp_index)
    size = block // parts
    width = map_ref.shape[0]
    half = width // 2
    tile = 256
    tiles = width // tile
    left, right = slice(0, half), slice(half, width)
    up = lambda v: v.astype(full)

    def remote(source, target, send, recv, device):
        return pltpu.make_async_remote_copy(
            src_ref=source,
            dst_ref=target,
            send_sem=send,
            recv_sem=recv,
            device_id=device,
            device_id_type=MESH,
        )

    def map_copy(i):
        at = pl.ds(pl.multiple_of(i * tile, tile), tile)
        return pltpu.make_async_copy(map_ref.at[at, :], maps.at[at, :], map_sem.at[i])

    for i in range(tiles):
        map_copy(i).start()

    barrier = pltpu.get_barrier_semaphore()
    for device in (by_x, by_y):
        pl.semaphore_signal(barrier, inc=1, device_id=device, device_id_type=MESH)
    pl.semaphore_wait(barrier, 2)

    sent = []

    def go(copy):
        copy.start()
        sent.append(copy)
        return copy

    def rows_of(u):
        return pl.ds(u * size, size)

    near_x, near_y = [], []
    for u in range(parts):
        at = rows_of(u)

        def product(i):
            if u == 0:
                map_copy(i).wait()
            rows = pl.ds(pl.multiple_of(i * tile, tile), tile)
            v = hidden_ref[:, at, :].reshape(4 * size, hidden_ref.shape[2])
            return mm_nt(v, maps[rows, :]).reshape(4, size, tile)

        def left_tile(i, carry):
            v = product(i)
            columns = pl.ds(pl.multiple_of(i * tile, tile), tile)
            own[at, columns] = v[0]
            keep_left[at, columns] = v[2]
            send_x[u, 0, :, columns] = v[3].astype(low)
            send_x[u, 1, :, columns] = v[1].astype(low)
            return carry

        def right_tile(i, carry):
            v = product(i + tiles // 2)
            columns = pl.ds(pl.multiple_of(i * tile, tile), tile)
            own[at, pl.ds(pl.multiple_of(half + i * tile, tile), tile)] = v[0]
            keep_right[at, columns] = v[1]
            send_y[u, 0, :, columns] = v[3].astype(low)
            send_y[u, 1, :, columns] = v[2].astype(low)
            return carry

        lax.fori_loop(0, tiles // 2, left_tile, 0)
        near_x.append(go(remote(send_x.at[u], got_x.at[u], sx_s.at[u], sx_r.at[u], by_x)))
        lax.fori_loop(0, tiles // 2, right_tile, 0)
        near_y.append(go(remote(send_y.at[u], got_y.at[u], sy_s.at[u], sy_r.at[u], by_y)))

    last_x, last_y = [], []
    for u in range(parts):
        at = rows_of(u)
        near_x[u].wait_recv()
        relay_y[u] = (keep_left[at, :] + up(got_x[u, 0])).astype(low)
        last_y.append(go(remote(relay_y.at[u], far_y.at[u], ry_s.at[u], ry_r.at[u], by_y)))
        near_y[u].wait_recv()
        relay_x[u] = (keep_right[at, :] + up(got_y[u, 0])).astype(low)
        last_x.append(go(remote(relay_x.at[u], far_x.at[u], rx_s.at[u], rx_r.at[u], by_x)))

    gain_out_ref[...] = jnp.zeros_like(gain_out_ref)
    ffn_gain, ple_gain = gain_ref[0:1, :], gain_ref[1:2, :]
    mean = lambda v: jnp.mean(v, -1, keepdims=True)
    total = lambda v: jnp.sum(v, 0, keepdims=True)
    slope, cubic = math.sqrt(2.0 / math.pi), 0.044715
    rows_x, rows_y = [], []
    for u in range(parts):
        at = rows_of(u)
        last_y[u].wait_recv()
        last_x[u].wait_recv()
        own[at, left] = own[at, left] + up(got_x[u, 1]) + up(far_y[u])
        own[at, right] = own[at, right] + up(got_y[u, 1]) + up(far_x[u])
        f = own[at, :]
        f_inverse = lax.rsqrt(mean(f * f) + eps)
        second = (mixed_ref[at, :] + f * f_inverse * ffn_gain).astype(low)
        second_ref[at, :] = second
        gate = mm(second, ple_gate_ref[...])
        bend = jnp.tanh(slope * (gate + cubic * gate * gate * gate))
        gate_slope = 0.5 * (1.0 + bend) + 0.5 * gate * (1.0 - bend * bend) * slope * (
            1.0 + 3.0 * cubic * gate * gate
        )
        given = up(ple_input_ref[at, :])
        ple_mixed = (0.5 * gate * (1.0 + bend) * given).astype(low)
        ple_mixed_ref[at, :] = ple_mixed
        proj = mm_nt(ple_mixed, ple_proj_ref[...])
        proj_inverse = lax.rsqrt(mean(proj * proj) + eps)
        out_ref[at, :] = (up(second) + proj * proj_inverse * ple_gain).astype(low)
        incoming = up(cotangent_ref[at, :])
        gain_out_ref[1:2, :] += total(incoming * proj * proj_inverse)
        scaled = incoming * ple_gain
        grad_proj = proj_inverse * (
            scaled - proj * (proj_inverse * proj_inverse * mean(scaled * proj))
        )
        grad_ple = grad_proj.astype(low)
        grad_ple_ref[at, :] = grad_ple
        grad_gate = (mm(grad_ple, ple_proj_ref[...]) * given * gate_slope).astype(low)
        grad_gate_ref[at, :] = grad_gate
        grad_second = incoming + mm_nt(grad_gate, ple_gate_ref[...])
        grad_second_ref[at, :] = grad_second
        f = own[at, :]
        gain_out_ref[0:1, :] += total(grad_second * f * f_inverse)
        scaled = grad_second * ffn_gain
        grad_f = f_inverse * (scaled - f * (f_inverse * f_inverse * mean(scaled * f)))
        rows_ref[0, at, :] = grad_f.astype(low)
        pair_x, pair_y = [], []
        for order in range(2):
            for pairs, device, send, recv, index, part in (
                (pair_x, by_x, gx_s, gx_r, 1, (left, right)[order]),
                (pair_y, by_y, gy_s, gy_r, 2, (right, left)[order]),
            ):
                pairs.append(
                    go(
                        remote(
                            rows_ref.at[0, at, part],
                            rows_ref.at[index, at, part],
                            send.at[u, order],
                            recv.at[u, order],
                            device,
                        )
                    )
                )
        rows_x.append(pair_x)
        rows_y.append(pair_y)

    far = []
    for u in range(parts):
        at = rows_of(u)
        rows_x[u][0].wait_recv()
        far.append(
            go(
                remote(
                    rows_ref.at[1, at, left],
                    rows_ref.at[3, at, left],
                    fy_s.at[u],
                    fy_r.at[u],
                    by_y,
                )
            )
        )
        rows_y[u][0].wait_recv()
        far.append(
            go(
                remote(
                    rows_ref.at[2, at, right],
                    rows_ref.at[3, at, right],
                    fx_s.at[u],
                    fx_r.at[u],
                    by_x,
                )
            )
        )
    for u in range(parts):
        rows_x[u][1].wait_recv()
        rows_y[u][1].wait_recv()
    for copy in far:
        copy.wait_recv()

    def stage_copy(i, slot):
        at = pl.ds(pl.multiple_of(i * tile, tile), tile)
        return pltpu.make_async_copy(stage.at[slot], grad_map_ref.at[at, :], stage_sem.at[slot])

    span = hidden_ref.shape[2]

    def grad_tile(i, carry):
        slot = i % 2

        @pl.when(i >= 2)
        def _():
            stage_copy(i - 2, slot).wait()

        columns = pl.ds(pl.multiple_of(i * tile, tile), tile)
        v = rows_ref[:, :, columns].reshape(4 * block, tile)
        for j in range(0, span, span // 2):
            w = hidden_ref[:, :, j : j + span // 2].reshape(4 * block, span // 2)
            stage[slot, :, j : j + span // 2] = mm_tn(v, w).astype(low)
        stage_copy(i, slot).start()
        return carry

    lax.fori_loop(0, tiles, grad_tile, 0)
    stage_copy(tiles - 2, 0).wait()
    stage_copy(tiles - 1, 1).wait()
    for copy in sent:
        copy.wait_send()


def middle(hidden, down_map, mixed, gains, ple, ple_input, cotangent):
    block, width = mixed.shape
    span = hidden.shape[1]
    parts, half = 2, width // 2
    size = block // parts
    hidden = hidden.reshape(4, block, span)
    dma = pltpu.SemaphoreType.DMA
    vmem = pl.BlockSpec(memory_space=pltpu.VMEM)
    anywhere = pl.BlockSpec(memory_space=pl.ANY)
    pieces = pltpu.VMEM((parts, 2, size, half), low)
    singles = pltpu.VMEM((parts, size, half), low)
    shapes = (
        ((4, block, width), low),
        ((width, span), low),
        ((block, width), low),
        ((block, width), low),
        ((block, width), full),
        ((block, width), low),
        ((block, PLE), low),
        ((block, PLE), low),
        ((8, width), full),
    )
    return pl.pallas_call(
        functools.partial(middle_kernel, block, parts),
        out_shape=tuple(jax.ShapeDtypeStruct(*v) for v in shapes),
        in_specs=[vmem, anywhere] + [vmem] * 6,
        out_specs=tuple(anywhere if i == 1 else vmem for i in range(len(shapes))),
        scratch_shapes=[
            pltpu.VMEM((width, span), low),
            pltpu.VMEM((block, width), full),
            pltpu.VMEM((block, half), full),
            pltpu.VMEM((block, half), full),
            *[pieces] * 4,
            *[singles] * 4,
            pltpu.VMEM((2, 256, span), low),
            dma((width // 256,)),
            dma((2,)),
            *[dma((parts,))] * 8,
            *[dma((parts, 2))] * 4,
            *[dma((parts,))] * 4,
        ],
        compiler_params=pltpu.CompilerParams(
            collective_id=1, has_side_effects=True, vmem_limit_bytes=56 << 20
        ),
        cost_estimate=pl.CostEstimate(
            flops=16 * block * width * span, bytes_accessed=100 << 20, transcendentals=0
        ),
    )(
        hidden,
        down_map,
        mixed,
        jnp.pad(jnp.stack(gains), ((0, 6), (0, 0))),
        ple[:, :PLE],
        ple[:, PLE:],
        ple_input,
        cotangent,
    )


def middle_plain(ranks, hidden, down_map, mixed, gains, ple, ple_input, cotangent):
    block = mixed.shape[0]
    parts = mm_nt(hidden, down_map).astype(low)
    ffn_out = sum_seq([parts[k * block : (k + 1) * block] for k in range(ranks)], ranks)
    ffn_normed, ffn_inverse = norm_rows(ffn_out, gains[0])
    h_second = (mixed + ffn_normed).astype(low)
    ple_gate = mm(h_second, ple[:, :PLE])
    ple_input = ple_input.astype(full)
    ple_mixed = (gelu_tanh(ple_gate) * ple_input).astype(low)
    ple_proj = mm_nt(ple_mixed, ple[:, PLE:])
    ple_normed, ple_inverse = norm_rows(ple_proj, gains[1])
    hidden_out = (h_second.astype(full) + ple_normed).astype(low)
    grad_out = cotangent.astype(full)
    grad_ple_proj, gain_grad_five = norm_back(ple_proj, ple_inverse, gains[1], grad_out)
    grad_ple_low = grad_ple_proj.astype(low)
    grad_ple_mixed = mm(grad_ple_low, ple[:, PLE:])
    unused_gelu, gelu_pull = jax.vjp(gelu_tanh, ple_gate)
    grad_ple_gate = gelu_pull(grad_ple_mixed * ple_input)[0].astype(low)
    grad_second = grad_out + mm_nt(grad_ple_gate, ple[:, :PLE])
    grad_ffn, gain_grad_four = norm_back(ffn_out, ffn_inverse, gains[0], grad_second)
    rows = whole_rows(gather_seq(grad_ffn.astype(low), ranks))
    return (
        rows,
        mm_tn(rows, hidden).astype(low),
        hidden_out,
        h_second,
        grad_second,
        grad_ple_low,
        ple_mixed,
        grad_ple_gate,
        jnp.stack([gain_grad_four, gain_grad_five]),
    )


def body(
    sizes,
    hidden_in,
    per_layer_input,
    segment_ids,
    positions,
    out_cotangent,
    w_query,
    key_matrix,
    value_matrix,
    w_out_t,
    laurel_maps,
    per_layer_maps,
    norm_gains,
    head_gains,
    w_mlp,
):
    ranks, pairs = sizes["seq"], sizes["pair"]
    block, _, width = hidden_in.shape
    rows = w_query.shape[0]
    q_width = QUERY_HEADS // ranks * HEAD_DIM
    share = QUERY_HEADS // KEY_VALUE_HEADS
    kv_of = [rank * (QUERY_HEADS // ranks) // share for rank in range(ranks)]
    length = block * ranks
    rank = lax.axis_index("seq")
    relative = [rank ^ k for k in range(ranks)]
    cut = lambda v: [v[k * block : (k + 1) * block] for k in range(ranks)]

    by_rank = lambda m: m.reshape(rows, ranks, q_width).transpose(1, 0, 2)
    by_kv = lambda m: jnp.stack([m[:, j * HEAD_DIM : (j + 1) * HEAD_DIM] for j in kv_of])
    head_pack = jnp.concatenate(
        [by_rank(w_query), by_kv(key_matrix), by_kv(value_matrix), by_rank(w_out_t)], 2
    )
    head_rows = head_gains.shape[0]
    small = jnp.concatenate(
        [norm_gains, jnp.pad(head_gains, ((0, rows - head_rows), (0, 0)))], 1
    )
    small = jnp.pad(small, ((0, 0), (0, 128 - small.shape[1])))
    rest_pack = jnp.concatenate([laurel_maps, small], 1)
    marks = jnp.pad(jnp.concatenate([segment_ids.T, positions.T], 0), ((0, 6), (0, 0)))
    x_local = hidden_in.reshape(block, width)

    head_all, rest_all, marks_all, x_all = gather_weights(
        sizes, head_pack, rest_pack, marks, x_local
    )
    in_rows, down_rows, head_all = lax.optimization_barrier(
        (w_mlp[:, :2], w_mlp[:, 2], head_all)
    )
    in_maps = lax.all_gather(in_rows, "fsdp", axis=0, tiled=True)
    down_map = lax.all_gather(down_rows, "fsdp", axis=0, tiled=True)
    x_all = x_all.reshape(length, width)
    ple = gather_everywhere(per_layer_maps, head_all, ranks, pairs)
    head_all = head_all.reshape(width, -1)
    rest_all = rest_all.reshape(width, -1)
    qkv_map, out_map = head_all[:, :-q_width], head_all[:, -q_width:]
    laurel = rest_all[:, : 2 * LR]
    gains = rest_all[:, 2 * LR :].astype(full)
    gain = [gains[:, i] for i in range(6)]
    head_scale = gains[:, 6:8].reshape(-1, rows, 2)[:, :head_rows].reshape(HEAD_DIM, 2)

    tokens_all = x_all.astype(full)
    normed_all = norm_rows(tokens_all, gain[0])[0].astype(low)
    tokens = x_local.astype(full)
    x_normed_f, x_inverse = norm_rows(tokens, gain[0])
    normed = x_normed_f.astype(low)
    indices = jnp.concatenate([r * block + jnp.arange(block) for r in relative])
    cos_table, sin_table = rope_tables(marks_all[:, 1].reshape(length))
    allowed = allowed_mask(marks_all[:, 0].reshape(length), indices)

    qkv = mm(normed_all, qkv_map)
    queries, keys, values = head_prep(qkv, head_scale, cos_table, sin_table)
    q_heads = queries.astype(low)
    k_head = keys[:, 0].astype(low)
    v_head = values[:, 0].astype(low)
    head_out, log_total = attend_heads(q_heads, k_head, v_head, allowed)
    attn_in = head_out.astype(low).reshape(length, q_width)
    attn_lin = sum_seq(cut(mm_nt(attn_in, out_map).astype(low)), ranks)

    attn_normed, attn_inverse = norm_rows(attn_lin, gain[1])
    laurel_low = mm(normed, laurel[:, :LR]).astype(low)
    laurel_high = mm_nt(laurel_low, laurel[:, LR:])
    laurel_normed, laurel_inverse = norm_rows(laurel_high, gain[2])
    mixed = (tokens + attn_normed + (normed.astype(full) + laurel_normed)) * root_half
    h_normed_f, h_inverse = norm_rows(mixed, gain[3])
    h_blocks = gather_seq(h_normed_f.astype(low), ranks)
    gate_up = dot(whole_rows(h_blocks), in_maps, ((1,), (0,)))
    gate_part, up_part = gate_up[:, 0], gate_up[:, 1]
    hidden = (gelu_tanh(gate_part) * up_part).astype(low)
    hidden, down_map = lax.optimization_barrier((hidden, down_map))
    run_middle = middle if ranks == 4 else functools.partial(middle_plain, ranks)
    (
        grad_ffn_rows,
        down_grad,
        hidden_out,
        h_second,
        grad_second,
        grad_ple_low,
        ple_mixed,
        grad_ple_gate,
        ffn_gain_grads,
    ) = run_middle(
        hidden,
        down_map,
        mixed,
        gain[4:6],
        ple,
        per_layer_input.reshape(block, PLE),
        out_cotangent.reshape(block, width),
    )
    gain_grad_four, gain_grad_five = ffn_gain_grads[0], ffn_gain_grads[1]
    grad_ffn_rows = grad_ffn_rows.reshape(length, width)
    down_sum = lax.psum_scatter(down_grad, "fsdp", scatter_dimension=0, tiled=True)
    grad_ffn_rows, down_grad = lax.optimization_barrier((grad_ffn_rows, down_grad))
    grad_hidden = mm(grad_ffn_rows, down_map)
    gate_act, act_pull = jax.vjp(gelu_tanh, gate_part)
    grad_gate_up = jnp.stack(
        [act_pull(grad_hidden * up_part)[0], grad_hidden * gate_act], 1
    ).astype(low)
    h_part = dot(grad_gate_up, in_maps, ((1, 2), (1, 2))).astype(low)
    grad_h_normed = sum_seq(cut(h_part), ranks)
    h_blocks, h_part = lax.optimization_barrier((h_blocks, h_part))
    in_grad = dot(whole_rows(h_blocks), grad_gate_up, ((0,), (0,))).astype(low)
    in_sum = lax.psum_scatter(in_grad, "fsdp", scatter_dimension=0, tiled=True)

    grad_ple_up = mm_tn(grad_ple_low, ple_mixed)
    grad_ple_down = mm_tn(h_second, grad_ple_gate)
    grad_mixed_norm, gain_grad_three = norm_back(mixed, h_inverse, gain[3], grad_h_normed)
    grad_mixed = grad_second + grad_mixed_norm
    grad_branch = grad_mixed * root_half
    grad_attn, gain_grad_one = norm_back(attn_lin, attn_inverse, gain[1], grad_branch)
    grad_attn_blocks = gather_seq(grad_attn.astype(low), ranks)
    grad_laurel_high, gain_grad_two = norm_back(
        laurel_high, laurel_inverse, gain[2], grad_branch
    )
    grad_high_low = grad_laurel_high.astype(low)
    grad_laurel_up = mm_tn(grad_high_low, laurel_low)
    grad_laurel_low = mm(grad_high_low, laurel[:, LR:]).astype(low)
    grad_laurel_down = mm_tn(normed, grad_laurel_low)

    x_here = grad_branch + mm_nt(grad_laurel_low, laurel[:, :LR])
    gain_grad_zero = jnp.sum(x_here * tokens * x_inverse, 0)
    small_grad = jnp.stack(
        [
            gain_grad_zero,
            gain_grad_one,
            gain_grad_two,
            gain_grad_three,
            gain_grad_four,
            gain_grad_five,
        ],
        1,
    )
    small_grad = jnp.pad(small_grad, ((0, 0), (0, 128 - small_grad.shape[1])))
    rest_grad = jnp.concatenate(
        [grad_ple_down, grad_ple_up, grad_laurel_down, grad_laurel_up, small_grad], 1
    ).astype(low)
    rest_grad = rest_grad.reshape(ranks, -1, rest_grad.shape[1])
    rest_grad, grad_attn_blocks = lax.optimization_barrier((rest_grad, grad_attn_blocks))
    rest_own = take(rest_grad, 0, rank).astype(full) + sum(
        permute(take(rest_grad, 0, relative[k]), "seq", k).astype(full) for k in range(1, ranks)
    )
    rest_own = rest_own.astype(low).reshape(pairs * 2, rows, -1)
    out_grad = weight_grad(ranks, pairs * 2, grad_attn_blocks, attn_in)
    grad_heads = mm(whole_rows(grad_attn_blocks), out_map).astype(low)
    codes = marks_all[:, 0].reshape(length) * (4 * length) + indices
    grad_qkv, grad_gains = attend_back(
        ranks,
        qkv,
        q_heads.reshape(length, q_width),
        k_head,
        v_head,
        grad_heads,
        log_total,
        codes,
        cos_table[:, 0, : HEAD_DIM // 2],
        sin_table[:, 0, : HEAD_DIM // 2],
        head_scale.T,
    )
    grad_head_scale = grad_gains[:2].T
    head_scale_grad = jnp.pad(
        grad_head_scale.reshape(-1, head_rows, 2), ((0, 0), (0, rows - head_rows), (0, 0))
    ).reshape(width, 2)
    late_grad = jnp.pad(head_scale_grad, ((0, 0), (1, 125)))
    last = weight_grad(
        ranks, pairs * 2, [normed_all], grad_qkv, head_all, gain[0][:, None], late_grad
    )
    last, grad_qkv = lax.optimization_barrier((last, grad_qkv))
    x_part = mm_nt(grad_qkv, qkv_map).astype(low)

    half = rows // 2
    folded = jnp.concatenate(
        [rest_own[:, :half, 2 * PLE :], rest_own[:, half:, 2 * PLE :]], 2
    )
    out_grad = out_grad.reshape(pairs * 2, ranks * rows, q_width)
    first = [out_grad, rest_own[:, :, : 2 * PLE], folded]
    if q_width != 2 * PLE:
        first[0] = out_grad.reshape(pairs * 2, -1, 2 * PLE)
    first = jnp.concatenate(first, 1)
    first, last, x_part, in_sum, down_sum = lax.optimization_barrier(
        (first, last, x_part, in_sum, down_sum)
    )
    first_sum = lax.psum_scatter(first, "fsdp", scatter_dimension=0, tiled=False).astype(low)
    last = last.reshape(width, -1)
    last_sum = lax.psum_scatter(last, "fsdp", scatter_dimension=0, tiled=True)
    last_sum = last_sum.reshape(ranks, rows, -1)

    out_end = first.shape[1] - rows - half
    out_sum = first_sum[:out_end].reshape(ranks, rows, q_width)
    ple_sum = first_sum[out_end : out_end + rows].astype(full)
    folded = first_sum[out_end + rows :].astype(full)
    other_sum = jnp.concatenate([folded[:, : folded.shape[1] // 2], folded[:, folded.shape[1] // 2 :]], 0)

    def across(part):
        got = jnp.stack(
            [take(part, 0, rank)]
            + [permute(take(part, 0, relative[k]), "seq", k) for k in range(1, ranks)]
        )
        return [take(got, 0, r ^ rank).astype(full) for r in range(ranks)]

    out_ranks, last_ranks = across(out_sum), across(last_sum)

    grad_x_normed = x_here + sum_seq(cut(x_part), ranks)
    grad_tokens_norm = norm_back(tokens, x_inverse, gain[0], grad_x_normed)[0]
    input_grad = grad_mixed * root_half + grad_tokens_norm

    late_sum = sum(part[:, q_width + 2 * HEAD_DIM :] for part in last_ranks)
    gain_sum = other_sum[:, 2 * LR : 2 * LR + 6]
    gain_sum = jnp.concatenate([gain_sum[:, :1] + late_sum[:, :1], gain_sum[:, 1:]], 1)
    scale_sum = late_sum[:head_rows, 1:3]

    def of_kv(parts):
        return jnp.concatenate(
            [
                sum(parts[r] for r in range(ranks) if kv_of[r] == j)
                for j in range(KEY_VALUE_HEADS)
            ],
            1,
        )

    grad_mlp = jnp.concatenate([in_sum, down_sum[:, None]], 1).astype(full)
    lead = (block, 1, width)
    return (
        hidden_out.reshape(lead),
        input_grad.reshape(lead),
        jnp.concatenate([part[:, :q_width] for part in last_ranks], 1),
        of_kv([part[:, q_width : q_width + HEAD_DIM] for part in last_ranks]),
        of_kv([part[:, q_width + HEAD_DIM : q_width + 2 * HEAD_DIM] for part in last_ranks]),
        jnp.concatenate(out_ranks, 1),
        other_sum[:, : 2 * LR],
        ple_sum,
        gain_sum,
        scale_sum,
        grad_mlp,
    )


def solution(mesh):
    sizes = {"seq": mesh.shape["seq"], "pair": mesh.shape["fsdp"] // 2, "core": 2}
    spread = P(("seq", "fsdp"), None)
    tokens = P("seq", "fsdp", None)
    return jax.shard_map(
        functools.partial(body, sizes),
        mesh=mesh,
        in_specs=(tokens, tokens, P("seq", "fsdp"), P("seq", "fsdp"), tokens)
        + (spread,) * 8
        + (P("fsdp", None, "seq"),),
        out_specs=(tokens, tokens) + (spread,) * 8 + (P("fsdp", None, "seq"),),
        check_vma=False,
    )
```

```python
import functools
import math

import jax
import jax.numpy as jnp
from jax import lax
from jax.experimental import pallas as pl
from jax.experimental.pallas import tpu as pltpu
from jax.sharding import PartitionSpec as P

QUERY_HEADS = 8
KEY_VALUE_HEADS = 2
HEAD_DIM = 256
LR = 64
PLE = 256
WIN = 512

MESH = pl.DeviceIdType.MESH
eps = 1e-06
theta = 10000.0
root_half = 1.0 / math.sqrt(2.0)
low = jnp.bfloat16
full = jnp.float32


def flip(index, offset, size):
    value, bit = 0, 1
    while bit < size:
        has = (index // bit) % 2
        value = value + bit * ((1 - has) if offset & bit else has)
        bit *= 2
    return value


def gather_kernel(
    sizes, head_ref, rest_ref, mark_ref, x_ref, head_out, rest_out, mark_out, x_out, *sems
):
    (local, head_s1, head_r1, right_s, right_r, left_s, left_r, head_s3, head_r3) = sems[:9]
    (rest_s1, rest_r1, rest_s2, rest_r2, rest_s3, rest_r3, mark_s, mark_r, x_s, x_r) = sems[9:]
    ranks, pairs = sizes["seq"], sizes["pair"]
    rank = lax.axis_index("seq")
    fsdp_index = lax.axis_index("fsdp")
    pair, core = fsdp_index // 2, fsdp_index % 2
    sibling = (rank, pair * 2 + 1 - core)

    def on_seq(step):
        return (flip(rank, step, ranks), fsdp_index)

    def on_pair(step):
        return (rank, ((pair + step) % pairs) * 2 + core)

    def remote(source, target, send, recv, device):
        return pltpu.make_async_remote_copy(
            src_ref=source,
            dst_ref=target,
            send_sem=send,
            recv_sem=recv,
            device_id=device,
            device_id_type=MESH,
        )

    barrier = pltpu.get_barrier_semaphore()
    devices = [on_seq(i) for i in range(1, ranks)] + [on_pair(i) for i in range(1, pairs)]
    for device in devices + [sibling]:
        pl.semaphore_signal(barrier, inc=1, device_id=device, device_id_type=MESH)
    pl.semaphore_wait(barrier, len(devices) + 1)

    sent = []

    def go(copy):
        copy.start()
        sent.append(copy)
        return copy

    def part(at, k):
        return head_out.at[flip(rank, k, ranks), at, core]

    def right(t, k):
        source = head_ref.at[rank] if t == 1 and k == 0 else part(pair - (t - 1), k)
        slot = (t - 1) * ranks + k
        target = part(pair - (t - 1), k)
        return remote(source, target, right_s.at[slot], right_r.at[slot], (rank, fsdp_index + 2))

    def left(t, k):
        source = head_ref.at[rank] if t == 1 and k == 0 else part(pair + (t - 1), k)
        slot = (t - 1) * ranks + k
        target = part(pair + (t - 1), k)
        return remote(source, target, left_s.at[slot], left_r.at[slot], (rank, fsdp_index - 2))

    def to_sibling(t, k):
        source = head_ref.at[rank] if t == 0 and k == 0 else part(pair - t, k)
        slot = (t + pairs - 1) * ranks + k
        return remote(source, part(pair - t, k), head_s3.at[slot], head_r3.at[slot], sibling)

    sends_right = lambda t: (pair - (t - 1) >= 0) & (pair + 1 < pairs)
    sends_left = lambda t: (pair + (t - 1) < pairs) & (pair - 1 >= 0)

    def begin(k):
        pl.when(sends_right(1))(lambda: right(1, k).start())
        pl.when(sends_left(1))(lambda: left(1, k).start())
        to_sibling(0, k).start()

    begin(0)
    head_seq = [
        go(
            remote(
                head_ref.at[on_seq(i)[0]],
                head_out.at[rank, pair, core],
                head_s1.at[i - 1],
                head_r1.at[i - 1],
                on_seq(i),
            )
        )
        for i in range(1, ranks)
    ]
    rest_pair = [
        go(
            remote(
                rest_ref,
                rest_out.at[rank, pair, core],
                rest_s1.at[i - 1],
                rest_r1.at[i - 1],
                on_pair(i),
            )
        )
        for i in range(1, pairs)
    ]
    owns = [
        pltpu.make_async_copy(head_ref.at[rank], head_out.at[rank, pair, core], local.at[0]),
        pltpu.make_async_copy(rest_ref, rest_out.at[rank, pair, core], local.at[1]),
        pltpu.make_async_copy(mark_ref, mark_out.at[0], local.at[2]),
        pltpu.make_async_copy(x_ref, x_out.at[0], local.at[3]),
    ]
    for copy in owns:
        copy.start()
    marks = [
        go(remote(mark_ref, mark_out.at[i], mark_s.at[i - 1], mark_r.at[i - 1], on_seq(i)))
        for i in range(1, ranks)
    ]
    for k in range(1, ranks):
        head_seq[k - 1].wait_recv()
        begin(k)

    half = x_ref.shape[1] // 2
    first, second = slice(0, half), slice(half, 2 * half)
    x_seq, relays = [], []
    if ranks == 4:
        for order in range(2):
            for i, columns in ((1, (first, second)[order]), (2, (second, first)[order])):
                slot = (i - 1) * 2 + order
                x_seq.append(
                    go(
                        remote(
                            x_ref.at[:, columns],
                            x_out.at[i, :, columns],
                            x_s.at[slot],
                            x_r.at[slot],
                            on_seq(i),
                        )
                    )
                )
    else:
        for i in range(1, ranks):
            x_seq.append(
                go(remote(x_ref, x_out.at[i], x_s.at[i - 1], x_r.at[i - 1], on_seq(i)))
            )

    owns[1].wait()
    for copy in rest_pair:
        copy.wait_recv()
    row = rest_out.at[rank, :, core]
    rest_seq = [
        go(remote(row, row, rest_s2.at[i - 1], rest_r2.at[i - 1], on_seq(i)))
        for i in range(1, ranks)
    ]
    rest_core = [go(remote(row, row, rest_s3.at[0], rest_r3.at[0], sibling))]

    for t in range(1, pairs):
        for k in range(ranks):

            def from_left(t=t, k=k):
                slot = (t - 1) * ranks + k
                target = part(pair - t, k)
                remote(target, target, right_s.at[slot], right_r.at[slot], sibling).wait_recv()
                if t + 1 < pairs:
                    pl.when(pair + 1 < pairs)(lambda: right(t + 1, k).start())
                to_sibling(t, k).start()

            def from_right(t=t, k=k):
                slot = (t - 1) * ranks + k
                target = part(pair + t, k)
                remote(target, target, left_s.at[slot], left_r.at[slot], sibling).wait_recv()
                if t + 1 < pairs:
                    pl.when(pair - 1 >= 0)(lambda: left(t + 1, k).start())
                to_sibling(-t, k).start()

            pl.when(pair - t >= 0)(from_left)
            pl.when(pair + t < pairs)(from_right)
        if t == 1 and ranks == 4:
            x_seq[0].wait_recv()
            x_seq[1].wait_recv()
            for slot, i, columns, to in ((4, 1, first, 2), (5, 2, second, 1)):
                relays.append(
                    go(
                        remote(
                            x_out.at[i, :, columns],
                            x_out.at[3, :, columns],
                            x_s.at[slot],
                            x_r.at[slot],
                            on_seq(to),
                        )
                    )
                )

    for i in range(1, ranks):
        rest_seq[i - 1].wait_recv()
        row = rest_out.at[flip(rank, i, ranks), :, core]
        rest_core.append(go(remote(row, row, rest_s3.at[i], rest_r3.at[i], sibling)))
    owns[0].wait()
    for copy in owns[2:]:
        copy.wait()
    for copy in marks + x_seq[2 if ranks == 4 else 0 :] + relays + rest_core:
        copy.wait_recv()
    for k in range(ranks):
        to_sibling(0, k).wait()
        for t in range(1, pairs):
            pl.when(pair - t >= 0)(lambda t=t, k=k: to_sibling(t, k).wait())
            pl.when(pair + t < pairs)(lambda t=t, k=k: to_sibling(-t, k).wait())
            pl.when(sends_right(t))(lambda t=t, k=k: right(t, k).wait_send())
            pl.when(sends_left(t))(lambda t=t, k=k: left(t, k).wait_send())
    for copy in sent:
        copy.wait_send()


def gather_weights(sizes, head, rest, marks, x):
    ranks, pairs = sizes["seq"], sizes["pair"]
    dma = lambda n: pltpu.SemaphoreType.DMA((n,))
    anywhere = pl.BlockSpec(memory_space=pl.ANY)
    return pl.pallas_call(
        functools.partial(gather_kernel, sizes),
        out_shape=(
            jax.ShapeDtypeStruct((ranks, pairs, 2) + head.shape[1:], head.dtype),
            jax.ShapeDtypeStruct((ranks, pairs, 2) + rest.shape, rest.dtype),
            jax.ShapeDtypeStruct((ranks,) + marks.shape, marks.dtype),
            jax.ShapeDtypeStruct((ranks,) + x.shape, x.dtype),
        ),
        in_specs=[anywhere] * 4,
        out_specs=(anywhere,) * 4,
        scratch_shapes=[
            dma(4),
            *[dma(ranks - 1)] * 2,
            *[dma((pairs - 1) * ranks)] * 4,
            *[dma((2 * pairs - 1) * ranks)] * 2,
            *[dma(pairs - 1)] * 2,
            *[dma(ranks - 1)] * 2,
            *[dma(ranks)] * 2,
            *[dma(ranks - 1)] * 2,
            *[dma(2 * ranks - 2)] * 2,
        ],
        compiler_params=pltpu.CompilerParams(collective_id=0, has_side_effects=True),
    )(head, rest, marks, x)


def permute(v, axis, offset):
    size = lax.axis_size(axis)
    return lax.ppermute(v, axis, [(i, i ^ offset) for i in range(size)])


def gather_seq(v, ranks):
    if ranks != 4:
        return [v] + [permute(v, "seq", k) for k in range(1, ranks)]
    half = v.shape[1] // 2
    first, second = permute(v, "seq", 1), permute(v, "seq", 2)
    left = permute(first[:, :half], "seq", 2)
    right = permute(second[:, half:], "seq", 1)
    return [v, first, second, left, right]


def whole_rows(blocks):
    if blocks[-1].shape[1] < blocks[0].shape[1]:
        blocks = blocks[:-2] + [jnp.concatenate(blocks[-2:], 1)]
    return jnp.concatenate(blocks, 0)


def sum_seq(blocks, ranks):
    up = lambda v: v.astype(full)
    if ranks != 4:
        return sum((up(permute(blocks[k], "seq", k)) for k in range(1, ranks)), up(blocks[0]))
    half = blocks[0].shape[1] // 2
    left = [b[:, :half] for b in blocks]
    right = [b[:, half:] for b in blocks]
    left_far, right_far = permute(left[3], "seq", 1), permute(right[3], "seq", 2)
    left_near, right_near = permute(left[1], "seq", 1), permute(right[2], "seq", 2)
    left_far = permute((up(left[2]) + up(left_far)).astype(low), "seq", 2)
    right_far = permute((up(right[1]) + up(right_far)).astype(low), "seq", 1)
    return jnp.concatenate(
        [
            up(left[0]) + up(left_near) + up(left_far),
            up(right[0]) + up(right_near) + up(right_far),
        ],
        1,
    )


def take(v, axis, index):
    return lax.dynamic_index_in_dim(v, index, axis, keepdims=False)


def gather_everywhere(v, ranks, pairs):
    index, rank = lax.axis_index("fsdp"), lax.axis_index("seq")
    pair, core = index // 2, index % 2

    def spread(part, axis, offsets, mine):
        got = jnp.stack([part] + [permute(part, axis, k) for k in offsets])
        return jnp.stack([take(got, 0, mine ^ i) for i in range(len(offsets) + 1)])

    v = spread(v, "fsdp", [2 * k for k in range(1, pairs)], pair)
    v = spread(v, "seq", range(1, ranks), rank)
    v = spread(v, "fsdp", [1], core)
    return jnp.moveaxis(v, 0, 2).reshape(-1, v.shape[-1])


def dot(left, right, over):
    return lax.dot_general(left, right, (over, ((), ())), preferred_element_type=full)


def mm(left, right):
    return dot(left, right, ((1,), (0,)))


def mm_nt(left, right):
    return dot(left, right, ((1,), (1,)))


def mm_tn(left, right):
    return dot(left, right, ((0,), (0,)))


def norm_rows(v, gain_vec):
    inverse = lax.rsqrt(jnp.mean(v * v, -1, keepdims=True) + eps)
    return (v * inverse * gain_vec, inverse)


def norm_back(v, inverse, gain_vec, incoming):
    scaled = incoming * gain_vec
    inner_mean = jnp.mean(scaled * v, -1, keepdims=True)
    return (
        inverse * (scaled - v * inverse * inverse * inner_mean),
        jnp.sum(incoming * v * inverse, axis=0),
    )


def gelu_tanh(v):
    return jax.nn.gelu(v, approximate=True)


def rope_tables(places):
    half_width = HEAD_DIM // 2
    frequency = theta ** (-jnp.arange(half_width).astype(full) * 2.0 / HEAD_DIM)
    angles = places.astype(full)[:, None] * frequency
    angles = jnp.concatenate([angles, angles], -1)[:, None, :]
    return (jnp.cos(angles), jnp.sin(angles))


def rotate(v, cos_table, sin_table):
    half_width = v.shape[-1] // 2
    turned = jnp.concatenate([-v[..., half_width:], v[..., :half_width]], -1)
    return v * cos_table + turned * sin_table


def head_prep(qkv, head_scale, cos_table, sin_table):
    per_head = qkv.reshape(qkv.shape[0], -1, HEAD_DIM)
    queries = rotate(norm_rows(per_head[:, :-2], head_scale[:, 0])[0], cos_table, sin_table)
    keys = rotate(norm_rows(per_head[:, -2:-1], head_scale[:, 1])[0], cos_table, sin_table)
    values = norm_rows(per_head[:, -1:], 1.0)[0]
    return (queries, keys, values)


def allowed_mask(segments, indices):
    offset = indices[:, None] - indices[None, :]
    nearby = (offset >= 0) & (offset < WIN)
    return (segments[:, None] == segments[None, :]) & nearby


def scores_of(q_heads, keys, allowed):
    raw_scores = jnp.einsum("qhd,kd->hqk", q_heads, keys, preferred_element_type=full)
    return jnp.where(allowed[None], raw_scores * HEAD_DIM ** (-0.5), -1000000000.0)


def attend_heads(q_heads, keys, values, allowed):
    scores = scores_of(q_heads, keys, allowed)
    row_peak = jnp.max(scores, -1, keepdims=True)
    exp_scores = jnp.exp(scores - row_peak)
    row_total = jnp.sum(exp_scores, -1, keepdims=True)
    attn_probs = exp_scores / row_total
    head_out = jnp.einsum(
        "hqk,kd->qhd", attn_probs.astype(low), values, preferred_element_type=full
    )
    return (head_out, row_peak + jnp.log(row_total))


def norm_rope_back(lin, gain, incoming):
    inverse = lax.rsqrt(jnp.mean(lin * lin, -1, keepdims=True) + eps)
    scaled = incoming * gain
    inner_mean = jnp.mean(scaled * lin, -1, keepdims=True)
    return (
        inverse * (scaled - lin * inverse * inverse * inner_mean),
        jnp.sum(incoming * lin * inverse, 0, keepdims=True),
    )


def attend_back_kernel(
    ranks,
    block,
    qkv_ref,
    q_ref,
    k_ref,
    v_ref,
    grad_ref,
    total_ref,
    code_col_ref,
    code_row_ref,
    cos_ref,
    sin_ref,
    gain_ref,
    out_ref,
    gain_out_ref,
    key_acc,
    value_acc,
    query_acc,
    row_acc,
    probs_ref,
    grad_probs_ref,
):
    head, mine = pl.program_id(0), pl.program_id(1)
    heads = pl.num_programs(0)
    rank = lax.axis_index("seq")
    scale = HEAD_DIM ** (-0.5)
    half = HEAD_DIM // 2

    @pl.when((head == 0) & (mine == 0))
    def _():
        key_acc[...] = jnp.zeros_like(key_acc)
        value_acc[...] = jnp.zeros_like(value_acc)
        gain_out_ref[...] = jnp.zeros_like(gain_out_ref)

    rows = pl.ds(pl.multiple_of(mine * block, block), block)
    columns = pl.ds(pl.multiple_of(head * HEAD_DIM, HEAD_DIM), HEAD_DIM)
    q, grad = q_ref[rows, columns], grad_ref[rows, columns]
    code = code_col_ref[rows, :]
    peaks = total_ref[head, rows, :]
    row_acc[...] = jnp.zeros_like(row_acc)
    query_acc[...] = jnp.zeros_like(query_acc)

    def reaches(other):
        apart = (rank ^ mine) - (rank ^ other)
        return (apart >= 0) & (apart * block - (block - 1) < WIN)

    for other in range(ranks):
        span = slice(other * block, (other + 1) * block)

        @pl.when(reaches(other))
        def _():
            scores = mm_nt(q, k_ref[span, :]) * scale
            offset = code - code_row_ref[:, span]
            probs = jnp.where((offset >= 0) & (offset < WIN), jnp.exp(scores - peaks), 0.0)
            grad_probs = mm_nt(grad, v_ref[span, :])
            probs_ref[other] = probs
            grad_probs_ref[other] = grad_probs
            row_acc[...] += jnp.sum(probs * grad_probs, -1, keepdims=True)

    inner = row_acc[...]
    for other in range(ranks):
        span = slice(other * block, (other + 1) * block)

        @pl.when(reaches(other))
        def _():
            probs = probs_ref[other]
            grad_scores = (probs * (grad_probs_ref[other] - inner) * scale).astype(low)
            query_acc[...] += mm(grad_scores, k_ref[span, :])
            key_acc[span, :] += mm_tn(grad_scores, q)
            value_acc[span, :] += mm_tn(probs.astype(low), grad)

    def turned_back(v, cos_table, sin_table):
        first, second = v[:, :half], v[:, half:]
        return jnp.concatenate(
            [
                first * cos_table + second * sin_table,
                second * cos_table - first * sin_table,
            ],
            1,
        )

    incoming = turned_back(query_acc[...].astype(low).astype(full), cos_ref[rows, :], sin_ref[rows, :])
    grad_lin, grad_gain = norm_rope_back(qkv_ref[rows, columns], gain_ref[0:1, :], incoming)
    out_ref[rows, columns] = grad_lin.astype(low)
    gain_out_ref[0:1, :] += grad_gain

    @pl.when((head == heads - 1) & (mine == ranks - 1))
    def _():
        base = out_ref.shape[1] - 2 * HEAD_DIM
        for other in range(ranks):
            span = slice(other * block, (other + 1) * block)
            incoming = turned_back(key_acc[span, :], cos_ref[span, :], sin_ref[span, :])
            grad_lin, grad_gain = norm_rope_back(
                qkv_ref[span, base : base + HEAD_DIM], gain_ref[1:2, :], incoming
            )
            out_ref[span, base : base + HEAD_DIM] = grad_lin.astype(low)
            gain_out_ref[1:2, :] += grad_gain
            grad_lin = norm_rope_back(qkv_ref[span, base + HEAD_DIM :], 1.0, value_acc[span, :])[0]
            out_ref[span, base + HEAD_DIM :] = grad_lin.astype(low)


def attend_back(ranks, qkv, q, k, v, grad, total, codes, cos_table, sin_table, gains):
    length = qkv.shape[0]
    block = length // ranks
    heads = q.shape[1] // HEAD_DIM
    whole = lambda v: pl.BlockSpec(
        v.shape, lambda i, j, n=len(v.shape): (0,) * n, pipeline_mode=pl.Buffered(1)
    )
    operands = (qkv, q, k, v, grad, total, codes[:, None], codes[None], cos_table, sin_table, gains)
    results = (
        jax.ShapeDtypeStruct(qkv.shape, low),
        jax.ShapeDtypeStruct((8, HEAD_DIM), full),
    )
    return pl.pallas_call(
        functools.partial(attend_back_kernel, ranks, block),
        grid=(heads, ranks),
        out_shape=results,
        in_specs=[whole(v) for v in operands],
        out_specs=tuple(whole(v) for v in results),
        scratch_shapes=[
            pltpu.VMEM((length, HEAD_DIM), full),
            pltpu.VMEM((length, HEAD_DIM), full),
            pltpu.VMEM((block, HEAD_DIM), full),
            pltpu.VMEM((block, 1), full),
            pltpu.VMEM((ranks, block, block), full),
            pltpu.VMEM((ranks, block, block), full),
        ],
        compiler_params=pltpu.CompilerParams(vmem_limit_bytes=40 << 20),
        cost_estimate=pl.CostEstimate(
            flops=10 * heads * length * length * HEAD_DIM * 9 // 16,
            bytes_accessed=16 * length * HEAD_DIM * (heads + 2),
            transcendentals=heads * length * length,
        ),
    )(*operands)


def weight_grad_kernel(count, half_tiles, *refs):
    lefts, right_ref, out_ref = refs[:count], refs[count], refs[-1]
    pieces = [ref[...] for ref in lefts]
    if half_tiles:
        pieces[-2:] = [jnp.where(pl.program_id(0) < half_tiles, pieces[-2], pieces[-1])]
    result, start = None, 0
    for piece in pieces:
        part = mm_tn(piece, right_ref[start : start + piece.shape[0], :])
        result = part if result is None else result + part
        start += piece.shape[0]
    if len(refs) > count + 2:
        map_ref, gain_ref, late_ref = refs[count + 1 : count + 4]
        maps = map_ref[:, : result.shape[1]].astype(full)
        of_gain = jnp.sum(maps * result, -1, keepdims=True) / gain_ref[...]
        late = late_ref[...]
        lane = lax.broadcasted_iota(jnp.int32, late.shape, 1)
        result = jnp.concatenate([result, jnp.where(lane == 0, of_gain, late)], 1)
    out_ref[...] = result.astype(low).reshape(out_ref.shape)


def weight_grad(ranks, parts, lefts, right, *extras):
    width = lefts[0].shape[1]
    length, columns = right.shape
    rows = width // (ranks * parts)
    tile = max(min(256, rows * parts), rows)
    each = tile // rows
    wide = columns + (128 if extras else 0)
    half_tiles = lefts[-1].shape[1] // tile if lefts[-1].shape[1] < width else 0

    def place(i):
        return (((i * each) % parts) // each, (i * each) // parts, 0, 0)

    left_specs = [pl.BlockSpec((v.shape[0], tile), lambda i: (0, i)) for v in lefts]
    if half_tiles:
        left_specs[-2:] = [
            pl.BlockSpec((lefts[-1].shape[0], tile), lambda i: (0, jnp.minimum(i, half_tiles - 1))),
            pl.BlockSpec((lefts[-1].shape[0], tile), lambda i: (0, jnp.maximum(i - half_tiles, 0))),
        ]
    return pl.pallas_call(
        functools.partial(weight_grad_kernel, len(lefts), half_tiles),
        grid=(width // tile,),
        out_shape=jax.ShapeDtypeStruct((parts, ranks, rows, wide), low),
        in_specs=left_specs
        + [pl.BlockSpec((length, columns), lambda i: (0, 0))]
        + [pl.BlockSpec((tile, v.shape[1]), lambda i: (i, 0)) for v in extras],
        out_specs=pl.BlockSpec((each, 1, rows, wide), place),
        compiler_params=pltpu.CompilerParams(vmem_limit_bytes=32 << 20),
        cost_estimate=pl.CostEstimate(
            flops=2 * length * width * columns,
            bytes_accessed=2 * (length * (width + columns) + width * columns),
            transcendentals=0,
        ),
    )(*lefts, right, *extras)


def middle_kernel(
    block,
    parts,
    hidden_ref,
    map_ref,
    mixed_ref,
    gain_ref,
    ple_gate_ref,
    ple_proj_ref,
    ple_input_ref,
    cotangent_ref,
    rows_ref,
    grad_map_ref,
    out_ref,
    second_ref,
    grad_second_ref,
    grad_ple_ref,
    ple_mixed_ref,
    grad_gate_ref,
    gain_out_ref,
    maps,
    own,
    keep_left,
    keep_right,
    send_x,
    send_y,
    got_x,
    got_y,
    relay_x,
    relay_y,
    far_x,
    far_y,
    stage,
    map_sem,
    stage_sem,
    *sems,
):
    (sx_s, sx_r, sy_s, sy_r, rx_s, rx_r, ry_s, ry_r) = sems[:8]
    (gx_s, gx_r, gy_s, gy_r, fx_s, fx_r, fy_s, fy_r) = sems[8:]
    rank = lax.axis_index("seq")
    fsdp_index = lax.axis_index("fsdp")
    by_x, by_y = (flip(rank, 1, 4), fsdp_index), (flip(rank, 2, 4), fsdp_index)
    size = block // parts
    width = map_ref.shape[0]
    half = width // 2
    tile = 256
    tiles = width // tile
    left, right = slice(0, half), slice(half, width)
    up = lambda v: v.astype(full)

    def remote(source, target, send, recv, device):
        return pltpu.make_async_remote_copy(
            src_ref=source,
            dst_ref=target,
            send_sem=send,
            recv_sem=recv,
            device_id=device,
            device_id_type=MESH,
        )

    def map_copy(i):
        at = pl.ds(pl.multiple_of(i * tile, tile), tile)
        return pltpu.make_async_copy(map_ref.at[at, :], maps.at[at, :], map_sem.at[i])

    for i in range(tiles):
        map_copy(i).start()

    barrier = pltpu.get_barrier_semaphore()
    for device in (by_x, by_y):
        pl.semaphore_signal(barrier, inc=1, device_id=device, device_id_type=MESH)
    pl.semaphore_wait(barrier, 2)

    sent = []

    def go(copy):
        copy.start()
        sent.append(copy)
        return copy

    def rows_of(u):
        return pl.ds(u * size, size)

    near_x, near_y = [], []
    for u in range(parts):
        at = rows_of(u)

        def product(i):
            if u == 0:
                map_copy(i).wait()
            rows = pl.ds(pl.multiple_of(i * tile, tile), tile)
            v = hidden_ref[:, at, :].reshape(4 * size, hidden_ref.shape[2])
            return mm_nt(v, maps[rows, :]).reshape(4, size, tile)

        def left_tile(i, carry):
            v = product(i)
            columns = pl.ds(pl.multiple_of(i * tile, tile), tile)
            own[at, columns] = v[0]
            keep_left[at, columns] = v[2]
            send_x[u, 0, :, columns] = v[3].astype(low)
            send_x[u, 1, :, columns] = v[1].astype(low)
            return carry

        def right_tile(i, carry):
            v = product(i + tiles // 2)
            columns = pl.ds(pl.multiple_of(i * tile, tile), tile)
            own[at, pl.ds(pl.multiple_of(half + i * tile, tile), tile)] = v[0]
            keep_right[at, columns] = v[1]
            send_y[u, 0, :, columns] = v[3].astype(low)
            send_y[u, 1, :, columns] = v[2].astype(low)
            return carry

        lax.fori_loop(0, tiles // 2, left_tile, 0)
        near_x.append(go(remote(send_x.at[u], got_x.at[u], sx_s.at[u], sx_r.at[u], by_x)))
        lax.fori_loop(0, tiles // 2, right_tile, 0)
        near_y.append(go(remote(send_y.at[u], got_y.at[u], sy_s.at[u], sy_r.at[u], by_y)))

    last_x, last_y = [], []
    for u in range(parts):
        at = rows_of(u)
        near_x[u].wait_recv()
        relay_y[u] = (keep_left[at, :] + up(got_x[u, 0])).astype(low)
        last_y.append(go(remote(relay_y.at[u], far_y.at[u], ry_s.at[u], ry_r.at[u], by_y)))
        near_y[u].wait_recv()
        relay_x[u] = (keep_right[at, :] + up(got_y[u, 0])).astype(low)
        last_x.append(go(remote(relay_x.at[u], far_x.at[u], rx_s.at[u], rx_r.at[u], by_x)))

    gain_out_ref[...] = jnp.zeros_like(gain_out_ref)
    ffn_gain, ple_gain = gain_ref[0:1, :], gain_ref[1:2, :]
    mean = lambda v: jnp.mean(v, -1, keepdims=True)
    total = lambda v: jnp.sum(v, 0, keepdims=True)
    slope, cubic = math.sqrt(2.0 / math.pi), 0.044715
    rows_x, rows_y = [], []
    for u in range(parts):
        at = rows_of(u)
        last_y[u].wait_recv()
        last_x[u].wait_recv()
        own[at, left] = own[at, left] + up(got_x[u, 1]) + up(far_y[u])
        own[at, right] = own[at, right] + up(got_y[u, 1]) + up(far_x[u])
        f = own[at, :]
        f_inverse = lax.rsqrt(mean(f * f) + eps)
        second = (mixed_ref[at, :] + f * f_inverse * ffn_gain).astype(low)
        second_ref[at, :] = second
        gate = mm(second, ple_gate_ref[...])
        bend = jnp.tanh(slope * (gate + cubic * gate * gate * gate))
        gate_slope = 0.5 * (1.0 + bend) + 0.5 * gate * (1.0 - bend * bend) * slope * (
            1.0 + 3.0 * cubic * gate * gate
        )
        given = up(ple_input_ref[at, :])
        ple_mixed = (0.5 * gate * (1.0 + bend) * given).astype(low)
        ple_mixed_ref[at, :] = ple_mixed
        proj = mm_nt(ple_mixed, ple_proj_ref[...])
        proj_inverse = lax.rsqrt(mean(proj * proj) + eps)
        out_ref[at, :] = (up(second) + proj * proj_inverse * ple_gain).astype(low)
        incoming = up(cotangent_ref[at, :])
        gain_out_ref[1:2, :] += total(incoming * proj * proj_inverse)
        scaled = incoming * ple_gain
        grad_proj = proj_inverse * (
            scaled - proj * (proj_inverse * proj_inverse * mean(scaled * proj))
        )
        grad_ple = grad_proj.astype(low)
        grad_ple_ref[at, :] = grad_ple
        grad_gate = (mm(grad_ple, ple_proj_ref[...]) * given * gate_slope).astype(low)
        grad_gate_ref[at, :] = grad_gate
        grad_second = incoming + mm_nt(grad_gate, ple_gate_ref[...])
        grad_second_ref[at, :] = grad_second
        f = own[at, :]
        gain_out_ref[0:1, :] += total(grad_second * f * f_inverse)
        scaled = grad_second * ffn_gain
        grad_f = f_inverse * (scaled - f * (f_inverse * f_inverse * mean(scaled * f)))
        rows_ref[0, at, :] = grad_f.astype(low)
        pair_x, pair_y = [], []
        for order in range(2):
            for pairs, device, send, recv, index, part in (
                (pair_x, by_x, gx_s, gx_r, 1, (left, right)[order]),
                (pair_y, by_y, gy_s, gy_r, 2, (right, left)[order]),
            ):
                pairs.append(
                    go(
                        remote(
                            rows_ref.at[0, at, part],
                            rows_ref.at[index, at, part],
                            send.at[u, order],
                            recv.at[u, order],
                            device,
                        )
                    )
                )
        rows_x.append(pair_x)
        rows_y.append(pair_y)

    far = []
    for u in range(parts):
        at = rows_of(u)
        rows_x[u][0].wait_recv()
        far.append(
            go(
                remote(
                    rows_ref.at[1, at, left],
                    rows_ref.at[3, at, left],
                    fy_s.at[u],
                    fy_r.at[u],
                    by_y,
                )
            )
        )
        rows_y[u][0].wait_recv()
        far.append(
            go(
                remote(
                    rows_ref.at[2, at, right],
                    rows_ref.at[3, at, right],
                    fx_s.at[u],
                    fx_r.at[u],
                    by_x,
                )
            )
        )
    for u in range(parts):
        rows_x[u][1].wait_recv()
        rows_y[u][1].wait_recv()
    for copy in far:
        copy.wait_recv()

    def stage_copy(i, slot):
        at = pl.ds(pl.multiple_of(i * tile, tile), tile)
        return pltpu.make_async_copy(stage.at[slot], grad_map_ref.at[at, :], stage_sem.at[slot])

    span = hidden_ref.shape[2]

    def grad_tile(i, carry):
        slot = i % 2

        @pl.when(i >= 2)
        def _():
            stage_copy(i - 2, slot).wait()

        columns = pl.ds(pl.multiple_of(i * tile, tile), tile)
        v = rows_ref[:, :, columns].reshape(4 * block, tile)
        for j in range(0, span, span // 2):
            w = hidden_ref[:, :, j : j + span // 2].reshape(4 * block, span // 2)
            stage[slot, :, j : j + span // 2] = mm_tn(v, w).astype(low)
        stage_copy(i, slot).start()
        return carry

    lax.fori_loop(0, tiles, grad_tile, 0)
    stage_copy(tiles - 2, 0).wait()
    stage_copy(tiles - 1, 1).wait()
    for copy in sent:
        copy.wait_send()


def middle(hidden, down_map, mixed, gains, ple, ple_input, cotangent):
    block, width = mixed.shape
    span = hidden.shape[1]
    parts, half = 2, width // 2
    size = block // parts
    hidden = hidden.reshape(4, block, span)
    dma = pltpu.SemaphoreType.DMA
    vmem = pl.BlockSpec(memory_space=pltpu.VMEM)
    anywhere = pl.BlockSpec(memory_space=pl.ANY)
    pieces = pltpu.VMEM((parts, 2, size, half), low)
    singles = pltpu.VMEM((parts, size, half), low)
    shapes = (
        ((4, block, width), low),
        ((width, span), low),
        ((block, width), low),
        ((block, width), low),
        ((block, width), full),
        ((block, width), low),
        ((block, PLE), low),
        ((block, PLE), low),
        ((8, width), full),
    )
    return pl.pallas_call(
        functools.partial(middle_kernel, block, parts),
        out_shape=tuple(jax.ShapeDtypeStruct(*v) for v in shapes),
        in_specs=[vmem, anywhere] + [vmem] * 6,
        out_specs=tuple(anywhere if i == 1 else vmem for i in range(len(shapes))),
        scratch_shapes=[
            pltpu.VMEM((width, span), low),
            pltpu.VMEM((block, width), full),
            pltpu.VMEM((block, half), full),
            pltpu.VMEM((block, half), full),
            *[pieces] * 4,
            *[singles] * 4,
            pltpu.VMEM((2, 256, span), low),
            dma((width // 256,)),
            dma((2,)),
            *[dma((parts,))] * 8,
            *[dma((parts, 2))] * 4,
            *[dma((parts,))] * 4,
        ],
        compiler_params=pltpu.CompilerParams(
            collective_id=1, has_side_effects=True, vmem_limit_bytes=56 << 20
        ),
        cost_estimate=pl.CostEstimate(
            flops=16 * block * width * span, bytes_accessed=100 << 20, transcendentals=0
        ),
    )(
        hidden,
        down_map,
        mixed,
        jnp.pad(jnp.stack(gains), ((0, 6), (0, 0))),
        ple[:, :PLE],
        ple[:, PLE:],
        ple_input,
        cotangent,
    )


def middle_plain(ranks, hidden, down_map, mixed, gains, ple, ple_input, cotangent):
    block = mixed.shape[0]
    parts = mm_nt(hidden, down_map).astype(low)
    ffn_out = sum_seq([parts[k * block : (k + 1) * block] for k in range(ranks)], ranks)
    ffn_normed, ffn_inverse = norm_rows(ffn_out, gains[0])
    h_second = (mixed + ffn_normed).astype(low)
    ple_gate = mm(h_second, ple[:, :PLE])
    ple_input = ple_input.astype(full)
    ple_mixed = (gelu_tanh(ple_gate) * ple_input).astype(low)
    ple_proj = mm_nt(ple_mixed, ple[:, PLE:])
    ple_normed, ple_inverse = norm_rows(ple_proj, gains[1])
    hidden_out = (h_second.astype(full) + ple_normed).astype(low)
    grad_out = cotangent.astype(full)
    grad_ple_proj, gain_grad_five = norm_back(ple_proj, ple_inverse, gains[1], grad_out)
    grad_ple_low = grad_ple_proj.astype(low)
    grad_ple_mixed = mm(grad_ple_low, ple[:, PLE:])
    unused_gelu, gelu_pull = jax.vjp(gelu_tanh, ple_gate)
    grad_ple_gate = gelu_pull(grad_ple_mixed * ple_input)[0].astype(low)
    grad_second = grad_out + mm_nt(grad_ple_gate, ple[:, :PLE])
    grad_ffn, gain_grad_four = norm_back(ffn_out, ffn_inverse, gains[0], grad_second)
    rows = whole_rows(gather_seq(grad_ffn.astype(low), ranks))
    return (
        rows,
        mm_tn(rows, hidden).astype(low),
        hidden_out,
        h_second,
        grad_second,
        grad_ple_low,
        ple_mixed,
        grad_ple_gate,
        jnp.stack([gain_grad_four, gain_grad_five]),
    )


def finish_kernel(sizes, with_x, *refs):
    ranks, pairs = sizes["seq"], sizes["pair"]
    refs = list(refs)

    def some(count):
        head = refs[:count]
        del refs[:count]
        return head

    owns = some(3)
    x_ref, branch_ref, tokens_ref, base_ref, gain_ref = some(5) if with_x else [None] * 5
    query_ref, key_ref, value_ref, out_ref, ple_ref, laurel_ref, small_ref = some(7)
    (input_ref,) = some(1) if with_x else [None]
    sums, from_left, from_right = some(3), some(3), some(3)
    got_last, got_out = some(2)
    if with_x:
        got_x, got_y, relay_x, relay_y, far_x, far_y = some(6)
    core_s, core_r, right_s, right_r, left_s, left_r, last_s, last_r, out_s, out_r = some(10)
    if with_x:
        x_s, x_r = some(2)

    rank = lax.axis_index("seq")
    fsdp_index = lax.axis_index("fsdp")
    pair, core = fsdp_index // 2, fsdp_index % 2
    sibling = (rank, pair * 2 + 1 - core)
    on_seq = lambda k: (flip(rank, k, ranks), fsdp_index)
    up = lambda v: v.astype(full)

    def remote(source, target, send, recv, device):
        return pltpu.make_async_remote_copy(
            src_ref=source,
            dst_ref=target,
            send_sem=send,
            recv_sem=recv,
            device_id=device,
            device_id_type=MESH,
        )

    barrier = pltpu.get_barrier_semaphore()
    devices = [on_seq(k) for k in range(1, ranks)]
    devices += [(rank, ((pair + i) % pairs) * 2 + core) for i in range(1, pairs)]
    for device in devices + [sibling]:
        pl.semaphore_signal(barrier, inc=1, device_id=device, device_id_type=MESH)
    pl.semaphore_wait(barrier, len(devices) + 1)

    sent = []

    def go(copy):
        copy.start()
        sent.append(copy)
        return copy

    half_ranks = ranks // 2
    pieces = [
        (1, slice(0, ranks)),
        (2, None),
        (0, slice(0, half_ranks)),
        (0, slice(half_ranks, ranks)),
    ]
    count = len(pieces)

    def view(group, lead, piece):
        number, rows = pieces[piece]
        ref = group[number]
        return ref.at[lead] if rows is None else ref.at[lead, rows]

    order = [i // 2 if i % 2 else pairs - 1 - i // 2 for i in range(pairs)]

    def swap(chip, piece):
        slot = chip * count + piece
        return remote(
            view(owns, chip * 2 + 1 - core, piece),
            view(sums, chip, piece),
            core_s.at[slot],
            core_r.at[slot],
            sibling,
        )

    for chip in order:
        for piece in range(count):
            go(swap(chip, piece))
    if with_x:
        half = x_ref.shape[2] // 2
        left, right = slice(0, half), slice(half, 2 * half)
        by_x, by_y = on_seq(1), on_seq(2)
        near = []
        for slot, block, columns, target, device in (
            (0, 3, left, got_x.at[0], by_x),
            (1, 3, right, got_y.at[0], by_y),
            (2, 1, left, got_x.at[1], by_x),
            (3, 2, right, got_y.at[1], by_y),
        ):
            near.append(
                go(remote(x_ref.at[block, :, columns], target, x_s.at[slot], x_r.at[slot], device))
            )

    def whole_chip(chip, piece):
        target = view(sums, chip, piece)
        remote(
            target, target, core_s.at[0], core_r.at[chip * count + piece], sibling
        ).wait_recv()
        target[...] = (up(target[...]) + up(view(owns, chip * 2 + core, piece)[...])).astype(low)

    def pass_right(t, piece):
        slot = (t - 1) * count + piece
        return remote(
            view(sums, pair + pairs - t, piece),
            view(from_left, t - 1, piece),
            right_s.at[slot],
            right_r.at[slot],
            (rank, fsdp_index + 2),
        )

    def pass_left(t, piece):
        slot = (t - 1) * count + piece
        return remote(
            view(sums, pair - (pairs - t), piece),
            view(from_right, t - 1, piece),
            left_s.at[slot],
            left_r.at[slot],
            (rank, fsdp_index - 2),
        )

    def add_left(t, piece, target):
        got = view(from_left, t - 1, piece)
        slot = (t - 1) * count + piece
        remote(got, got, right_s.at[slot], right_r.at[slot], sibling).wait_recv()
        target[...] = (up(target[...]) + up(got[...])).astype(low)

    def add_right(t, piece, target):
        got = view(from_right, t - 1, piece)
        slot = (t - 1) * count + piece
        remote(got, got, left_s.at[slot], left_r.at[slot], sibling).wait_recv()
        target[...] = (up(target[...]) + up(got[...])).astype(low)

    mirrored = pairs - 1 - pair
    relays = []
    for t in range(1, pairs):
        for piece in range(count):

            def to_right(t=t, piece=piece):
                chip = pair + pairs - t
                whole_chip(chip, piece)
                if t > 1:
                    pl.when(pair > 0)(lambda: add_left(t - 1, piece, view(sums, chip, piece)))
                pass_right(t, piece).start()

            def to_left(t=t, piece=piece):
                chip = pair - (pairs - t)
                whole_chip(chip, piece)
                if t > 1:
                    pl.when(mirrored > 0)(lambda: add_right(t - 1, piece, view(sums, chip, piece)))
                pass_left(t, piece).start()

            pl.when(t >= pair + 1)(to_right)
            pl.when(t >= mirrored + 1)(to_left)
        if with_x and t == 1:
            near[0].wait_recv()
            relay_y[...] = (up(x_ref[2, :, left]) + up(got_x[0])).astype(low)
            relays.append(go(remote(relay_y, far_y, x_s.at[4], x_r.at[4], by_y)))
            near[1].wait_recv()
            relay_x[...] = (up(x_ref[1, :, right]) + up(got_y[0])).astype(low)
            relays.append(go(remote(relay_x, far_x, x_s.at[5], x_r.at[5], by_x)))
            for piece in range(count):
                whole_chip(pair, piece)
    if with_x:
        for copy in near[2:] + relays:
            copy.wait_recv()
        mean = lambda v: jnp.mean(v, -1, keepdims=True)
        step = x_ref.shape[1] // 2
        for i in range(2):
            at = slice(i * step, (i + 1) * step)
            incoming = branch_ref[at, :] + jnp.concatenate(
                [
                    up(x_ref[0, at, left]) + up(got_x[1, at, :]) + up(far_y[at, :]),
                    up(x_ref[0, at, right]) + up(got_y[1, at, :]) + up(far_x[at, :]),
                ],
                1,
            )
            v = up(tokens_ref[at, :])
            inverse = lax.rsqrt(mean(v * v) + eps)
            scaled = incoming * gain_ref[0:1, :]
            input_ref[at, 0, :] = base_ref[at, :] * root_half + inverse * (
                scaled - v * (inverse * inverse * mean(scaled * v))
            )
    else:
        for piece in range(count):
            whole_chip(pair, piece)

    for piece in range(count):
        target = view(sums, pair, piece)
        pl.when(pair > 0)(lambda: add_left(pairs - 1, piece, target))
        pl.when(mirrored > 0)(lambda: add_right(pairs - 1, piece, target))

    last_sum, out_sum, rest_sum = [ref.at[pair] for ref in sums]
    across = []
    for k in range(1, ranks):
        peer = flip(rank, k, ranks)
        across.append(
            (
                go(remote(last_sum.at[peer], got_last.at[k], last_s.at[k], last_r.at[k], on_seq(k))),
                go(remote(out_sum.at[peer], got_out.at[k], out_s.at[k], out_r.at[k], on_seq(k))),
            )
        )
    ple_ref[...] = up(rest_sum[:, : 2 * PLE])
    laurel_ref[...] = up(rest_sum[:, 2 * PLE : 2 * PLE + 2 * LR])
    small_ref[...] = up(rest_sum[:, 2 * PLE + 2 * LR :])
    key_ref[...] = jnp.zeros_like(key_ref)
    value_ref[...] = jnp.zeros_like(value_ref)
    q_width = out_sum.shape[2]
    for k in range(ranks):
        if k:
            for copy in across[k - 1]:
                copy.wait_recv()
            last, out = up(got_last[k]), up(got_out[k])
        else:
            last, out = up(last_sum[rank]), up(out_sum[rank])
        sender = flip(rank, k, ranks)
        columns = pl.ds(pl.multiple_of(sender * q_width, q_width), q_width)
        group = sender * (QUERY_HEADS // ranks) // (QUERY_HEADS // KEY_VALUE_HEADS)
        head = pl.ds(pl.multiple_of(group * HEAD_DIM, HEAD_DIM), HEAD_DIM)
        query_ref[:, columns] = last[:, :q_width]
        out_ref[:, columns] = out
        key_ref[:, head] += last[:, q_width : q_width + HEAD_DIM]
        value_ref[:, head] += last[:, q_width + HEAD_DIM : q_width + 2 * HEAD_DIM]
        small_ref[...] += last[:, q_width + 2 * HEAD_DIM :]

    for t in range(1, pairs):
        for piece in range(count):
            pl.when(t >= pair + 1)(lambda t=t, piece=piece: pass_right(t, piece).wait_send())
            pl.when(t >= mirrored + 1)(lambda t=t, piece=piece: pass_left(t, piece).wait_send())
    for copy in sent:
        copy.wait_send()


def finish(sizes, last, out, rest, x=None):
    ranks, pairs = sizes["seq"], sizes["pair"]
    rows = last.shape[2]
    arrays = [last, out, rest]
    vmem = pl.BlockSpec(memory_space=pltpu.VMEM)
    dma = lambda n: pltpu.SemaphoreType.DMA((n,))
    width = KEY_VALUE_HEADS * HEAD_DIM
    shapes = [
        (rows, QUERY_HEADS * HEAD_DIM),
        (rows, width),
        (rows, width),
        (rows, QUERY_HEADS * HEAD_DIM),
        (rows, 2 * PLE),
        (rows, 2 * LR),
        (rows, rest.shape[-1] - 2 * PLE - 2 * LR),
    ]
    scratch = [pltpu.VMEM((pairs,) + v.shape[1:], low) for v in arrays]
    scratch += [pltpu.VMEM((pairs - 1,) + v.shape[1:], low) for v in arrays] * 2
    scratch += [pltpu.VMEM((ranks,) + v.shape[2:], low) for v in arrays[:2]]
    if x is not None:
        block, columns = x[0].shape[1], x[0].shape[2] // 2
        shapes.append((block, 1, 2 * columns))
        scratch += [pltpu.VMEM((2, block, columns), low)] * 2
        scratch += [pltpu.VMEM((block, columns), low)] * 4
    scratch += [dma(4 * pairs)] * 2 + [dma(4 * (pairs - 1))] * 4 + [dma(ranks)] * 4
    if x is not None:
        scratch += [dma(6)] * 2
    operands = arrays + list(x or ())
    return pl.pallas_call(
        functools.partial(finish_kernel, sizes, x is not None),
        out_shape=tuple(jax.ShapeDtypeStruct(v, full) for v in shapes),
        in_specs=[vmem] * len(operands),
        out_specs=(vmem,) * len(shapes),
        scratch_shapes=scratch,
        compiler_params=pltpu.CompilerParams(
            collective_id=2, has_side_effects=True, vmem_limit_bytes=56 << 20
        ),
    )(*operands)


def body(
    sizes,
    hidden_in,
    per_layer_input,
    segment_ids,
    positions,
    out_cotangent,
    w_query,
    key_matrix,
    value_matrix,
    w_out_t,
    laurel_maps,
    per_layer_maps,
    norm_gains,
    head_gains,
    w_mlp,
):
    ranks, pairs = sizes["seq"], sizes["pair"]
    block, _, width = hidden_in.shape
    rows = w_query.shape[0]
    q_width = QUERY_HEADS // ranks * HEAD_DIM
    share = QUERY_HEADS // KEY_VALUE_HEADS
    kv_of = [rank * (QUERY_HEADS // ranks) // share for rank in range(ranks)]
    length = block * ranks
    rank = lax.axis_index("seq")
    relative = [rank ^ k for k in range(ranks)]
    cut = lambda v: [v[k * block : (k + 1) * block] for k in range(ranks)]

    by_rank = lambda m: m.reshape(rows, ranks, q_width).transpose(1, 0, 2)
    by_kv = lambda m: jnp.stack([m[:, j * HEAD_DIM : (j + 1) * HEAD_DIM] for j in kv_of])
    head_pack = jnp.concatenate(
        [by_rank(w_query), by_kv(key_matrix), by_kv(value_matrix), by_rank(w_out_t)], 2
    )
    head_rows = head_gains.shape[0]
    small = jnp.concatenate(
        [norm_gains, jnp.pad(head_gains, ((0, rows - head_rows), (0, 0)))], 1
    )
    small = jnp.pad(small, ((0, 0), (0, 128 - small.shape[1])))
    rest_pack = jnp.concatenate([laurel_maps, small], 1)
    marks = jnp.pad(jnp.concatenate([segment_ids.T, positions.T], 0), ((0, 6), (0, 0)))
    x_local = hidden_in.reshape(block, width)

    head_all, rest_all, marks_all, x_all = gather_weights(
        sizes, head_pack, rest_pack, marks, x_local
    )
    in_rows, down_rows, head_all = lax.optimization_barrier(
        (w_mlp[:, :2], w_mlp[:, 2], head_all)
    )
    in_maps = lax.all_gather(in_rows, "fsdp", axis=0, tiled=True)
    down_map = lax.all_gather(down_rows, "fsdp", axis=0, tiled=True)
    x_all = x_all.reshape(length, width)
    head_all = head_all.reshape(width, -1)
    rest_all = rest_all.reshape(width, -1)
    qkv_map, out_map = head_all[:, :-q_width], head_all[:, -q_width:]
    laurel = rest_all[:, : 2 * LR]
    gains = rest_all[:, 2 * LR :].astype(full)
    gain = [gains[:, i] for i in range(6)]
    head_scale = gains[:, 6:8].reshape(-1, rows, 2)[:, :head_rows].reshape(HEAD_DIM, 2)

    tokens_all = x_all.astype(full)
    normed_all = norm_rows(tokens_all, gain[0])[0].astype(low)
    tokens = x_local.astype(full)
    x_normed_f, x_inverse = norm_rows(tokens, gain[0])
    normed = x_normed_f.astype(low)
    indices = jnp.concatenate([r * block + jnp.arange(block) for r in relative])
    cos_table, sin_table = rope_tables(marks_all[:, 1].reshape(length))
    allowed = allowed_mask(marks_all[:, 0].reshape(length), indices)

    qkv = mm(normed_all, qkv_map)
    queries, keys, values = head_prep(qkv, head_scale, cos_table, sin_table)
    q_heads = queries.astype(low)
    k_head = keys[:, 0].astype(low)
    v_head = values[:, 0].astype(low)
    head_out, log_total = attend_heads(q_heads, k_head, v_head, allowed)
    attn_in = head_out.astype(low).reshape(length, q_width)
    attn_lin = sum_seq(cut(mm_nt(attn_in, out_map).astype(low)), ranks)

    attn_normed, attn_inverse = norm_rows(attn_lin, gain[1])
    laurel_low = mm(normed, laurel[:, :LR]).astype(low)
    laurel_high = mm_nt(laurel_low, laurel[:, LR:])
    laurel_normed, laurel_inverse = norm_rows(laurel_high, gain[2])
    mixed = (tokens + attn_normed + (normed.astype(full) + laurel_normed)) * root_half
    h_normed_f, h_inverse = norm_rows(mixed, gain[3])
    h_blocks = gather_seq(h_normed_f.astype(low), ranks)
    h_blocks, per_layer_maps = lax.optimization_barrier((h_blocks, per_layer_maps))
    ple = gather_everywhere(per_layer_maps, ranks, pairs)
    gate_up = dot(whole_rows(h_blocks), in_maps, ((1,), (0,)))
    gate_part, up_part = gate_up[:, 0], gate_up[:, 1]
    hidden = (gelu_tanh(gate_part) * up_part).astype(low)
    hidden, down_map = lax.optimization_barrier((hidden, down_map))
    run_middle = middle if ranks == 4 else functools.partial(middle_plain, ranks)
    (
        grad_ffn_rows,
        down_grad,
        hidden_out,
        h_second,
        grad_second,
        grad_ple_low,
        ple_mixed,
        grad_ple_gate,
        ffn_gain_grads,
    ) = run_middle(
        hidden,
        down_map,
        mixed,
        gain[4:6],
        ple,
        per_layer_input.reshape(block, PLE),
        out_cotangent.reshape(block, width),
    )
    gain_grad_four, gain_grad_five = ffn_gain_grads[0], ffn_gain_grads[1]
    grad_ffn_rows = grad_ffn_rows.reshape(length, width)
    down_sum = lax.psum_scatter(down_grad, "fsdp", scatter_dimension=0, tiled=True)
    grad_ffn_rows, down_grad = lax.optimization_barrier((grad_ffn_rows, down_grad))
    grad_hidden = mm(grad_ffn_rows, down_map)
    gate_act, act_pull = jax.vjp(gelu_tanh, gate_part)
    grad_gate_up = jnp.stack(
        [act_pull(grad_hidden * up_part)[0], grad_hidden * gate_act], 1
    ).astype(low)
    h_part = dot(grad_gate_up, in_maps, ((1, 2), (1, 2))).astype(low)
    h_parts = cut(h_part)
    if ranks == 4:
        h_parts = [jnp.split(v, 2, axis=1) for v in h_parts]
    h_blocks, h_parts = lax.optimization_barrier((h_blocks, h_parts))
    if ranks == 4:
        h_parts = [jnp.concatenate(v, 1) for v in h_parts]
    grad_h_normed = sum_seq(h_parts, ranks)
    in_grad = dot(whole_rows(h_blocks), grad_gate_up, ((0,), (0,))).astype(low)
    in_sum = lax.psum_scatter(in_grad, "fsdp", scatter_dimension=0, tiled=True)

    grad_ple_up = mm_tn(grad_ple_low, ple_mixed)
    grad_ple_down = mm_tn(h_second, grad_ple_gate)
    grad_mixed_norm, gain_grad_three = norm_back(mixed, h_inverse, gain[3], grad_h_normed)
    grad_mixed = grad_second + grad_mixed_norm
    grad_branch = grad_mixed * root_half
    grad_attn, gain_grad_one = norm_back(attn_lin, attn_inverse, gain[1], grad_branch)
    grad_attn_blocks = gather_seq(grad_attn.astype(low), ranks)
    grad_laurel_high, gain_grad_two = norm_back(
        laurel_high, laurel_inverse, gain[2], grad_branch
    )
    grad_high_low = grad_laurel_high.astype(low)
    grad_laurel_up = mm_tn(grad_high_low, laurel_low)
    grad_laurel_low = mm(grad_high_low, laurel[:, LR:]).astype(low)
    grad_laurel_down = mm_tn(normed, grad_laurel_low)

    x_here = grad_branch + mm_nt(grad_laurel_low, laurel[:, :LR])
    gain_grad_zero = jnp.sum(x_here * tokens * x_inverse, 0)
    small_grad = jnp.stack(
        [
            gain_grad_zero,
            gain_grad_one,
            gain_grad_two,
            gain_grad_three,
            gain_grad_four,
            gain_grad_five,
        ],
        1,
    )
    small_grad = jnp.pad(small_grad, ((0, 0), (0, 128 - small_grad.shape[1])))
    rest_grad = jnp.concatenate(
        [grad_ple_down, grad_ple_up, grad_laurel_down, grad_laurel_up, small_grad], 1
    ).astype(low)
    rest_grad = rest_grad.reshape(ranks, -1, rest_grad.shape[1])
    rest_grad, grad_attn_blocks = lax.optimization_barrier((rest_grad, grad_attn_blocks))
    rest_own = take(rest_grad, 0, rank).astype(full) + sum(
        permute(take(rest_grad, 0, relative[k]), "seq", k).astype(full) for k in range(1, ranks)
    )
    rest_own = rest_own.astype(low).reshape(pairs * 2, rows, -1)
    out_grad = weight_grad(ranks, pairs * 2, grad_attn_blocks, attn_in)
    grad_heads = mm(whole_rows(grad_attn_blocks), out_map).astype(low)
    codes = marks_all[:, 0].reshape(length) * (4 * length) + indices
    grad_qkv, grad_gains = attend_back(
        ranks,
        qkv,
        q_heads.reshape(length, q_width),
        k_head,
        v_head,
        grad_heads,
        log_total,
        codes,
        cos_table[:, 0, : HEAD_DIM // 2],
        sin_table[:, 0, : HEAD_DIM // 2],
        head_scale.T,
    )
    grad_head_scale = grad_gains[:2].T
    head_scale_grad = jnp.pad(
        grad_head_scale.reshape(-1, head_rows, 2), ((0, 0), (0, rows - head_rows), (0, 0))
    ).reshape(width, 2)
    late_grad = jnp.pad(head_scale_grad, ((0, 0), (6, 120)))
    last = weight_grad(
        ranks, pairs * 2, [normed_all], grad_qkv, head_all, gain[0][:, None], late_grad
    )
    last, grad_qkv = lax.optimization_barrier((last, grad_qkv))
    x_part = mm_nt(grad_qkv, qkv_map).astype(low)

    if ranks == 4:
        gain_row = jnp.broadcast_to(gain[0], (8, width))
        x_parts = x_part.reshape(ranks, block, width)
        extras = (x_parts, x_here, x_local, grad_mixed, gain_row)
        *sums, input_grad = finish(sizes, last, out_grad, rest_own, extras)
    else:
        sums = finish(sizes, last, out_grad, rest_own)
        grad_x_normed = x_here + sum_seq(cut(x_part), ranks)
        grad_tokens_norm = norm_back(tokens, x_inverse, gain[0], grad_x_normed)[0]
        input_grad = grad_mixed * root_half + grad_tokens_norm
    small_sum = sums[6]

    grad_mlp = jnp.concatenate([in_sum, down_sum[:, None]], 1).astype(full)
    lead = (block, 1, width)
    return (
        hidden_out.reshape(lead),
        input_grad.reshape(lead),
        *sums[:4],
        sums[5],
        sums[4],
        small_sum[:, :6],
        small_sum[:head_rows, 6:8],
        grad_mlp,
    )


def solution(mesh):
    sizes = {"seq": mesh.shape["seq"], "pair": mesh.shape["fsdp"] // 2, "core": 2}
    spread = P(("seq", "fsdp"), None)
    tokens = P("seq", "fsdp", None)
    return jax.shard_map(
        functools.partial(body, sizes),
        mesh=mesh,
        in_specs=(tokens, tokens, P("seq", "fsdp"), P("seq", "fsdp"), tokens)
        + (spread,) * 8
        + (P("fsdp", None, "seq"),),
        out_specs=(tokens, tokens) + (spread,) * 8 + (P("fsdp", None, "seq"),),
        check_vma=False,
    )
```

```python
import functools
import math

import jax
import jax.numpy as jnp
from jax import lax
from jax.experimental import pallas as pl
from jax.experimental.pallas import tpu as pltpu
from jax.sharding import PartitionSpec as P

QUERY_HEADS = 8
KEY_VALUE_HEADS = 2
HEAD_DIM = 256
LR = 64
PLE = 256
WIN = 512

MESH = pl.DeviceIdType.MESH
eps = 1e-06
theta = 10000.0
root_half = 1.0 / math.sqrt(2.0)
low = jnp.bfloat16
full = jnp.float32


def flip(index, offset, size):
    value, bit = 0, 1
    while bit < size:
        has = (index // bit) % 2
        value = value + bit * ((1 - has) if offset & bit else has)
        bit *= 2
    return value


def gather_kernel(
    sizes, head_ref, rest_ref, mark_ref, x_ref, head_out, rest_out, mark_out, x_out, *sems
):
    (local, head_s1, head_r1, right_s, right_r, left_s, left_r, head_s3, head_r3) = sems[:9]
    (rest_s1, rest_r1, rest_s2, rest_r2, rest_s3, rest_r3, mark_s, mark_r, x_s, x_r) = sems[9:]
    ranks, pairs = sizes["seq"], sizes["pair"]
    rank = lax.axis_index("seq")
    fsdp_index = lax.axis_index("fsdp")
    pair, core = fsdp_index // 2, fsdp_index % 2
    sibling = (rank, pair * 2 + 1 - core)

    def on_seq(step):
        return (flip(rank, step, ranks), fsdp_index)

    def on_pair(step):
        return (rank, ((pair + step) % pairs) * 2 + core)

    def remote(source, target, send, recv, device):
        return pltpu.make_async_remote_copy(
            src_ref=source,
            dst_ref=target,
            send_sem=send,
            recv_sem=recv,
            device_id=device,
            device_id_type=MESH,
        )

    barrier = pltpu.get_barrier_semaphore()
    devices = [on_seq(i) for i in range(1, ranks)] + [on_pair(i) for i in range(1, pairs)]
    for device in devices + [sibling]:
        pl.semaphore_signal(barrier, inc=1, device_id=device, device_id_type=MESH)
    pl.semaphore_wait(barrier, len(devices) + 1)

    sent = []

    def go(copy):
        copy.start()
        sent.append(copy)
        return copy

    def part(at, k):
        return head_out.at[flip(rank, k, ranks), at, core]

    def right(t, k):
        source = head_ref.at[rank] if t == 1 and k == 0 else part(pair - (t - 1), k)
        slot = (t - 1) * ranks + k
        target = part(pair - (t - 1), k)
        return remote(source, target, right_s.at[slot], right_r.at[slot], (rank, fsdp_index + 2))

    def left(t, k):
        source = head_ref.at[rank] if t == 1 and k == 0 else part(pair + (t - 1), k)
        slot = (t - 1) * ranks + k
        target = part(pair + (t - 1), k)
        return remote(source, target, left_s.at[slot], left_r.at[slot], (rank, fsdp_index - 2))

    def to_sibling(t, k):
        source = head_ref.at[rank] if t == 0 and k == 0 else part(pair - t, k)
        slot = (t + pairs - 1) * ranks + k
        return remote(source, part(pair - t, k), head_s3.at[slot], head_r3.at[slot], sibling)

    sends_right = lambda t: (pair - (t - 1) >= 0) & (pair + 1 < pairs)
    sends_left = lambda t: (pair + (t - 1) < pairs) & (pair - 1 >= 0)

    def begin(k):
        pl.when(sends_right(1))(lambda: right(1, k).start())
        pl.when(sends_left(1))(lambda: left(1, k).start())
        to_sibling(0, k).start()

    begin(0)
    head_seq = [
        go(
            remote(
                head_ref.at[on_seq(i)[0]],
                head_out.at[rank, pair, core],
                head_s1.at[i - 1],
                head_r1.at[i - 1],
                on_seq(i),
            )
        )
        for i in range(1, ranks)
    ]
    rest_pair = [
        go(
            remote(
                rest_ref,
                rest_out.at[rank, pair, core],
                rest_s1.at[i - 1],
                rest_r1.at[i - 1],
                on_pair(i),
            )
        )
        for i in range(1, pairs)
    ]
    owns = [
        pltpu.make_async_copy(head_ref.at[rank], head_out.at[rank, pair, core], local.at[0]),
        pltpu.make_async_copy(rest_ref, rest_out.at[rank, pair, core], local.at[1]),
        pltpu.make_async_copy(mark_ref, mark_out.at[0], local.at[2]),
        pltpu.make_async_copy(x_ref, x_out.at[0], local.at[3]),
    ]
    for copy in owns:
        copy.start()
    marks = [
        go(remote(mark_ref, mark_out.at[i], mark_s.at[i - 1], mark_r.at[i - 1], on_seq(i)))
        for i in range(1, ranks)
    ]
    for k in range(1, ranks):
        head_seq[k - 1].wait_recv()
        begin(k)

    half = x_ref.shape[1] // 2
    first, second = slice(0, half), slice(half, 2 * half)
    x_seq, relays = [], []
    if ranks == 4:
        for order in range(2):
            for i, columns in ((1, (first, second)[order]), (2, (second, first)[order])):
                slot = (i - 1) * 2 + order
                x_seq.append(
                    go(
                        remote(
                            x_ref.at[:, columns],
                            x_out.at[i, :, columns],
                            x_s.at[slot],
                            x_r.at[slot],
                            on_seq(i),
                        )
                    )
                )
    else:
        for i in range(1, ranks):
            x_seq.append(
                go(remote(x_ref, x_out.at[i], x_s.at[i - 1], x_r.at[i - 1], on_seq(i)))
            )

    owns[1].wait()
    for copy in rest_pair:
        copy.wait_recv()
    row = rest_out.at[rank, :, core]
    rest_seq = [
        go(remote(row, row, rest_s2.at[i - 1], rest_r2.at[i - 1], on_seq(i)))
        for i in range(1, ranks)
    ]
    rest_core = [go(remote(row, row, rest_s3.at[0], rest_r3.at[0], sibling))]

    for t in range(1, pairs):
        for k in range(ranks):

            def from_left(t=t, k=k):
                slot = (t - 1) * ranks + k
                target = part(pair - t, k)
                remote(target, target, right_s.at[slot], right_r.at[slot], sibling).wait_recv()
                if t + 1 < pairs:
                    pl.when(pair + 1 < pairs)(lambda: right(t + 1, k).start())
                to_sibling(t, k).start()

            def from_right(t=t, k=k):
                slot = (t - 1) * ranks + k
                target = part(pair + t, k)
                remote(target, target, left_s.at[slot], left_r.at[slot], sibling).wait_recv()
                if t + 1 < pairs:
                    pl.when(pair - 1 >= 0)(lambda: left(t + 1, k).start())
                to_sibling(-t, k).start()

            pl.when(pair - t >= 0)(from_left)
            pl.when(pair + t < pairs)(from_right)
        if t == 1 and ranks == 4:
            x_seq[0].wait_recv()
            x_seq[1].wait_recv()
            for slot, i, columns, to in ((4, 1, first, 2), (5, 2, second, 1)):
                relays.append(
                    go(
                        remote(
                            x_out.at[i, :, columns],
                            x_out.at[3, :, columns],
                            x_s.at[slot],
                            x_r.at[slot],
                            on_seq(to),
                        )
                    )
                )

    for i in range(1, ranks):
        rest_seq[i - 1].wait_recv()
        row = rest_out.at[flip(rank, i, ranks), :, core]
        rest_core.append(go(remote(row, row, rest_s3.at[i], rest_r3.at[i], sibling)))
    owns[0].wait()
    for copy in owns[2:]:
        copy.wait()
    for copy in marks + x_seq[2 if ranks == 4 else 0 :] + relays + rest_core:
        copy.wait_recv()
    for k in range(ranks):
        to_sibling(0, k).wait()
        for t in range(1, pairs):
            pl.when(pair - t >= 0)(lambda t=t, k=k: to_sibling(t, k).wait())
            pl.when(pair + t < pairs)(lambda t=t, k=k: to_sibling(-t, k).wait())
            pl.when(sends_right(t))(lambda t=t, k=k: right(t, k).wait_send())
            pl.when(sends_left(t))(lambda t=t, k=k: left(t, k).wait_send())
    for copy in sent:
        copy.wait_send()


def gather_weights(sizes, head, rest, marks, x):
    ranks, pairs = sizes["seq"], sizes["pair"]
    dma = lambda n: pltpu.SemaphoreType.DMA((n,))
    anywhere = pl.BlockSpec(memory_space=pl.ANY)
    return pl.pallas_call(
        functools.partial(gather_kernel, sizes),
        out_shape=(
            jax.ShapeDtypeStruct((ranks, pairs, 2) + head.shape[1:], head.dtype),
            jax.ShapeDtypeStruct((ranks, pairs, 2) + rest.shape, rest.dtype),
            jax.ShapeDtypeStruct((ranks,) + marks.shape, marks.dtype),
            jax.ShapeDtypeStruct((ranks,) + x.shape, x.dtype),
        ),
        in_specs=[anywhere] * 4,
        out_specs=(anywhere,) * 4,
        scratch_shapes=[
            dma(4),
            *[dma(ranks - 1)] * 2,
            *[dma((pairs - 1) * ranks)] * 4,
            *[dma((2 * pairs - 1) * ranks)] * 2,
            *[dma(pairs - 1)] * 2,
            *[dma(ranks - 1)] * 2,
            *[dma(ranks)] * 2,
            *[dma(ranks - 1)] * 2,
            *[dma(2 * ranks - 2)] * 2,
        ],
        compiler_params=pltpu.CompilerParams(collective_id=0, has_side_effects=True),
    )(head, rest, marks, x)


def permute(v, axis, offset):
    size = lax.axis_size(axis)
    return lax.ppermute(v, axis, [(i, i ^ offset) for i in range(size)])


def gather_seq(v, ranks):
    if ranks != 4:
        return [v] + [permute(v, "seq", k) for k in range(1, ranks)]
    half = v.shape[1] // 2
    first, second = permute(v, "seq", 1), permute(v, "seq", 2)
    left = permute(first[:, :half], "seq", 2)
    right = permute(second[:, half:], "seq", 1)
    return [v, first, second, left, right]


def whole_rows(blocks):
    if blocks[-1].shape[1] < blocks[0].shape[1]:
        blocks = blocks[:-2] + [jnp.concatenate(blocks[-2:], 1)]
    return jnp.concatenate(blocks, 0)


def sum_seq(blocks, ranks):
    up = lambda v: v.astype(full)
    if ranks != 4:
        return sum((up(permute(blocks[k], "seq", k)) for k in range(1, ranks)), up(blocks[0]))
    half = blocks[0].shape[1] // 2
    left = [b[:, :half] for b in blocks]
    right = [b[:, half:] for b in blocks]
    left_far, right_far = permute(left[3], "seq", 1), permute(right[3], "seq", 2)
    left_near, right_near = permute(left[1], "seq", 1), permute(right[2], "seq", 2)
    left_far = permute((up(left[2]) + up(left_far)).astype(low), "seq", 2)
    right_far = permute((up(right[1]) + up(right_far)).astype(low), "seq", 1)
    return jnp.concatenate(
        [
            up(left[0]) + up(left_near) + up(left_far),
            up(right[0]) + up(right_near) + up(right_far),
        ],
        1,
    )


def take(v, axis, index):
    return lax.dynamic_index_in_dim(v, index, axis, keepdims=False)


def gather_everywhere(v, ranks, pairs):
    index, rank = lax.axis_index("fsdp"), lax.axis_index("seq")
    pair, core = index // 2, index % 2

    def spread(part, axis, offsets, mine):
        got = jnp.stack([part] + [permute(part, axis, k) for k in offsets])
        return jnp.stack([take(got, 0, mine ^ i) for i in range(len(offsets) + 1)])

    v = spread(v, "fsdp", [2 * k for k in range(1, pairs)], pair)
    v = spread(v, "seq", range(1, ranks), rank)
    v = spread(v, "fsdp", [1], core)
    return jnp.moveaxis(v, 0, 2).reshape(-1, v.shape[-1])


def dot(left, right, over):
    return lax.dot_general(left, right, (over, ((), ())), preferred_element_type=full)


def mm(left, right):
    return dot(left, right, ((1,), (0,)))


def mm_nt(left, right):
    return dot(left, right, ((1,), (1,)))


def mm_tn(left, right):
    return dot(left, right, ((0,), (0,)))


def norm_rows(v, gain_vec):
    inverse = lax.rsqrt(jnp.mean(v * v, -1, keepdims=True) + eps)
    return (v * inverse * gain_vec, inverse)


def norm_back(v, inverse, gain_vec, incoming):
    scaled = incoming * gain_vec
    inner_mean = jnp.mean(scaled * v, -1, keepdims=True)
    return (
        inverse * (scaled - v * inverse * inverse * inner_mean),
        jnp.sum(incoming * v * inverse, axis=0),
    )


def gelu_tanh(v):
    return jax.nn.gelu(v, approximate=True)


def rope_tables(places):
    half_width = HEAD_DIM // 2
    frequency = theta ** (-jnp.arange(half_width).astype(full) * 2.0 / HEAD_DIM)
    angles = places.astype(full)[:, None] * frequency
    return (jnp.cos(angles), jnp.sin(angles))


def reaches(rank, mine, other, block):
    apart = (rank ^ mine) - (rank ^ other)
    return (apart >= 0) & (apart * block - (block - 1) < WIN)


def attend_kernel(
    ranks,
    block,
    qkv_ref,
    code_col_ref,
    code_row_ref,
    cos_ref,
    sin_ref,
    gain_ref,
    q_ref,
    k_ref,
    v_ref,
    out_ref,
    total_ref,
    scores_ref,
    peak_acc,
    sum_acc,
    out_acc,
):
    head, mine = pl.program_id(0), pl.program_id(1)
    rank = lax.axis_index("seq")
    half = HEAD_DIM // 2
    base = qkv_ref.shape[1] - 2 * HEAD_DIM

    def normed(v):
        return v * lax.rsqrt(jnp.mean(v * v, -1, keepdims=True) + eps)

    def turned(v, cos_table, sin_table):
        first, second = v[:, :half], v[:, half:]
        return jnp.concatenate(
            [
                first * cos_table - second * sin_table,
                second * cos_table + first * sin_table,
            ],
            1,
        )

    @pl.when((head == 0) & (mine == 0))
    def _():
        for other in range(ranks):
            span = slice(other * block, (other + 1) * block)
            keys = normed(qkv_ref[span, base : base + HEAD_DIM]) * gain_ref[1:2, :]
            k_ref[span, :] = turned(keys, cos_ref[span, :], sin_ref[span, :]).astype(low)
            v_ref[span, :] = normed(qkv_ref[span, base + HEAD_DIM :]).astype(low)

    rows = pl.ds(pl.multiple_of(mine * block, block), block)
    columns = pl.ds(pl.multiple_of(head * HEAD_DIM, HEAD_DIM), HEAD_DIM)
    queries = normed(qkv_ref[rows, columns]) * gain_ref[0:1, :]
    q = turned(queries, cos_ref[rows, :], sin_ref[rows, :]).astype(low)
    q_ref[rows, columns] = q
    code = code_col_ref[rows, :]
    peak_acc[...] = jnp.full_like(peak_acc, -1000000000.0)
    sum_acc[...] = jnp.zeros_like(sum_acc)
    out_acc[...] = jnp.zeros_like(out_acc)
    for other in range(ranks):
        span = slice(other * block, (other + 1) * block)

        @pl.when(reaches(rank, mine, other, block))
        def _():
            scores = mm_nt(q, k_ref[span, :]) * HEAD_DIM ** (-0.5)
            offset = code - code_row_ref[:, span]
            scores = jnp.where((offset >= 0) & (offset < WIN), scores, -1000000000.0)
            scores_ref[other] = scores
            peak_acc[...] = jnp.maximum(peak_acc[...], jnp.max(scores, -1, keepdims=True))

    peak = peak_acc[...]
    for other in range(ranks):

        @pl.when(reaches(rank, mine, other, block))
        def _():
            weights = jnp.exp(scores_ref[other] - peak)
            scores_ref[other] = weights
            sum_acc[...] += jnp.sum(weights, -1, keepdims=True)

    row_total = sum_acc[...]
    for other in range(ranks):
        span = slice(other * block, (other + 1) * block)

        @pl.when(reaches(rank, mine, other, block))
        def _():
            probs = (scores_ref[other] / row_total).astype(low)
            out_acc[...] += mm(probs, v_ref[span, :])

    out_ref[rows, columns] = out_acc[...].astype(low)
    total_ref[head, rows, :] = peak + jnp.log(row_total)


def attend(ranks, qkv, codes, cos_table, sin_table, gains):
    length = qkv.shape[0]
    block = length // ranks
    heads = qkv.shape[1] // HEAD_DIM - 2
    whole = lambda v: pl.BlockSpec(
        v.shape, lambda i, j, n=len(v.shape): (0,) * n, pipeline_mode=pl.Buffered(1)
    )
    operands = (qkv, codes[:, None], codes[None], cos_table, sin_table, gains)
    results = (
        jax.ShapeDtypeStruct((length, heads * HEAD_DIM), low),
        jax.ShapeDtypeStruct((length, HEAD_DIM), low),
        jax.ShapeDtypeStruct((length, HEAD_DIM), low),
        jax.ShapeDtypeStruct((length, heads * HEAD_DIM), low),
        jax.ShapeDtypeStruct((heads, length, 1), full),
    )
    return pl.pallas_call(
        functools.partial(attend_kernel, ranks, block),
        grid=(heads, ranks),
        out_shape=results,
        in_specs=[whole(v) for v in operands],
        out_specs=tuple(whole(v) for v in results),
        scratch_shapes=[
            pltpu.VMEM((ranks, block, block), full),
            pltpu.VMEM((block, 1), full),
            pltpu.VMEM((block, 1), full),
            pltpu.VMEM((block, HEAD_DIM), full),
        ],
        compiler_params=pltpu.CompilerParams(vmem_limit_bytes=40 << 20),
        cost_estimate=pl.CostEstimate(
            flops=4 * heads * length * length * HEAD_DIM * 9 // 16,
            bytes_accessed=12 * length * HEAD_DIM * (heads + 2),
            transcendentals=heads * length * length,
        ),
    )(*operands)


def norm_rope_back(lin, gain, incoming):
    inverse = lax.rsqrt(jnp.mean(lin * lin, -1, keepdims=True) + eps)
    scaled = incoming * gain
    inner_mean = jnp.mean(scaled * lin, -1, keepdims=True)
    return (
        inverse * (scaled - lin * inverse * inverse * inner_mean),
        jnp.sum(incoming * lin * inverse, 0, keepdims=True),
    )


def attend_back_kernel(
    ranks,
    block,
    qkv_ref,
    q_ref,
    k_ref,
    v_ref,
    grad_ref,
    total_ref,
    code_col_ref,
    code_row_ref,
    cos_ref,
    sin_ref,
    gain_ref,
    out_ref,
    gain_out_ref,
    key_acc,
    value_acc,
    query_acc,
    row_acc,
    probs_ref,
    grad_probs_ref,
):
    head, mine = pl.program_id(0), pl.program_id(1)
    heads = pl.num_programs(0)
    rank = lax.axis_index("seq")
    scale = HEAD_DIM ** (-0.5)
    half = HEAD_DIM // 2

    @pl.when((head == 0) & (mine == 0))
    def _():
        key_acc[...] = jnp.zeros_like(key_acc)
        value_acc[...] = jnp.zeros_like(value_acc)
        gain_out_ref[...] = jnp.zeros_like(gain_out_ref)

    rows = pl.ds(pl.multiple_of(mine * block, block), block)
    columns = pl.ds(pl.multiple_of(head * HEAD_DIM, HEAD_DIM), HEAD_DIM)
    q, grad = q_ref[rows, columns], grad_ref[rows, columns]
    code = code_col_ref[rows, :]
    peaks = total_ref[head, rows, :]
    row_acc[...] = jnp.zeros_like(row_acc)
    query_acc[...] = jnp.zeros_like(query_acc)

    for other in range(ranks):
        span = slice(other * block, (other + 1) * block)

        @pl.when(reaches(rank, mine, other, block))
        def _():
            scores = mm_nt(q, k_ref[span, :]) * scale
            offset = code - code_row_ref[:, span]
            probs = jnp.where((offset >= 0) & (offset < WIN), jnp.exp(scores - peaks), 0.0)
            grad_probs = mm_nt(grad, v_ref[span, :])
            probs_ref[other] = probs
            grad_probs_ref[other] = grad_probs
            row_acc[...] += jnp.sum(probs * grad_probs, -1, keepdims=True)

    inner = row_acc[...]
    for other in range(ranks):
        span = slice(other * block, (other + 1) * block)

        @pl.when(reaches(rank, mine, other, block))
        def _():
            probs = probs_ref[other]
            grad_scores = (probs * (grad_probs_ref[other] - inner) * scale).astype(low)
            query_acc[...] += mm(grad_scores, k_ref[span, :])
            key_acc[span, :] += mm_tn(grad_scores, q)
            value_acc[span, :] += mm_tn(probs.astype(low), grad)

    def turned_back(v, cos_table, sin_table):
        first, second = v[:, :half], v[:, half:]
        return jnp.concatenate(
            [
                first * cos_table + second * sin_table,
                second * cos_table - first * sin_table,
            ],
            1,
        )

    incoming = turned_back(query_acc[...].astype(low).astype(full), cos_ref[rows, :], sin_ref[rows, :])
    grad_lin, grad_gain = norm_rope_back(qkv_ref[rows, columns], gain_ref[0:1, :], incoming)
    out_ref[rows, columns] = grad_lin.astype(low)
    gain_out_ref[0:1, :] += grad_gain

    @pl.when((head == heads - 1) & (mine == ranks - 1))
    def _():
        base = out_ref.shape[1] - 2 * HEAD_DIM
        for other in range(ranks):
            span = slice(other * block, (other + 1) * block)
            incoming = turned_back(key_acc[span, :], cos_ref[span, :], sin_ref[span, :])
            grad_lin, grad_gain = norm_rope_back(
                qkv_ref[span, base : base + HEAD_DIM], gain_ref[1:2, :], incoming
            )
            out_ref[span, base : base + HEAD_DIM] = grad_lin.astype(low)
            gain_out_ref[1:2, :] += grad_gain
            grad_lin = norm_rope_back(qkv_ref[span, base + HEAD_DIM :], 1.0, value_acc[span, :])[0]
            out_ref[span, base + HEAD_DIM :] = grad_lin.astype(low)


def attend_back(ranks, qkv, q, k, v, grad, total, codes, cos_table, sin_table, gains):
    length = qkv.shape[0]
    block = length // ranks
    heads = q.shape[1] // HEAD_DIM
    whole = lambda v: pl.BlockSpec(
        v.shape, lambda i, j, n=len(v.shape): (0,) * n, pipeline_mode=pl.Buffered(1)
    )
    operands = (qkv, q, k, v, grad, total, codes[:, None], codes[None], cos_table, sin_table, gains)
    results = (
        jax.ShapeDtypeStruct(qkv.shape, low),
        jax.ShapeDtypeStruct((8, HEAD_DIM), full),
    )
    return pl.pallas_call(
        functools.partial(attend_back_kernel, ranks, block),
        grid=(heads, ranks),
        out_shape=results,
        in_specs=[whole(v) for v in operands],
        out_specs=tuple(whole(v) for v in results),
        scratch_shapes=[
            pltpu.VMEM((length, HEAD_DIM), full),
            pltpu.VMEM((length, HEAD_DIM), full),
            pltpu.VMEM((block, HEAD_DIM), full),
            pltpu.VMEM((block, 1), full),
            pltpu.VMEM((ranks, block, block), full),
            pltpu.VMEM((ranks, block, block), full),
        ],
        compiler_params=pltpu.CompilerParams(vmem_limit_bytes=40 << 20),
        cost_estimate=pl.CostEstimate(
            flops=10 * heads * length * length * HEAD_DIM * 9 // 16,
            bytes_accessed=16 * length * HEAD_DIM * (heads + 2),
            transcendentals=heads * length * length,
        ),
    )(*operands)


def weight_grad_kernel(count, half_tiles, *refs):
    lefts, right_ref, out_ref = refs[:count], refs[count], refs[-1]
    pieces = [ref[...] for ref in lefts]
    if half_tiles:
        pieces[-2:] = [jnp.where(pl.program_id(0) < half_tiles, pieces[-2], pieces[-1])]
    result, start = None, 0
    for piece in pieces:
        part = mm_tn(piece, right_ref[start : start + piece.shape[0], :])
        result = part if result is None else result + part
        start += piece.shape[0]
    if len(refs) > count + 2:
        map_ref, gain_ref, late_ref = refs[count + 1 : count + 4]
        maps = map_ref[:, : result.shape[1]].astype(full)
        of_gain = jnp.sum(maps * result, -1, keepdims=True) / gain_ref[...]
        late = late_ref[...]
        lane = lax.broadcasted_iota(jnp.int32, late.shape, 1)
        result = jnp.concatenate([result, jnp.where(lane == 0, of_gain, late)], 1)
    out_ref[...] = result.astype(low).reshape(out_ref.shape)


def weight_grad(ranks, parts, lefts, right, *extras):
    width = lefts[0].shape[1]
    length, columns = right.shape
    rows = width // (ranks * parts)
    tile = max(min(256, rows * parts), rows)
    each = tile // rows
    wide = columns + (128 if extras else 0)
    half_tiles = lefts[-1].shape[1] // tile if lefts[-1].shape[1] < width else 0

    def place(i):
        return (((i * each) % parts) // each, (i * each) // parts, 0, 0)

    left_specs = [pl.BlockSpec((v.shape[0], tile), lambda i: (0, i)) for v in lefts]
    if half_tiles:
        left_specs[-2:] = [
            pl.BlockSpec((lefts[-1].shape[0], tile), lambda i: (0, jnp.minimum(i, half_tiles - 1))),
            pl.BlockSpec((lefts[-1].shape[0], tile), lambda i: (0, jnp.maximum(i - half_tiles, 0))),
        ]
    return pl.pallas_call(
        functools.partial(weight_grad_kernel, len(lefts), half_tiles),
        grid=(width // tile,),
        out_shape=jax.ShapeDtypeStruct((parts, ranks, rows, wide), low),
        in_specs=left_specs
        + [pl.BlockSpec((length, columns), lambda i: (0, 0))]
        + [pl.BlockSpec((tile, v.shape[1]), lambda i: (i, 0)) for v in extras],
        out_specs=pl.BlockSpec((each, 1, rows, wide), place),
        compiler_params=pltpu.CompilerParams(vmem_limit_bytes=60 << 20),
        cost_estimate=pl.CostEstimate(
            flops=2 * length * width * columns,
            bytes_accessed=2 * (length * (width + columns) + width * columns),
            transcendentals=0,
        ),
    )(*lefts, right, *extras)


def middle_kernel(
    pairs,
    block,
    parts,
    rows_own,
    rows_x_in,
    rows_y_in,
    rows_left_in,
    rows_right_in,
    in_maps_ref,
    shard_ref,
    mixed_ref,
    gain_ref,
    ple_gate_ref,
    ple_proj_ref,
    ple_input_ref,
    cotangent_ref,
    rows_out_ref,
    grad_map_ref,
    map_ref,
    gate_part_ref,
    up_part_ref,
    out_ref,
    second_ref,
    grad_second_ref,
    grad_ple_ref,
    ple_mixed_ref,
    grad_gate_ref,
    gain_out_ref,
    rows_ref,
    in_tiles,
    wide_stage,
    hidden_ref,
    maps,
    product_ref,
    own,
    keep,
    send,
    got,
    relay,
    far,
    stage,
    load_sem,
    tile_sem,
    wide_sem,
    stage_sem,
    map_sem,
    right_s,
    right_r,
    left_s,
    left_r,
    core_s,
    core_r,
    near_s,
    near_r,
    far_s,
    far_r,
    gx_s,
    gx_r,
    gy_s,
    gy_r,
    fx_s,
    fx_r,
    fy_s,
    fy_r,
):
    rank = lax.axis_index("seq")
    fsdp_index = lax.axis_index("fsdp")
    pair, core = fsdp_index // 2, fsdp_index % 2
    sibling = (rank, pair * 2 + 1 - core)
    rank_x, rank_y = flip(rank, 1, 4), flip(rank, 2, 4)
    by_x, by_y = (rank_x, fsdp_index), (rank_y, fsdp_index)
    size = block // parts
    width, span = in_maps_ref.shape[1], in_maps_ref.shape[2]
    half = width // 2
    tile = 256
    tiles = span // tile
    shard = shard_ref.shape[0]
    cut = shard // 2
    left, right = slice(0, half), slice(half, width)
    up = lambda v: v.astype(full)

    def remote(source, target, send_sem, recv_sem, device):
        return pltpu.make_async_remote_copy(
            src_ref=source,
            dst_ref=target,
            send_sem=send_sem,
            recv_sem=recv_sem,
            device_id=device,
            device_id_type=MESH,
        )

    def columns_of(i):
        return pl.ds(pl.multiple_of(i * tile, tile), tile)

    loads = [
        pltpu.make_async_copy(source, target, load_sem.at[i])
        for i, (source, target) in enumerate(
            (
                (rows_own, rows_ref.at[0]),
                (rows_x_in, rows_ref.at[1]),
                (rows_y_in, rows_ref.at[2]),
                (rows_left_in, rows_ref.at[3, :, left]),
                (rows_right_in, rows_ref.at[3, :, right]),
                (shard_ref, maps.at[pair, core]),
            )
        )
    ]

    def tile_copy(i, slot):
        return pltpu.make_async_copy(
            in_maps_ref.at[:, :, columns_of(i)], in_tiles.at[slot], tile_sem.at[slot]
        )

    for copy in loads:
        copy.start()
    tile_copy(0, 0).start()

    barrier = pltpu.get_barrier_semaphore()
    devices = [by_x, by_y, sibling]
    devices += [(rank, ((pair + i) % pairs) * 2 + core) for i in range(1, pairs)]
    for device in devices:
        pl.semaphore_signal(barrier, inc=1, device_id=device, device_id_type=MESH)
    pl.semaphore_wait(barrier, len(devices))

    def piece(at, k):
        return maps.at[at, core, pl.ds(k * cut, cut), :]

    def source_of(at, k, t):
        return shard_ref.at[pl.ds(k * cut, cut), :] if t == 0 else piece(at, k)

    def pass_right(t, k):
        at, slot = pair - (t - 1), (t - 1) * 2 + k
        return remote(
            source_of(at, k, t - 1),
            piece(at, k),
            right_s.at[slot],
            right_r.at[slot],
            (rank, fsdp_index + 2),
        )

    def pass_left(t, k):
        at, slot = pair + (t - 1), (t - 1) * 2 + k
        return remote(
            source_of(at, k, t - 1),
            piece(at, k),
            left_s.at[slot],
            left_r.at[slot],
            (rank, fsdp_index - 2),
        )

    def to_sibling(at, k, own_shard=False):
        slot = at * 2 + k
        return remote(
            source_of(at, k, 0 if own_shard else 1),
            piece(at, k),
            core_s.at[slot],
            core_r.at[slot],
            sibling,
        )

    sends_right = lambda t: (pair - (t - 1) >= 0) & (pair + 1 < pairs)
    sends_left = lambda t: (pair + (t - 1) < pairs) & (pair - 1 >= 0)
    for k in range(2):
        pl.when(sends_right(1))(lambda k=k: pass_right(1, k).start())
        pl.when(sends_left(1))(lambda k=k: pass_left(1, k).start())
        to_sibling(pair, k, True).start()

    def chain_step(t, k):
        slot = (t - 1) * 2 + k

        def from_left():
            target = piece(pair - t, k)
            remote(target, target, right_s.at[slot], right_r.at[slot], sibling).wait_recv()
            if t + 1 < pairs:
                pl.when(pair + 1 < pairs)(lambda: pass_right(t + 1, k).start())
            to_sibling(pair - t, k).start()

        def from_right():
            target = piece(pair + t, k)
            remote(target, target, left_s.at[slot], left_r.at[slot], sibling).wait_recv()
            if t + 1 < pairs:
                pl.when(pair - 1 >= 0)(lambda: pass_left(t + 1, k).start())
            to_sibling(pair + t, k).start()

        pl.when(pair - t >= 0)(from_left)
        pl.when(pair + t < pairs)(from_right)

    for copy in loads:
        copy.wait()

    def wide_copies(i, slot):
        return [
            pltpu.make_async_copy(
                wide_stage.at[slot, n], target.at[:, columns_of(i)], wide_sem.at[slot, n]
            )
            for n, target in enumerate((gate_part_ref, up_part_ref))
        ]

    slope, cubic = math.sqrt(2.0 / math.pi), 0.044715

    def gate_up_tile(i, carry):
        slot = i % 2
        tile_copy(i, slot).wait()
        pl.when(i + 1 < tiles)(lambda: tile_copy(i + 1, 1 - slot).start())

        @pl.when(i >= 2)
        def _():
            for copy in wide_copies(i - 2, slot):
                copy.wait()

        v = rows_ref[...].reshape(4 * block, width)
        gate = mm(v, in_tiles[slot, 0])
        wide_stage[slot, 0] = gate
        upper = mm(v, in_tiles[slot, 1])
        wide_stage[slot, 1] = upper
        bend = jnp.tanh(slope * (gate + cubic * gate * gate * gate))
        hidden_ref[:, columns_of(i)] = (0.5 * gate * (1.0 + bend) * upper).astype(low)
        for copy in wide_copies(i, slot):
            copy.start()
        return carry

    steps = [(t, k) for t in range(1, pairs) for k in range(2)]
    early = min(len(steps), 4)
    at_tile = [tiles * (n + 1) // early for n in range(early)]
    done = 0
    for n in range(early):
        lax.fori_loop(done, at_tile[n], gate_up_tile, 0)
        done = at_tile[n]
        chain_step(*steps[n])
    for i in (tiles - 2, tiles - 1):
        for copy in wide_copies(i, i % 2):
            copy.wait()

    def chip_of(j):
        orders = [sorted(range(pairs), key=lambda p: (abs(p - z), p)) for z in range(pairs)]
        return sum(jnp.where(pair == z, orders[z][j], 0) for z in range(pairs))

    def shard_of(j):
        chip = chip_of(j // 2)
        at_core = core if j % 2 == 0 else 1 - core
        return chip, at_core, chip * 2 + at_core, 1 - chip // (pairs // 2)

    def near_copy(j):
        chip, at_core, place, is_left = shard_of(j)
        to = rank_x * is_left + rank_y * (1 - is_left)
        return remote(
            send.at[place], got.at[place], near_s.at[place], near_r.at[place], (to, fsdp_index)
        )

    def far_copy(j):
        chip, at_core, place, is_left = shard_of(j)
        to = rank_y * is_left + rank_x * (1 - is_left)
        return remote(
            relay.at[place], far.at[place], far_s.at[place], far_r.at[place], (to, fsdp_index)
        )

    def product(j):
        chip, at_core, place, is_left = shard_of(j)
        if j % 2:
            for k in range(2):
                target = maps.at[chip, at_core, pl.ds(k * cut, cut), :]
                remote(
                    target, target, core_s.at[0], core_r.at[chip * 2 + k], sibling
                ).wait_recv()
        v = mm_nt(hidden_ref[...], maps[chip, at_core])
        product_ref[...] = v.reshape(4, block, shard)
        near = 2 - is_left
        own[:, columns_of(place)] = product_ref[0]
        send[place, 0] = product_ref[3].astype(low)
        send[place, 1] = product_ref[near].astype(low)
        keep[place] = product_ref[3 - near]
        near_copy(j).start()

    def pass_on(j):
        place = shard_of(j)[2]
        near_copy(j).wait_recv()
        relay[place] = (keep[place] + up(got[place, 0])).astype(low)
        far_copy(j).start()

    def collect(j):
        place = shard_of(j)[2]
        far_copy(j).wait_recv()
        columns = columns_of(place)
        own[:, columns] += up(got[place, 1]) + up(far[place])

    count = 2 * pairs
    rest = steps[early:]
    for j in range(count):
        need = j // 2
        while rest and rest[0][0] <= need:
            chain_step(*rest.pop(0))
        product(j)
        if j >= 2:
            pass_on(j - 2)
        if j >= 4:
            collect(j - 4)
    for j in (count - 2, count - 1):
        pass_on(j)
    for j in range(count - 4, count):
        collect(j)

    def map_copy(i):
        return pltpu.make_async_copy(
            maps.at[i // 2, i % 2], map_ref.at[pl.ds(i * shard, shard), :], map_sem.at[i]
        )

    for i in range(count):
        map_copy(i).start()
    sent = []

    def go(copy):
        copy.start()
        sent.append(copy)
        return copy

    def rows_of(u):
        return pl.ds(u * size, size)

    gain_out_ref[...] = jnp.zeros_like(gain_out_ref)
    ffn_gain, ple_gain = gain_ref[0:1, :], gain_ref[1:2, :]
    mean = lambda v: jnp.mean(v, -1, keepdims=True)
    total = lambda v: jnp.sum(v, 0, keepdims=True)
    rows_x, rows_y = [], []
    for u in range(parts):
        at = rows_of(u)
        f = own[at, :]
        f_inverse = lax.rsqrt(mean(f * f) + eps)
        second = (mixed_ref[at, :] + f * f_inverse * ffn_gain).astype(low)
        second_ref[at, :] = second
        gate = mm(second, ple_gate_ref[...])
        bend = jnp.tanh(slope * (gate + cubic * gate * gate * gate))
        gate_slope = 0.5 * (1.0 + bend) + 0.5 * gate * (1.0 - bend * bend) * slope * (
            1.0 + 3.0 * cubic * gate * gate
        )
        given = up(ple_input_ref[at, :])
        ple_mixed = (0.5 * gate * (1.0 + bend) * given).astype(low)
        ple_mixed_ref[at, :] = ple_mixed
        proj = mm_nt(ple_mixed, ple_proj_ref[...])
        proj_inverse = lax.rsqrt(mean(proj * proj) + eps)
        out_ref[at, :] = (up(second) + proj * proj_inverse * ple_gain).astype(low)
        incoming = up(cotangent_ref[at, :])
        gain_out_ref[1:2, :] += total(incoming * proj * proj_inverse)
        scaled = incoming * ple_gain
        grad_proj = proj_inverse * (
            scaled - proj * (proj_inverse * proj_inverse * mean(scaled * proj))
        )
        grad_ple = grad_proj.astype(low)
        grad_ple_ref[at, :] = grad_ple
        grad_gate = (mm(grad_ple, ple_proj_ref[...]) * given * gate_slope).astype(low)
        grad_gate_ref[at, :] = grad_gate
        grad_second = incoming + mm_nt(grad_gate, ple_gate_ref[...])
        grad_second_ref[at, :] = grad_second
        f = own[at, :]
        gain_out_ref[0:1, :] += total(grad_second * f * f_inverse)
        scaled = grad_second * ffn_gain
        grad_f = f_inverse * (scaled - f * (f_inverse * f_inverse * mean(scaled * f)))
        rows_ref[0, at, :] = grad_f.astype(low)
        pair_x, pair_y = [], []
        for order in range(2):
            for copies, device, send_sem, recv_sem, index, part in (
                (pair_x, by_x, gx_s, gx_r, 1, (left, right)[order]),
                (pair_y, by_y, gy_s, gy_r, 2, (right, left)[order]),
            ):
                copies.append(
                    go(
                        remote(
                            rows_ref.at[0, at, part],
                            rows_ref.at[index, at, part],
                            send_sem.at[u, order],
                            recv_sem.at[u, order],
                            device,
                        )
                    )
                )
        rows_x.append(pair_x)
        rows_y.append(pair_y)

    forwards = []
    for u in range(parts):
        at = rows_of(u)
        rows_x[u][0].wait_recv()
        forwards.append(
            go(
                remote(
                    rows_ref.at[1, at, left],
                    rows_ref.at[3, at, left],
                    fy_s.at[u],
                    fy_r.at[u],
                    by_y,
                )
            )
        )
        rows_y[u][0].wait_recv()
        forwards.append(
            go(
                remote(
                    rows_ref.at[2, at, right],
                    rows_ref.at[3, at, right],
                    fx_s.at[u],
                    fx_r.at[u],
                    by_x,
                )
            )
        )
    for u in range(parts):
        rows_x[u][1].wait_recv()
        rows_y[u][1].wait_recv()
    for copy in forwards:
        copy.wait_recv()

    def stage_copy(i, slot):
        at = pl.ds(pl.multiple_of(i * tile, tile), tile)
        return pltpu.make_async_copy(stage.at[slot], grad_map_ref.at[at, :], stage_sem.at[slot])

    rows_copy = pltpu.make_async_copy(rows_ref, rows_out_ref, load_sem.at[0])
    rows_copy.start()

    def grad_tile(i, carry):
        slot = i % 2

        @pl.when(i >= 2)
        def _():
            stage_copy(i - 2, slot).wait()

        columns = pl.ds(pl.multiple_of(i * tile, tile), tile)
        v = rows_ref[:, :, columns].reshape(4 * block, tile)
        for j in range(0, span, span // 2):
            stage[slot, :, j : j + span // 2] = mm_tn(v, hidden_ref[:, j : j + span // 2]).astype(low)
        stage_copy(i, slot).start()
        return carry

    lax.fori_loop(0, count, grad_tile, 0)
    stage_copy(count - 2, 0).wait()
    stage_copy(count - 1, 1).wait()
    for copy in sent:
        copy.wait_send()
    rows_copy.wait()
    for i in range(count):
        map_copy(i).wait()
    for j in range(count):
        near_copy(j).wait_send()
        far_copy(j).wait_send()
    for k in range(2):
        to_sibling(pair, k, True).wait_send()
        for t in range(1, pairs):
            pl.when(pair - t >= 0)(lambda t=t, k=k: to_sibling(pair - t, k).wait_send())
            pl.when(pair + t < pairs)(lambda t=t, k=k: to_sibling(pair + t, k).wait_send())
            pl.when(sends_right(t))(lambda t=t, k=k: pass_right(t, k).wait_send())
            pl.when(sends_left(t))(lambda t=t, k=k: pass_left(t, k).wait_send())


def middle(pairs, h_blocks, in_maps, down_rows, mixed, gains, ple, ple_input, cotangent):
    block, width = mixed.shape
    span = in_maps.shape[2]
    shard = down_rows.shape[0]
    parts, length = 2, 4 * block
    count = 2 * pairs
    dma = lambda *n: pltpu.SemaphoreType.DMA(n)
    vmem = pl.BlockSpec(memory_space=pltpu.VMEM)
    anywhere = pl.BlockSpec(memory_space=pl.ANY)
    shapes = (
        ((4, block, width), low),
        ((width, span), low),
        ((width, span), low),
        ((length, span), full),
        ((length, span), full),
        ((block, width), low),
        ((block, width), low),
        ((block, width), full),
        ((block, width), low),
        ((block, PLE), low),
        ((block, PLE), low),
        ((8, width), full),
    )
    return pl.pallas_call(
        functools.partial(middle_kernel, pairs, block, parts),
        out_shape=tuple(jax.ShapeDtypeStruct(*v) for v in shapes),
        in_specs=[anywhere] * 7 + [vmem] * 6,
        out_specs=tuple(anywhere if i < 5 else vmem for i in range(len(shapes))),
        scratch_shapes=[
            pltpu.VMEM((4, block, width), low),
            pltpu.VMEM((2, 2, width, 256), low),
            pltpu.VMEM((2, 2, length, 256), full),
            pltpu.VMEM((length, span), low),
            pltpu.VMEM((pairs, 2, shard, span), low),
            pltpu.VMEM((4, block, shard), full),
            pltpu.VMEM((block, width), full),
            pltpu.VMEM((count, block, shard), full),
            pltpu.VMEM((count, 2, block, shard), low),
            pltpu.VMEM((count, 2, block, shard), low),
            pltpu.VMEM((count, block, shard), low),
            pltpu.VMEM((count, block, shard), low),
            pltpu.VMEM((2, 256, span), low),
            dma(6),
            dma(2),
            dma(2, 2),
            dma(2),
            dma(count),
            *[dma(2 * (pairs - 1))] * 4,
            *[dma(count)] * 2,
            *[dma(count)] * 4,
            *[dma(parts, 2)] * 4,
            *[dma(parts)] * 4,
        ],
        compiler_params=pltpu.CompilerParams(
            collective_id=1, has_side_effects=True, vmem_limit_bytes=62 << 20
        ),
        cost_estimate=pl.CostEstimate(
            flops=16 * block * width * span, bytes_accessed=100 << 20, transcendentals=0
        ),
    )(
        *h_blocks,
        in_maps,
        down_rows,
        mixed,
        jnp.pad(jnp.stack(gains), ((0, 6), (0, 0))),
        ple[:, :PLE],
        ple[:, PLE:],
        ple_input,
        cotangent,
    )


def middle_plain(ranks, h_blocks, in_maps, down_rows, mixed, gains, ple, ple_input, cotangent):
    block = mixed.shape[0]
    down_map = lax.all_gather(down_rows, "fsdp", axis=0, tiled=True)
    gate_up = dot(whole_rows(h_blocks), in_maps, ((1,), (1,)))
    gate_part, up_part = gate_up[:, 0], gate_up[:, 1]
    hidden = (gelu_tanh(gate_part) * up_part).astype(low)
    parts = mm_nt(hidden, down_map).astype(low)
    ffn_out = sum_seq([parts[k * block : (k + 1) * block] for k in range(ranks)], ranks)
    ffn_normed, ffn_inverse = norm_rows(ffn_out, gains[0])
    h_second = (mixed + ffn_normed).astype(low)
    ple_gate = mm(h_second, ple[:, :PLE])
    ple_input = ple_input.astype(full)
    ple_mixed = (gelu_tanh(ple_gate) * ple_input).astype(low)
    ple_proj = mm_nt(ple_mixed, ple[:, PLE:])
    ple_normed, ple_inverse = norm_rows(ple_proj, gains[1])
    hidden_out = (h_second.astype(full) + ple_normed).astype(low)
    grad_out = cotangent.astype(full)
    grad_ple_proj, gain_grad_five = norm_back(ple_proj, ple_inverse, gains[1], grad_out)
    grad_ple_low = grad_ple_proj.astype(low)
    grad_ple_mixed = mm(grad_ple_low, ple[:, PLE:])
    unused_gelu, gelu_pull = jax.vjp(gelu_tanh, ple_gate)
    grad_ple_gate = gelu_pull(grad_ple_mixed * ple_input)[0].astype(low)
    grad_second = grad_out + mm_nt(grad_ple_gate, ple[:, :PLE])
    grad_ffn, gain_grad_four = norm_back(ffn_out, ffn_inverse, gains[0], grad_second)
    rows = whole_rows(gather_seq(grad_ffn.astype(low), ranks))
    return (
        rows,
        mm_tn(rows, hidden).astype(low),
        down_map,
        gate_part,
        up_part,
        hidden_out,
        h_second,
        grad_second,
        grad_ple_low,
        ple_mixed,
        grad_ple_gate,
        jnp.stack([gain_grad_four, gain_grad_five]),
    )


def back_kernel(
    block,
    gate_ref,
    up_ref,
    maps_ref,
    rows_own,
    rows_x,
    rows_y,
    rows_left,
    rows_right,
    grad_maps_ref,
    sum_ref,
    maps,
    keep_left,
    keep_right,
    send_x,
    send_y,
    got_x,
    got_y,
    relay_x,
    relay_y,
    far_x,
    far_y,
    stage,
    map_sem,
    stage_sem,
    sx_s,
    sx_r,
    sy_s,
    sy_r,
    rx_s,
    rx_r,
    ry_s,
    ry_r,
):
    rank = lax.axis_index("seq")
    fsdp_index = lax.axis_index("fsdp")
    by_x, by_y = (flip(rank, 1, 4), fsdp_index), (flip(rank, 2, 4), fsdp_index)
    width, span = maps_ref.shape[1], maps_ref.shape[2]
    tile = 256
    tiles = width // tile
    each = tiles // 2
    up = lambda v: v.astype(full)

    def columns_of(i):
        return pl.ds(pl.multiple_of(i * tile, tile), tile)

    def remote(source, target, send, recv, device):
        return pltpu.make_async_remote_copy(
            src_ref=source,
            dst_ref=target,
            send_sem=send,
            recv_sem=recv,
            device_id=device,
            device_id_type=MESH,
        )

    def map_copy(i):
        return pltpu.make_async_copy(
            maps_ref.at[:, columns_of(i), :], maps.at[:, columns_of(i), :], map_sem.at[i]
        )

    def near_x(j):
        return remote(send_x.at[j], got_x.at[j], sx_s.at[j], sx_r.at[j], by_x)

    def near_y(j):
        return remote(send_y.at[j], got_y.at[j], sy_s.at[j], sy_r.at[j], by_y)

    def last_x(j):
        return remote(relay_x.at[j], far_x.at[j], rx_s.at[j], rx_r.at[j], by_x)

    def last_y(j):
        return remote(relay_y.at[j], far_y.at[j], ry_s.at[j], ry_r.at[j], by_y)

    for j in range(each):
        map_copy(j).start()
        map_copy(j + each).start()

    barrier = pltpu.get_barrier_semaphore()
    for device in (by_x, by_y):
        pl.semaphore_signal(barrier, inc=1, device_id=device, device_id_type=MESH)
    pl.semaphore_wait(barrier, 2)

    def product(i):
        map_copy(i).wait()
        v = mm_nt(gate_ref[...], maps[0, columns_of(i), :])
        v = v + mm_nt(up_ref[...], maps[1, columns_of(i), :])
        return v.reshape(4, block, tile)

    def send_tiles(j, carry):
        v = product(j)
        sum_ref[:, columns_of(j)] = v[0]
        keep_left[j] = v[2]
        send_x[j, 0] = v[3].astype(low)
        send_x[j, 1] = v[1].astype(low)
        near_x(j).start()
        v = product(j + each)
        sum_ref[:, columns_of(j + each)] = v[0]
        keep_right[j] = v[1]
        send_y[j, 0] = v[3].astype(low)
        send_y[j, 1] = v[2].astype(low)
        near_y(j).start()
        return carry

    lax.fori_loop(0, each, send_tiles, 0)

    def stage_copy(i, slot):
        return pltpu.make_async_copy(
            stage.at[slot], grad_maps_ref.at[:, columns_of(i), :], stage_sem.at[slot]
        )

    def grad_tile(i, j, far_ref):
        slot = j % 2
        pl.when(i >= 2)(lambda: stage_copy(i - 2, slot).wait())
        near = columns_of(i)
        v = jnp.concatenate(
            [rows_own[:, near], rows_x[:, near], rows_y[:, near], far_ref[:, columns_of(j)]], 0
        )
        for k in range(0, span, span // 2):
            part = slice(k, k + span // 2)
            stage[slot, 0, :, part] = mm_tn(v, gate_ref[:, part]).astype(low)
            stage[slot, 1, :, part] = mm_tn(v, up_ref[:, part]).astype(low)
        stage_copy(i, slot).start()

    def left_tile(j, carry):
        grad_tile(j, j, rows_left)
        near_x(j).wait_recv()
        relay_y[j] = (keep_left[j] + up(got_x[j, 0])).astype(low)
        last_y(j).start()
        near_y(j).wait_recv()
        relay_x[j] = (keep_right[j] + up(got_y[j, 0])).astype(low)
        last_x(j).start()
        return carry

    def right_tile(j, carry):
        grad_tile(j + each, j, rows_right)
        last_y(j).wait_recv()
        sum_ref[:, columns_of(j)] += up(got_x[j, 1]) + up(far_y[j])
        last_x(j).wait_recv()
        sum_ref[:, columns_of(j + each)] += up(got_y[j, 1]) + up(far_x[j])
        return carry

    lax.fori_loop(0, each, left_tile, 0)
    lax.fori_loop(0, each, right_tile, 0)
    stage_copy(tiles - 2, 0).wait()
    stage_copy(tiles - 1, 1).wait()

    def sent(j, carry):
        for copy in (near_x(j), near_y(j), last_x(j), last_y(j)):
            copy.wait_send()
        return carry

    lax.fori_loop(0, each, sent, 0)


def back(grad_gate, grad_up, in_maps, h_blocks):
    length, span = grad_gate.shape
    block, width = h_blocks[0].shape
    each = width // 512
    dma = pltpu.SemaphoreType.DMA
    vmem = pl.BlockSpec(memory_space=pltpu.VMEM)
    anywhere = pl.BlockSpec(memory_space=pl.ANY)
    keep = pltpu.VMEM((each, block, 256), full)
    pieces = pltpu.VMEM((each, 2, block, 256), low)
    singles = pltpu.VMEM((each, block, 256), low)
    return pl.pallas_call(
        functools.partial(back_kernel, block),
        out_shape=(
            jax.ShapeDtypeStruct((2, width, span), low),
            jax.ShapeDtypeStruct((block, width), full),
        ),
        in_specs=[vmem, vmem, anywhere] + [vmem] * 5,
        out_specs=(anywhere, vmem),
        scratch_shapes=[
            pltpu.VMEM((2, width, span), low),
            keep,
            keep,
            *[pieces] * 4,
            *[singles] * 4,
            pltpu.VMEM((2, 2, 256, span), low),
            dma((width // 256,)),
            dma((2,)),
            *[dma((each,))] * 8,
        ],
        compiler_params=pltpu.CompilerParams(
            collective_id=3, has_side_effects=True, vmem_limit_bytes=58 << 20
        ),
        cost_estimate=pl.CostEstimate(
            flops=8 * length * width * span, bytes_accessed=50 << 20, transcendentals=0
        ),
    )(grad_gate, grad_up, in_maps, *h_blocks)


def finish_kernel(sizes, with_x, *refs):
    ranks, pairs = sizes["seq"], sizes["pair"]
    refs = list(refs)

    def some(count):
        head = refs[:count]
        del refs[:count]
        return head

    owns = some(3)
    x_ref, branch_ref, tokens_ref, base_ref, gain_ref = some(5) if with_x else [None] * 5
    query_ref, key_ref, value_ref, out_ref, ple_ref, laurel_ref, small_ref = some(7)
    (input_ref,) = some(1) if with_x else [None]
    sums, from_left, from_right = some(3), some(3), some(3)
    got_last, got_out = some(2)
    if with_x:
        got_x, got_y, relay_x, relay_y, far_x, far_y = some(6)
    core_s, core_r, right_s, right_r, left_s, left_r, last_s, last_r, out_s, out_r = some(10)
    if with_x:
        x_s, x_r = some(2)

    rank = lax.axis_index("seq")
    fsdp_index = lax.axis_index("fsdp")
    pair, core = fsdp_index // 2, fsdp_index % 2
    sibling = (rank, pair * 2 + 1 - core)
    on_seq = lambda k: (flip(rank, k, ranks), fsdp_index)
    up = lambda v: v.astype(full)

    def remote(source, target, send, recv, device):
        return pltpu.make_async_remote_copy(
            src_ref=source,
            dst_ref=target,
            send_sem=send,
            recv_sem=recv,
            device_id=device,
            device_id_type=MESH,
        )

    barrier = pltpu.get_barrier_semaphore()
    devices = [on_seq(k) for k in range(1, ranks)]
    devices += [(rank, ((pair + i) % pairs) * 2 + core) for i in range(1, pairs)]
    for device in devices + [sibling]:
        pl.semaphore_signal(barrier, inc=1, device_id=device, device_id_type=MESH)
    pl.semaphore_wait(barrier, len(devices) + 1)

    sent = []

    def go(copy):
        copy.start()
        sent.append(copy)
        return copy

    half_ranks = ranks // 2
    pieces = [
        (1, slice(0, ranks)),
        (2, None),
        (0, slice(0, half_ranks)),
        (0, slice(half_ranks, ranks)),
    ]
    count = len(pieces)

    def view(group, lead, piece):
        number, rows = pieces[piece]
        ref = group[number]
        return ref.at[lead] if rows is None else ref.at[lead, rows]

    order = [i // 2 if i % 2 else pairs - 1 - i // 2 for i in range(pairs)]

    def swap(chip, piece):
        slot = chip * count + piece
        return remote(
            view(owns, chip * 2 + 1 - core, piece),
            view(sums, chip, piece),
            core_s.at[slot],
            core_r.at[slot],
            sibling,
        )

    for chip in order:
        for piece in range(count):
            go(swap(chip, piece))
    if with_x:
        half = x_ref.shape[2] // 2
        left, right = slice(0, half), slice(half, 2 * half)
        by_x, by_y = on_seq(1), on_seq(2)
        near = []
        for slot, block, columns, target, device in (
            (0, 3, left, got_x.at[0], by_x),
            (1, 3, right, got_y.at[0], by_y),
            (2, 1, left, got_x.at[1], by_x),
            (3, 2, right, got_y.at[1], by_y),
        ):
            near.append(
                go(remote(x_ref.at[block, :, columns], target, x_s.at[slot], x_r.at[slot], device))
            )

    def whole_chip(chip, piece):
        target = view(sums, chip, piece)
        remote(
            target, target, core_s.at[0], core_r.at[chip * count + piece], sibling
        ).wait_recv()
        target[...] = (up(target[...]) + up(view(owns, chip * 2 + core, piece)[...])).astype(low)

    def pass_right(t, piece):
        slot = (t - 1) * count + piece
        return remote(
            view(sums, pair + pairs - t, piece),
            view(from_left, t - 1, piece),
            right_s.at[slot],
            right_r.at[slot],
            (rank, fsdp_index + 2),
        )

    def pass_left(t, piece):
        slot = (t - 1) * count + piece
        return remote(
            view(sums, pair - (pairs - t), piece),
            view(from_right, t - 1, piece),
            left_s.at[slot],
            left_r.at[slot],
            (rank, fsdp_index - 2),
        )

    def add_left(t, piece, target):
        got = view(from_left, t - 1, piece)
        slot = (t - 1) * count + piece
        remote(got, got, right_s.at[slot], right_r.at[slot], sibling).wait_recv()
        target[...] = (up(target[...]) + up(got[...])).astype(low)

    def add_right(t, piece, target):
        got = view(from_right, t - 1, piece)
        slot = (t - 1) * count + piece
        remote(got, got, left_s.at[slot], left_r.at[slot], sibling).wait_recv()
        target[...] = (up(target[...]) + up(got[...])).astype(low)

    mirrored = pairs - 1 - pair
    relays = []
    for t in range(1, pairs):
        for piece in range(count):

            def to_right(t=t, piece=piece):
                chip = pair + pairs - t
                whole_chip(chip, piece)
                if t > 1:
                    pl.when(pair > 0)(lambda: add_left(t - 1, piece, view(sums, chip, piece)))
                pass_right(t, piece).start()

            def to_left(t=t, piece=piece):
                chip = pair - (pairs - t)
                whole_chip(chip, piece)
                if t > 1:
                    pl.when(mirrored > 0)(lambda: add_right(t - 1, piece, view(sums, chip, piece)))
                pass_left(t, piece).start()

            pl.when(t >= pair + 1)(to_right)
            pl.when(t >= mirrored + 1)(to_left)
        if with_x and t == 1:
            near[0].wait_recv()
            relay_y[...] = (up(x_ref[2, :, left]) + up(got_x[0])).astype(low)
            relays.append(go(remote(relay_y, far_y, x_s.at[4], x_r.at[4], by_y)))
            near[1].wait_recv()
            relay_x[...] = (up(x_ref[1, :, right]) + up(got_y[0])).astype(low)
            relays.append(go(remote(relay_x, far_x, x_s.at[5], x_r.at[5], by_x)))
            for piece in range(count):
                whole_chip(pair, piece)
    if with_x:
        for copy in near[2:] + relays:
            copy.wait_recv()
        mean = lambda v: jnp.mean(v, -1, keepdims=True)
        step = x_ref.shape[1] // 2
        for i in range(2):
            at = slice(i * step, (i + 1) * step)
            incoming = branch_ref[at, :] + jnp.concatenate(
                [
                    up(x_ref[0, at, left]) + up(got_x[1, at, :]) + up(far_y[at, :]),
                    up(x_ref[0, at, right]) + up(got_y[1, at, :]) + up(far_x[at, :]),
                ],
                1,
            )
            v = up(tokens_ref[at, :])
            inverse = lax.rsqrt(mean(v * v) + eps)
            scaled = incoming * gain_ref[0:1, :]
            input_ref[at, 0, :] = base_ref[at, :] * root_half + inverse * (
                scaled - v * (inverse * inverse * mean(scaled * v))
            )
    else:
        for piece in range(count):
            whole_chip(pair, piece)

    for piece in range(count):
        target = view(sums, pair, piece)
        pl.when(pair > 0)(lambda: add_left(pairs - 1, piece, target))
        pl.when(mirrored > 0)(lambda: add_right(pairs - 1, piece, target))

    last_sum, out_sum, rest_sum = [ref.at[pair] for ref in sums]
    across = []
    for k in range(1, ranks):
        peer = flip(rank, k, ranks)
        across.append(
            (
                go(remote(last_sum.at[peer], got_last.at[k], last_s.at[k], last_r.at[k], on_seq(k))),
                go(remote(out_sum.at[peer], got_out.at[k], out_s.at[k], out_r.at[k], on_seq(k))),
            )
        )
    ple_ref[...] = up(rest_sum[:, : 2 * PLE])
    laurel_ref[...] = up(rest_sum[:, 2 * PLE : 2 * PLE + 2 * LR])
    small_ref[...] = up(rest_sum[:, 2 * PLE + 2 * LR :])
    key_ref[...] = jnp.zeros_like(key_ref)
    value_ref[...] = jnp.zeros_like(value_ref)
    q_width = out_sum.shape[2]
    for k in range(ranks):
        if k:
            for copy in across[k - 1]:
                copy.wait_recv()
            last, out = up(got_last[k]), up(got_out[k])
        else:
            last, out = up(last_sum[rank]), up(out_sum[rank])
        sender = flip(rank, k, ranks)
        columns = pl.ds(pl.multiple_of(sender * q_width, q_width), q_width)
        group = sender * (QUERY_HEADS // ranks) // (QUERY_HEADS // KEY_VALUE_HEADS)
        head = pl.ds(pl.multiple_of(group * HEAD_DIM, HEAD_DIM), HEAD_DIM)
        query_ref[:, columns] = last[:, :q_width]
        out_ref[:, columns] = out
        key_ref[:, head] += last[:, q_width : q_width + HEAD_DIM]
        value_ref[:, head] += last[:, q_width + HEAD_DIM : q_width + 2 * HEAD_DIM]
        small_ref[...] += last[:, q_width + 2 * HEAD_DIM :]

    for t in range(1, pairs):
        for piece in range(count):
            pl.when(t >= pair + 1)(lambda t=t, piece=piece: pass_right(t, piece).wait_send())
            pl.when(t >= mirrored + 1)(lambda t=t, piece=piece: pass_left(t, piece).wait_send())
    for copy in sent:
        copy.wait_send()


def finish(sizes, last, out, rest, x=None):
    ranks, pairs = sizes["seq"], sizes["pair"]
    rows = last.shape[2]
    arrays = [last, out, rest]
    vmem = pl.BlockSpec(memory_space=pltpu.VMEM)
    dma = lambda n: pltpu.SemaphoreType.DMA((n,))
    width = KEY_VALUE_HEADS * HEAD_DIM
    shapes = [
        (rows, QUERY_HEADS * HEAD_DIM),
        (rows, width),
        (rows, width),
        (rows, QUERY_HEADS * HEAD_DIM),
        (rows, 2 * PLE),
        (rows, 2 * LR),
        (rows, rest.shape[-1] - 2 * PLE - 2 * LR),
    ]
    scratch = [pltpu.VMEM((pairs,) + v.shape[1:], low) for v in arrays]
    scratch += [pltpu.VMEM((pairs - 1,) + v.shape[1:], low) for v in arrays] * 2
    scratch += [pltpu.VMEM((ranks,) + v.shape[2:], low) for v in arrays[:2]]
    if x is not None:
        block, columns = x[0].shape[1], x[0].shape[2] // 2
        shapes.append((block, 1, 2 * columns))
        scratch += [pltpu.VMEM((2, block, columns), low)] * 2
        scratch += [pltpu.VMEM((block, columns), low)] * 4
    scratch += [dma(4 * pairs)] * 2 + [dma(4 * (pairs - 1))] * 4 + [dma(ranks)] * 4
    if x is not None:
        scratch += [dma(6)] * 2
    operands = arrays + list(x or ())
    return pl.pallas_call(
        functools.partial(finish_kernel, sizes, x is not None),
        out_shape=tuple(jax.ShapeDtypeStruct(v, full) for v in shapes),
        in_specs=[vmem] * len(operands),
        out_specs=(vmem,) * len(shapes),
        scratch_shapes=scratch,
        compiler_params=pltpu.CompilerParams(
            collective_id=2, has_side_effects=True, vmem_limit_bytes=56 << 20
        ),
    )(*operands)


def body(
    sizes,
    hidden_in,
    per_layer_input,
    segment_ids,
    positions,
    out_cotangent,
    w_query,
    key_matrix,
    value_matrix,
    w_out_t,
    laurel_maps,
    per_layer_maps,
    norm_gains,
    head_gains,
    w_mlp,
):
    ranks, pairs = sizes["seq"], sizes["pair"]
    block, _, width = hidden_in.shape
    rows = w_query.shape[0]
    q_width = QUERY_HEADS // ranks * HEAD_DIM
    share = QUERY_HEADS // KEY_VALUE_HEADS
    kv_of = [rank * (QUERY_HEADS // ranks) // share for rank in range(ranks)]
    length = block * ranks
    rank = lax.axis_index("seq")
    relative = [rank ^ k for k in range(ranks)]
    cut = lambda v: [v[k * block : (k + 1) * block] for k in range(ranks)]

    by_rank = lambda m: m.reshape(rows, ranks, q_width).transpose(1, 0, 2)
    by_kv = lambda m: jnp.stack([m[:, j * HEAD_DIM : (j + 1) * HEAD_DIM] for j in kv_of])
    head_pack = jnp.concatenate(
        [by_rank(w_query), by_kv(key_matrix), by_kv(value_matrix), by_rank(w_out_t)], 2
    )
    head_rows = head_gains.shape[0]
    small = jnp.concatenate(
        [norm_gains, jnp.pad(head_gains, ((0, rows - head_rows), (0, 0)))], 1
    )
    small = jnp.pad(small, ((0, 0), (0, 128 - small.shape[1])))
    rest_pack = jnp.concatenate([laurel_maps, small], 1)
    marks = jnp.pad(jnp.concatenate([segment_ids.T, positions.T], 0), ((0, 6), (0, 0)))
    x_local = hidden_in.reshape(block, width)

    head_all, rest_all, marks_all, x_all = gather_weights(
        sizes, head_pack, rest_pack, marks, x_local
    )
    in_rows, down_rows, head_all = lax.optimization_barrier(
        (jnp.moveaxis(w_mlp[:, :2], 1, 0), w_mlp[:, 2], head_all)
    )
    in_maps = lax.all_gather(in_rows, "fsdp", axis=1, tiled=True)
    x_all = x_all.reshape(length, width)
    head_all = head_all.reshape(width, -1)
    rest_all = rest_all.reshape(width, -1)
    qkv_map, out_map = head_all[:, :-q_width], head_all[:, -q_width:]
    laurel = rest_all[:, : 2 * LR]
    gains = rest_all[:, 2 * LR :].astype(full)
    gain = [gains[:, i] for i in range(6)]
    head_scale = gains[:, 6:8].reshape(-1, rows, 2)[:, :head_rows].reshape(HEAD_DIM, 2)

    tokens_all = x_all.astype(full)
    normed_all = norm_rows(tokens_all, gain[0])[0].astype(low)
    tokens = x_local.astype(full)
    x_normed_f, x_inverse = norm_rows(tokens, gain[0])
    normed = x_normed_f.astype(low)
    indices = jnp.concatenate([r * block + jnp.arange(block) for r in relative])
    cos_table, sin_table = rope_tables(marks_all[:, 1].reshape(length))
    codes = marks_all[:, 0].reshape(length) * (4 * length) + indices
    qkv = mm(normed_all, qkv_map)
    q_heads, k_head, v_head, attn_in, log_total = attend(
        ranks, qkv, codes, cos_table, sin_table, head_scale.T
    )
    attn_lin = sum_seq(cut(mm_nt(attn_in, out_map).astype(low)), ranks)

    attn_normed, attn_inverse = norm_rows(attn_lin, gain[1])
    laurel_low = mm(normed, laurel[:, :LR]).astype(low)
    laurel_high = mm_nt(laurel_low, laurel[:, LR:])
    laurel_normed, laurel_inverse = norm_rows(laurel_high, gain[2])
    mixed = (tokens + attn_normed + (normed.astype(full) + laurel_normed)) * root_half
    h_normed_f, h_inverse = norm_rows(mixed, gain[3])
    h_blocks = gather_seq(h_normed_f.astype(low), ranks)
    h_blocks, per_layer_maps = lax.optimization_barrier((h_blocks, per_layer_maps))
    ple = gather_everywhere(per_layer_maps, ranks, pairs)
    run_middle = functools.partial(
        *((middle, pairs) if ranks == 4 else (middle_plain, ranks))
    )
    (
        grad_ffn_rows,
        down_grad,
        down_map,
        gate_part,
        up_part,
        hidden_out,
        h_second,
        grad_second,
        grad_ple_low,
        ple_mixed,
        grad_ple_gate,
        ffn_gain_grads,
    ) = run_middle(
        h_blocks,
        in_maps,
        down_rows,
        mixed,
        gain[4:6],
        ple,
        per_layer_input.reshape(block, PLE),
        out_cotangent.reshape(block, width),
    )
    gain_grad_four, gain_grad_five = ffn_gain_grads[0], ffn_gain_grads[1]
    grad_ffn_rows = grad_ffn_rows.reshape(length, width)
    down_sum = lax.psum_scatter(down_grad, "fsdp", scatter_dimension=0, tiled=True)
    grad_ffn_rows, down_grad = lax.optimization_barrier((grad_ffn_rows, down_grad))
    grad_hidden = mm(grad_ffn_rows, down_map)
    gate_act, act_pull = jax.vjp(gelu_tanh, gate_part)
    grad_gate = act_pull(grad_hidden * up_part)[0].astype(low)
    grad_up = (grad_hidden * gate_act).astype(low)
    if ranks == 4:
        in_grad, grad_h_normed = back(grad_gate, grad_up, in_maps, h_blocks)
    else:
        h_part = mm_nt(grad_gate, in_maps[0]) + mm_nt(grad_up, in_maps[1])
        h_part = h_part.astype(low)
        grad_h_normed = sum_seq(cut(h_part), ranks)
        h_rows = whole_rows(h_blocks)
        in_grad = jnp.stack([mm_tn(h_rows, grad_gate), mm_tn(h_rows, grad_up)]).astype(low)
    in_sum = lax.psum_scatter(in_grad, "fsdp", scatter_dimension=1, tiled=True)
    in_sum = jnp.moveaxis(in_sum, 0, 1)

    grad_ple_up = mm_tn(grad_ple_low, ple_mixed)
    grad_ple_down = mm_tn(h_second, grad_ple_gate)
    grad_mixed_norm, gain_grad_three = norm_back(mixed, h_inverse, gain[3], grad_h_normed)
    grad_mixed = grad_second + grad_mixed_norm
    grad_branch = grad_mixed * root_half
    grad_attn, gain_grad_one = norm_back(attn_lin, attn_inverse, gain[1], grad_branch)
    grad_attn_blocks = gather_seq(grad_attn.astype(low), ranks)
    grad_laurel_high, gain_grad_two = norm_back(
        laurel_high, laurel_inverse, gain[2], grad_branch
    )
    grad_high_low = grad_laurel_high.astype(low)
    grad_laurel_up = mm_tn(grad_high_low, laurel_low)
    grad_laurel_low = mm(grad_high_low, laurel[:, LR:]).astype(low)
    grad_laurel_down = mm_tn(normed, grad_laurel_low)

    x_here = grad_branch + mm_nt(grad_laurel_low, laurel[:, :LR])
    gain_grad_zero = jnp.sum(x_here * tokens * x_inverse, 0)
    small_grad = jnp.stack(
        [
            gain_grad_zero,
            gain_grad_one,
            gain_grad_two,
            gain_grad_three,
            gain_grad_four,
            gain_grad_five,
        ],
        1,
    )
    small_grad = jnp.pad(small_grad, ((0, 0), (0, 128 - small_grad.shape[1])))
    rest_grad = jnp.concatenate(
        [grad_ple_down, grad_ple_up, grad_laurel_down, grad_laurel_up, small_grad], 1
    ).astype(low)
    rest_grad = rest_grad.reshape(ranks, -1, rest_grad.shape[1])
    rest_grad, grad_attn_blocks = lax.optimization_barrier((rest_grad, grad_attn_blocks))
    rest_others = [permute(take(rest_grad, 0, relative[k]), "seq", k) for k in range(1, ranks)]
    out_grad = weight_grad(ranks, pairs * 2, grad_attn_blocks, attn_in)
    grad_heads = mm(whole_rows(grad_attn_blocks), out_map).astype(low)
    grad_qkv, grad_gains = attend_back(
        ranks,
        qkv,
        q_heads,
        k_head,
        v_head,
        grad_heads,
        log_total,
        codes,
        cos_table,
        sin_table,
        head_scale.T,
    )
    grad_head_scale = grad_gains[:2].T
    rest_others, grad_qkv = lax.optimization_barrier((rest_others, grad_qkv))
    rest_own = sum((v.astype(full) for v in rest_others), take(rest_grad, 0, rank).astype(full))
    rest_own = rest_own.astype(low).reshape(pairs * 2, rows, -1)
    head_scale_grad = jnp.pad(
        grad_head_scale.reshape(-1, head_rows, 2), ((0, 0), (0, rows - head_rows), (0, 0))
    ).reshape(width, 2)
    late_grad = jnp.pad(head_scale_grad, ((0, 0), (6, 120)))
    last = weight_grad(
        ranks, pairs * 2, [normed_all], grad_qkv, head_all, gain[0][:, None], late_grad
    )
    last, grad_qkv = lax.optimization_barrier((last, grad_qkv))
    x_part = mm_nt(grad_qkv, qkv_map).astype(low)

    if ranks == 4:
        gain_row = jnp.broadcast_to(gain[0], (8, width))
        x_parts = x_part.reshape(ranks, block, width)
        extras = (x_parts, x_here, x_local, grad_mixed, gain_row)
        *sums, input_grad = finish(sizes, last, out_grad, rest_own, extras)
    else:
        sums = finish(sizes, last, out_grad, rest_own)
        grad_x_normed = x_here + sum_seq(cut(x_part), ranks)
        grad_tokens_norm = norm_back(tokens, x_inverse, gain[0], grad_x_normed)[0]
        input_grad = grad_mixed * root_half + grad_tokens_norm
    small_sum = sums[6]

    grad_mlp = jnp.concatenate([in_sum, down_sum[:, None]], 1).astype(full)
    lead = (block, 1, width)
    return (
        hidden_out.reshape(lead),
        input_grad.reshape(lead),
        *sums[:4],
        sums[5],
        sums[4],
        small_sum[:, :6],
        small_sum[:head_rows, 6:8],
        grad_mlp,
    )


def solution(mesh):
    sizes = {"seq": mesh.shape["seq"], "pair": mesh.shape["fsdp"] // 2, "core": 2}
    spread = P(("seq", "fsdp"), None)
    tokens = P("seq", "fsdp", None)
    return jax.shard_map(
        functools.partial(body, sizes),
        mesh=mesh,
        in_specs=(tokens, tokens, P("seq", "fsdp"), P("seq", "fsdp"), tokens)
        + (spread,) * 8
        + (P("fsdp", None, "seq"),),
        out_specs=(tokens, tokens) + (spread,) * 8 + (P("fsdp", None, "seq"),),
        check_vma=False,
    )
```

```python
import functools
import math

import jax
import jax.numpy as jnp
from jax import lax
from jax.experimental import pallas as pl
from jax.experimental.pallas import tpu as pltpu
from jax.sharding import PartitionSpec as P

QUERY_HEADS = 8
KEY_VALUE_HEADS = 2
HEAD_DIM = 256
LR = 64
PLE = 256
WIN = 512

MESH = pl.DeviceIdType.MESH
eps = 1e-06
theta = 10000.0
root_half = 1.0 / math.sqrt(2.0)
low = jnp.bfloat16
full = jnp.float32


def flip(index, offset, size):
    value, bit = 0, 1
    while bit < size:
        has = (index // bit) % 2
        value = value + bit * ((1 - has) if offset & bit else has)
        bit *= 2
    return value


def gather_kernel(
    sizes,
    head_ref,
    rest_ref,
    mark_ref,
    x_ref,
    planes_ref,
    head_out,
    rest_out,
    mark_out,
    x_out,
    planes_out,
    planes,
    *sems,
):
    (local, head_s1, head_r1, right_s, right_r, left_s, left_r, head_s3, head_r3) = sems[:9]
    (rest_s1, rest_r1, rest_s2, rest_r2, rest_s3, rest_r3, mark_s, mark_r, x_s, x_r) = sems[9:]
    ranks, pairs = sizes["seq"], sizes["pair"]
    rank = lax.axis_index("seq")
    fsdp_index = lax.axis_index("fsdp")
    pair, core = fsdp_index // 2, fsdp_index % 2
    sibling = (rank, pair * 2 + 1 - core)

    def on_seq(step):
        return (flip(rank, step, ranks), fsdp_index)

    def on_pair(step):
        return (rank, ((pair + step) % pairs) * 2 + core)

    def remote(source, target, send, recv, device):
        return pltpu.make_async_remote_copy(
            src_ref=source,
            dst_ref=target,
            send_sem=send,
            recv_sem=recv,
            device_id=device,
            device_id_type=MESH,
        )

    load = pltpu.make_async_copy(planes_ref.at[pl.ds(0, 2)], planes, local.at[4])
    load.start()
    barrier = pltpu.get_barrier_semaphore()
    devices = [on_seq(i) for i in range(1, ranks)] + [on_pair(i) for i in range(1, pairs)]
    for device in devices + [sibling]:
        pl.semaphore_signal(barrier, inc=1, device_id=device, device_id_type=MESH)
    pl.semaphore_wait(barrier, len(devices) + 1)

    sent = []

    def go(copy):
        copy.start()
        sent.append(copy)
        return copy

    def part(at, k):
        return head_out.at[flip(rank, k, ranks), at, core]

    def right(t, k):
        source = head_ref.at[rank] if t == 1 and k == 0 else part(pair - (t - 1), k)
        slot = (t - 1) * ranks + k
        target = part(pair - (t - 1), k)
        return remote(source, target, right_s.at[slot], right_r.at[slot], (rank, fsdp_index + 2))

    def left(t, k):
        source = head_ref.at[rank] if t == 1 and k == 0 else part(pair + (t - 1), k)
        slot = (t - 1) * ranks + k
        target = part(pair + (t - 1), k)
        return remote(source, target, left_s.at[slot], left_r.at[slot], (rank, fsdp_index - 2))

    def to_sibling(t, k):
        source = head_ref.at[rank] if t == 0 and k == 0 else part(pair - t, k)
        slot = (t + pairs - 1) * ranks + k
        return remote(source, part(pair - t, k), head_s3.at[slot], head_r3.at[slot], sibling)

    sends_right = lambda t: (pair - (t - 1) >= 0) & (pair + 1 < pairs)
    sends_left = lambda t: (pair + (t - 1) < pairs) & (pair - 1 >= 0)

    def begin(k):
        pl.when(sends_right(1))(lambda: right(1, k).start())
        pl.when(sends_left(1))(lambda: left(1, k).start())
        to_sibling(0, k).start()

    begin(0)
    head_seq = [
        go(
            remote(
                head_ref.at[on_seq(i)[0]],
                head_out.at[rank, pair, core],
                head_s1.at[i - 1],
                head_r1.at[i - 1],
                on_seq(i),
            )
        )
        for i in range(1, ranks)
    ]
    rest_pair = [
        go(
            remote(
                rest_ref,
                rest_out.at[rank, pair, core],
                rest_s1.at[i - 1],
                rest_r1.at[i - 1],
                on_pair(i),
            )
        )
        for i in range(1, pairs)
    ]
    owns = [
        pltpu.make_async_copy(head_ref.at[rank], head_out.at[rank, pair, core], local.at[0]),
        pltpu.make_async_copy(rest_ref, rest_out.at[rank, pair, core], local.at[1]),
        pltpu.make_async_copy(mark_ref, mark_out.at[0], local.at[2]),
        pltpu.make_async_copy(x_ref, x_out.at[0], local.at[3]),
    ]
    for copy in owns:
        copy.start()
    marks = [
        go(remote(mark_ref, mark_out.at[i], mark_s.at[i - 1], mark_r.at[i - 1], on_seq(i)))
        for i in range(1, ranks)
    ]
    for k in range(1, ranks):
        head_seq[k - 1].wait_recv()
        begin(k)

    half = x_ref.shape[1] // 2
    first, second = slice(0, half), slice(half, 2 * half)
    x_seq, relays = [], []
    if ranks == 4:
        for order in range(2):
            for i, columns in ((1, (first, second)[order]), (2, (second, first)[order])):
                slot = (i - 1) * 2 + order
                x_seq.append(
                    go(
                        remote(
                            x_ref.at[:, columns],
                            x_out.at[i, :, columns],
                            x_s.at[slot],
                            x_r.at[slot],
                            on_seq(i),
                        )
                    )
                )
    else:
        for i in range(1, ranks):
            x_seq.append(
                go(remote(x_ref, x_out.at[i], x_s.at[i - 1], x_r.at[i - 1], on_seq(i)))
            )

    load.wait()
    store = pltpu.make_async_copy(planes, planes_out, local.at[4])
    store.start()
    owns[1].wait()
    for copy in rest_pair:
        copy.wait_recv()
    row = rest_out.at[rank, :, core]
    rest_seq = [
        go(remote(row, row, rest_s2.at[i - 1], rest_r2.at[i - 1], on_seq(i)))
        for i in range(1, ranks)
    ]
    rest_core = [go(remote(row, row, rest_s3.at[0], rest_r3.at[0], sibling))]

    for t in range(1, pairs):
        for k in range(ranks):

            def from_left(t=t, k=k):
                slot = (t - 1) * ranks + k
                target = part(pair - t, k)
                remote(target, target, right_s.at[slot], right_r.at[slot], sibling).wait_recv()
                if t + 1 < pairs:
                    pl.when(pair + 1 < pairs)(lambda: right(t + 1, k).start())
                to_sibling(t, k).start()

            def from_right(t=t, k=k):
                slot = (t - 1) * ranks + k
                target = part(pair + t, k)
                remote(target, target, left_s.at[slot], left_r.at[slot], sibling).wait_recv()
                if t + 1 < pairs:
                    pl.when(pair - 1 >= 0)(lambda: left(t + 1, k).start())
                to_sibling(-t, k).start()

            pl.when(pair - t >= 0)(from_left)
            pl.when(pair + t < pairs)(from_right)
        if t == 1 and ranks == 4:
            x_seq[0].wait_recv()
            x_seq[1].wait_recv()
            for slot, i, columns, to in ((4, 1, first, 2), (5, 2, second, 1)):
                relays.append(
                    go(
                        remote(
                            x_out.at[i, :, columns],
                            x_out.at[3, :, columns],
                            x_s.at[slot],
                            x_r.at[slot],
                            on_seq(to),
                        )
                    )
                )

    for i in range(1, ranks):
        rest_seq[i - 1].wait_recv()
        row = rest_out.at[flip(rank, i, ranks), :, core]
        rest_core.append(go(remote(row, row, rest_s3.at[i], rest_r3.at[i], sibling)))
    owns[0].wait()
    store.wait()
    for copy in owns[2:]:
        copy.wait()
    for copy in marks + x_seq[2 if ranks == 4 else 0 :] + relays + rest_core:
        copy.wait_recv()
    for k in range(ranks):
        to_sibling(0, k).wait()
        for t in range(1, pairs):
            pl.when(pair - t >= 0)(lambda t=t, k=k: to_sibling(t, k).wait())
            pl.when(pair + t < pairs)(lambda t=t, k=k: to_sibling(-t, k).wait())
            pl.when(sends_right(t))(lambda t=t, k=k: right(t, k).wait_send())
            pl.when(sends_left(t))(lambda t=t, k=k: left(t, k).wait_send())
    for copy in sent:
        copy.wait_send()


def gather_weights(sizes, head, rest, marks, x, planes):
    ranks, pairs = sizes["seq"], sizes["pair"]
    dma = lambda n: pltpu.SemaphoreType.DMA((n,))
    anywhere = pl.BlockSpec(memory_space=pl.ANY)
    return pl.pallas_call(
        functools.partial(gather_kernel, sizes),
        out_shape=(
            jax.ShapeDtypeStruct((ranks, pairs, 2) + head.shape[1:], head.dtype),
            jax.ShapeDtypeStruct((ranks, pairs, 2) + rest.shape, rest.dtype),
            jax.ShapeDtypeStruct((ranks,) + marks.shape, marks.dtype),
            jax.ShapeDtypeStruct((ranks,) + x.shape, x.dtype),
            jax.ShapeDtypeStruct((2,) + planes.shape[1:], planes.dtype),
        ),
        in_specs=[anywhere] * 5,
        out_specs=(anywhere,) * 5,
        scratch_shapes=[
            pltpu.VMEM((2,) + planes.shape[1:], planes.dtype),
            dma(5),
            *[dma(ranks - 1)] * 2,
            *[dma((pairs - 1) * ranks)] * 4,
            *[dma((2 * pairs - 1) * ranks)] * 2,
            *[dma(pairs - 1)] * 2,
            *[dma(ranks - 1)] * 2,
            *[dma(ranks)] * 2,
            *[dma(ranks - 1)] * 2,
            *[dma(2 * ranks - 2)] * 2,
        ],
        compiler_params=pltpu.CompilerParams(collective_id=0, has_side_effects=True),
    )(head, rest, marks, x, planes)


def permute(v, axis, offset):
    size = lax.axis_size(axis)
    return lax.ppermute(v, axis, [(i, i ^ offset) for i in range(size)])


def gather_seq(v, ranks):
    if ranks != 4:
        return [v] + [permute(v, "seq", k) for k in range(1, ranks)]
    half = v.shape[1] // 2
    first, second = permute(v, "seq", 1), permute(v, "seq", 2)
    left = permute(first[:, :half], "seq", 2)
    right = permute(second[:, half:], "seq", 1)
    return [v, first, second, left, right]


def whole_rows(blocks):
    if blocks[-1].shape[1] < blocks[0].shape[1]:
        blocks = blocks[:-2] + [jnp.concatenate(blocks[-2:], 1)]
    return jnp.concatenate(blocks, 0)


def sum_seq(blocks, ranks):
    up = lambda v: v.astype(full)
    if ranks != 4:
        return sum((up(permute(blocks[k], "seq", k)) for k in range(1, ranks)), up(blocks[0]))
    half = blocks[0].shape[1] // 2
    left = [b[:, :half] for b in blocks]
    right = [b[:, half:] for b in blocks]
    left_far, right_far = permute(left[3], "seq", 1), permute(right[3], "seq", 2)
    left_near, right_near = permute(left[1], "seq", 1), permute(right[2], "seq", 2)
    left_far = permute((up(left[2]) + up(left_far)).astype(low), "seq", 2)
    right_far = permute((up(right[1]) + up(right_far)).astype(low), "seq", 1)
    return jnp.concatenate(
        [
            up(left[0]) + up(left_near) + up(left_far),
            up(right[0]) + up(right_near) + up(right_far),
        ],
        1,
    )


def take(v, axis, index):
    return lax.dynamic_index_in_dim(v, index, axis, keepdims=False)


def gather_everywhere(v, ranks, pairs):
    index, rank = lax.axis_index("fsdp"), lax.axis_index("seq")
    pair, core = index // 2, index % 2

    def spread(part, axis, offsets, mine):
        got = jnp.stack([part] + [permute(part, axis, k) for k in offsets])
        return jnp.stack([take(got, 0, mine ^ i) for i in range(len(offsets) + 1)])

    v = spread(v, "fsdp", [2 * k for k in range(1, pairs)], pair)
    v = spread(v, "seq", range(1, ranks), rank)
    v = spread(v, "fsdp", [1], core)
    return jnp.moveaxis(v, 0, 2).reshape(-1, v.shape[-1])


def dot(left, right, over):
    return lax.dot_general(left, right, (over, ((), ())), preferred_element_type=full)


def mm(left, right):
    return dot(left, right, ((1,), (0,)))


def mm_nt(left, right):
    return dot(left, right, ((1,), (1,)))


def mm_tn(left, right):
    return dot(left, right, ((0,), (0,)))


def norm_rows(v, gain_vec):
    inverse = lax.rsqrt(jnp.mean(v * v, -1, keepdims=True) + eps)
    return (v * inverse * gain_vec, inverse)


def norm_back(v, inverse, gain_vec, incoming):
    scaled = incoming * gain_vec
    inner_mean = jnp.mean(scaled * v, -1, keepdims=True)
    return (
        inverse * (scaled - v * inverse * inverse * inner_mean),
        jnp.sum(incoming * v * inverse, axis=0),
    )


def gelu_tanh(v):
    return jax.nn.gelu(v, approximate=True)


def rope_tables(places):
    half_width = HEAD_DIM // 2
    frequency = theta ** (-jnp.arange(half_width).astype(full) * 2.0 / HEAD_DIM)
    angles = places.astype(full)[:, None] * frequency
    return (jnp.cos(angles), jnp.sin(angles))


def reaches(rank, mine, other, block):
    apart = (rank ^ mine) - (rank ^ other)
    return (apart >= 0) & (apart * block - (block - 1) < WIN)


def attend_kernel(
    ranks,
    block,
    qkv_ref,
    code_col_ref,
    code_row_ref,
    cos_ref,
    sin_ref,
    gain_ref,
    q_ref,
    k_ref,
    v_ref,
    out_ref,
    total_ref,
    scores_ref,
    peak_acc,
    sum_acc,
    out_acc,
):
    head, mine = pl.program_id(0), pl.program_id(1)
    rank = lax.axis_index("seq")
    half = HEAD_DIM // 2
    base = qkv_ref.shape[1] - 2 * HEAD_DIM

    def normed(v):
        return v * lax.rsqrt(jnp.mean(v * v, -1, keepdims=True) + eps)

    def turned(v, cos_table, sin_table):
        first, second = v[:, :half], v[:, half:]
        return jnp.concatenate(
            [
                first * cos_table - second * sin_table,
                second * cos_table + first * sin_table,
            ],
            1,
        )

    @pl.when((head == 0) & (mine == 0))
    def _():
        for other in range(ranks):
            span = slice(other * block, (other + 1) * block)
            keys = normed(qkv_ref[span, base : base + HEAD_DIM]) * gain_ref[1:2, :]
            k_ref[span, :] = turned(keys, cos_ref[span, :], sin_ref[span, :]).astype(low)
            v_ref[span, :] = normed(qkv_ref[span, base + HEAD_DIM :]).astype(low)

    rows = pl.ds(pl.multiple_of(mine * block, block), block)
    columns = pl.ds(pl.multiple_of(head * HEAD_DIM, HEAD_DIM), HEAD_DIM)
    queries = normed(qkv_ref[rows, columns]) * gain_ref[0:1, :]
    q = turned(queries, cos_ref[rows, :], sin_ref[rows, :]).astype(low)
    q_ref[rows, columns] = q
    code = code_col_ref[rows, :]
    peak_acc[...] = jnp.full_like(peak_acc, -1000000000.0)
    sum_acc[...] = jnp.zeros_like(sum_acc)
    out_acc[...] = jnp.zeros_like(out_acc)
    for other in range(ranks):
        span = slice(other * block, (other + 1) * block)

        @pl.when(reaches(rank, mine, other, block))
        def _():
            scores = mm_nt(q, k_ref[span, :]) * HEAD_DIM ** (-0.5)
            offset = code - code_row_ref[:, span]
            scores = jnp.where((offset >= 0) & (offset < WIN), scores, -1000000000.0)
            scores_ref[other] = scores
            peak_acc[...] = jnp.maximum(peak_acc[...], jnp.max(scores, -1, keepdims=True))

    peak = peak_acc[...]
    for other in range(ranks):

        @pl.when(reaches(rank, mine, other, block))
        def _():
            weights = jnp.exp(scores_ref[other] - peak)
            scores_ref[other] = weights
            sum_acc[...] += jnp.sum(weights, -1, keepdims=True)

    row_total = sum_acc[...]
    for other in range(ranks):
        span = slice(other * block, (other + 1) * block)

        @pl.when(reaches(rank, mine, other, block))
        def _():
            probs = (scores_ref[other] / row_total).astype(low)
            out_acc[...] += mm(probs, v_ref[span, :])

    out_ref[rows, columns] = out_acc[...].astype(low)
    total_ref[head, rows, :] = peak + jnp.log(row_total)


def attend(ranks, qkv, codes, cos_table, sin_table, gains):
    length = qkv.shape[0]
    block = length // ranks
    heads = qkv.shape[1] // HEAD_DIM - 2
    whole = lambda v: pl.BlockSpec(
        v.shape, lambda i, j, n=len(v.shape): (0,) * n, pipeline_mode=pl.Buffered(1)
    )
    operands = (qkv, codes[:, None], codes[None], cos_table, sin_table, gains)
    results = (
        jax.ShapeDtypeStruct((length, heads * HEAD_DIM), low),
        jax.ShapeDtypeStruct((length, HEAD_DIM), low),
        jax.ShapeDtypeStruct((length, HEAD_DIM), low),
        jax.ShapeDtypeStruct((length, heads * HEAD_DIM), low),
        jax.ShapeDtypeStruct((heads, length, 1), full),
    )
    return pl.pallas_call(
        functools.partial(attend_kernel, ranks, block),
        grid=(heads, ranks),
        out_shape=results,
        in_specs=[whole(v) for v in operands],
        out_specs=tuple(whole(v) for v in results),
        scratch_shapes=[
            pltpu.VMEM((ranks, block, block), full),
            pltpu.VMEM((block, 1), full),
            pltpu.VMEM((block, 1), full),
            pltpu.VMEM((block, HEAD_DIM), full),
        ],
        compiler_params=pltpu.CompilerParams(vmem_limit_bytes=40 << 20),
        cost_estimate=pl.CostEstimate(
            flops=4 * heads * length * length * HEAD_DIM * 9 // 16,
            bytes_accessed=12 * length * HEAD_DIM * (heads + 2),
            transcendentals=heads * length * length,
        ),
    )(*operands)


def norm_rope_back(lin, gain, incoming):
    inverse = lax.rsqrt(jnp.mean(lin * lin, -1, keepdims=True) + eps)
    scaled = incoming * gain
    inner_mean = jnp.mean(scaled * lin, -1, keepdims=True)
    return (
        inverse * (scaled - lin * inverse * inverse * inner_mean),
        jnp.sum(incoming * lin * inverse, 0, keepdims=True),
    )


def attend_back_kernel(
    ranks,
    block,
    qkv_ref,
    q_ref,
    k_ref,
    v_ref,
    grad_ref,
    total_ref,
    code_col_ref,
    code_row_ref,
    cos_ref,
    sin_ref,
    gain_ref,
    out_ref,
    gain_out_ref,
    key_acc,
    value_acc,
    query_acc,
    row_acc,
    probs_ref,
    grad_probs_ref,
):
    head, mine = pl.program_id(0), pl.program_id(1)
    heads = pl.num_programs(0)
    rank = lax.axis_index("seq")
    scale = HEAD_DIM ** (-0.5)
    half = HEAD_DIM // 2

    @pl.when((head == 0) & (mine == 0))
    def _():
        key_acc[...] = jnp.zeros_like(key_acc)
        value_acc[...] = jnp.zeros_like(value_acc)
        gain_out_ref[...] = jnp.zeros_like(gain_out_ref)

    rows = pl.ds(pl.multiple_of(mine * block, block), block)
    columns = pl.ds(pl.multiple_of(head * HEAD_DIM, HEAD_DIM), HEAD_DIM)
    q, grad = q_ref[rows, columns], grad_ref[rows, columns]
    code = code_col_ref[rows, :]
    peaks = total_ref[head, rows, :]
    row_acc[...] = jnp.zeros_like(row_acc)
    query_acc[...] = jnp.zeros_like(query_acc)

    for other in range(ranks):
        span = slice(other * block, (other + 1) * block)

        @pl.when(reaches(rank, mine, other, block))
        def _():
            scores = mm_nt(q, k_ref[span, :]) * scale
            offset = code - code_row_ref[:, span]
            probs = jnp.where((offset >= 0) & (offset < WIN), jnp.exp(scores - peaks), 0.0)
            grad_probs = mm_nt(grad, v_ref[span, :])
            probs_ref[other] = probs
            grad_probs_ref[other] = grad_probs
            row_acc[...] += jnp.sum(probs * grad_probs, -1, keepdims=True)

    inner = row_acc[...]
    for other in range(ranks):
        span = slice(other * block, (other + 1) * block)

        @pl.when(reaches(rank, mine, other, block))
        def _():
            probs = probs_ref[other]
            grad_scores = (probs * (grad_probs_ref[other] - inner) * scale).astype(low)
            query_acc[...] += mm(grad_scores, k_ref[span, :])
            key_acc[span, :] += mm_tn(grad_scores, q)
            value_acc[span, :] += mm_tn(probs.astype(low), grad)

    def turned_back(v, cos_table, sin_table):
        first, second = v[:, :half], v[:, half:]
        return jnp.concatenate(
            [
                first * cos_table + second * sin_table,
                second * cos_table - first * sin_table,
            ],
            1,
        )

    incoming = turned_back(query_acc[...].astype(low).astype(full), cos_ref[rows, :], sin_ref[rows, :])
    grad_lin, grad_gain = norm_rope_back(qkv_ref[rows, columns], gain_ref[0:1, :], incoming)
    out_ref[rows, columns] = grad_lin.astype(low)
    gain_out_ref[0:1, :] += grad_gain

    @pl.when((head == heads - 1) & (mine == ranks - 1))
    def _():
        base = out_ref.shape[1] - 2 * HEAD_DIM
        for other in range(ranks):
            span = slice(other * block, (other + 1) * block)
            incoming = turned_back(key_acc[span, :], cos_ref[span, :], sin_ref[span, :])
            grad_lin, grad_gain = norm_rope_back(
                qkv_ref[span, base : base + HEAD_DIM], gain_ref[1:2, :], incoming
            )
            out_ref[span, base : base + HEAD_DIM] = grad_lin.astype(low)
            gain_out_ref[1:2, :] += grad_gain
            grad_lin = norm_rope_back(qkv_ref[span, base + HEAD_DIM :], 1.0, value_acc[span, :])[0]
            out_ref[span, base + HEAD_DIM :] = grad_lin.astype(low)


def attend_back(ranks, qkv, q, k, v, grad, total, codes, cos_table, sin_table, gains):
    length = qkv.shape[0]
    block = length // ranks
    heads = q.shape[1] // HEAD_DIM
    whole = lambda v: pl.BlockSpec(
        v.shape, lambda i, j, n=len(v.shape): (0,) * n, pipeline_mode=pl.Buffered(1)
    )
    operands = (qkv, q, k, v, grad, total, codes[:, None], codes[None], cos_table, sin_table, gains)
    results = (
        jax.ShapeDtypeStruct(qkv.shape, low),
        jax.ShapeDtypeStruct((8, HEAD_DIM), full),
    )
    return pl.pallas_call(
        functools.partial(attend_back_kernel, ranks, block),
        grid=(heads, ranks),
        out_shape=results,
        in_specs=[whole(v) for v in operands],
        out_specs=tuple(whole(v) for v in results),
        scratch_shapes=[
            pltpu.VMEM((length, HEAD_DIM), full),
            pltpu.VMEM((length, HEAD_DIM), full),
            pltpu.VMEM((block, HEAD_DIM), full),
            pltpu.VMEM((block, 1), full),
            pltpu.VMEM((ranks, block, block), full),
            pltpu.VMEM((ranks, block, block), full),
        ],
        compiler_params=pltpu.CompilerParams(vmem_limit_bytes=40 << 20),
        cost_estimate=pl.CostEstimate(
            flops=10 * heads * length * length * HEAD_DIM * 9 // 16,
            bytes_accessed=16 * length * HEAD_DIM * (heads + 2),
            transcendentals=heads * length * length,
        ),
    )(*operands)


def weight_grad_kernel(count, half_tiles, *refs):
    lefts, right_ref = refs[:count], refs[count]
    out_ref = refs[-1] if len(refs) == count + 2 else refs[-2]
    pieces = [ref[...] for ref in lefts]
    if half_tiles:
        pieces[-2:] = [jnp.where(pl.program_id(0) < half_tiles, pieces[-2], pieces[-1])]
    result, start = None, 0
    for piece in pieces:
        part = mm_tn(piece, right_ref[start : start + piece.shape[0], :])
        result = part if result is None else result + part
        start += piece.shape[0]
    if len(refs) > count + 2:
        map_ref, gain_ref, late_ref = refs[count + 1 : count + 4]
        maps = map_ref[:, : result.shape[1]].astype(full)
        of_gain = jnp.sum(maps * result, -1, keepdims=True) / gain_ref[...]
        late = late_ref[...]
        lane = lax.broadcasted_iota(jnp.int32, late.shape, 1)
        split = result.shape[1] - 2 * HEAD_DIM
        refs[-1][...] = result[:, split:].astype(low).reshape(refs[-1].shape)
        result = jnp.concatenate([result[:, :split], jnp.where(lane == 0, of_gain, late)], 1)
    out_ref[...] = result.astype(low).reshape(out_ref.shape)


def weight_grad(ranks, parts, lefts, right, *extras):
    width = lefts[0].shape[1]
    length, columns = right.shape
    rows = width // (ranks * parts)
    tile = max(min(256, rows * parts), rows)
    each = tile // rows
    wides = [columns + 128 - 2 * HEAD_DIM, 2 * HEAD_DIM] if extras else [columns]
    half_tiles = lefts[-1].shape[1] // tile if lefts[-1].shape[1] < width else 0

    def place(i):
        return (((i * each) % parts) // each, (i * each) // parts, 0, 0)

    left_specs = [pl.BlockSpec((v.shape[0], tile), lambda i: (0, i)) for v in lefts]
    if half_tiles:
        left_specs[-2:] = [
            pl.BlockSpec((lefts[-1].shape[0], tile), lambda i: (0, jnp.minimum(i, half_tiles - 1))),
            pl.BlockSpec((lefts[-1].shape[0], tile), lambda i: (0, jnp.maximum(i - half_tiles, 0))),
        ]
    results = pl.pallas_call(
        functools.partial(weight_grad_kernel, len(lefts), half_tiles),
        grid=(width // tile,),
        out_shape=tuple(jax.ShapeDtypeStruct((parts, ranks, rows, n), low) for n in wides),
        in_specs=left_specs
        + [pl.BlockSpec((length, columns), lambda i: (0, 0))]
        + [pl.BlockSpec((tile, v.shape[1]), lambda i: (i, 0)) for v in extras],
        out_specs=tuple(pl.BlockSpec((each, 1, rows, n), place) for n in wides),
        compiler_params=pltpu.CompilerParams(vmem_limit_bytes=60 << 20),
        cost_estimate=pl.CostEstimate(
            flops=2 * length * width * columns,
            bytes_accessed=2 * (length * (width + columns) + width * columns),
            transcendentals=0,
        ),
    )(*lefts, right, *extras)
    return results if extras else results[0]


def middle_kernel(
    pairs,
    block,
    parts,
    rows_own,
    rows_x_in,
    rows_y_in,
    rows_left_in,
    rows_right_in,
    in_maps_ref,
    shard_ref,
    mixed_ref,
    gain_ref,
    ple_gate_ref,
    ple_proj_ref,
    ple_input_ref,
    cotangent_ref,
    rows_out_ref,
    grad_map_ref,
    map_ref,
    gate_part_ref,
    up_part_ref,
    out_ref,
    second_ref,
    grad_second_ref,
    grad_ple_ref,
    ple_mixed_ref,
    grad_gate_ref,
    gain_out_ref,
    rows_ref,
    in_tiles,
    wide_stage,
    hidden_ref,
    maps,
    product_ref,
    own,
    keep,
    send,
    got,
    relay,
    far,
    stage,
    load_sem,
    tile_sem,
    wide_sem,
    stage_sem,
    map_sem,
    right_s,
    right_r,
    left_s,
    left_r,
    core_s,
    core_r,
    near_s,
    near_r,
    far_s,
    far_r,
    gx_s,
    gx_r,
    gy_s,
    gy_r,
    fx_s,
    fx_r,
    fy_s,
    fy_r,
):
    rank = lax.axis_index("seq")
    fsdp_index = lax.axis_index("fsdp")
    pair, core = fsdp_index // 2, fsdp_index % 2
    sibling = (rank, pair * 2 + 1 - core)
    rank_x, rank_y = flip(rank, 1, 4), flip(rank, 2, 4)
    by_x, by_y = (rank_x, fsdp_index), (rank_y, fsdp_index)
    size = block // parts
    width, span = in_maps_ref.shape[1], in_maps_ref.shape[2]
    half = width // 2
    tile = 256
    tiles = span // tile
    shard = shard_ref.shape[1]
    shard_ref = shard_ref.at[2]
    cut = shard // 2
    left, right = slice(0, half), slice(half, width)
    up = lambda v: v.astype(full)

    def remote(source, target, send_sem, recv_sem, device):
        return pltpu.make_async_remote_copy(
            src_ref=source,
            dst_ref=target,
            send_sem=send_sem,
            recv_sem=recv_sem,
            device_id=device,
            device_id_type=MESH,
        )

    def columns_of(i):
        return pl.ds(pl.multiple_of(i * tile, tile), tile)

    loads = [
        pltpu.make_async_copy(source, target, load_sem.at[i])
        for i, (source, target) in enumerate(
            (
                (rows_own, rows_ref.at[0]),
                (rows_x_in, rows_ref.at[1]),
                (rows_y_in, rows_ref.at[2]),
                (rows_left_in, rows_ref.at[3, :, left]),
                (rows_right_in, rows_ref.at[3, :, right]),
                (shard_ref, maps.at[pair, core]),
            )
        )
    ]

    def tile_copy(i, slot):
        return pltpu.make_async_copy(
            in_maps_ref.at[:, :, columns_of(i)], in_tiles.at[slot], tile_sem.at[slot]
        )

    for copy in loads:
        copy.start()
    tile_copy(0, 0).start()

    barrier = pltpu.get_barrier_semaphore()
    devices = [by_x, by_y, sibling]
    devices += [(rank, ((pair + i) % pairs) * 2 + core) for i in range(1, pairs)]
    for device in devices:
        pl.semaphore_signal(barrier, inc=1, device_id=device, device_id_type=MESH)
    pl.semaphore_wait(barrier, len(devices))

    def piece(at, k):
        return maps.at[at, core, pl.ds(k * cut, cut), :]

    def source_of(at, k, t):
        return shard_ref.at[pl.ds(k * cut, cut), :] if t == 0 else piece(at, k)

    def pass_right(t, k):
        at, slot = pair - (t - 1), (t - 1) * 2 + k
        return remote(
            source_of(at, k, t - 1),
            piece(at, k),
            right_s.at[slot],
            right_r.at[slot],
            (rank, fsdp_index + 2),
        )

    def pass_left(t, k):
        at, slot = pair + (t - 1), (t - 1) * 2 + k
        return remote(
            source_of(at, k, t - 1),
            piece(at, k),
            left_s.at[slot],
            left_r.at[slot],
            (rank, fsdp_index - 2),
        )

    def to_sibling(at, k, own_shard=False):
        slot = at * 2 + k
        return remote(
            source_of(at, k, 0 if own_shard else 1),
            piece(at, k),
            core_s.at[slot],
            core_r.at[slot],
            sibling,
        )

    sends_right = lambda t: (pair - (t - 1) >= 0) & (pair + 1 < pairs)
    sends_left = lambda t: (pair + (t - 1) < pairs) & (pair - 1 >= 0)
    for k in range(2):
        pl.when(sends_right(1))(lambda k=k: pass_right(1, k).start())
        pl.when(sends_left(1))(lambda k=k: pass_left(1, k).start())
        to_sibling(pair, k, True).start()

    def chain_step(t, k):
        slot = (t - 1) * 2 + k

        def from_left():
            target = piece(pair - t, k)
            remote(target, target, right_s.at[slot], right_r.at[slot], sibling).wait_recv()
            if t + 1 < pairs:
                pl.when(pair + 1 < pairs)(lambda: pass_right(t + 1, k).start())
            to_sibling(pair - t, k).start()

        def from_right():
            target = piece(pair + t, k)
            remote(target, target, left_s.at[slot], left_r.at[slot], sibling).wait_recv()
            if t + 1 < pairs:
                pl.when(pair - 1 >= 0)(lambda: pass_left(t + 1, k).start())
            to_sibling(pair + t, k).start()

        pl.when(pair - t >= 0)(from_left)
        pl.when(pair + t < pairs)(from_right)

    for copy in loads:
        copy.wait()

    def wide_copies(i, slot):
        return [
            pltpu.make_async_copy(
                wide_stage.at[slot, n], target.at[:, columns_of(i)], wide_sem.at[slot, n]
            )
            for n, target in enumerate((gate_part_ref, up_part_ref))
        ]

    slope, cubic = math.sqrt(2.0 / math.pi), 0.044715

    def gate_up_tile(i, carry):
        slot = i % 2
        tile_copy(i, slot).wait()
        pl.when(i + 1 < tiles)(lambda: tile_copy(i + 1, 1 - slot).start())

        @pl.when(i >= 2)
        def _():
            for copy in wide_copies(i - 2, slot):
                copy.wait()

        v = rows_ref[...].reshape(4 * block, width)
        gate = mm(v, in_tiles[slot, 0])
        wide_stage[slot, 0] = gate
        upper = mm(v, in_tiles[slot, 1])
        wide_stage[slot, 1] = upper
        bend = jnp.tanh(slope * (gate + cubic * gate * gate * gate))
        hidden_ref[:, columns_of(i)] = (0.5 * gate * (1.0 + bend) * upper).astype(low)
        for copy in wide_copies(i, slot):
            copy.start()
        return carry

    steps = [(t, k) for t in range(1, pairs) for k in range(2)]
    early = min(len(steps), 4)
    at_tile = [tiles * (n + 1) // early for n in range(early)]
    done = 0
    for n in range(early):
        lax.fori_loop(done, at_tile[n], gate_up_tile, 0)
        done = at_tile[n]
        chain_step(*steps[n])
    for i in (tiles - 2, tiles - 1):
        for copy in wide_copies(i, i % 2):
            copy.wait()

    def chip_of(j):
        orders = [sorted(range(pairs), key=lambda p: (abs(p - z), p)) for z in range(pairs)]
        return sum(jnp.where(pair == z, orders[z][j], 0) for z in range(pairs))

    def shard_of(j):
        chip = chip_of(j // 2)
        at_core = core if j % 2 == 0 else 1 - core
        return chip, at_core, chip * 2 + at_core, 1 - chip // (pairs // 2)

    def near_copy(j):
        chip, at_core, place, is_left = shard_of(j)
        to = rank_x * is_left + rank_y * (1 - is_left)
        return remote(
            send.at[place], got.at[place], near_s.at[place], near_r.at[place], (to, fsdp_index)
        )

    def far_copy(j):
        chip, at_core, place, is_left = shard_of(j)
        to = rank_y * is_left + rank_x * (1 - is_left)
        return remote(
            relay.at[place], far.at[place], far_s.at[place], far_r.at[place], (to, fsdp_index)
        )

    def product(j):
        chip, at_core, place, is_left = shard_of(j)
        if j % 2:
            for k in range(2):
                target = maps.at[chip, at_core, pl.ds(k * cut, cut), :]
                remote(
                    target, target, core_s.at[0], core_r.at[chip * 2 + k], sibling
                ).wait_recv()
        v = mm_nt(hidden_ref[...], maps[chip, at_core])
        product_ref[...] = v.reshape(4, block, shard)
        near = 2 - is_left
        own[:, columns_of(place)] = product_ref[0]
        send[place, 0] = product_ref[3].astype(low)
        send[place, 1] = product_ref[near].astype(low)
        keep[place] = product_ref[3 - near]
        near_copy(j).start()

    def pass_on(j):
        place = shard_of(j)[2]
        near_copy(j).wait_recv()
        relay[place] = (keep[place] + up(got[place, 0])).astype(low)
        far_copy(j).start()

    def collect(j):
        place = shard_of(j)[2]
        far_copy(j).wait_recv()
        columns = columns_of(place)
        own[:, columns] += up(got[place, 1]) + up(far[place])

    count = 2 * pairs
    rest = steps[early:]
    for j in range(count):
        need = j // 2
        while rest and rest[0][0] <= need:
            chain_step(*rest.pop(0))
        product(j)
        if j >= 2:
            pass_on(j - 2)
        if j >= 4:
            collect(j - 4)
    for j in (count - 2, count - 1):
        pass_on(j)
    for j in range(count - 4, count):
        collect(j)

    def map_copy(i):
        return pltpu.make_async_copy(
            maps.at[i // 2, i % 2], map_ref.at[pl.ds(i * shard, shard), :], map_sem.at[i]
        )

    for i in range(count):
        map_copy(i).start()
    sent = []

    def go(copy):
        copy.start()
        sent.append(copy)
        return copy

    def rows_of(u):
        return pl.ds(u * size, size)

    gain_out_ref[...] = jnp.zeros_like(gain_out_ref)
    ffn_gain, ple_gain = gain_ref[0:1, :], gain_ref[1:2, :]
    mean = lambda v: jnp.mean(v, -1, keepdims=True)
    total = lambda v: jnp.sum(v, 0, keepdims=True)
    rows_x, rows_y = [], []
    for u in range(parts):
        at = rows_of(u)
        f = own[at, :]
        f_inverse = lax.rsqrt(mean(f * f) + eps)
        second = (mixed_ref[at, :] + f * f_inverse * ffn_gain).astype(low)
        second_ref[at, :] = second
        gate = mm(second, ple_gate_ref[...])
        bend = jnp.tanh(slope * (gate + cubic * gate * gate * gate))
        gate_slope = 0.5 * (1.0 + bend) + 0.5 * gate * (1.0 - bend * bend) * slope * (
            1.0 + 3.0 * cubic * gate * gate
        )
        given = up(ple_input_ref[at, :])
        ple_mixed = (0.5 * gate * (1.0 + bend) * given).astype(low)
        ple_mixed_ref[at, :] = ple_mixed
        proj = mm_nt(ple_mixed, ple_proj_ref[...])
        proj_inverse = lax.rsqrt(mean(proj * proj) + eps)
        out_ref[at, :] = (up(second) + proj * proj_inverse * ple_gain).astype(low)
        incoming = up(cotangent_ref[at, :])
        gain_out_ref[1:2, :] += total(incoming * proj * proj_inverse)
        scaled = incoming * ple_gain
        grad_proj = proj_inverse * (
            scaled - proj * (proj_inverse * proj_inverse * mean(scaled * proj))
        )
        grad_ple = grad_proj.astype(low)
        grad_ple_ref[at, :] = grad_ple
        grad_gate = (mm(grad_ple, ple_proj_ref[...]) * given * gate_slope).astype(low)
        grad_gate_ref[at, :] = grad_gate
        grad_second = incoming + mm_nt(grad_gate, ple_gate_ref[...])
        grad_second_ref[at, :] = grad_second
        f = own[at, :]
        gain_out_ref[0:1, :] += total(grad_second * f * f_inverse)
        scaled = grad_second * ffn_gain
        grad_f = f_inverse * (scaled - f * (f_inverse * f_inverse * mean(scaled * f)))
        rows_ref[0, at, :] = grad_f.astype(low)
        pair_x, pair_y = [], []
        for order in range(2):
            for copies, device, send_sem, recv_sem, index, part in (
                (pair_x, by_x, gx_s, gx_r, 1, (left, right)[order]),
                (pair_y, by_y, gy_s, gy_r, 2, (right, left)[order]),
            ):
                copies.append(
                    go(
                        remote(
                            rows_ref.at[0, at, part],
                            rows_ref.at[index, at, part],
                            send_sem.at[u, order],
                            recv_sem.at[u, order],
                            device,
                        )
                    )
                )
        rows_x.append(pair_x)
        rows_y.append(pair_y)

    forwards = []
    for u in range(parts):
        at = rows_of(u)
        rows_x[u][0].wait_recv()
        forwards.append(
            go(
                remote(
                    rows_ref.at[1, at, left],
                    rows_ref.at[3, at, left],
                    fy_s.at[u],
                    fy_r.at[u],
                    by_y,
                )
            )
        )
        rows_y[u][0].wait_recv()
        forwards.append(
            go(
                remote(
                    rows_ref.at[2, at, right],
                    rows_ref.at[3, at, right],
                    fx_s.at[u],
                    fx_r.at[u],
                    by_x,
                )
            )
        )
    for u in range(parts):
        rows_x[u][1].wait_recv()
        rows_y[u][1].wait_recv()
    for copy in forwards:
        copy.wait_recv()

    def stage_copy(i, slot):
        at = pl.ds(pl.multiple_of(i * tile, tile), tile)
        return pltpu.make_async_copy(stage.at[slot], grad_map_ref.at[at, :], stage_sem.at[slot])

    rows_copy = pltpu.make_async_copy(rows_ref, rows_out_ref, load_sem.at[0])
    rows_copy.start()

    def grad_tile(i, carry):
        slot = i % 2

        @pl.when(i >= 2)
        def _():
            stage_copy(i - 2, slot).wait()

        columns = pl.ds(pl.multiple_of(i * tile, tile), tile)
        v = rows_ref[:, :, columns].reshape(4 * block, tile)
        for j in range(0, span, span // 2):
            stage[slot, :, j : j + span // 2] = mm_tn(v, hidden_ref[:, j : j + span // 2]).astype(low)
        stage_copy(i, slot).start()
        return carry

    lax.fori_loop(0, count, grad_tile, 0)
    stage_copy(count - 2, 0).wait()
    stage_copy(count - 1, 1).wait()
    for copy in sent:
        copy.wait_send()
    rows_copy.wait()
    for i in range(count):
        map_copy(i).wait()
    for j in range(count):
        near_copy(j).wait_send()
        far_copy(j).wait_send()
    for k in range(2):
        to_sibling(pair, k, True).wait_send()
        for t in range(1, pairs):
            pl.when(pair - t >= 0)(lambda t=t, k=k: to_sibling(pair - t, k).wait_send())
            pl.when(pair + t < pairs)(lambda t=t, k=k: to_sibling(pair + t, k).wait_send())
            pl.when(sends_right(t))(lambda t=t, k=k: pass_right(t, k).wait_send())
            pl.when(sends_left(t))(lambda t=t, k=k: pass_left(t, k).wait_send())


def middle(pairs, h_blocks, in_maps, planes, mixed, gains, ple, ple_input, cotangent):
    block, width = mixed.shape
    span = in_maps.shape[2]
    shard = planes.shape[1]
    parts, length = 2, 4 * block
    count = 2 * pairs
    dma = lambda *n: pltpu.SemaphoreType.DMA(n)
    vmem = pl.BlockSpec(memory_space=pltpu.VMEM)
    anywhere = pl.BlockSpec(memory_space=pl.ANY)
    shapes = (
        ((4, block, width), low),
        ((width, span), low),
        ((width, span), low),
        ((length, span), full),
        ((length, span), full),
        ((block, width), low),
        ((block, width), low),
        ((block, width), full),
        ((block, width), low),
        ((block, PLE), low),
        ((block, PLE), low),
        ((8, width), full),
    )
    return pl.pallas_call(
        functools.partial(middle_kernel, pairs, block, parts),
        out_shape=tuple(jax.ShapeDtypeStruct(*v) for v in shapes),
        in_specs=[anywhere] * 7 + [vmem] * 6,
        out_specs=tuple(anywhere if i < 5 else vmem for i in range(len(shapes))),
        scratch_shapes=[
            pltpu.VMEM((4, block, width), low),
            pltpu.VMEM((2, 2, width, 256), low),
            pltpu.VMEM((2, 2, length, 256), full),
            pltpu.VMEM((length, span), low),
            pltpu.VMEM((pairs, 2, shard, span), low),
            pltpu.VMEM((4, block, shard), full),
            pltpu.VMEM((block, width), full),
            pltpu.VMEM((count, block, shard), full),
            pltpu.VMEM((count, 2, block, shard), low),
            pltpu.VMEM((count, 2, block, shard), low),
            pltpu.VMEM((count, block, shard), low),
            pltpu.VMEM((count, block, shard), low),
            pltpu.VMEM((2, 256, span), low),
            dma(6),
            dma(2),
            dma(2, 2),
            dma(2),
            dma(count),
            *[dma(2 * (pairs - 1))] * 4,
            *[dma(count)] * 2,
            *[dma(count)] * 4,
            *[dma(parts, 2)] * 4,
            *[dma(parts)] * 4,
        ],
        compiler_params=pltpu.CompilerParams(
            collective_id=1, has_side_effects=True, vmem_limit_bytes=62 << 20
        ),
        cost_estimate=pl.CostEstimate(
            flops=16 * block * width * span, bytes_accessed=100 << 20, transcendentals=0
        ),
    )(
        *h_blocks,
        in_maps,
        planes,
        mixed,
        jnp.pad(jnp.stack(gains), ((0, 6), (0, 0))),
        ple[:, :PLE],
        ple[:, PLE:],
        ple_input,
        cotangent,
    )


def middle_plain(ranks, h_blocks, in_maps, planes, mixed, gains, ple, ple_input, cotangent):
    block = mixed.shape[0]
    down_map = lax.all_gather(planes[2], "fsdp", axis=0, tiled=True)
    gate_up = dot(whole_rows(h_blocks), in_maps, ((1,), (1,)))
    gate_part, up_part = gate_up[:, 0], gate_up[:, 1]
    hidden = (gelu_tanh(gate_part) * up_part).astype(low)
    parts = mm_nt(hidden, down_map).astype(low)
    ffn_out = sum_seq([parts[k * block : (k + 1) * block] for k in range(ranks)], ranks)
    ffn_normed, ffn_inverse = norm_rows(ffn_out, gains[0])
    h_second = (mixed + ffn_normed).astype(low)
    ple_gate = mm(h_second, ple[:, :PLE])
    ple_input = ple_input.astype(full)
    ple_mixed = (gelu_tanh(ple_gate) * ple_input).astype(low)
    ple_proj = mm_nt(ple_mixed, ple[:, PLE:])
    ple_normed, ple_inverse = norm_rows(ple_proj, gains[1])
    hidden_out = (h_second.astype(full) + ple_normed).astype(low)
    grad_out = cotangent.astype(full)
    grad_ple_proj, gain_grad_five = norm_back(ple_proj, ple_inverse, gains[1], grad_out)
    grad_ple_low = grad_ple_proj.astype(low)
    grad_ple_mixed = mm(grad_ple_low, ple[:, PLE:])
    unused_gelu, gelu_pull = jax.vjp(gelu_tanh, ple_gate)
    grad_ple_gate = gelu_pull(grad_ple_mixed * ple_input)[0].astype(low)
    grad_second = grad_out + mm_nt(grad_ple_gate, ple[:, :PLE])
    grad_ffn, gain_grad_four = norm_back(ffn_out, ffn_inverse, gains[0], grad_second)
    rows = whole_rows(gather_seq(grad_ffn.astype(low), ranks))
    return (
        rows,
        mm_tn(rows, hidden).astype(low),
        down_map,
        gate_part,
        up_part,
        hidden_out,
        h_second,
        grad_second,
        grad_ple_low,
        ple_mixed,
        grad_ple_gate,
        jnp.stack([gain_grad_four, gain_grad_five]),
    )


def back_kernel(
    block,
    gate_ref,
    up_ref,
    maps_ref,
    rows_own,
    rows_x,
    rows_y,
    rows_left,
    rows_right,
    grad_maps_ref,
    sum_ref,
    maps,
    keep_left,
    keep_right,
    send_x,
    send_y,
    got_x,
    got_y,
    relay_x,
    relay_y,
    far_x,
    far_y,
    stage,
    map_sem,
    stage_sem,
    sx_s,
    sx_r,
    sy_s,
    sy_r,
    rx_s,
    rx_r,
    ry_s,
    ry_r,
):
    rank = lax.axis_index("seq")
    fsdp_index = lax.axis_index("fsdp")
    by_x, by_y = (flip(rank, 1, 4), fsdp_index), (flip(rank, 2, 4), fsdp_index)
    width, span = maps_ref.shape[1], maps_ref.shape[2]
    tile = 256
    tiles = width // tile
    each = tiles // 2
    up = lambda v: v.astype(full)

    def columns_of(i):
        return pl.ds(pl.multiple_of(i * tile, tile), tile)

    def remote(source, target, send, recv, device):
        return pltpu.make_async_remote_copy(
            src_ref=source,
            dst_ref=target,
            send_sem=send,
            recv_sem=recv,
            device_id=device,
            device_id_type=MESH,
        )

    def map_copy(i):
        return pltpu.make_async_copy(
            maps_ref.at[:, columns_of(i), :], maps.at[:, columns_of(i), :], map_sem.at[i]
        )

    def near_x(j):
        return remote(send_x.at[j], got_x.at[j], sx_s.at[j], sx_r.at[j], by_x)

    def near_y(j):
        return remote(send_y.at[j], got_y.at[j], sy_s.at[j], sy_r.at[j], by_y)

    def last_x(j):
        return remote(relay_x.at[j], far_x.at[j], rx_s.at[j], rx_r.at[j], by_x)

    def last_y(j):
        return remote(relay_y.at[j], far_y.at[j], ry_s.at[j], ry_r.at[j], by_y)

    for j in range(each):
        map_copy(j).start()
        map_copy(j + each).start()

    barrier = pltpu.get_barrier_semaphore()
    for device in (by_x, by_y):
        pl.semaphore_signal(barrier, inc=1, device_id=device, device_id_type=MESH)
    pl.semaphore_wait(barrier, 2)

    def product(i):
        map_copy(i).wait()
        v = mm_nt(gate_ref[...], maps[0, columns_of(i), :])
        v = v + mm_nt(up_ref[...], maps[1, columns_of(i), :])
        return v.reshape(4, block, tile)

    def send_tiles(j, carry):
        v = product(j)
        sum_ref[:, columns_of(j)] = v[0]
        keep_left[j] = v[2]
        send_x[j, 0] = v[3].astype(low)
        send_x[j, 1] = v[1].astype(low)
        near_x(j).start()
        v = product(j + each)
        sum_ref[:, columns_of(j + each)] = v[0]
        keep_right[j] = v[1]
        send_y[j, 0] = v[3].astype(low)
        send_y[j, 1] = v[2].astype(low)
        near_y(j).start()
        return carry

    lax.fori_loop(0, each, send_tiles, 0)

    def stage_copy(i, slot):
        return pltpu.make_async_copy(
            stage.at[slot], grad_maps_ref.at[:, columns_of(i), :], stage_sem.at[slot]
        )

    def grad_tile(i, j, far_ref):
        slot = j % 2
        pl.when(i >= 2)(lambda: stage_copy(i - 2, slot).wait())
        near = columns_of(i)
        v = jnp.concatenate(
            [rows_own[:, near], rows_x[:, near], rows_y[:, near], far_ref[:, columns_of(j)]], 0
        )
        for k in range(0, span, span // 2):
            part = slice(k, k + span // 2)
            stage[slot, 0, :, part] = mm_tn(v, gate_ref[:, part]).astype(low)
            stage[slot, 1, :, part] = mm_tn(v, up_ref[:, part]).astype(low)
        stage_copy(i, slot).start()

    def left_tile(j, carry):
        grad_tile(j, j, rows_left)
        near_x(j).wait_recv()
        relay_y[j] = (keep_left[j] + up(got_x[j, 0])).astype(low)
        last_y(j).start()
        near_y(j).wait_recv()
        relay_x[j] = (keep_right[j] + up(got_y[j, 0])).astype(low)
        last_x(j).start()
        return carry

    def right_tile(j, carry):
        grad_tile(j + each, j, rows_right)
        last_y(j).wait_recv()
        sum_ref[:, columns_of(j)] += up(got_x[j, 1]) + up(far_y[j])
        last_x(j).wait_recv()
        sum_ref[:, columns_of(j + each)] += up(got_y[j, 1]) + up(far_x[j])
        return carry

    lax.fori_loop(0, each, left_tile, 0)
    lax.fori_loop(0, each, right_tile, 0)
    stage_copy(tiles - 2, 0).wait()
    stage_copy(tiles - 1, 1).wait()

    def sent(j, carry):
        for copy in (near_x(j), near_y(j), last_x(j), last_y(j)):
            copy.wait_send()
        return carry

    lax.fori_loop(0, each, sent, 0)


def back(grad_gate, grad_up, in_maps, h_blocks):
    length, span = grad_gate.shape
    block, width = h_blocks[0].shape
    each = width // 512
    dma = pltpu.SemaphoreType.DMA
    vmem = pl.BlockSpec(memory_space=pltpu.VMEM)
    anywhere = pl.BlockSpec(memory_space=pl.ANY)
    keep = pltpu.VMEM((each, block, 256), full)
    pieces = pltpu.VMEM((each, 2, block, 256), low)
    singles = pltpu.VMEM((each, block, 256), low)
    return pl.pallas_call(
        functools.partial(back_kernel, block),
        out_shape=(
            jax.ShapeDtypeStruct((2, width, span), low),
            jax.ShapeDtypeStruct((block, width), full),
        ),
        in_specs=[vmem, vmem, anywhere] + [vmem] * 5,
        out_specs=(anywhere, vmem),
        scratch_shapes=[
            pltpu.VMEM((2, width, span), low),
            keep,
            keep,
            *[pieces] * 4,
            *[singles] * 4,
            pltpu.VMEM((2, 2, 256, span), low),
            dma((width // 256,)),
            dma((2,)),
            *[dma((each,))] * 8,
        ],
        compiler_params=pltpu.CompilerParams(
            collective_id=3, has_side_effects=True, vmem_limit_bytes=58 << 20
        ),
        cost_estimate=pl.CostEstimate(
            flops=8 * length * width * span, bytes_accessed=50 << 20, transcendentals=0
        ),
    )(grad_gate, grad_up, in_maps, *h_blocks)


def finish_kernel(sizes, with_x, *refs):
    ranks, pairs = sizes["seq"], sizes["pair"]
    refs = list(refs)

    def some(count):
        head = refs[:count]
        del refs[:count]
        return head

    shared = ranks == 4
    owns = some(3 + shared)
    x_ref, branch_ref, tokens_ref, base_ref, gain_ref = some(5) if with_x else [None] * 5
    query_ref, key_ref, value_ref, out_ref, ple_ref, laurel_ref, small_ref = some(7)
    (input_ref,) = some(1) if with_x else [None]
    sums, from_left, from_right = some(3 + shared), some(3 + shared), some(3 + shared)
    got_last, got_out = some(2)
    (got_pair,) = some(1) if shared else [None]
    if with_x:
        got_x, got_y, relay_x, relay_y, far_x, far_y = some(6)
    core_s, core_r, right_s, right_r, left_s, left_r, last_s, last_r, out_s, out_r = some(10)
    if with_x:
        x_s, x_r = some(2)
    if shared:
        pair_s, pair_r = some(2)

    rank = lax.axis_index("seq")
    fsdp_index = lax.axis_index("fsdp")
    pair, core = fsdp_index // 2, fsdp_index % 2
    sibling = (rank, pair * 2 + 1 - core)
    on_seq = lambda k: (flip(rank, k, ranks), fsdp_index)
    up = lambda v: v.astype(full)

    def remote(source, target, send, recv, device):
        return pltpu.make_async_remote_copy(
            src_ref=source,
            dst_ref=target,
            send_sem=send,
            recv_sem=recv,
            device_id=device,
            device_id_type=MESH,
        )

    barrier = pltpu.get_barrier_semaphore()
    devices = [on_seq(k) for k in range(1, ranks)]
    devices += [(rank, ((pair + i) % pairs) * 2 + core) for i in range(1, pairs)]
    for device in devices + [sibling]:
        pl.semaphore_signal(barrier, inc=1, device_id=device, device_id_type=MESH)
    pl.semaphore_wait(barrier, len(devices) + 1)

    sent = []

    def go(copy):
        copy.start()
        sent.append(copy)
        return copy

    half_ranks = ranks // 2
    pieces = [
        (1, slice(0, ranks)),
        (2, None),
        (0, slice(0, half_ranks)),
        (0, slice(half_ranks, ranks)),
    ] + [(3, None)] * shared
    count = len(pieces)

    def view(group, lead, piece):
        number, rows = pieces[piece]
        ref = group[number]
        return ref.at[lead] if rows is None else ref.at[lead, rows]

    order = [i // 2 if i % 2 else pairs - 1 - i // 2 for i in range(pairs)]

    def swap(chip, piece):
        slot = chip * count + piece
        return remote(
            view(owns, chip * 2 + 1 - core, piece),
            view(sums, chip, piece),
            core_s.at[slot],
            core_r.at[slot],
            sibling,
        )

    for chip in order:
        for piece in range(count):
            go(swap(chip, piece))
    if with_x:
        half = x_ref.shape[2] // 2
        left, right = slice(0, half), slice(half, 2 * half)
        by_x, by_y = on_seq(1), on_seq(2)
        near = []
        for slot, block, columns, target, device in (
            (0, 3, left, got_x.at[0], by_x),
            (1, 3, right, got_y.at[0], by_y),
            (2, 1, left, got_x.at[1], by_x),
            (3, 2, right, got_y.at[1], by_y),
        ):
            near.append(
                go(remote(x_ref.at[block, :, columns], target, x_s.at[slot], x_r.at[slot], device))
            )

    def whole_chip(chip, piece):
        target = view(sums, chip, piece)
        remote(
            target, target, core_s.at[0], core_r.at[chip * count + piece], sibling
        ).wait_recv()
        target[...] = (up(target[...]) + up(view(owns, chip * 2 + core, piece)[...])).astype(low)

    def pass_right(t, piece):
        slot = (t - 1) * count + piece
        return remote(
            view(sums, pair + pairs - t, piece),
            view(from_left, t - 1, piece),
            right_s.at[slot],
            right_r.at[slot],
            (rank, fsdp_index + 2),
        )

    def pass_left(t, piece):
        slot = (t - 1) * count + piece
        return remote(
            view(sums, pair - (pairs - t), piece),
            view(from_right, t - 1, piece),
            left_s.at[slot],
            left_r.at[slot],
            (rank, fsdp_index - 2),
        )

    def add_left(t, piece, target):
        got = view(from_left, t - 1, piece)
        slot = (t - 1) * count + piece
        remote(got, got, right_s.at[slot], right_r.at[slot], sibling).wait_recv()
        target[...] = (up(target[...]) + up(got[...])).astype(low)

    def add_right(t, piece, target):
        got = view(from_right, t - 1, piece)
        slot = (t - 1) * count + piece
        remote(got, got, left_s.at[slot], left_r.at[slot], sibling).wait_recv()
        target[...] = (up(target[...]) + up(got[...])).astype(low)

    mirrored = pairs - 1 - pair
    relays = []
    for t in range(1, pairs):
        for piece in range(count):

            def to_right(t=t, piece=piece):
                chip = pair + pairs - t
                whole_chip(chip, piece)
                if t > 1:
                    pl.when(pair > 0)(lambda: add_left(t - 1, piece, view(sums, chip, piece)))
                pass_right(t, piece).start()

            def to_left(t=t, piece=piece):
                chip = pair - (pairs - t)
                whole_chip(chip, piece)
                if t > 1:
                    pl.when(mirrored > 0)(lambda: add_right(t - 1, piece, view(sums, chip, piece)))
                pass_left(t, piece).start()

            pl.when(t >= pair + 1)(to_right)
            pl.when(t >= mirrored + 1)(to_left)
        if with_x and t == 1:
            near[0].wait_recv()
            relay_y[...] = (up(x_ref[2, :, left]) + up(got_x[0])).astype(low)
            relays.append(go(remote(relay_y, far_y, x_s.at[4], x_r.at[4], by_y)))
            near[1].wait_recv()
            relay_x[...] = (up(x_ref[1, :, right]) + up(got_y[0])).astype(low)
            relays.append(go(remote(relay_x, far_x, x_s.at[5], x_r.at[5], by_x)))
            for piece in range(count):
                whole_chip(pair, piece)
    if with_x:
        for copy in near[2:] + relays:
            copy.wait_recv()
        mean = lambda v: jnp.mean(v, -1, keepdims=True)
        step = x_ref.shape[1] // 2
        for i in range(2):
            at = slice(i * step, (i + 1) * step)
            incoming = branch_ref[at, :] + jnp.concatenate(
                [
                    up(x_ref[0, at, left]) + up(got_x[1, at, :]) + up(far_y[at, :]),
                    up(x_ref[0, at, right]) + up(got_y[1, at, :]) + up(far_x[at, :]),
                ],
                1,
            )
            v = up(tokens_ref[at, :])
            inverse = lax.rsqrt(mean(v * v) + eps)
            scaled = incoming * gain_ref[0:1, :]
            input_ref[at, 0, :] = base_ref[at, :] * root_half + inverse * (
                scaled - v * (inverse * inverse * mean(scaled * v))
            )
    else:
        for piece in range(count):
            whole_chip(pair, piece)

    for piece in range(count):
        target = view(sums, pair, piece)
        pl.when(pair > 0)(lambda: add_left(pairs - 1, piece, target))
        pl.when(mirrored > 0)(lambda: add_right(pairs - 1, piece, target))

    last_sum, out_sum, rest_sum = [ref.at[pair] for ref in sums[:3]]
    across = []
    for k in range(1, ranks):
        peer = flip(rank, k, ranks)
        across.append(
            (
                go(remote(last_sum.at[peer], got_last.at[k], last_s.at[k], last_r.at[k], on_seq(k))),
                go(remote(out_sum.at[peer], got_out.at[k], out_s.at[k], out_r.at[k], on_seq(k))),
            )
        )
    def put_pair(group, v):
        head = pl.ds(pl.multiple_of(group * HEAD_DIM, HEAD_DIM), HEAD_DIM)
        key_ref[:, head] = v[:, :HEAD_DIM]
        value_ref[:, head] = v[:, HEAD_DIM:]

    def pair_copy(k):
        to = flip(rank, k, ranks)
        return remote(
            sums[3].at[pair, to % 2],
            got_pair.at[rank // 2],
            pair_s.at[k],
            pair_r.at[k],
            on_seq(k),
        )

    goes = lambda k: flip(rank, k, ranks) // 2 == rank % 2
    if shared:
        for k in range(1, ranks):
            pl.when(goes(k))(lambda k=k: pair_copy(k).start())
    ple_ref[...] = up(rest_sum[:, : 2 * PLE])
    laurel_ref[...] = up(rest_sum[:, 2 * PLE : 2 * PLE + 2 * LR])
    small_ref[...] = up(rest_sum[:, 2 * PLE + 2 * LR :])
    if not shared:
        key_ref[...] = jnp.zeros_like(key_ref)
        value_ref[...] = jnp.zeros_like(value_ref)
    q_width = out_sum.shape[2]
    for k in range(ranks):
        if k:
            for copy in across[k - 1]:
                copy.wait_recv()
            last, out = up(got_last[k]), up(got_out[k])
        else:
            last, out = up(last_sum[rank]), up(out_sum[rank])
        sender = flip(rank, k, ranks)
        columns = pl.ds(pl.multiple_of(sender * q_width, q_width), q_width)
        group = sender * (QUERY_HEADS // ranks) // (QUERY_HEADS // KEY_VALUE_HEADS)
        head = pl.ds(pl.multiple_of(group * HEAD_DIM, HEAD_DIM), HEAD_DIM)
        query_ref[:, columns] = last[:, :q_width]
        out_ref[:, columns] = out
        small_ref[...] += last[:, q_width : q_width + small_ref.shape[1]]
        if not shared:
            key_ref[:, head] += last[:, -2 * HEAD_DIM : -HEAD_DIM]
            value_ref[:, head] += last[:, -HEAD_DIM:]
    if shared:
        pl.when(rank // 2 == rank % 2)(
            lambda: put_pair(rank // 2, up(sums[3][pair, rank % 2]))
        )
        for k in range(1, ranks):

            def arrived(k=k):
                sender = flip(rank, k, ranks)
                target = got_pair.at[sender // 2]
                remote(target, target, pair_s.at[k], pair_r.at[k], sibling).wait_recv()
                put_pair(sender // 2, up(got_pair[sender // 2]))

            pl.when(flip(rank, k, ranks) % 2 == rank // 2)(arrived)
        for k in range(1, ranks):
            pl.when(goes(k))(lambda k=k: pair_copy(k).wait_send())

    for t in range(1, pairs):
        for piece in range(count):
            pl.when(t >= pair + 1)(lambda t=t, piece=piece: pass_right(t, piece).wait_send())
            pl.when(t >= mirrored + 1)(lambda t=t, piece=piece: pass_left(t, piece).wait_send())
    for copy in sent:
        copy.wait_send()


def finish(sizes, last, out, rest, key_value, x=None):
    ranks, pairs = sizes["seq"], sizes["pair"]
    rows = last.shape[2]
    shared = ranks == 4
    if shared:
        arrays = [last, out, rest, key_value]
    else:
        arrays = [jnp.concatenate([last, key_value], 3), out, rest]
    vmem = pl.BlockSpec(memory_space=pltpu.VMEM)
    dma = lambda n: pltpu.SemaphoreType.DMA((n,))
    width = KEY_VALUE_HEADS * HEAD_DIM
    shapes = [
        (rows, QUERY_HEADS * HEAD_DIM),
        (rows, width),
        (rows, width),
        (rows, QUERY_HEADS * HEAD_DIM),
        (rows, 2 * PLE),
        (rows, 2 * LR),
        (rows, rest.shape[-1] - 2 * PLE - 2 * LR),
    ]
    scratch = [pltpu.VMEM((pairs,) + v.shape[1:], low) for v in arrays]
    scratch += [pltpu.VMEM((pairs - 1,) + v.shape[1:], low) for v in arrays] * 2
    scratch += [pltpu.VMEM((ranks,) + v.shape[2:], low) for v in arrays[:2]]
    if shared:
        scratch.append(pltpu.VMEM((KEY_VALUE_HEADS,) + key_value.shape[2:], low))
    if x is not None:
        block, columns = x[0].shape[1], x[0].shape[2] // 2
        shapes.append((block, 1, 2 * columns))
        scratch += [pltpu.VMEM((2, block, columns), low)] * 2
        scratch += [pltpu.VMEM((block, columns), low)] * 4
    count = 4 + shared
    scratch += [dma(count * pairs)] * 2 + [dma(count * (pairs - 1))] * 4 + [dma(ranks)] * 4
    if x is not None:
        scratch += [dma(6)] * 2
    if shared:
        scratch += [dma(ranks)] * 2
    operands = arrays + list(x or ())
    return pl.pallas_call(
        functools.partial(finish_kernel, sizes, x is not None),
        out_shape=tuple(jax.ShapeDtypeStruct(v, full) for v in shapes),
        in_specs=[vmem] * len(operands),
        out_specs=(vmem,) * len(shapes),
        scratch_shapes=scratch,
        compiler_params=pltpu.CompilerParams(
            collective_id=2, has_side_effects=True, vmem_limit_bytes=56 << 20
        ),
    )(*operands)


def body(
    sizes,
    hidden_in,
    per_layer_input,
    segment_ids,
    positions,
    out_cotangent,
    w_query,
    key_matrix,
    value_matrix,
    w_out_t,
    laurel_maps,
    per_layer_maps,
    norm_gains,
    head_gains,
    w_mlp,
):
    ranks, pairs = sizes["seq"], sizes["pair"]
    block, _, width = hidden_in.shape
    rows = w_query.shape[0]
    q_width = QUERY_HEADS // ranks * HEAD_DIM
    share = QUERY_HEADS // KEY_VALUE_HEADS
    kv_of = [rank * (QUERY_HEADS // ranks) // share for rank in range(ranks)]
    length = block * ranks
    rank = lax.axis_index("seq")
    relative = [rank ^ k for k in range(ranks)]
    cut = lambda v: [v[k * block : (k + 1) * block] for k in range(ranks)]

    by_rank = lambda m: m.reshape(rows, ranks, q_width).transpose(1, 0, 2)
    by_kv = lambda m: jnp.stack([m[:, j * HEAD_DIM : (j + 1) * HEAD_DIM] for j in kv_of])
    head_pack = jnp.concatenate(
        [by_rank(w_query), by_kv(key_matrix), by_kv(value_matrix), by_rank(w_out_t)], 2
    )
    head_rows = head_gains.shape[0]
    small = jnp.concatenate(
        [norm_gains, jnp.pad(head_gains, ((0, rows - head_rows), (0, 0)))], 1
    )
    small = jnp.pad(small, ((0, 0), (0, 128 - small.shape[1])))
    rest_pack = jnp.concatenate([laurel_maps, small], 1)
    marks = jnp.pad(jnp.concatenate([segment_ids.T, positions.T], 0), ((0, 6), (0, 0)))
    x_local = hidden_in.reshape(block, width)

    planes = jnp.moveaxis(w_mlp, 1, 0)
    head_all, rest_all, marks_all, x_all, in_rows = gather_weights(
        sizes, head_pack, rest_pack, marks, x_local, planes
    )
    in_maps = lax.all_gather(in_rows, "fsdp", axis=1, tiled=True)
    x_all = x_all.reshape(length, width)
    head_all = head_all.reshape(width, -1)
    rest_all = rest_all.reshape(width, -1)
    qkv_map, out_map = head_all[:, :-q_width], head_all[:, -q_width:]
    laurel = rest_all[:, : 2 * LR]
    gains = rest_all[:, 2 * LR :].astype(full)
    gain = [gains[:, i] for i in range(6)]
    head_scale = gains[:, 6:8].reshape(-1, rows, 2)[:, :head_rows].reshape(HEAD_DIM, 2)

    tokens_all = x_all.astype(full)
    normed_all = norm_rows(tokens_all, gain[0])[0].astype(low)
    tokens = x_local.astype(full)
    x_normed_f, x_inverse = norm_rows(tokens, gain[0])
    normed = x_normed_f.astype(low)
    indices = jnp.concatenate([r * block + jnp.arange(block) for r in relative])
    cos_table, sin_table = rope_tables(marks_all[:, 1].reshape(length))
    codes = marks_all[:, 0].reshape(length) * (4 * length) + indices
    qkv = mm(normed_all, qkv_map)
    q_heads, k_head, v_head, attn_in, log_total = attend(
        ranks, qkv, codes, cos_table, sin_table, head_scale.T
    )
    attn_lin = sum_seq(cut(mm_nt(attn_in, out_map).astype(low)), ranks)

    attn_normed, attn_inverse = norm_rows(attn_lin, gain[1])
    laurel_low = mm(normed, laurel[:, :LR]).astype(low)
    laurel_high = mm_nt(laurel_low, laurel[:, LR:])
    laurel_normed, laurel_inverse = norm_rows(laurel_high, gain[2])
    mixed = (tokens + attn_normed + (normed.astype(full) + laurel_normed)) * root_half
    h_normed_f, h_inverse = norm_rows(mixed, gain[3])
    h_blocks = gather_seq(h_normed_f.astype(low), ranks)
    h_blocks, per_layer_maps = lax.optimization_barrier((h_blocks, per_layer_maps))
    ple = gather_everywhere(per_layer_maps, ranks, pairs)
    run_middle = functools.partial(
        *((middle, pairs) if ranks == 4 else (middle_plain, ranks))
    )
    (
        grad_ffn_rows,
        down_grad,
        down_map,
        gate_part,
        up_part,
        hidden_out,
        h_second,
        grad_second,
        grad_ple_low,
        ple_mixed,
        grad_ple_gate,
        ffn_gain_grads,
    ) = run_middle(
        h_blocks,
        in_maps,
        planes,
        mixed,
        gain[4:6],
        ple,
        per_layer_input.reshape(block, PLE),
        out_cotangent.reshape(block, width),
    )
    gain_grad_four, gain_grad_five = ffn_gain_grads[0], ffn_gain_grads[1]
    grad_ffn_rows = grad_ffn_rows.reshape(length, width)
    down_sum = lax.psum_scatter(down_grad, "fsdp", scatter_dimension=0, tiled=True)
    grad_ffn_rows, down_grad = lax.optimization_barrier((grad_ffn_rows, down_grad))
    grad_hidden = mm(grad_ffn_rows, down_map)
    gate_act, act_pull = jax.vjp(gelu_tanh, gate_part)
    grad_gate = act_pull(grad_hidden * up_part)[0].astype(low)
    grad_up = (grad_hidden * gate_act).astype(low)
    if ranks == 4:
        in_grad, grad_h_normed = back(grad_gate, grad_up, in_maps, h_blocks)
    else:
        h_part = mm_nt(grad_gate, in_maps[0]) + mm_nt(grad_up, in_maps[1])
        h_part = h_part.astype(low)
        grad_h_normed = sum_seq(cut(h_part), ranks)
        h_rows = whole_rows(h_blocks)
        in_grad = jnp.stack([mm_tn(h_rows, grad_gate), mm_tn(h_rows, grad_up)]).astype(low)
    in_sum = lax.psum_scatter(in_grad, "fsdp", scatter_dimension=1, tiled=True)
    in_sum = jnp.moveaxis(in_sum, 0, 1)

    grad_ple_up = mm_tn(grad_ple_low, ple_mixed)
    grad_ple_down = mm_tn(h_second, grad_ple_gate)
    grad_mixed_norm, gain_grad_three = norm_back(mixed, h_inverse, gain[3], grad_h_normed)
    grad_mixed = grad_second + grad_mixed_norm
    grad_branch = grad_mixed * root_half
    grad_attn, gain_grad_one = norm_back(attn_lin, attn_inverse, gain[1], grad_branch)
    grad_attn_blocks = gather_seq(grad_attn.astype(low), ranks)
    grad_laurel_high, gain_grad_two = norm_back(
        laurel_high, laurel_inverse, gain[2], grad_branch
    )
    grad_high_low = grad_laurel_high.astype(low)
    grad_laurel_up = mm_tn(grad_high_low, laurel_low)
    grad_laurel_low = mm(grad_high_low, laurel[:, LR:]).astype(low)
    grad_laurel_down = mm_tn(normed, grad_laurel_low)

    x_here = grad_branch + mm_nt(grad_laurel_low, laurel[:, :LR])
    gain_grad_zero = jnp.sum(x_here * tokens * x_inverse, 0)
    small_grad = jnp.stack(
        [
            gain_grad_zero,
            gain_grad_one,
            gain_grad_two,
            gain_grad_three,
            gain_grad_four,
            gain_grad_five,
        ],
        1,
    )
    small_grad = jnp.pad(small_grad, ((0, 0), (0, 128 - small_grad.shape[1])))
    rest_grad = jnp.concatenate(
        [grad_ple_down, grad_ple_up, grad_laurel_down, grad_laurel_up, small_grad], 1
    ).astype(low)
    rest_grad = rest_grad.reshape(ranks, -1, rest_grad.shape[1])
    rest_grad, grad_attn_blocks = lax.optimization_barrier((rest_grad, grad_attn_blocks))
    rest_others = [permute(take(rest_grad, 0, relative[k]), "seq", k) for k in range(1, ranks)]
    out_grad = weight_grad(ranks, pairs * 2, grad_attn_blocks, attn_in)
    grad_heads = mm(whole_rows(grad_attn_blocks), out_map).astype(low)
    grad_qkv, grad_gains = attend_back(
        ranks,
        qkv,
        q_heads,
        k_head,
        v_head,
        grad_heads,
        log_total,
        codes,
        cos_table,
        sin_table,
        head_scale.T,
    )
    grad_head_scale = grad_gains[:2].T
    rest_others, grad_qkv = lax.optimization_barrier((rest_others, grad_qkv))
    rest_own = sum((v.astype(full) for v in rest_others), take(rest_grad, 0, rank).astype(full))
    rest_own = rest_own.astype(low).reshape(pairs * 2, rows, -1)
    head_scale_grad = jnp.pad(
        grad_head_scale.reshape(-1, head_rows, 2), ((0, 0), (0, rows - head_rows), (0, 0))
    ).reshape(width, 2)
    late_grad = jnp.pad(head_scale_grad, ((0, 0), (6, 120)))
    last, pair_grad = weight_grad(
        ranks, pairs * 2, [normed_all], grad_qkv, head_all, gain[0][:, None], late_grad
    )
    last, pair_grad, grad_qkv = lax.optimization_barrier((last, pair_grad, grad_qkv))
    x_part = mm_nt(grad_qkv, qkv_map).astype(low)

    if ranks == 4:
        gain_row = jnp.broadcast_to(gain[0], (8, width))
        x_parts = x_part.reshape(ranks, block, width)
        extras = (x_parts, x_here, x_local, grad_mixed, gain_row)
        side = rank % 2 * 2
        mine = lax.dynamic_slice_in_dim(pair_grad, side, 2, 1)
        other = permute(lax.dynamic_slice_in_dim(pair_grad, 2 - side, 2, 1), "seq", 1)
        pair_grad = (mine.astype(full) + other.astype(full)).astype(low)
        *sums, input_grad = finish(sizes, last, out_grad, rest_own, pair_grad, extras)
    else:
        sums = finish(sizes, last, out_grad, rest_own, pair_grad)
        grad_x_normed = x_here + sum_seq(cut(x_part), ranks)
        grad_tokens_norm = norm_back(tokens, x_inverse, gain[0], grad_x_normed)[0]
        input_grad = grad_mixed * root_half + grad_tokens_norm
    small_sum = sums[6]

    grad_mlp = jnp.concatenate([in_sum, down_sum[:, None]], 1).astype(full)
    lead = (block, 1, width)
    return (
        hidden_out.reshape(lead),
        input_grad.reshape(lead),
        *sums[:4],
        sums[5],
        sums[4],
        small_sum[:, :6],
        small_sum[:head_rows, 6:8],
        grad_mlp,
    )


def solution(mesh):
    sizes = {"seq": mesh.shape["seq"], "pair": mesh.shape["fsdp"] // 2, "core": 2}
    spread = P(("seq", "fsdp"), None)
    tokens = P("seq", "fsdp", None)
    return jax.shard_map(
        functools.partial(body, sizes),
        mesh=mesh,
        in_specs=(tokens, tokens, P("seq", "fsdp"), P("seq", "fsdp"), tokens)
        + (spread,) * 8
        + (P("fsdp", None, "seq"),),
        out_specs=(tokens, tokens) + (spread,) * 8 + (P("fsdp", None, "seq"),),
        check_vma=False,
    )
```

```python
import functools
import math

import jax
import jax.numpy as jnp
from jax import lax
from jax.experimental import pallas as pl
from jax.experimental.pallas import tpu as pltpu
from jax.sharding import PartitionSpec as P

QUERY_HEADS = 8
KEY_VALUE_HEADS = 2
HEAD_DIM = 256
LR = 64
PLE = 256
WIN = 512

MESH = pl.DeviceIdType.MESH
eps = 1e-06
theta = 10000.0
root_half = 1.0 / math.sqrt(2.0)
low = jnp.bfloat16
full = jnp.float32


def flip(index, offset, size):
    value, bit = 0, 1
    while bit < size:
        has = (index // bit) % 2
        value = value + bit * ((1 - has) if offset & bit else has)
        bit *= 2
    return value


def gather_kernel(
    sizes,
    head_ref,
    rest_ref,
    mark_ref,
    x_ref,
    planes_ref,
    head_out,
    rest_out,
    mark_out,
    x_out,
    planes_out,
    planes,
    *sems,
):
    (local, head_s1, head_r1, right_s, right_r, left_s, left_r, head_s3, head_r3) = sems[:9]
    (rest_s1, rest_r1, rest_s2, rest_r2, rest_s3, rest_r3, mark_s, mark_r, x_s, x_r) = sems[9:]
    ranks, pairs = sizes["seq"], sizes["pair"]
    rank = lax.axis_index("seq")
    fsdp_index = lax.axis_index("fsdp")
    pair, core = fsdp_index // 2, fsdp_index % 2
    sibling = (rank, pair * 2 + 1 - core)

    def on_seq(step):
        return (flip(rank, step, ranks), fsdp_index)

    def on_pair(step):
        return (rank, ((pair + step) % pairs) * 2 + core)

    def remote(source, target, send, recv, device):
        return pltpu.make_async_remote_copy(
            src_ref=source,
            dst_ref=target,
            send_sem=send,
            recv_sem=recv,
            device_id=device,
            device_id_type=MESH,
        )

    load = pltpu.make_async_copy(planes_ref.at[pl.ds(0, 2)], planes, local.at[4])
    load.start()
    barrier = pltpu.get_barrier_semaphore()
    devices = [on_seq(i) for i in range(1, ranks)] + [on_pair(i) for i in range(1, pairs)]
    for device in devices + [sibling]:
        pl.semaphore_signal(barrier, inc=1, device_id=device, device_id_type=MESH)
    pl.semaphore_wait(barrier, len(devices) + 1)

    sent = []

    def go(copy):
        copy.start()
        sent.append(copy)
        return copy

    def part(at, k):
        return head_out.at[flip(rank, k, ranks), at, core]

    def right(t, k):
        source = head_ref.at[rank] if t == 1 and k == 0 else part(pair - (t - 1), k)
        slot = (t - 1) * ranks + k
        target = part(pair - (t - 1), k)
        return remote(source, target, right_s.at[slot], right_r.at[slot], (rank, fsdp_index + 2))

    def left(t, k):
        source = head_ref.at[rank] if t == 1 and k == 0 else part(pair + (t - 1), k)
        slot = (t - 1) * ranks + k
        target = part(pair + (t - 1), k)
        return remote(source, target, left_s.at[slot], left_r.at[slot], (rank, fsdp_index - 2))

    def to_sibling(t, k):
        source = head_ref.at[rank] if t == 0 and k == 0 else part(pair - t, k)
        slot = (t + pairs - 1) * ranks + k
        return remote(source, part(pair - t, k), head_s3.at[slot], head_r3.at[slot], sibling)

    sends_right = lambda t: (pair - (t - 1) >= 0) & (pair + 1 < pairs)
    sends_left = lambda t: (pair + (t - 1) < pairs) & (pair - 1 >= 0)

    def begin(k):
        pl.when(sends_right(1))(lambda: right(1, k).start())
        pl.when(sends_left(1))(lambda: left(1, k).start())
        to_sibling(0, k).start()

    begin(0)
    head_seq = [
        go(
            remote(
                head_ref.at[on_seq(i)[0]],
                head_out.at[rank, pair, core],
                head_s1.at[i - 1],
                head_r1.at[i - 1],
                on_seq(i),
            )
        )
        for i in range(1, ranks)
    ]
    rest_pair = [
        go(
            remote(
                rest_ref,
                rest_out.at[rank, pair, core],
                rest_s1.at[i - 1],
                rest_r1.at[i - 1],
                on_pair(i),
            )
        )
        for i in range(1, pairs)
    ]
    owns = [
        pltpu.make_async_copy(head_ref.at[rank], head_out.at[rank, pair, core], local.at[0]),
        pltpu.make_async_copy(rest_ref, rest_out.at[rank, pair, core], local.at[1]),
        pltpu.make_async_copy(mark_ref, mark_out.at[0], local.at[2]),
        pltpu.make_async_copy(x_ref, x_out.at[0], local.at[3]),
    ]
    for copy in owns:
        copy.start()
    marks = [
        go(remote(mark_ref, mark_out.at[i], mark_s.at[i - 1], mark_r.at[i - 1], on_seq(i)))
        for i in range(1, ranks)
    ]
    for k in range(1, ranks):
        head_seq[k - 1].wait_recv()
        begin(k)

    half = x_ref.shape[1] // 2
    first, second = slice(0, half), slice(half, 2 * half)
    x_seq, relays = [], []
    if ranks == 4:
        for order in range(2):
            for i, columns in ((1, (first, second)[order]), (2, (second, first)[order])):
                slot = (i - 1) * 2 + order
                x_seq.append(
                    go(
                        remote(
                            x_ref.at[:, columns],
                            x_out.at[i, :, columns],
                            x_s.at[slot],
                            x_r.at[slot],
                            on_seq(i),
                        )
                    )
                )
    else:
        for i in range(1, ranks):
            x_seq.append(
                go(remote(x_ref, x_out.at[i], x_s.at[i - 1], x_r.at[i - 1], on_seq(i)))
            )

    load.wait()
    store = pltpu.make_async_copy(planes, planes_out, local.at[4])
    store.start()
    owns[1].wait()
    for copy in rest_pair:
        copy.wait_recv()
    row = rest_out.at[rank, :, core]
    rest_seq = [
        go(remote(row, row, rest_s2.at[i - 1], rest_r2.at[i - 1], on_seq(i)))
        for i in range(1, ranks)
    ]
    rest_core = [go(remote(row, row, rest_s3.at[0], rest_r3.at[0], sibling))]

    for t in range(1, pairs):
        for k in range(ranks):

            def from_left(t=t, k=k):
                slot = (t - 1) * ranks + k
                target = part(pair - t, k)
                remote(target, target, right_s.at[slot], right_r.at[slot], sibling).wait_recv()
                if t + 1 < pairs:
                    pl.when(pair + 1 < pairs)(lambda: right(t + 1, k).start())
                to_sibling(t, k).start()

            def from_right(t=t, k=k):
                slot = (t - 1) * ranks + k
                target = part(pair + t, k)
                remote(target, target, left_s.at[slot], left_r.at[slot], sibling).wait_recv()
                if t + 1 < pairs:
                    pl.when(pair - 1 >= 0)(lambda: left(t + 1, k).start())
                to_sibling(-t, k).start()

            pl.when(pair - t >= 0)(from_left)
            pl.when(pair + t < pairs)(from_right)
        if t == 1 and ranks == 4:
            x_seq[0].wait_recv()
            x_seq[1].wait_recv()
            for slot, i, columns, to in ((4, 1, first, 2), (5, 2, second, 1)):
                relays.append(
                    go(
                        remote(
                            x_out.at[i, :, columns],
                            x_out.at[3, :, columns],
                            x_s.at[slot],
                            x_r.at[slot],
                            on_seq(to),
                        )
                    )
                )

    for i in range(1, ranks):
        rest_seq[i - 1].wait_recv()
        row = rest_out.at[flip(rank, i, ranks), :, core]
        rest_core.append(go(remote(row, row, rest_s3.at[i], rest_r3.at[i], sibling)))
    owns[0].wait()
    store.wait()
    for copy in owns[2:]:
        copy.wait()
    for copy in marks + x_seq[2 if ranks == 4 else 0 :] + relays + rest_core:
        copy.wait_recv()
    for k in range(ranks):
        to_sibling(0, k).wait()
        for t in range(1, pairs):
            pl.when(pair - t >= 0)(lambda t=t, k=k: to_sibling(t, k).wait())
            pl.when(pair + t < pairs)(lambda t=t, k=k: to_sibling(-t, k).wait())
            pl.when(sends_right(t))(lambda t=t, k=k: right(t, k).wait_send())
            pl.when(sends_left(t))(lambda t=t, k=k: left(t, k).wait_send())
    for copy in sent:
        copy.wait_send()


def gather_weights(sizes, head, rest, marks, x, planes):
    ranks, pairs = sizes["seq"], sizes["pair"]
    dma = lambda n: pltpu.SemaphoreType.DMA((n,))
    anywhere = pl.BlockSpec(memory_space=pl.ANY)
    return pl.pallas_call(
        functools.partial(gather_kernel, sizes),
        out_shape=(
            jax.ShapeDtypeStruct((ranks, pairs, 2) + head.shape[1:], head.dtype),
            jax.ShapeDtypeStruct((ranks, pairs, 2) + rest.shape, rest.dtype),
            jax.ShapeDtypeStruct((ranks,) + marks.shape, marks.dtype),
            jax.ShapeDtypeStruct((ranks,) + x.shape, x.dtype),
            jax.ShapeDtypeStruct((2,) + planes.shape[1:], planes.dtype),
        ),
        in_specs=[anywhere] * 5,
        out_specs=(anywhere,) * 5,
        scratch_shapes=[
            pltpu.VMEM((2,) + planes.shape[1:], planes.dtype),
            dma(5),
            *[dma(ranks - 1)] * 2,
            *[dma((pairs - 1) * ranks)] * 4,
            *[dma((2 * pairs - 1) * ranks)] * 2,
            *[dma(pairs - 1)] * 2,
            *[dma(ranks - 1)] * 2,
            *[dma(ranks)] * 2,
            *[dma(ranks - 1)] * 2,
            *[dma(2 * ranks - 2)] * 2,
        ],
        compiler_params=pltpu.CompilerParams(collective_id=0, has_side_effects=True),
    )(head, rest, marks, x, planes)


def permute(v, axis, offset):
    size = lax.axis_size(axis)
    return lax.ppermute(v, axis, [(i, i ^ offset) for i in range(size)])


def gather_seq(v, ranks):
    if ranks != 4:
        return [v] + [permute(v, "seq", k) for k in range(1, ranks)]
    half = v.shape[1] // 2
    first, second = permute(v, "seq", 1), permute(v, "seq", 2)
    left = permute(first[:, :half], "seq", 2)
    right = permute(second[:, half:], "seq", 1)
    return [v, first, second, left, right]


def whole_rows(blocks):
    if blocks[-1].shape[1] < blocks[0].shape[1]:
        blocks = blocks[:-2] + [jnp.concatenate(blocks[-2:], 1)]
    return jnp.concatenate(blocks, 0)


def sum_seq(blocks, ranks):
    up = lambda v: v.astype(full)
    if ranks != 4:
        return sum((up(permute(blocks[k], "seq", k)) for k in range(1, ranks)), up(blocks[0]))
    half = blocks[0].shape[1] // 2
    left = [b[:, :half] for b in blocks]
    right = [b[:, half:] for b in blocks]
    left_far, right_far = permute(left[3], "seq", 1), permute(right[3], "seq", 2)
    left_near, right_near = permute(left[1], "seq", 1), permute(right[2], "seq", 2)
    left_far = permute((up(left[2]) + up(left_far)).astype(low), "seq", 2)
    right_far = permute((up(right[1]) + up(right_far)).astype(low), "seq", 1)
    return jnp.concatenate(
        [
            up(left[0]) + up(left_near) + up(left_far),
            up(right[0]) + up(right_near) + up(right_far),
        ],
        1,
    )


def take(v, axis, index):
    return lax.dynamic_index_in_dim(v, index, axis, keepdims=False)


def gather_everywhere(v, ranks, pairs):
    index, rank = lax.axis_index("fsdp"), lax.axis_index("seq")
    pair, core = index // 2, index % 2

    def spread(part, axis, offsets, mine):
        got = jnp.stack([part] + [permute(part, axis, k) for k in offsets])
        return jnp.stack([take(got, 0, mine ^ i) for i in range(len(offsets) + 1)])

    v = spread(v, "fsdp", [2 * k for k in range(1, pairs)], pair)
    v = spread(v, "seq", range(1, ranks), rank)
    v = spread(v, "fsdp", [1], core)
    return jnp.moveaxis(v, 0, 2).reshape(-1, v.shape[-1])


def dot(left, right, over):
    return lax.dot_general(left, right, (over, ((), ())), preferred_element_type=full)


def mm(left, right):
    return dot(left, right, ((1,), (0,)))


def mm_nt(left, right):
    return dot(left, right, ((1,), (1,)))


def mm_tn(left, right):
    return dot(left, right, ((0,), (0,)))


def norm_rows(v, gain_vec):
    inverse = lax.rsqrt(jnp.mean(v * v, -1, keepdims=True) + eps)
    return (v * inverse * gain_vec, inverse)


def norm_back(v, inverse, gain_vec, incoming):
    scaled = incoming * gain_vec
    inner_mean = jnp.mean(scaled * v, -1, keepdims=True)
    return (
        inverse * (scaled - v * inverse * inverse * inner_mean),
        jnp.sum(incoming * v * inverse, axis=0),
    )


def gelu_tanh(v):
    return jax.nn.gelu(v, approximate=True)


def rope_tables(places):
    half_width = HEAD_DIM // 2
    frequency = theta ** (-jnp.arange(half_width).astype(full) * 2.0 / HEAD_DIM)
    angles = places.astype(full)[:, None] * frequency
    return (jnp.cos(angles), jnp.sin(angles))


def reaches(rank, mine, other, block):
    apart = (rank ^ mine) - (rank ^ other)
    return (apart >= 0) & (apart * block - (block - 1) < WIN)


def attend_kernel(
    ranks,
    block,
    qkv_ref,
    code_col_ref,
    code_row_ref,
    cos_ref,
    sin_ref,
    gain_ref,
    q_ref,
    k_ref,
    v_ref,
    out_ref,
    total_ref,
    scores_ref,
    peak_acc,
    sum_acc,
    out_acc,
):
    head, mine = pl.program_id(0), pl.program_id(1)
    rank = lax.axis_index("seq")
    half = HEAD_DIM // 2
    base = qkv_ref.shape[1] - 2 * HEAD_DIM

    def normed(v):
        return v * lax.rsqrt(jnp.mean(v * v, -1, keepdims=True) + eps)

    def turned(v, cos_table, sin_table):
        first, second = v[:, :half], v[:, half:]
        return jnp.concatenate(
            [
                first * cos_table - second * sin_table,
                second * cos_table + first * sin_table,
            ],
            1,
        )

    @pl.when((head == 0) & (mine == 0))
    def _():
        for other in range(ranks):
            span = slice(other * block, (other + 1) * block)
            keys = normed(qkv_ref[span, base : base + HEAD_DIM]) * gain_ref[1:2, :]
            k_ref[span, :] = turned(keys, cos_ref[span, :], sin_ref[span, :]).astype(low)
            v_ref[span, :] = normed(qkv_ref[span, base + HEAD_DIM :]).astype(low)

    rows = pl.ds(pl.multiple_of(mine * block, block), block)
    columns = pl.ds(pl.multiple_of(head * HEAD_DIM, HEAD_DIM), HEAD_DIM)
    queries = normed(qkv_ref[rows, columns]) * gain_ref[0:1, :]
    q = turned(queries, cos_ref[rows, :], sin_ref[rows, :]).astype(low)
    q_ref[rows, columns] = q
    code = code_col_ref[rows, :]
    peak_acc[...] = jnp.full_like(peak_acc, -1000000000.0)
    sum_acc[...] = jnp.zeros_like(sum_acc)
    out_acc[...] = jnp.zeros_like(out_acc)
    for other in range(ranks):
        span = slice(other * block, (other + 1) * block)

        @pl.when(reaches(rank, mine, other, block))
        def _():
            scores = mm_nt(q, k_ref[span, :]) * HEAD_DIM ** (-0.5)
            offset = code - code_row_ref[:, span]
            scores = jnp.where((offset >= 0) & (offset < WIN), scores, -1000000000.0)
            scores_ref[other] = scores
            peak_acc[...] = jnp.maximum(peak_acc[...], jnp.max(scores, -1, keepdims=True))

    peak = peak_acc[...]
    for other in range(ranks):

        @pl.when(reaches(rank, mine, other, block))
        def _():
            weights = jnp.exp(scores_ref[other] - peak)
            scores_ref[other] = weights
            sum_acc[...] += jnp.sum(weights, -1, keepdims=True)

    row_total = sum_acc[...]
    for other in range(ranks):
        span = slice(other * block, (other + 1) * block)

        @pl.when(reaches(rank, mine, other, block))
        def _():
            probs = (scores_ref[other] / row_total).astype(low)
            out_acc[...] += mm(probs, v_ref[span, :])

    out_ref[rows, columns] = out_acc[...].astype(low)
    total_ref[head, rows, :] = peak + jnp.log(row_total)


def attend(ranks, qkv, codes, cos_table, sin_table, gains):
    length = qkv.shape[0]
    block = length // ranks
    heads = qkv.shape[1] // HEAD_DIM - 2
    whole = lambda v: pl.BlockSpec(
        v.shape, lambda i, j, n=len(v.shape): (0,) * n, pipeline_mode=pl.Buffered(1)
    )
    operands = (qkv, codes[:, None], codes[None], cos_table, sin_table, gains)
    results = (
        jax.ShapeDtypeStruct((length, heads * HEAD_DIM), low),
        jax.ShapeDtypeStruct((length, HEAD_DIM), low),
        jax.ShapeDtypeStruct((length, HEAD_DIM), low),
        jax.ShapeDtypeStruct((length, heads * HEAD_DIM), low),
        jax.ShapeDtypeStruct((heads, length, 1), full),
    )
    return pl.pallas_call(
        functools.partial(attend_kernel, ranks, block),
        grid=(heads, ranks),
        out_shape=results,
        in_specs=[whole(v) for v in operands],
        out_specs=tuple(whole(v) for v in results),
        scratch_shapes=[
            pltpu.VMEM((ranks, block, block), full),
            pltpu.VMEM((block, 1), full),
            pltpu.VMEM((block, 1), full),
            pltpu.VMEM((block, HEAD_DIM), full),
        ],
        compiler_params=pltpu.CompilerParams(vmem_limit_bytes=40 << 20),
        cost_estimate=pl.CostEstimate(
            flops=4 * heads * length * length * HEAD_DIM * 9 // 16,
            bytes_accessed=12 * length * HEAD_DIM * (heads + 2),
            transcendentals=heads * length * length,
        ),
    )(*operands)


def norm_rope_back(lin, gain, incoming):
    inverse = lax.rsqrt(jnp.mean(lin * lin, -1, keepdims=True) + eps)
    scaled = incoming * gain
    inner_mean = jnp.mean(scaled * lin, -1, keepdims=True)
    return (
        inverse * (scaled - lin * inverse * inverse * inner_mean),
        jnp.sum(incoming * lin * inverse, 0, keepdims=True),
    )


def attend_back_kernel(
    ranks,
    block,
    qkv_ref,
    q_ref,
    k_ref,
    v_ref,
    grad_ref,
    total_ref,
    code_col_ref,
    code_row_ref,
    cos_ref,
    sin_ref,
    gain_ref,
    out_ref,
    gain_out_ref,
    key_acc,
    value_acc,
    query_acc,
    row_acc,
    probs_ref,
    grad_probs_ref,
):
    head, mine = pl.program_id(0), pl.program_id(1)
    heads = pl.num_programs(0)
    rank = lax.axis_index("seq")
    scale = HEAD_DIM ** (-0.5)
    half = HEAD_DIM // 2

    @pl.when((head == 0) & (mine == 0))
    def _():
        key_acc[...] = jnp.zeros_like(key_acc)
        value_acc[...] = jnp.zeros_like(value_acc)
        gain_out_ref[...] = jnp.zeros_like(gain_out_ref)

    rows = pl.ds(pl.multiple_of(mine * block, block), block)
    columns = pl.ds(pl.multiple_of(head * HEAD_DIM, HEAD_DIM), HEAD_DIM)
    q, grad = q_ref[rows, columns], grad_ref[rows, columns]
    code = code_col_ref[rows, :]
    peaks = total_ref[head, rows, :]
    row_acc[...] = jnp.zeros_like(row_acc)
    query_acc[...] = jnp.zeros_like(query_acc)

    for other in range(ranks):
        span = slice(other * block, (other + 1) * block)

        @pl.when(reaches(rank, mine, other, block))
        def _():
            scores = mm_nt(q, k_ref[span, :]) * scale
            offset = code - code_row_ref[:, span]
            probs = jnp.where((offset >= 0) & (offset < WIN), jnp.exp(scores - peaks), 0.0)
            grad_probs = mm_nt(grad, v_ref[span, :])
            probs_ref[other] = probs
            grad_probs_ref[other] = grad_probs
            row_acc[...] += jnp.sum(probs * grad_probs, -1, keepdims=True)

    inner = row_acc[...]
    for other in range(ranks):
        span = slice(other * block, (other + 1) * block)

        @pl.when(reaches(rank, mine, other, block))
        def _():
            probs = probs_ref[other]
            grad_scores = (probs * (grad_probs_ref[other] - inner) * scale).astype(low)
            query_acc[...] += mm(grad_scores, k_ref[span, :])
            key_acc[span, :] += mm_tn(grad_scores, q)
            value_acc[span, :] += mm_tn(probs.astype(low), grad)

    def turned_back(v, cos_table, sin_table):
        first, second = v[:, :half], v[:, half:]
        return jnp.concatenate(
            [
                first * cos_table + second * sin_table,
                second * cos_table - first * sin_table,
            ],
            1,
        )

    incoming = turned_back(query_acc[...].astype(low).astype(full), cos_ref[rows, :], sin_ref[rows, :])
    grad_lin, grad_gain = norm_rope_back(qkv_ref[rows, columns], gain_ref[0:1, :], incoming)
    out_ref[rows, columns] = grad_lin.astype(low)
    gain_out_ref[0:1, :] += grad_gain

    @pl.when((head == heads - 1) & (mine == ranks - 1))
    def _():
        base = out_ref.shape[1] - 2 * HEAD_DIM
        for other in range(ranks):
            span = slice(other * block, (other + 1) * block)
            incoming = turned_back(key_acc[span, :], cos_ref[span, :], sin_ref[span, :])
            grad_lin, grad_gain = norm_rope_back(
                qkv_ref[span, base : base + HEAD_DIM], gain_ref[1:2, :], incoming
            )
            out_ref[span, base : base + HEAD_DIM] = grad_lin.astype(low)
            gain_out_ref[1:2, :] += grad_gain
            grad_lin = norm_rope_back(qkv_ref[span, base + HEAD_DIM :], 1.0, value_acc[span, :])[0]
            out_ref[span, base + HEAD_DIM :] = grad_lin.astype(low)


def attend_back(ranks, qkv, q, k, v, grad, total, codes, cos_table, sin_table, gains):
    length = qkv.shape[0]
    block = length // ranks
    heads = q.shape[1] // HEAD_DIM
    whole = lambda v: pl.BlockSpec(
        v.shape, lambda i, j, n=len(v.shape): (0,) * n, pipeline_mode=pl.Buffered(1)
    )
    operands = (qkv, q, k, v, grad, total, codes[:, None], codes[None], cos_table, sin_table, gains)
    results = (
        jax.ShapeDtypeStruct(qkv.shape, low),
        jax.ShapeDtypeStruct((8, HEAD_DIM), full),
    )
    return pl.pallas_call(
        functools.partial(attend_back_kernel, ranks, block),
        grid=(heads, ranks),
        out_shape=results,
        in_specs=[whole(v) for v in operands],
        out_specs=tuple(whole(v) for v in results),
        scratch_shapes=[
            pltpu.VMEM((length, HEAD_DIM), full),
            pltpu.VMEM((length, HEAD_DIM), full),
            pltpu.VMEM((block, HEAD_DIM), full),
            pltpu.VMEM((block, 1), full),
            pltpu.VMEM((ranks, block, block), full),
            pltpu.VMEM((ranks, block, block), full),
        ],
        compiler_params=pltpu.CompilerParams(vmem_limit_bytes=40 << 20),
        cost_estimate=pl.CostEstimate(
            flops=10 * heads * length * length * HEAD_DIM * 9 // 16,
            bytes_accessed=16 * length * HEAD_DIM * (heads + 2),
            transcendentals=heads * length * length,
        ),
    )(*operands)


def weight_grad_kernel(count, half_tiles, *refs):
    lefts, right_ref = refs[:count], refs[count]
    out_ref = refs[-1] if len(refs) == count + 2 else refs[-3]
    pieces = [ref[...] for ref in lefts]
    if half_tiles:
        pieces[-2:] = [jnp.where(pl.program_id(0) < half_tiles, pieces[-2], pieces[-1])]
    result, start = None, 0
    for piece in pieces:
        part = mm_tn(piece, right_ref[start : start + piece.shape[0], :])
        result = part if result is None else result + part
        start += piece.shape[0]
    if len(refs) > count + 2:
        map_ref, gain_ref, late_ref = refs[count + 1 : count + 4]
        maps = map_ref[:, : result.shape[1]].astype(full)
        of_gain = jnp.sum(maps * result, -1, keepdims=True) / gain_ref[...]
        late = late_ref[...]
        lane = lax.broadcasted_iota(jnp.int32, late.shape, 1)
        split = result.shape[1] - 2 * HEAD_DIM
        refs[-2][...] = result[:, split:].astype(low).reshape(refs[-2].shape)
        late = jnp.where(lane == 0, of_gain, late)
        refs[-1][...] = late.astype(low).reshape(refs[-1].shape)
        result = result[:, :split]
    out_ref[...] = result.astype(low).reshape(out_ref.shape)


def weight_grad(ranks, parts, lefts, right, *extras):
    width = lefts[0].shape[1]
    length, columns = right.shape
    rows = width // (ranks * parts)
    tile = max(min(256, rows * parts), rows)
    each = tile // rows
    wides = [columns - 2 * HEAD_DIM, 2 * HEAD_DIM, 128] if extras else [columns]
    half_tiles = lefts[-1].shape[1] // tile if lefts[-1].shape[1] < width else 0

    def place(i):
        return (((i * each) % parts) // each, (i * each) // parts, 0, 0)

    left_specs = [pl.BlockSpec((v.shape[0], tile), lambda i: (0, i)) for v in lefts]
    if half_tiles:
        left_specs[-2:] = [
            pl.BlockSpec((lefts[-1].shape[0], tile), lambda i: (0, jnp.minimum(i, half_tiles - 1))),
            pl.BlockSpec((lefts[-1].shape[0], tile), lambda i: (0, jnp.maximum(i - half_tiles, 0))),
        ]
    results = pl.pallas_call(
        functools.partial(weight_grad_kernel, len(lefts), half_tiles),
        grid=(width // tile,),
        out_shape=tuple(jax.ShapeDtypeStruct((parts, ranks, rows, n), low) for n in wides),
        in_specs=left_specs
        + [pl.BlockSpec((length, columns), lambda i: (0, 0))]
        + [pl.BlockSpec((tile, v.shape[1]), lambda i: (i, 0)) for v in extras],
        out_specs=tuple(pl.BlockSpec((each, 1, rows, n), place) for n in wides),
        compiler_params=pltpu.CompilerParams(vmem_limit_bytes=60 << 20),
        cost_estimate=pl.CostEstimate(
            flops=2 * length * width * columns,
            bytes_accessed=2 * (length * (width + columns) + width * columns),
            transcendentals=0,
        ),
    )(*lefts, right, *extras)
    return results if extras else results[0]


def middle_kernel(
    pairs,
    block,
    parts,
    rows_own,
    rows_x_in,
    rows_y_in,
    rows_left_in,
    rows_right_in,
    in_maps_ref,
    shard_ref,
    mixed_ref,
    gain_ref,
    ple_gate_ref,
    ple_proj_ref,
    ple_input_ref,
    cotangent_ref,
    rows_out_ref,
    grad_map_ref,
    map_ref,
    gate_part_ref,
    up_part_ref,
    out_ref,
    second_ref,
    grad_second_ref,
    grad_ple_ref,
    ple_mixed_ref,
    grad_gate_ref,
    gain_out_ref,
    rows_ref,
    in_tiles,
    wide_stage,
    hidden_ref,
    maps,
    product_ref,
    own,
    keep,
    send,
    got,
    relay,
    far,
    stage,
    load_sem,
    tile_sem,
    wide_sem,
    stage_sem,
    map_sem,
    right_s,
    right_r,
    left_s,
    left_r,
    core_s,
    core_r,
    near_s,
    near_r,
    far_s,
    far_r,
    gx_s,
    gx_r,
    gy_s,
    gy_r,
    fx_s,
    fx_r,
    fy_s,
    fy_r,
):
    rank = lax.axis_index("seq")
    fsdp_index = lax.axis_index("fsdp")
    pair, core = fsdp_index // 2, fsdp_index % 2
    sibling = (rank, pair * 2 + 1 - core)
    rank_x, rank_y = flip(rank, 1, 4), flip(rank, 2, 4)
    by_x, by_y = (rank_x, fsdp_index), (rank_y, fsdp_index)
    size = block // parts
    width, span = in_maps_ref.shape[1], in_maps_ref.shape[2]
    half = width // 2
    tile = 256
    tiles = span // tile
    shard = shard_ref.shape[1]
    shard_ref = shard_ref.at[2]
    cut = shard // 2
    left, right = slice(0, half), slice(half, width)
    up = lambda v: v.astype(full)

    def remote(source, target, send_sem, recv_sem, device):
        return pltpu.make_async_remote_copy(
            src_ref=source,
            dst_ref=target,
            send_sem=send_sem,
            recv_sem=recv_sem,
            device_id=device,
            device_id_type=MESH,
        )

    def columns_of(i):
        return pl.ds(pl.multiple_of(i * tile, tile), tile)

    loads = [
        pltpu.make_async_copy(source, target, load_sem.at[i])
        for i, (source, target) in enumerate(
            (
                (rows_own, rows_ref.at[0]),
                (rows_x_in, rows_ref.at[1]),
                (rows_y_in, rows_ref.at[2]),
                (rows_left_in, rows_ref.at[3, :, left]),
                (rows_right_in, rows_ref.at[3, :, right]),
                (shard_ref, maps.at[pair, core]),
            )
        )
    ]

    def tile_copy(i, slot):
        return pltpu.make_async_copy(
            in_maps_ref.at[:, :, columns_of(i)], in_tiles.at[slot], tile_sem.at[slot]
        )

    for copy in loads:
        copy.start()
    tile_copy(0, 0).start()

    barrier = pltpu.get_barrier_semaphore()
    devices = [by_x, by_y, sibling]
    devices += [(rank, ((pair + i) % pairs) * 2 + core) for i in range(1, pairs)]
    for device in devices:
        pl.semaphore_signal(barrier, inc=1, device_id=device, device_id_type=MESH)
    pl.semaphore_wait(barrier, len(devices))

    def piece(at, k):
        return maps.at[at, core, pl.ds(k * cut, cut), :]

    def source_of(at, k, t):
        return shard_ref.at[pl.ds(k * cut, cut), :] if t == 0 else piece(at, k)

    def pass_right(t, k):
        at, slot = pair - (t - 1), (t - 1) * 2 + k
        return remote(
            source_of(at, k, t - 1),
            piece(at, k),
            right_s.at[slot],
            right_r.at[slot],
            (rank, fsdp_index + 2),
        )

    def pass_left(t, k):
        at, slot = pair + (t - 1), (t - 1) * 2 + k
        return remote(
            source_of(at, k, t - 1),
            piece(at, k),
            left_s.at[slot],
            left_r.at[slot],
            (rank, fsdp_index - 2),
        )

    def to_sibling(at, k, own_shard=False):
        slot = at * 2 + k
        return remote(
            source_of(at, k, 0 if own_shard else 1),
            piece(at, k),
            core_s.at[slot],
            core_r.at[slot],
            sibling,
        )

    sends_right = lambda t: (pair - (t - 1) >= 0) & (pair + 1 < pairs)
    sends_left = lambda t: (pair + (t - 1) < pairs) & (pair - 1 >= 0)
    for k in range(2):
        pl.when(sends_right(1))(lambda k=k: pass_right(1, k).start())
        pl.when(sends_left(1))(lambda k=k: pass_left(1, k).start())
        to_sibling(pair, k, True).start()

    def chain_step(t, k):
        slot = (t - 1) * 2 + k

        def from_left():
            target = piece(pair - t, k)
            remote(target, target, right_s.at[slot], right_r.at[slot], sibling).wait_recv()
            if t + 1 < pairs:
                pl.when(pair + 1 < pairs)(lambda: pass_right(t + 1, k).start())
            to_sibling(pair - t, k).start()

        def from_right():
            target = piece(pair + t, k)
            remote(target, target, left_s.at[slot], left_r.at[slot], sibling).wait_recv()
            if t + 1 < pairs:
                pl.when(pair - 1 >= 0)(lambda: pass_left(t + 1, k).start())
            to_sibling(pair + t, k).start()

        pl.when(pair - t >= 0)(from_left)
        pl.when(pair + t < pairs)(from_right)

    for copy in loads:
        copy.wait()

    def wide_copies(i, slot):
        return [
            pltpu.make_async_copy(
                wide_stage.at[slot, n], target.at[:, columns_of(i)], wide_sem.at[slot, n]
            )
            for n, target in enumerate((gate_part_ref, up_part_ref))
        ]

    slope, cubic = math.sqrt(2.0 / math.pi), 0.044715

    def gate_up_tile(i, carry):
        slot = i % 2
        tile_copy(i, slot).wait()
        pl.when(i + 1 < tiles)(lambda: tile_copy(i + 1, 1 - slot).start())

        @pl.when(i >= 2)
        def _():
            for copy in wide_copies(i - 2, slot):
                copy.wait()

        v = rows_ref[...].reshape(4 * block, width)
        gate = mm(v, in_tiles[slot, 0])
        wide_stage[slot, 0] = gate
        upper = mm(v, in_tiles[slot, 1])
        wide_stage[slot, 1] = upper
        bend = jnp.tanh(slope * (gate + cubic * gate * gate * gate))
        hidden_ref[:, columns_of(i)] = (0.5 * gate * (1.0 + bend) * upper).astype(low)
        for copy in wide_copies(i, slot):
            copy.start()
        return carry

    steps = [(t, k) for t in range(1, pairs) for k in range(2)]
    early = min(len(steps), 4)
    at_tile = [tiles * (n + 1) // early for n in range(early)]
    done = 0
    for n in range(early):
        lax.fori_loop(done, at_tile[n], gate_up_tile, 0)
        done = at_tile[n]
        chain_step(*steps[n])
    for i in (tiles - 2, tiles - 1):
        for copy in wide_copies(i, i % 2):
            copy.wait()

    def chip_of(j):
        orders = [sorted(range(pairs), key=lambda p: (abs(p - z), p)) for z in range(pairs)]
        return sum(jnp.where(pair == z, orders[z][j], 0) for z in range(pairs))

    def shard_of(j):
        chip = chip_of(j // 2)
        at_core = core if j % 2 == 0 else 1 - core
        return chip, at_core, chip * 2 + at_core, 1 - chip // (pairs // 2)

    def near_copy(j):
        chip, at_core, place, is_left = shard_of(j)
        to = rank_x * is_left + rank_y * (1 - is_left)
        return remote(
            send.at[place], got.at[place], near_s.at[place], near_r.at[place], (to, fsdp_index)
        )

    def far_copy(j):
        chip, at_core, place, is_left = shard_of(j)
        to = rank_y * is_left + rank_x * (1 - is_left)
        return remote(
            relay.at[place], far.at[place], far_s.at[place], far_r.at[place], (to, fsdp_index)
        )

    def product(j):
        chip, at_core, place, is_left = shard_of(j)
        if j % 2:
            for k in range(2):
                target = maps.at[chip, at_core, pl.ds(k * cut, cut), :]
                remote(
                    target, target, core_s.at[0], core_r.at[chip * 2 + k], sibling
                ).wait_recv()
        v = mm_nt(hidden_ref[...], maps[chip, at_core])
        product_ref[...] = v.reshape(4, block, shard)
        near = 2 - is_left
        own[:, columns_of(place)] = product_ref[0]
        send[place, 0] = product_ref[3].astype(low)
        send[place, 1] = product_ref[near].astype(low)
        keep[place] = product_ref[3 - near]
        near_copy(j).start()

    def pass_on(j):
        place = shard_of(j)[2]
        near_copy(j).wait_recv()
        relay[place] = (keep[place] + up(got[place, 0])).astype(low)
        far_copy(j).start()

    def collect(j):
        place = shard_of(j)[2]
        far_copy(j).wait_recv()
        columns = columns_of(place)
        own[:, columns] += up(got[place, 1]) + up(far[place])

    count = 2 * pairs
    rest = steps[early:]
    for j in range(count):
        need = j // 2
        while rest and rest[0][0] <= need:
            chain_step(*rest.pop(0))
        product(j)
        if j >= 2:
            pass_on(j - 2)
        if j >= 4:
            collect(j - 4)
    for j in (count - 2, count - 1):
        pass_on(j)
    for j in range(count - 4, count):
        collect(j)

    def map_copy(i):
        return pltpu.make_async_copy(
            maps.at[i // 2, i % 2], map_ref.at[pl.ds(i * shard, shard), :], map_sem.at[i]
        )

    for i in range(count):
        map_copy(i).start()
    sent = []

    def go(copy):
        copy.start()
        sent.append(copy)
        return copy

    def rows_of(u):
        return pl.ds(u * size, size)

    gain_out_ref[...] = jnp.zeros_like(gain_out_ref)
    ffn_gain, ple_gain = gain_ref[0:1, :], gain_ref[1:2, :]
    mean = lambda v: jnp.mean(v, -1, keepdims=True)
    total = lambda v: jnp.sum(v, 0, keepdims=True)
    rows_x, rows_y = [], []
    for u in range(parts):
        at = rows_of(u)
        f = own[at, :]
        f_inverse = lax.rsqrt(mean(f * f) + eps)
        second = (mixed_ref[at, :] + f * f_inverse * ffn_gain).astype(low)
        second_ref[at, :] = second
        gate = mm(second, ple_gate_ref[...])
        bend = jnp.tanh(slope * (gate + cubic * gate * gate * gate))
        gate_slope = 0.5 * (1.0 + bend) + 0.5 * gate * (1.0 - bend * bend) * slope * (
            1.0 + 3.0 * cubic * gate * gate
        )
        given = up(ple_input_ref[at, :])
        ple_mixed = (0.5 * gate * (1.0 + bend) * given).astype(low)
        ple_mixed_ref[at, :] = ple_mixed
        proj = mm_nt(ple_mixed, ple_proj_ref[...])
        proj_inverse = lax.rsqrt(mean(proj * proj) + eps)
        out_ref[at, :] = (up(second) + proj * proj_inverse * ple_gain).astype(low)
        incoming = up(cotangent_ref[at, :])
        gain_out_ref[1:2, :] += total(incoming * proj * proj_inverse)
        scaled = incoming * ple_gain
        grad_proj = proj_inverse * (
            scaled - proj * (proj_inverse * proj_inverse * mean(scaled * proj))
        )
        grad_ple = grad_proj.astype(low)
        grad_ple_ref[at, :] = grad_ple
        grad_gate = (mm(grad_ple, ple_proj_ref[...]) * given * gate_slope).astype(low)
        grad_gate_ref[at, :] = grad_gate
        grad_second = incoming + mm_nt(grad_gate, ple_gate_ref[...])
        grad_second_ref[at, :] = grad_second
        f = own[at, :]
        gain_out_ref[0:1, :] += total(grad_second * f * f_inverse)
        scaled = grad_second * ffn_gain
        grad_f = f_inverse * (scaled - f * (f_inverse * f_inverse * mean(scaled * f)))
        rows_ref[0, at, :] = grad_f.astype(low)
        pair_x, pair_y = [], []
        for order in range(2):
            for copies, device, send_sem, recv_sem, index, part in (
                (pair_x, by_x, gx_s, gx_r, 1, (left, right)[order]),
                (pair_y, by_y, gy_s, gy_r, 2, (right, left)[order]),
            ):
                copies.append(
                    go(
                        remote(
                            rows_ref.at[0, at, part],
                            rows_ref.at[index, at, part],
                            send_sem.at[u, order],
                            recv_sem.at[u, order],
                            device,
                        )
                    )
                )
        rows_x.append(pair_x)
        rows_y.append(pair_y)

    forwards = []
    for u in range(parts):
        at = rows_of(u)
        rows_x[u][0].wait_recv()
        forwards.append(
            go(
                remote(
                    rows_ref.at[1, at, left],
                    rows_ref.at[3, at, left],
                    fy_s.at[u],
                    fy_r.at[u],
                    by_y,
                )
            )
        )
        rows_y[u][0].wait_recv()
        forwards.append(
            go(
                remote(
                    rows_ref.at[2, at, right],
                    rows_ref.at[3, at, right],
                    fx_s.at[u],
                    fx_r.at[u],
                    by_x,
                )
            )
        )
    for u in range(parts):
        rows_x[u][1].wait_recv()
        rows_y[u][1].wait_recv()
    for copy in forwards:
        copy.wait_recv()

    def stage_copy(i, slot):
        at = pl.ds(pl.multiple_of(i * tile, tile), tile)
        return pltpu.make_async_copy(stage.at[slot], grad_map_ref.at[at, :], stage_sem.at[slot])

    rows_copy = pltpu.make_async_copy(rows_ref, rows_out_ref, load_sem.at[0])
    rows_copy.start()

    def grad_tile(i, carry):
        slot = i % 2

        @pl.when(i >= 2)
        def _():
            stage_copy(i - 2, slot).wait()

        columns = pl.ds(pl.multiple_of(i * tile, tile), tile)
        v = rows_ref[:, :, columns].reshape(4 * block, tile)
        for j in range(0, span, span // 2):
            stage[slot, :, j : j + span // 2] = mm_tn(v, hidden_ref[:, j : j + span // 2]).astype(low)
        stage_copy(i, slot).start()
        return carry

    lax.fori_loop(0, count, grad_tile, 0)
    stage_copy(count - 2, 0).wait()
    stage_copy(count - 1, 1).wait()
    for copy in sent:
        copy.wait_send()
    rows_copy.wait()
    for i in range(count):
        map_copy(i).wait()
    for j in range(count):
        near_copy(j).wait_send()
        far_copy(j).wait_send()
    for k in range(2):
        to_sibling(pair, k, True).wait_send()
        for t in range(1, pairs):
            pl.when(pair - t >= 0)(lambda t=t, k=k: to_sibling(pair - t, k).wait_send())
            pl.when(pair + t < pairs)(lambda t=t, k=k: to_sibling(pair + t, k).wait_send())
            pl.when(sends_right(t))(lambda t=t, k=k: pass_right(t, k).wait_send())
            pl.when(sends_left(t))(lambda t=t, k=k: pass_left(t, k).wait_send())


def middle(pairs, h_blocks, in_maps, planes, mixed, gains, ple, ple_input, cotangent):
    block, width = mixed.shape
    span = in_maps.shape[2]
    shard = planes.shape[1]
    parts, length = 2, 4 * block
    count = 2 * pairs
    dma = lambda *n: pltpu.SemaphoreType.DMA(n)
    vmem = pl.BlockSpec(memory_space=pltpu.VMEM)
    anywhere = pl.BlockSpec(memory_space=pl.ANY)
    shapes = (
        ((4, block, width), low),
        ((width, span), low),
        ((width, span), low),
        ((length, span), full),
        ((length, span), full),
        ((block, width), low),
        ((block, width), low),
        ((block, width), full),
        ((block, width), low),
        ((block, PLE), low),
        ((block, PLE), low),
        ((8, width), full),
    )
    return pl.pallas_call(
        functools.partial(middle_kernel, pairs, block, parts),
        out_shape=tuple(jax.ShapeDtypeStruct(*v) for v in shapes),
        in_specs=[anywhere] * 7 + [vmem] * 6,
        out_specs=tuple(anywhere if i < 5 else vmem for i in range(len(shapes))),
        scratch_shapes=[
            pltpu.VMEM((4, block, width), low),
            pltpu.VMEM((2, 2, width, 256), low),
            pltpu.VMEM((2, 2, length, 256), full),
            pltpu.VMEM((length, span), low),
            pltpu.VMEM((pairs, 2, shard, span), low),
            pltpu.VMEM((4, block, shard), full),
            pltpu.VMEM((block, width), full),
            pltpu.VMEM((count, block, shard), full),
            pltpu.VMEM((count, 2, block, shard), low),
            pltpu.VMEM((count, 2, block, shard), low),
            pltpu.VMEM((count, block, shard), low),
            pltpu.VMEM((count, block, shard), low),
            pltpu.VMEM((2, 256, span), low),
            dma(6),
            dma(2),
            dma(2, 2),
            dma(2),
            dma(count),
            *[dma(2 * (pairs - 1))] * 4,
            *[dma(count)] * 2,
            *[dma(count)] * 4,
            *[dma(parts, 2)] * 4,
            *[dma(parts)] * 4,
        ],
        compiler_params=pltpu.CompilerParams(
            collective_id=1, has_side_effects=True, vmem_limit_bytes=62 << 20
        ),
        cost_estimate=pl.CostEstimate(
            flops=16 * block * width * span, bytes_accessed=100 << 20, transcendentals=0
        ),
    )(
        *h_blocks,
        in_maps,
        planes,
        mixed,
        jnp.pad(jnp.stack(gains), ((0, 6), (0, 0))),
        ple[:, :PLE],
        ple[:, PLE:],
        ple_input,
        cotangent,
    )


def middle_plain(ranks, h_blocks, in_maps, planes, mixed, gains, ple, ple_input, cotangent):
    block = mixed.shape[0]
    down_map = lax.all_gather(planes[2], "fsdp", axis=0, tiled=True)
    gate_up = dot(whole_rows(h_blocks), in_maps, ((1,), (1,)))
    gate_part, up_part = gate_up[:, 0], gate_up[:, 1]
    hidden = (gelu_tanh(gate_part) * up_part).astype(low)
    parts = mm_nt(hidden, down_map).astype(low)
    ffn_out = sum_seq([parts[k * block : (k + 1) * block] for k in range(ranks)], ranks)
    ffn_normed, ffn_inverse = norm_rows(ffn_out, gains[0])
    h_second = (mixed + ffn_normed).astype(low)
    ple_gate = mm(h_second, ple[:, :PLE])
    ple_input = ple_input.astype(full)
    ple_mixed = (gelu_tanh(ple_gate) * ple_input).astype(low)
    ple_proj = mm_nt(ple_mixed, ple[:, PLE:])
    ple_normed, ple_inverse = norm_rows(ple_proj, gains[1])
    hidden_out = (h_second.astype(full) + ple_normed).astype(low)
    grad_out = cotangent.astype(full)
    grad_ple_proj, gain_grad_five = norm_back(ple_proj, ple_inverse, gains[1], grad_out)
    grad_ple_low = grad_ple_proj.astype(low)
    grad_ple_mixed = mm(grad_ple_low, ple[:, PLE:])
    unused_gelu, gelu_pull = jax.vjp(gelu_tanh, ple_gate)
    grad_ple_gate = gelu_pull(grad_ple_mixed * ple_input)[0].astype(low)
    grad_second = grad_out + mm_nt(grad_ple_gate, ple[:, :PLE])
    grad_ffn, gain_grad_four = norm_back(ffn_out, ffn_inverse, gains[0], grad_second)
    rows = whole_rows(gather_seq(grad_ffn.astype(low), ranks))
    return (
        rows,
        mm_tn(rows, hidden).astype(low),
        down_map,
        gate_part,
        up_part,
        hidden_out,
        h_second,
        grad_second,
        grad_ple_low,
        ple_mixed,
        grad_ple_gate,
        jnp.stack([gain_grad_four, gain_grad_five]),
    )


def back_kernel(
    block,
    gate_ref,
    up_ref,
    maps_ref,
    rows_own,
    rows_x,
    rows_y,
    rows_left,
    rows_right,
    grad_maps_ref,
    sum_ref,
    maps,
    keep_left,
    keep_right,
    send_x,
    send_y,
    got_x,
    got_y,
    relay_x,
    relay_y,
    far_x,
    far_y,
    stage,
    map_sem,
    stage_sem,
    sx_s,
    sx_r,
    sy_s,
    sy_r,
    rx_s,
    rx_r,
    ry_s,
    ry_r,
):
    rank = lax.axis_index("seq")
    fsdp_index = lax.axis_index("fsdp")
    by_x, by_y = (flip(rank, 1, 4), fsdp_index), (flip(rank, 2, 4), fsdp_index)
    width, span = maps_ref.shape[1], maps_ref.shape[2]
    tile = 256
    tiles = width // tile
    each = tiles // 2
    up = lambda v: v.astype(full)

    def columns_of(i):
        return pl.ds(pl.multiple_of(i * tile, tile), tile)

    def remote(source, target, send, recv, device):
        return pltpu.make_async_remote_copy(
            src_ref=source,
            dst_ref=target,
            send_sem=send,
            recv_sem=recv,
            device_id=device,
            device_id_type=MESH,
        )

    def map_copy(i):
        return pltpu.make_async_copy(
            maps_ref.at[:, columns_of(i), :], maps.at[:, columns_of(i), :], map_sem.at[i]
        )

    def near_x(j):
        return remote(send_x.at[j], got_x.at[j], sx_s.at[j], sx_r.at[j], by_x)

    def near_y(j):
        return remote(send_y.at[j], got_y.at[j], sy_s.at[j], sy_r.at[j], by_y)

    def last_x(j):
        return remote(relay_x.at[j], far_x.at[j], rx_s.at[j], rx_r.at[j], by_x)

    def last_y(j):
        return remote(relay_y.at[j], far_y.at[j], ry_s.at[j], ry_r.at[j], by_y)

    for j in range(each):
        map_copy(j).start()
        map_copy(j + each).start()

    barrier = pltpu.get_barrier_semaphore()
    for device in (by_x, by_y):
        pl.semaphore_signal(barrier, inc=1, device_id=device, device_id_type=MESH)
    pl.semaphore_wait(barrier, 2)

    def product(i):
        map_copy(i).wait()
        v = mm_nt(gate_ref[...], maps[0, columns_of(i), :])
        v = v + mm_nt(up_ref[...], maps[1, columns_of(i), :])
        return v.reshape(4, block, tile)

    def send_tiles(j, carry):
        v = product(j)
        sum_ref[:, columns_of(j)] = v[0]
        keep_left[j] = v[2]
        send_x[j, 0] = v[3].astype(low)
        send_x[j, 1] = v[1].astype(low)
        near_x(j).start()
        v = product(j + each)
        sum_ref[:, columns_of(j + each)] = v[0]
        keep_right[j] = v[1]
        send_y[j, 0] = v[3].astype(low)
        send_y[j, 1] = v[2].astype(low)
        near_y(j).start()
        return carry

    lax.fori_loop(0, each, send_tiles, 0)

    def stage_copy(i, slot):
        return pltpu.make_async_copy(
            stage.at[slot], grad_maps_ref.at[:, columns_of(i), :], stage_sem.at[slot]
        )

    def grad_tile(i, j, far_ref):
        slot = j % 2
        pl.when(i >= 2)(lambda: stage_copy(i - 2, slot).wait())
        near = columns_of(i)
        v = jnp.concatenate(
            [rows_own[:, near], rows_x[:, near], rows_y[:, near], far_ref[:, columns_of(j)]], 0
        )
        for k in range(0, span, span // 2):
            part = slice(k, k + span // 2)
            stage[slot, 0, :, part] = mm_tn(v, gate_ref[:, part]).astype(low)
            stage[slot, 1, :, part] = mm_tn(v, up_ref[:, part]).astype(low)
        stage_copy(i, slot).start()

    def left_tile(j, carry):
        grad_tile(j, j, rows_left)
        near_x(j).wait_recv()
        relay_y[j] = (keep_left[j] + up(got_x[j, 0])).astype(low)
        last_y(j).start()
        near_y(j).wait_recv()
        relay_x[j] = (keep_right[j] + up(got_y[j, 0])).astype(low)
        last_x(j).start()
        return carry

    def right_tile(j, carry):
        grad_tile(j + each, j, rows_right)
        last_y(j).wait_recv()
        sum_ref[:, columns_of(j)] += up(got_x[j, 1]) + up(far_y[j])
        last_x(j).wait_recv()
        sum_ref[:, columns_of(j + each)] += up(got_y[j, 1]) + up(far_x[j])
        return carry

    lax.fori_loop(0, each, left_tile, 0)
    lax.fori_loop(0, each, right_tile, 0)
    stage_copy(tiles - 2, 0).wait()
    stage_copy(tiles - 1, 1).wait()

    def sent(j, carry):
        for copy in (near_x(j), near_y(j), last_x(j), last_y(j)):
            copy.wait_send()
        return carry

    lax.fori_loop(0, each, sent, 0)


def back(grad_gate, grad_up, in_maps, h_blocks):
    length, span = grad_gate.shape
    block, width = h_blocks[0].shape
    each = width // 512
    dma = pltpu.SemaphoreType.DMA
    vmem = pl.BlockSpec(memory_space=pltpu.VMEM)
    anywhere = pl.BlockSpec(memory_space=pl.ANY)
    keep = pltpu.VMEM((each, block, 256), full)
    pieces = pltpu.VMEM((each, 2, block, 256), low)
    singles = pltpu.VMEM((each, block, 256), low)
    return pl.pallas_call(
        functools.partial(back_kernel, block),
        out_shape=(
            jax.ShapeDtypeStruct((2, width, span), low),
            jax.ShapeDtypeStruct((block, width), full),
        ),
        in_specs=[vmem, vmem, anywhere] + [vmem] * 5,
        out_specs=(anywhere, vmem),
        scratch_shapes=[
            pltpu.VMEM((2, width, span), low),
            keep,
            keep,
            *[pieces] * 4,
            *[singles] * 4,
            pltpu.VMEM((2, 2, 256, span), low),
            dma((width // 256,)),
            dma((2,)),
            *[dma((each,))] * 8,
        ],
        compiler_params=pltpu.CompilerParams(
            collective_id=3, has_side_effects=True, vmem_limit_bytes=58 << 20
        ),
        cost_estimate=pl.CostEstimate(
            flops=8 * length * width * span, bytes_accessed=50 << 20, transcendentals=0
        ),
    )(grad_gate, grad_up, in_maps, *h_blocks)


def finish_kernel(sizes, with_x, *refs):
    ranks, pairs = sizes["seq"], sizes["pair"]
    refs = list(refs)

    def some(count):
        head = refs[:count]
        del refs[:count]
        return head

    shared = ranks == 4
    owns = some(3 + shared)
    x_ref, branch_ref, tokens_ref, base_ref, gain_ref = some(5) if with_x else [None] * 5
    query_ref, key_ref, value_ref, out_ref, ple_ref, laurel_ref, small_ref = some(7)
    (input_ref,) = some(1) if with_x else [None]
    sums, from_left, from_right = some(3 + shared), some(3 + shared), some(3 + shared)
    got_last, got_out = some(2)
    (got_pair,) = some(1) if shared else [None]
    if with_x:
        got_x, got_y, relay_x, relay_y, far_x, far_y = some(6)
    core_s, core_r, right_s, right_r, left_s, left_r, last_s, last_r, out_s, out_r = some(10)
    if with_x:
        x_s, x_r = some(2)
    if shared:
        pair_s, pair_r = some(2)

    rank = lax.axis_index("seq")
    fsdp_index = lax.axis_index("fsdp")
    pair, core = fsdp_index // 2, fsdp_index % 2
    sibling = (rank, pair * 2 + 1 - core)
    on_seq = lambda k: (flip(rank, k, ranks), fsdp_index)
    up = lambda v: v.astype(full)

    def remote(source, target, send, recv, device):
        return pltpu.make_async_remote_copy(
            src_ref=source,
            dst_ref=target,
            send_sem=send,
            recv_sem=recv,
            device_id=device,
            device_id_type=MESH,
        )

    barrier = pltpu.get_barrier_semaphore()
    devices = [on_seq(k) for k in range(1, ranks)]
    devices += [(rank, ((pair + i) % pairs) * 2 + core) for i in range(1, pairs)]
    for device in devices + [sibling]:
        pl.semaphore_signal(barrier, inc=1, device_id=device, device_id_type=MESH)
    pl.semaphore_wait(barrier, len(devices) + 1)

    sent = []

    def go(copy):
        copy.start()
        sent.append(copy)
        return copy

    half_ranks = ranks // 2
    pieces = [
        (1, slice(0, ranks)),
        (2, None),
        (0, slice(0, half_ranks)),
        (0, slice(half_ranks, ranks)),
    ] + [(3, None)] * shared
    count = len(pieces)

    def view(group, lead, piece):
        number, rows = pieces[piece]
        ref = group[number]
        return ref.at[lead] if rows is None else ref.at[lead, rows]

    order = [i // 2 if i % 2 else pairs - 1 - i // 2 for i in range(pairs)]

    def swap(chip, piece):
        slot = chip * count + piece
        return remote(
            view(owns, chip * 2 + 1 - core, piece),
            view(sums, chip, piece),
            core_s.at[slot],
            core_r.at[slot],
            sibling,
        )

    for chip in order:
        for piece in range(count):
            go(swap(chip, piece))
    if with_x:
        half = x_ref.shape[2] // 2
        left, right = slice(0, half), slice(half, 2 * half)
        by_x, by_y = on_seq(1), on_seq(2)
        near = []
        for slot, block, columns, target, device in (
            (0, 3, left, got_x.at[0], by_x),
            (1, 3, right, got_y.at[0], by_y),
            (2, 1, left, got_x.at[1], by_x),
            (3, 2, right, got_y.at[1], by_y),
        ):
            near.append(
                go(remote(x_ref.at[block, :, columns], target, x_s.at[slot], x_r.at[slot], device))
            )

    def whole_chip(chip, piece):
        target = view(sums, chip, piece)
        remote(
            target, target, core_s.at[0], core_r.at[chip * count + piece], sibling
        ).wait_recv()
        target[...] = (up(target[...]) + up(view(owns, chip * 2 + core, piece)[...])).astype(low)

    def pass_right(t, piece):
        slot = (t - 1) * count + piece
        return remote(
            view(sums, pair + pairs - t, piece),
            view(from_left, t - 1, piece),
            right_s.at[slot],
            right_r.at[slot],
            (rank, fsdp_index + 2),
        )

    def pass_left(t, piece):
        slot = (t - 1) * count + piece
        return remote(
            view(sums, pair - (pairs - t), piece),
            view(from_right, t - 1, piece),
            left_s.at[slot],
            left_r.at[slot],
            (rank, fsdp_index - 2),
        )

    def add_left(t, piece, target):
        got = view(from_left, t - 1, piece)
        slot = (t - 1) * count + piece
        remote(got, got, right_s.at[slot], right_r.at[slot], sibling).wait_recv()
        target[...] = (up(target[...]) + up(got[...])).astype(low)

    def add_right(t, piece, target):
        got = view(from_right, t - 1, piece)
        slot = (t - 1) * count + piece
        remote(got, got, left_s.at[slot], left_r.at[slot], sibling).wait_recv()
        target[...] = (up(target[...]) + up(got[...])).astype(low)

    mirrored = pairs - 1 - pair
    relays = []
    for t in range(1, pairs):
        for piece in range(count):

            def to_right(t=t, piece=piece):
                chip = pair + pairs - t
                whole_chip(chip, piece)
                if t > 1:
                    pl.when(pair > 0)(lambda: add_left(t - 1, piece, view(sums, chip, piece)))
                pass_right(t, piece).start()

            def to_left(t=t, piece=piece):
                chip = pair - (pairs - t)
                whole_chip(chip, piece)
                if t > 1:
                    pl.when(mirrored > 0)(lambda: add_right(t - 1, piece, view(sums, chip, piece)))
                pass_left(t, piece).start()

            pl.when(t >= pair + 1)(to_right)
            pl.when(t >= mirrored + 1)(to_left)
        if with_x and t == 1:
            near[0].wait_recv()
            relay_y[...] = (up(x_ref[2, :, left]) + up(got_x[0])).astype(low)
            relays.append(go(remote(relay_y, far_y, x_s.at[4], x_r.at[4], by_y)))
            near[1].wait_recv()
            relay_x[...] = (up(x_ref[1, :, right]) + up(got_y[0])).astype(low)
            relays.append(go(remote(relay_x, far_x, x_s.at[5], x_r.at[5], by_x)))
            for piece in range(count):
                whole_chip(pair, piece)
    if with_x:
        for copy in near[2:] + relays:
            copy.wait_recv()
        mean = lambda v: jnp.mean(v, -1, keepdims=True)
        step = x_ref.shape[1] // 2
        for i in range(2):
            at = slice(i * step, (i + 1) * step)
            incoming = branch_ref[at, :] + jnp.concatenate(
                [
                    up(x_ref[0, at, left]) + up(got_x[1, at, :]) + up(far_y[at, :]),
                    up(x_ref[0, at, right]) + up(got_y[1, at, :]) + up(far_x[at, :]),
                ],
                1,
            )
            v = up(tokens_ref[at, :])
            inverse = lax.rsqrt(mean(v * v) + eps)
            scaled = incoming * gain_ref[0:1, :]
            input_ref[at, 0, :] = base_ref[at, :] * root_half + inverse * (
                scaled - v * (inverse * inverse * mean(scaled * v))
            )
    else:
        for piece in range(count):
            whole_chip(pair, piece)

    for piece in range(count):
        target = view(sums, pair, piece)
        pl.when(pair > 0)(lambda: add_left(pairs - 1, piece, target))
        pl.when(mirrored > 0)(lambda: add_right(pairs - 1, piece, target))

    last_sum, out_sum, rest_sum = [ref.at[pair] for ref in sums[:3]]
    across = []
    for k in range(1, ranks):
        peer = flip(rank, k, ranks)
        across.append(
            (
                go(remote(last_sum.at[peer], got_last.at[k], last_s.at[k], last_r.at[k], on_seq(k))),
                go(remote(out_sum.at[peer], got_out.at[k], out_s.at[k], out_r.at[k], on_seq(k))),
            )
        )
    def put_pair(group, v):
        head = pl.ds(pl.multiple_of(group * HEAD_DIM, HEAD_DIM), HEAD_DIM)
        key_ref[:, head] = v[:, :HEAD_DIM]
        value_ref[:, head] = v[:, HEAD_DIM:]

    def pair_copy(k):
        to = flip(rank, k, ranks)
        return remote(
            sums[3].at[pair, to % 2],
            got_pair.at[rank // 2],
            pair_s.at[k],
            pair_r.at[k],
            on_seq(k),
        )

    goes = lambda k: flip(rank, k, ranks) // 2 == rank % 2
    if shared:
        for k in range(1, ranks):
            pl.when(goes(k))(lambda k=k: pair_copy(k).start())
    ple_ref[...] = up(rest_sum[:, : 2 * PLE])
    laurel_ref[...] = up(rest_sum[:, 2 * PLE : 2 * PLE + 2 * LR])
    small_ref[...] = up(rest_sum[:, 2 * PLE + 2 * LR :])
    if not shared:
        key_ref[...] = jnp.zeros_like(key_ref)
        value_ref[...] = jnp.zeros_like(value_ref)
    q_width = out_sum.shape[2]
    for k in range(ranks):
        if k:
            for copy in across[k - 1]:
                copy.wait_recv()
            last, out = up(got_last[k]), up(got_out[k])
        else:
            last, out = up(last_sum[rank]), up(out_sum[rank])
        sender = flip(rank, k, ranks)
        columns = pl.ds(pl.multiple_of(sender * q_width, q_width), q_width)
        group = sender * (QUERY_HEADS // ranks) // (QUERY_HEADS // KEY_VALUE_HEADS)
        head = pl.ds(pl.multiple_of(group * HEAD_DIM, HEAD_DIM), HEAD_DIM)
        query_ref[:, columns] = last[:, :q_width]
        out_ref[:, columns] = out
        if not shared:
            key_ref[:, head] += last[:, -2 * HEAD_DIM : -HEAD_DIM]
            value_ref[:, head] += last[:, -HEAD_DIM:]
    if shared:
        pl.when(rank // 2 == rank % 2)(
            lambda: put_pair(rank // 2, up(sums[3][pair, rank % 2]))
        )
        for k in range(1, ranks):

            def arrived(k=k):
                sender = flip(rank, k, ranks)
                target = got_pair.at[sender // 2]
                remote(target, target, pair_s.at[k], pair_r.at[k], sibling).wait_recv()
                put_pair(sender // 2, up(got_pair[sender // 2]))

            pl.when(flip(rank, k, ranks) % 2 == rank // 2)(arrived)
        for k in range(1, ranks):
            pl.when(goes(k))(lambda k=k: pair_copy(k).wait_send())

    for t in range(1, pairs):
        for piece in range(count):
            pl.when(t >= pair + 1)(lambda t=t, piece=piece: pass_right(t, piece).wait_send())
            pl.when(t >= mirrored + 1)(lambda t=t, piece=piece: pass_left(t, piece).wait_send())
    for copy in sent:
        copy.wait_send()


def finish(sizes, last, out, rest, key_value, x=None):
    ranks, pairs = sizes["seq"], sizes["pair"]
    rows = last.shape[2]
    shared = ranks == 4
    if shared:
        arrays = [last, out, rest, key_value]
    else:
        arrays = [jnp.concatenate([last, key_value], 3), out, rest]
    vmem = pl.BlockSpec(memory_space=pltpu.VMEM)
    dma = lambda n: pltpu.SemaphoreType.DMA((n,))
    width = KEY_VALUE_HEADS * HEAD_DIM
    shapes = [
        (rows, QUERY_HEADS * HEAD_DIM),
        (rows, width),
        (rows, width),
        (rows, QUERY_HEADS * HEAD_DIM),
        (rows, 2 * PLE),
        (rows, 2 * LR),
        (rows, rest.shape[-1] - 2 * PLE - 2 * LR),
    ]
    scratch = [pltpu.VMEM((pairs,) + v.shape[1:], low) for v in arrays]
    scratch += [pltpu.VMEM((pairs - 1,) + v.shape[1:], low) for v in arrays] * 2
    scratch += [pltpu.VMEM((ranks,) + v.shape[2:], low) for v in arrays[:2]]
    if shared:
        scratch.append(pltpu.VMEM((KEY_VALUE_HEADS,) + key_value.shape[2:], low))
    if x is not None:
        block, columns = x[0].shape[1], x[0].shape[2] // 2
        shapes.append((block, 1, 2 * columns))
        scratch += [pltpu.VMEM((2, block, columns), low)] * 2
        scratch += [pltpu.VMEM((block, columns), low)] * 4
    count = 4 + shared
    scratch += [dma(count * pairs)] * 2 + [dma(count * (pairs - 1))] * 4 + [dma(ranks)] * 4
    if x is not None:
        scratch += [dma(6)] * 2
    if shared:
        scratch += [dma(ranks)] * 2
    operands = arrays + list(x or ())
    return pl.pallas_call(
        functools.partial(finish_kernel, sizes, x is not None),
        out_shape=tuple(jax.ShapeDtypeStruct(v, full) for v in shapes),
        in_specs=[vmem] * len(operands),
        out_specs=(vmem,) * len(shapes),
        scratch_shapes=scratch,
        compiler_params=pltpu.CompilerParams(
            collective_id=2, has_side_effects=True, vmem_limit_bytes=56 << 20
        ),
    )(*operands)


def body(
    sizes,
    hidden_in,
    per_layer_input,
    segment_ids,
    positions,
    out_cotangent,
    w_query,
    key_matrix,
    value_matrix,
    w_out_t,
    laurel_maps,
    per_layer_maps,
    norm_gains,
    head_gains,
    w_mlp,
):
    ranks, pairs = sizes["seq"], sizes["pair"]
    block, _, width = hidden_in.shape
    rows = w_query.shape[0]
    q_width = QUERY_HEADS // ranks * HEAD_DIM
    share = QUERY_HEADS // KEY_VALUE_HEADS
    kv_of = [rank * (QUERY_HEADS // ranks) // share for rank in range(ranks)]
    length = block * ranks
    rank = lax.axis_index("seq")
    relative = [rank ^ k for k in range(ranks)]
    cut = lambda v: [v[k * block : (k + 1) * block] for k in range(ranks)]

    by_rank = lambda m: m.reshape(rows, ranks, q_width).transpose(1, 0, 2)
    by_kv = lambda m: jnp.stack([m[:, j * HEAD_DIM : (j + 1) * HEAD_DIM] for j in kv_of])
    head_pack = jnp.concatenate(
        [by_rank(w_query), by_kv(key_matrix), by_kv(value_matrix), by_rank(w_out_t)], 2
    )
    head_rows = head_gains.shape[0]
    small = jnp.concatenate(
        [norm_gains, jnp.pad(head_gains, ((0, rows - head_rows), (0, 0)))], 1
    )
    small = jnp.pad(small, ((0, 0), (0, 128 - small.shape[1])))
    rest_pack = jnp.concatenate([laurel_maps, small], 1)
    marks = jnp.pad(jnp.concatenate([segment_ids.T, positions.T], 0), ((0, 6), (0, 0)))
    x_local = hidden_in.reshape(block, width)

    planes = jnp.moveaxis(w_mlp, 1, 0)
    head_all, rest_all, marks_all, x_all, in_rows = gather_weights(
        sizes, head_pack, rest_pack, marks, x_local, planes
    )
    in_maps = lax.all_gather(in_rows, "fsdp", axis=1, tiled=True)
    x_all = x_all.reshape(length, width)
    head_all = head_all.reshape(width, -1)
    rest_all = rest_all.reshape(width, -1)
    qkv_map, out_map = head_all[:, :-q_width], head_all[:, -q_width:]
    laurel = rest_all[:, : 2 * LR]
    gains = rest_all[:, 2 * LR :].astype(full)
    gain = [gains[:, i] for i in range(6)]
    head_scale = gains[:, 6:8].reshape(-1, rows, 2)[:, :head_rows].reshape(HEAD_DIM, 2)

    tokens_all = x_all.astype(full)
    normed_all = norm_rows(tokens_all, gain[0])[0].astype(low)
    tokens = x_local.astype(full)
    x_normed_f, x_inverse = norm_rows(tokens, gain[0])
    normed = x_normed_f.astype(low)
    indices = jnp.concatenate([r * block + jnp.arange(block) for r in relative])
    cos_table, sin_table = rope_tables(marks_all[:, 1].reshape(length))
    codes = marks_all[:, 0].reshape(length) * (4 * length) + indices
    qkv = mm(normed_all, qkv_map)
    q_heads, k_head, v_head, attn_in, log_total = attend(
        ranks, qkv, codes, cos_table, sin_table, head_scale.T
    )
    attn_lin = sum_seq(cut(mm_nt(attn_in, out_map).astype(low)), ranks)

    attn_normed, attn_inverse = norm_rows(attn_lin, gain[1])
    laurel_low = mm(normed, laurel[:, :LR]).astype(low)
    laurel_high = mm_nt(laurel_low, laurel[:, LR:])
    laurel_normed, laurel_inverse = norm_rows(laurel_high, gain[2])
    mixed = (tokens + attn_normed + (normed.astype(full) + laurel_normed)) * root_half
    h_normed_f, h_inverse = norm_rows(mixed, gain[3])
    h_blocks = gather_seq(h_normed_f.astype(low), ranks)
    h_blocks, per_layer_maps = lax.optimization_barrier((h_blocks, per_layer_maps))
    ple = gather_everywhere(per_layer_maps, ranks, pairs)
    run_middle = functools.partial(
        *((middle, pairs) if ranks == 4 else (middle_plain, ranks))
    )
    (
        grad_ffn_rows,
        down_grad,
        down_map,
        gate_part,
        up_part,
        hidden_out,
        h_second,
        grad_second,
        grad_ple_low,
        ple_mixed,
        grad_ple_gate,
        ffn_gain_grads,
    ) = run_middle(
        h_blocks,
        in_maps,
        planes,
        mixed,
        gain[4:6],
        ple,
        per_layer_input.reshape(block, PLE),
        out_cotangent.reshape(block, width),
    )
    gain_grad_four, gain_grad_five = ffn_gain_grads[0], ffn_gain_grads[1]
    grad_ffn_rows = grad_ffn_rows.reshape(length, width)
    down_sum = lax.psum_scatter(down_grad, "fsdp", scatter_dimension=0, tiled=True)
    grad_ffn_rows, down_grad = lax.optimization_barrier((grad_ffn_rows, down_grad))
    grad_hidden = mm(grad_ffn_rows, down_map)
    gate_act, act_pull = jax.vjp(gelu_tanh, gate_part)
    grad_gate = act_pull(grad_hidden * up_part)[0].astype(low)
    grad_up = (grad_hidden * gate_act).astype(low)
    if ranks == 4:
        in_grad, grad_h_normed = back(grad_gate, grad_up, in_maps, h_blocks)
    else:
        h_part = mm_nt(grad_gate, in_maps[0]) + mm_nt(grad_up, in_maps[1])
        h_part = h_part.astype(low)
        grad_h_normed = sum_seq(cut(h_part), ranks)
        h_rows = whole_rows(h_blocks)
        in_grad = jnp.stack([mm_tn(h_rows, grad_gate), mm_tn(h_rows, grad_up)]).astype(low)
    in_sum = lax.psum_scatter(in_grad, "fsdp", scatter_dimension=1, tiled=True)
    in_sum = jnp.moveaxis(in_sum, 0, 1)

    grad_ple_up = mm_tn(grad_ple_low, ple_mixed)
    grad_ple_down = mm_tn(h_second, grad_ple_gate)
    grad_mixed_norm, gain_grad_three = norm_back(mixed, h_inverse, gain[3], grad_h_normed)
    grad_mixed = grad_second + grad_mixed_norm
    grad_branch = grad_mixed * root_half
    grad_attn, gain_grad_one = norm_back(attn_lin, attn_inverse, gain[1], grad_branch)
    grad_attn_blocks = gather_seq(grad_attn.astype(low), ranks)
    grad_laurel_high, gain_grad_two = norm_back(
        laurel_high, laurel_inverse, gain[2], grad_branch
    )
    grad_high_low = grad_laurel_high.astype(low)
    grad_laurel_up = mm_tn(grad_high_low, laurel_low)
    grad_laurel_low = mm(grad_high_low, laurel[:, LR:]).astype(low)
    grad_laurel_down = mm_tn(normed, grad_laurel_low)

    x_here = grad_branch + mm_nt(grad_laurel_low, laurel[:, :LR])
    gain_grad_zero = jnp.sum(x_here * tokens * x_inverse, 0)
    small_grad = jnp.stack(
        [
            gain_grad_zero,
            gain_grad_one,
            gain_grad_two,
            gain_grad_three,
            gain_grad_four,
            gain_grad_five,
        ],
        1,
    )
    small_grad = jnp.pad(small_grad, ((0, 0), (0, 128 - small_grad.shape[1])))
    rest_grad = jnp.concatenate(
        [grad_ple_down, grad_ple_up, grad_laurel_down, grad_laurel_up, small_grad], 1
    ).astype(low)
    rest_grad = rest_grad.reshape(ranks, -1, rest_grad.shape[1])
    rest_grad, grad_attn_blocks = lax.optimization_barrier((rest_grad, grad_attn_blocks))
    rest_others = [permute(take(rest_grad, 0, relative[k]), "seq", k) for k in range(1, ranks)]
    out_grad = weight_grad(ranks, pairs * 2, grad_attn_blocks, attn_in)
    grad_heads = mm(whole_rows(grad_attn_blocks), out_map).astype(low)
    grad_qkv, grad_gains = attend_back(
        ranks,
        qkv,
        q_heads,
        k_head,
        v_head,
        grad_heads,
        log_total,
        codes,
        cos_table,
        sin_table,
        head_scale.T,
    )
    grad_head_scale = grad_gains[:2].T
    rest_others, grad_qkv = lax.optimization_barrier((rest_others, grad_qkv))
    rest_own = sum((v.astype(full) for v in rest_others), take(rest_grad, 0, rank).astype(full))
    rest_own = rest_own.astype(low).reshape(pairs * 2, rows, -1)
    head_scale_grad = jnp.pad(
        grad_head_scale.reshape(-1, head_rows, 2), ((0, 0), (0, rows - head_rows), (0, 0))
    ).reshape(width, 2)
    late_grad = jnp.pad(head_scale_grad, ((0, 0), (6, 120)))
    last, pair_grad, late_grad = weight_grad(
        ranks, pairs * 2, [normed_all], grad_qkv, head_all, gain[0][:, None], late_grad
    )
    last, pair_grad, late_grad, grad_qkv = lax.optimization_barrier(
        (last, pair_grad, late_grad, grad_qkv)
    )
    late_sum = take(late_grad, 1, rank).astype(full)
    for k in range(1, ranks):
        late_sum = late_sum + permute(take(late_grad, 1, relative[k]), "seq", k).astype(full)
    small_at = rest_own.shape[2] - 128
    rest_own = jnp.concatenate(
        [
            rest_own[:, :, :small_at],
            (rest_own[:, :, small_at:].astype(full) + late_sum).astype(low),
        ],
        2,
    )
    x_part = mm_nt(grad_qkv, qkv_map).astype(low)

    if ranks == 4:
        gain_row = jnp.broadcast_to(gain[0], (8, width))
        x_parts = x_part.reshape(ranks, block, width)
        extras = (x_parts, x_here, x_local, grad_mixed, gain_row)
        side = rank % 2 * 2
        mine = lax.dynamic_slice_in_dim(pair_grad, side, 2, 1)
        other = permute(lax.dynamic_slice_in_dim(pair_grad, 2 - side, 2, 1), "seq", 1)
        pair_grad = (mine.astype(full) + other.astype(full)).astype(low)
        *sums, input_grad = finish(sizes, last, out_grad, rest_own, pair_grad, extras)
    else:
        sums = finish(sizes, last, out_grad, rest_own, pair_grad)
        grad_x_normed = x_here + sum_seq(cut(x_part), ranks)
        grad_tokens_norm = norm_back(tokens, x_inverse, gain[0], grad_x_normed)[0]
        input_grad = grad_mixed * root_half + grad_tokens_norm
    small_sum = sums[6]

    grad_mlp = jnp.concatenate([in_sum, down_sum[:, None]], 1).astype(full)
    lead = (block, 1, width)
    return (
        hidden_out.reshape(lead),
        input_grad.reshape(lead),
        *sums[:4],
        sums[5],
        sums[4],
        small_sum[:, :6],
        small_sum[:head_rows, 6:8],
        grad_mlp,
    )


def solution(mesh):
    sizes = {"seq": mesh.shape["seq"], "pair": mesh.shape["fsdp"] // 2, "core": 2}
    spread = P(("seq", "fsdp"), None)
    tokens = P("seq", "fsdp", None)
    return jax.shard_map(
        functools.partial(body, sizes),
        mesh=mesh,
        in_specs=(tokens, tokens, P("seq", "fsdp"), P("seq", "fsdp"), tokens)
        + (spread,) * 8
        + (P("fsdp", None, "seq"),),
        out_specs=(tokens, tokens) + (spread,) * 8 + (P("fsdp", None, "seq"),),
        check_vma=False,
    )
```
